32 devices in a mesh: leaf: 4 (over z), seq: 8 (over y, x, core).
Axes of the slice: x: 2, y: 2, z: 4, core: 2. Of those that a mesh axis runs over, the one named last changes fastest.
Arguments:
- tokens: bfloat16 [4, 2048, 768], P('leaf', 'seq'), may hold values from -6 to 6
- cotangent: bfloat16 [4, 2048, 768], P('leaf', 'seq'), may hold values from -6 to 6
- timesteps: int32 [4], replicated, may hold values from 0 to 999
- parent: int32 [4, 8], P('leaf'), may hold values from 0 to 4, as said below
- positions: int32 [4, 2048], P('leaf', 'seq'), may hold values from 0 to 1535, as said below
- block_live: int32 [4, 8, 4], P('leaf'), may hold values from 0 to 1, as said below
- qkv_weight: bfloat16 [768, 2304], P(('leaf', 'seq')), may hold values from -0.21875 to 0.21875
- out_weight: bfloat16 [768, 768], P(('leaf', 'seq')), may hold values from -3.5 to 3.5
- up_weight: bfloat16 [768, 3072], P(('leaf', 'seq')), may hold values from -0.21875 to 0.21875
- down_weight: bfloat16 [3072, 768], P(('leaf', 'seq')), may hold values from -0.109375 to 0.109375
- mod_weight: bfloat16 [768, 4608], P(('leaf', 'seq')), may hold values from -0.4375 to 0.4375
Outputs:
- layer_out: bfloat16 [4, 2048, 768], P('leaf', 'seq')
- grad_tokens: float32 [4, 2048, 768], P('leaf', 'seq')
- grad_qkv: float32 [768, 2304], P(('leaf', 'seq'))
- grad_out: float32 [768, 768], P(('leaf', 'seq'))
- grad_up: float32 [768, 3072], P(('leaf', 'seq'))
- grad_down: float32 [3072, 768], P(('leaf', 'seq'))
- grad_mod: float32 [768, 4608], P(('leaf', 'seq'))
The draws below stay inside these ranges and needn't reach their ends.
Inputs may be any that keep to these rules, and one draw needn't show every extreme that they name: parent[t, 0] = 0 and parent[t, s] < s otherwise; segments 0 to 3 form a chain (parent s - 1); segment 8/2 has parent 8/2 - 1, segment 8 - 1 has parent 8/2, every other later segment's parent is 3 or 4. `positions`: 256 times the number of strict ancestors of the token's segment, plus the token's index in its segment. `block_live`: every block of segments 0 to 3 is live; a later segment has 1 to 4 live blocks, its first ones; segment 8 - 1 has exactly one.
All inputs are finite; a program needn't handle non-finite values.
Results may differ from the reference program's by a relative error of at most 0.015.
The reference program's roundings to bfloat16 on the way count: a program that leaves them out, or rounds other values in their place, can miss the bound.
Values may be sent and summed in bfloat16 or wider, within the bound.
A program may use at most 192 MiB of HBM per device.

```python
import math
from functools import partial
import jax
import jax.numpy as jnp
from jax import lax

D = 768
HEADS = 12
FF = 3072
TOK_DEV = 256
NBLK = 4
SEGS = 8
TREES = 4
TREE_TOK = 2048


def tree_layout(key):
    base = jax.random.fold_in(key, 7)
    seg_range = jnp.arange(SEGS, dtype=jnp.int32)
    trunk_len = SEGS // 2
    lowest = trunk_len - 1
    picked = jax.random.randint(jax.random.fold_in(base, 1), (TREES, SEGS), lowest, lowest + 2, dtype=jnp.int32)
    picked = jnp.where(seg_range[None, :] == trunk_len, lowest, picked)
    picked = jnp.where(seg_range[None, :] == SEGS - 1, trunk_len, picked)
    chain = jnp.maximum(seg_range - 1, 0)
    parent = jnp.where(seg_range[None, :] < trunk_len, chain[None, :], picked).astype(jnp.int32)

    def deepen(step_index, depth):
        above = parent[:, step_index]
        found = jnp.take_along_axis(depth, above[:, None], axis=1)[:, 0] + 1
        return depth.at[:, step_index].set(found)
    depth = lax.fori_loop(1, SEGS, deepen, jnp.zeros((TREES, SEGS), jnp.int32))
    counts = jax.random.randint(jax.random.fold_in(base, 2), (TREES, SEGS), 1, NBLK + 1, dtype=jnp.int32)
    counts = jnp.where(seg_range[None, :] < trunk_len, NBLK, counts)
    counts = jnp.where(seg_range[None, :] == SEGS - 1, 1, counts)
    live = (jnp.arange(NBLK, dtype=jnp.int32)[None, None, :] < counts[..., None]).astype(jnp.int32)
    places = depth[:, :, None] * TOK_DEV + jnp.arange(TOK_DEV, dtype=jnp.int32)[None, None, :]
    return (parent, places.reshape(TREES, TREE_TOK).astype(jnp.int32), live)


def draw_parent(key, part):
    return tree_layout(key)[0]


def draw_positions(key, part):
    return tree_layout(key)[1]


def draw_block_live(key, part):
    return tree_layout(key)[2]


def plant(result, key, least, largest):
    shape = result.shape
    index_at = [jax.random.randint(jax.random.fold_in(key, axis), (), 0, shape[axis]) for axis in range(len(shape))]
    result = result.at[tuple(index_at)].set(least)
    longest = shape.index(max(shape))
    index_at[longest] = (index_at[longest] + 1) % shape[longest]
    return result.at[tuple(index_at)].set(largest)


def steps_of(key, shape, cuts, low, high):
    level, own = 1.0, jax.random.fold_in(key, 6)
    for position, blocks in cuts:
        steps = jnp.exp(jax.random.uniform(jax.random.fold_in(own, position), (blocks,), jnp.float32, low / len(cuts), high / len(cuts)))
        level = level * jnp.repeat(steps, shape[position] // blocks).reshape([-1 if axis == position else 1 for axis in range(len(shape))])
    return level


def bell_draw(stream_key, extent, scale, most, cuts=(), held_as=jnp.bfloat16):
    values = jax.random.normal(stream_key, extent, jnp.float32) * scale
    if len(cuts) > 0:
        values = steps_of(stream_key, extent, cuts, -0.22, 0.18) * values
    return jnp.clip(values, min=-most, max=most).astype(held_as)


def setup_inputs(seed: int = 0) -> dict:
    key_list = jax.random.split(jax.random.key(seed), 12)
    tokens = bell_draw(key_list[0], (TREES, TREE_TOK, D), 1.0, 6.0, ((0, 4), (1, 8)))
    cotangent = bell_draw(key_list[1], (TREES, TREE_TOK, D), 1.0, 6.0, ((0, 4), (1, 8)))
    timesteps = plant(jax.random.randint(key_list[2], (TREES,), 0, 1000), jax.random.fold_in(key_list[2], 1), 0, 999).astype(jnp.int32)
    parent = draw_parent(jax.random.fold_in(key_list[11], 71), 0)
    positions = draw_positions(jax.random.fold_in(key_list[11], 71), 0)
    block_live = draw_block_live(jax.random.fold_in(key_list[11], 71), 0)
    qkv_weight = bell_draw(key_list[6], (D, 3 * D), D ** -0.5, 0.21875, ((0, 32),))
    out_weight = bell_draw(key_list[7], (D, D), 3 ** -0.5, 3.5, ((0, 32),))
    up_weight = bell_draw(key_list[8], (D, FF), D ** -0.5, 0.21875, ((0, 32),))
    down_weight = bell_draw(key_list[9], (FF, D), FF ** -0.5, 0.109375, ((0, 32),))
    mod_weight = bell_draw(key_list[10], (D, 6 * D), (D // 4) ** -0.5, 0.4375, ((0, 32),))
    return {"tokens": tokens, "cotangent": cotangent, "timesteps": timesteps, "parent": parent, "positions": positions, "block_live": block_live, "qkv_weight": qkv_weight, "out_weight": out_weight, "up_weight": up_weight, "down_weight": down_weight, "mod_weight": mod_weight}


@jax.custom_vjp
def low(v):
    return lax.optimization_barrier(v.astype(jnp.bfloat16)).astype(jnp.float32)

@jax.custom_vjp
def low_back(v):
    return v

def low_keep(v):
    return (low(v), None)

def low_pass(kept, grad):
    return (grad,)

def back_keep(v):
    return (v, None)

def back_low(kept, grad):
    return (low(grad),)
low.defvjp(low_keep, low_pass)
low_back.defvjp(back_keep, back_low)
EPSILON = 1e-06
NEGATIVE = -1e+30
HIGHEST = lax.Precision.HIGHEST

def matmul(left, right):
    return jnp.dot(left, right, precision=HIGHEST, preferred_element_type=jnp.float32)

def layer_norm(values):
    centred = values - lax.optimization_barrier(jnp.mean(values, axis=-1, keepdims=True))
    variance = lax.optimization_barrier(jnp.mean(centred * centred, axis=-1, keepdims=True))
    return centred * lax.rsqrt(variance + EPSILON)

def time_embed(step_values, model_width):
    half_width = model_width // 2
    freqs = jnp.exp(-math.log(10000.0) * jnp.arange(half_width, dtype=jnp.float32) / half_width)
    angles = step_values.astype(jnp.float32)[..., None] * freqs
    return jnp.concatenate([jnp.cos(angles), jnp.sin(angles)], axis=-1)

def rope_tables(places, head_dim):
    half_dim = head_dim // 2
    inverse = jnp.exp(-math.log(10000.0) * 2.0 * jnp.arange(half_dim, dtype=jnp.float32) / head_dim)
    angles = places.astype(jnp.float32)[:, None] * inverse[None, :]
    return (jnp.cos(angles), jnp.sin(angles))

def rotate(values, cosine, sine):
    half_dim = values.shape[-1] // 2
    first = values[..., :half_dim]
    second = values[..., half_dim:]
    cos_wide = cosine[:, None, :]
    sin_wide = sine[:, None, :]
    return jnp.concatenate([first * cos_wide - second * sin_wide, second * cos_wide + first * sin_wide], axis=-1)

def tree_layer(weights, tree_in):
    qkv_weight, out_weight, up_weight, down_weight, mod_weight = weights
    tree_tokens, step_value, allowed, places = tree_in
    model_width = tree_tokens.shape[-1]
    head_dim = model_width // HEADS
    condition = low(jax.nn.silu(time_embed(step_value, model_width)))
    modulation = matmul(condition[None, :], mod_weight)[0]
    shift_a, scale_a, gate_a, shift_b, scale_b, gate_b = jnp.split(modulation, 6)
    hidden_a = low(layer_norm(tree_tokens) * (1.0 + scale_a) + shift_a)
    projected = low_back(matmul(hidden_a, qkv_weight)).reshape(-1, 3, HEADS, head_dim)
    cosine, sine = rope_tables(places, head_dim)
    queries = low(rotate(projected[:, 0], cosine, sine))
    keys_rot = low(rotate(projected[:, 1], cosine, sine))
    values = low(projected[:, 2])
    score_scale = head_dim ** (-0.5)

    def attend_block(block_in):
        query_block, allow_row = block_in
        scores = jnp.einsum('qhd,khd->hqk', query_block, keys_rot, precision=HIGHEST)
        scores = low_back(scores * score_scale)
        scores = jnp.where(allow_row[None, None, :], scores, NEGATIVE)
        probs = low(jax.nn.softmax(scores, axis=-1))
        return jnp.einsum('hqk,khd->qhd', probs, values, precision=HIGHEST)
    blocks = lax.map(jax.checkpoint(attend_block), (queries.reshape(SEGS, TOK_DEV, HEADS, head_dim), allowed))
    attended = low(low_back(blocks.reshape(-1, model_width)))
    branch_a = low_back(matmul(attended, out_weight))
    middle = tree_tokens + gate_a * branch_a
    hidden_b = low(layer_norm(middle) * (1.0 + scale_b) + shift_b)
    upper = low_back(matmul(hidden_b, up_weight))
    active = low(jax.nn.gelu(upper))
    branch_b = low_back(matmul(active, down_weight))
    return middle + gate_b * branch_b

def reference(tokens, cotangent, timesteps, parent, positions, block_live, qkv_weight, out_weight, up_weight, down_weight, mod_weight):
    seg_range = jnp.arange(SEGS, dtype=jnp.int32)

    def climb(step_index, state_now):
        current, reached = state_now
        current = jnp.take_along_axis(parent, current, axis=1)
        return (current, reached | (current[..., None] == seg_range))
    start_state = (jnp.broadcast_to(seg_range, (TREES, SEGS)).astype(jnp.int32), jnp.broadcast_to(seg_range[:, None] == seg_range[None, :], (TREES, SEGS, SEGS)))
    ancestors = lax.fori_loop(0, SEGS, climb, start_state)[1]
    live_tokens = jnp.repeat(block_live > 0, TOK_DEV // NBLK, axis=2)
    allowed = (ancestors[..., None] & live_tokens[:, None, :, :]).reshape(TREES, SEGS, TREE_TOK)

    def forward(tokens_f, qkv_f, out_f, up_f, down_f, mod_f):
        weights = (qkv_f, out_f, up_f, down_f, mod_f)
        return lax.map(jax.checkpoint(partial(tree_layer, weights)), (tokens_f, timesteps, allowed, positions))
    outputs, pull = jax.vjp(forward, tokens.astype(jnp.float32), qkv_weight.astype(jnp.float32), out_weight.astype(jnp.float32), up_weight.astype(jnp.float32), down_weight.astype(jnp.float32), mod_weight.astype(jnp.float32))
    grads = pull(cotangent.astype(jnp.float32))
    return (outputs.astype(jnp.bfloat16), grads[0], grads[1], grads[2], grads[3], grads[4], grads[5])
```

```python
import functools
import math

import jax
import jax.numpy as jnp
from jax import lax
from jax.experimental import pallas as pl
from jax.experimental.pallas import tpu as pltpu
from jax.sharding import PartitionSpec as P

MESH = pl.DeviceIdType.MESH

HEADS = 12


EPSILON = 1e-06
NEGATIVE = -1e30


def layer_norm(values):
    centred = values - jnp.mean(values, axis=-1, keepdims=True)
    variance = jnp.mean(centred * centred, axis=-1, keepdims=True)
    return centred * lax.rsqrt(variance + EPSILON)


def time_embed(step_values, model_width):
    half_width = model_width // 2
    freqs = jnp.exp(-math.log(10000.0) * jnp.arange(half_width, dtype=jnp.float32) / half_width)
    angles = step_values.astype(jnp.float32)[..., None] * freqs
    return jnp.concatenate([jnp.cos(angles), jnp.sin(angles)], axis=-1)


def rope_tables(places, head_dim):
    half_dim = head_dim // 2
    inverse = jnp.exp(-math.log(10000.0) * 2.0 * jnp.arange(half_dim, dtype=jnp.float32) / head_dim)
    angles = places.astype(jnp.float32)[:, None] * inverse[None, :]
    return (jnp.cos(angles), jnp.sin(angles))


def rotate(values, cosine, sine):
    half_dim = values.shape[-1] // 2
    first = values[..., :half_dim]
    second = values[..., half_dim:]
    cos_wide = cosine[:, None, :]
    sin_wide = sine[:, None, :]
    return jnp.concatenate(
        [first * cos_wide - second * sin_wide, second * cos_wide + first * sin_wide], axis=-1
    )


def rotate_back(grads, cosine, sine):
    half_dim = grads.shape[-1] // 2
    first = grads[..., :half_dim]
    second = grads[..., half_dim:]
    cos_wide = cosine[:, None, :]
    sin_wide = sine[:, None, :]
    return jnp.concatenate(
        [first * cos_wide + second * sin_wide, second * cos_wide - first * sin_wide], axis=-1
    )


def ancestor_row(parent_row, seg_index, seg_count):
    seg_range = jnp.arange(seg_count, dtype=jnp.int32)

    def climb(step_index, state_now):
        current, reached = state_now
        current = parent_row[current]
        return (current, reached | (seg_range == current))

    return lax.fori_loop(0, seg_count, climb, (seg_index, seg_range == seg_index))[1]


def attend_keys(state_now, query_rot, key_block, value_block, key_ok, score_scale):
    maximum_old, total_old, accum_old = state_now
    scores = (
        jnp.einsum("qhd,khd->hqk", query_rot, key_block, preferred_element_type=jnp.float32)
        * score_scale
    )
    visible = key_ok[None, None, :]
    scores = jnp.where(visible, scores, NEGATIVE)
    maximum_new = jnp.maximum(maximum_old, jnp.max(scores, axis=-1))
    weights_p = jnp.where(visible, jnp.exp(scores - maximum_new[..., None]), 0.0)
    rescale = jnp.exp(maximum_old - maximum_new)
    total_new = total_old * rescale + jnp.sum(weights_p, axis=-1)
    accum_new = accum_old * rescale[..., None] + jnp.einsum(
        "hqk,khd->hqd",
        weights_p.astype(jnp.bfloat16),
        value_block,
        preferred_element_type=jnp.float32,
    )
    return (maximum_new, total_new, accum_new)


def score_grads(
    query_rot, grad_attended, log_total, delta_rows, key_block, value_block, mask_wide, score_scale
):
    scores = (
        jnp.einsum("qhd,khd->hqk", query_rot, key_block, preferred_element_type=jnp.float32)
        * score_scale
    )
    probs = jnp.where(mask_wide, jnp.exp(scores - log_total[..., None]), 0.0)
    grad_probs = jnp.einsum(
        "qhd,khd->hqk", grad_attended, value_block, preferred_element_type=jnp.float32
    )
    grad_scores = (probs * (grad_probs - delta_rows[..., None])).astype(jnp.bfloat16)
    return (probs, grad_scores)


def query_only(
    grad_query,
    query_rot,
    grad_attended,
    log_total,
    delta_rows,
    key_block,
    value_block,
    key_ok,
    score_scale,
):
    probs, grad_scores = score_grads(
        query_rot,
        grad_attended,
        log_total,
        delta_rows,
        key_block,
        value_block,
        key_ok[None, None, :],
        score_scale,
    )
    return (
        grad_query
        + jnp.einsum("hqk,khd->qhd", grad_scores, key_block, preferred_element_type=jnp.float32)
        * score_scale
    )


def rdma(src,dst,ss,rs,dev):
    return pltpu.make_async_remote_copy(src_ref=src,dst_ref=dst,send_sem=ss,recv_sem=rs,device_id=dev,device_id_type=MESH)

def ag_kernel(L,S,NW,mode,*refs):
    sh=refs[:NW]; G=refs[NW:2*NW];
    loc,zs,zr,ps,pr,ds_,dr,ss,sr=refs[2*NW:]
    l=lax.axis_index("leaf"); s=lax.axis_index("seq")
    c=lax.rem(s,2); p=s//2; Pn=S//2
    sib=s+1-2*c
    bar=pltpu.get_barrier_semaphore()
    zp=[lax.rem(l+k,L) for k in range(1,L)]
    if mode=="fwd":
        px=p+1-2*lax.rem(p,2); py=lax.rem(p+2,4); pd=lax.rem(px+2,4)
        peers=[px,py]
    else:
        peers=[lax.rem(p+k,Pn) for k in range(1,Pn)]
    n=0
    for q in zp: pl.semaphore_signal(bar,inc=1,device_id=(q,s),device_id_type=MESH); n+=1
    for q in peers: pl.semaphore_signal(bar,inc=1,device_id=(l,2*q+c),device_id_type=MESH); n+=1
    pl.semaphore_signal(bar,inc=1,device_id=(l,sib),device_id_type=MESH); n+=1
    pl.semaphore_wait(bar,n)
    zsend=[];
    for w in range(NW):
        pltpu.make_async_copy(sh[w],G[w].at[l,s],loc.at[w]).start()
        for k,q in enumerate(zp):
            d=rdma(sh[w],G[w].at[l,s],zs.at[w,k],zr.at[w,k],(q,s)); d.start(); zsend.append(d)
    def pcopy(w,q,k):
        return rdma(G[w].at[:,s],G[w].at[:,s],ps.at[w,k],pr.at[w,k],(l,2*q+c))
    def scopy(w,q,k):
        return rdma(G[w].at[:,2*q+c],G[w].at[:,2*q+c],ss.at[w,k],sr.at[w,k],(l,sib))
    def start1(w):
        pltpu.make_async_copy(sh[w],G[w].at[l,s],loc.at[w]).wait()
        for k,q in enumerate(zp):
            rdma(sh[w],G[w].at[l,s],zs.at[w,k],zr.at[w,k],(q,s)).wait_recv()
        for k,q in enumerate(peers): pcopy(w,q,k).start()
        scopy(w,p,0).start()
    H=L//2
    if mode=="fwd":
        def half(w,q,h):
            sl=pl.ds(h*H,H)
            to=[py,px][h]
            return rdma(G[w].at[sl,2*q+c],G[w].at[sl,2*q+c],ds_.at[w,h],dr.at[w,h],(l,2*to+c))
        def start2(w):
            for k,q in enumerate(peers):
                pcopy(w,q,k).wait_recv()
                half(w,q,k).start()
                scopy(w,q,1+k).start()
        def start3(w):
            half(w,pd,0).wait_recv(); half(w,pd,1).wait_recv()
            scopy(w,pd,3).start()
        nS=4
    else:
        def start2(w):
            for k in range(1,Pn):
                q=lax.rem(p+Pn-k,Pn)
                pcopy(w,q,k-1).wait_recv()
                scopy(w,q,k).start()
        def start3(w): pass
        nS=Pn
    stages=[start1,start2,start3]
    for t in range(NW+2):
        for i,f in enumerate(stages):
            if 0<=t-i<NW: f(t-i)
    for w in range(NW):
        for k in range(nS): scopy(w,p,k).wait_recv()
    for d in zsend: d.wait_send()
    for w in range(NW):
        for k,q in enumerate(peers): pcopy(w,q,k).wait_send()
        for k in range(nS): scopy(w,p,k).wait_send()
        if mode=="fwd":
            half(w,px,0).wait_send(); half(w,py,1).wait_send()

def ag(L,S,mode,*sh):
    NW=len(sh); Pn=S//2
    DM=pltpu.SemaphoreType.DMA
    return pl.pallas_call(functools.partial(ag_kernel,L,S,NW,mode),
      out_shape=[jax.ShapeDtypeStruct((L,S)+x.shape,x.dtype) for x in sh],
      in_specs=[pl.BlockSpec(memory_space=pltpu.HBM)]*NW,
      out_specs=[pl.BlockSpec(memory_space=pltpu.HBM)]*NW,
      scratch_shapes=[DM((NW,)),DM((NW,L-1)),DM((NW,L-1)),DM((NW,Pn)),DM((NW,Pn)),DM((NW,2)),DM((NW,2)),DM((NW,Pn)),DM((NW,Pn))],
      compiler_params=pltpu.CompilerParams(collective_id=1,has_side_effects=True))(*sh)


def gather_weights(shards):
    leaf_count, seg_count = lax.axis_size("leaf"), lax.axis_size("seq")
    if seg_count != 8:
        return [lax.all_gather(x, ("leaf", "seq"), axis=0, tiled=True) for x in shards]
    outs = ag(leaf_count, seg_count, "fwd", *shards)
    return [a.reshape(-1, a.shape[-1]) for a in outs]


def per_device(
    tokens,
    cotangent,
    timesteps,
    parent,
    positions,
    block_live,
    qkv_weight,
    out_weight,
    up_weight,
    down_weight,
    mod_weight,
):
    seg_count = lax.axis_size("seq")
    seg_index = lax.axis_index("seq")
    tree_index = lax.axis_index("leaf")
    tok_rows = tokens.shape[1]
    model_width = tokens.shape[2]
    head_count = HEADS
    head_dim = model_width // head_count
    score_scale = head_dim ** (-0.5)
    tree_rows = tok_rows * seg_count
    qkv_all, out_all, up_all, down_all = gather_weights((qkv_weight, out_weight, up_weight, down_weight))
    condition = jax.nn.silu(time_embed(timesteps, model_width)).astype(jnp.bfloat16)
    mod_rows = mod_weight.shape[0]
    first_row = (tree_index * seg_count + seg_index) * mod_rows
    cond_rows = lax.dynamic_slice_in_dim(condition, first_row, mod_rows, 1)
    mod_part = jnp.dot(cond_rows, mod_weight, preferred_element_type=jnp.float32)
    mod_sum = lax.psum(mod_part, ("leaf", "seq"))
    modulation = lax.dynamic_index_in_dim(mod_sum, tree_index, 0, keepdims=False)
    shift_a, scale_a, gate_a, shift_b, scale_b, gate_b = jnp.split(modulation, 6)
    inputs_f = tokens[0].astype(jnp.float32)
    normed_a = layer_norm(inputs_f)
    hidden_a = (normed_a * (1.0 + scale_a) + shift_a).astype(jnp.bfloat16)
    projected = jnp.dot(hidden_a, qkv_all, preferred_element_type=jnp.float32).reshape(
        tok_rows, 3, head_count, head_dim
    )
    cosine, sine = rope_tables(positions[0], head_dim)
    query_rot = rotate(projected[:, 0], cosine, sine).astype(jnp.bfloat16)
    key_rot = rotate(projected[:, 1], cosine, sine).astype(jnp.bfloat16)
    value_rows = projected[:, 2].astype(jnp.bfloat16)
    key_flat = key_rot.reshape(tok_rows, model_width)
    value_flat = value_rows.reshape(tok_rows, model_width)
    reached = ancestor_row(parent[0], seg_index, seg_count)
    live_blocks = block_live.shape[2]
    live_tokens = jnp.repeat(block_live[0] > 0, tok_rows // live_blocks, axis=1)
    key_allowed = (reached[:, None] & live_tokens).reshape(tree_rows)
    start_state = (
        jnp.full((head_count, tok_rows), NEGATIVE, jnp.float32),
        jnp.zeros((head_count, tok_rows), jnp.float32),
        jnp.zeros((head_count, tok_rows, head_dim), jnp.float32),
    )
    key_part = lax.all_gather(key_flat, "seq", axis=0, tiled=True)
    value_part = lax.all_gather(value_flat, "seq", axis=0, tiled=True)
    count_keys = key_part.shape[0]
    block_size = tok_rows
    block_count = count_keys // block_size
    allow_part = key_allowed.reshape(block_count, block_size)
    key_blocks = key_part.reshape(block_count, block_size, head_count, head_dim)
    value_blocks = value_part.reshape(block_count, block_size, head_count, head_dim)

    def advance(state_now, block_in):
        return (
            attend_keys(state_now, query_rot, block_in[0], block_in[1], block_in[2], score_scale),
            None,
        )

    maximum_run, total_run, accum_run = lax.scan(
        advance, start_state, (key_blocks, value_blocks, allow_part)
    )[0]
    attended_heads = jnp.transpose(accum_run / total_run[..., None], (1, 0, 2))
    log_total = maximum_run + jnp.log(total_run)
    attended = attended_heads.reshape(tok_rows, model_width).astype(jnp.bfloat16)
    branch_a = jnp.dot(attended, out_all, preferred_element_type=jnp.float32)
    middle = inputs_f + gate_a * branch_a
    normed_b = layer_norm(middle)
    hidden_b = (normed_b * (1.0 + scale_b) + shift_b).astype(jnp.bfloat16)
    upper = jnp.dot(hidden_b, up_all, preferred_element_type=jnp.float32)
    active = jax.nn.gelu(upper).astype(jnp.bfloat16)
    branch_b = jnp.dot(active, down_all, preferred_element_type=jnp.float32)
    layer_out = (middle + gate_b * branch_b).astype(jnp.bfloat16)
    out_back, up_back, down_back, qkv_back = out_all, up_all, down_all, qkv_all
    grad_out_rows = cotangent[0].astype(jnp.float32)
    grad_branch_b = (gate_b * grad_out_rows).astype(jnp.bfloat16)
    dgate_b = jnp.sum(grad_out_rows * branch_b, axis=0)
    grad_down = jnp.einsum("qf,qd->fd", active, grad_branch_b, preferred_element_type=jnp.float32)
    grad_active = jnp.einsum(
        "qd,fd->qf", grad_branch_b, down_back, preferred_element_type=jnp.float32
    )
    gelu_pull = jax.vjp(jax.nn.gelu, upper)[1]
    grad_upper = gelu_pull(grad_active)[0].astype(jnp.bfloat16)
    grad_up = jnp.einsum("qd,qf->df", hidden_b, grad_upper, preferred_element_type=jnp.float32)
    grad_hidden_b = jnp.einsum("qf,df->qd", grad_upper, up_back, preferred_element_type=jnp.float32)
    dshift_b = jnp.sum(grad_hidden_b, axis=0)
    dscale_b = jnp.sum(grad_hidden_b * normed_b, axis=0)
    norm_pull_b = jax.vjp(layer_norm, middle)[1]
    grad_middle = grad_out_rows + norm_pull_b(grad_hidden_b * (1.0 + scale_b))[0]
    grad_branch_a = (gate_a * grad_middle).astype(jnp.bfloat16)
    dgate_a = jnp.sum(grad_middle * branch_a, axis=0)
    grad_out = jnp.einsum("qi,qd->id", attended, grad_branch_a, preferred_element_type=jnp.float32)
    grad_attended = jnp.einsum(
        "qd,id->qi", grad_branch_a, out_back, preferred_element_type=jnp.float32
    ).astype(jnp.bfloat16)
    grad_att_heads = grad_attended.reshape(tok_rows, head_count, head_dim)
    delta_rows = jnp.einsum("qhd,qhd->hq", grad_att_heads.astype(jnp.float32), attended_heads)
    start_query = jnp.zeros((tok_rows, head_count, head_dim), jnp.float32)
    key_part = lax.all_gather(key_flat, "seq", axis=0, tiled=True)
    value_part = lax.all_gather(value_flat, "seq", axis=0, tiled=True)
    count_keys = key_part.shape[0]
    block_size = tok_rows
    block_count = count_keys // block_size
    allow_part = key_allowed.reshape(block_count, block_size)
    key_blocks = key_part.reshape(block_count, block_size, head_count, head_dim)
    value_blocks = value_part.reshape(block_count, block_size, head_count, head_dim)

    def advance(grad_now, block_in):
        return (
            query_only(
                grad_now,
                query_rot,
                grad_att_heads,
                log_total,
                delta_rows,
                block_in[0],
                block_in[1],
                block_in[2],
                score_scale,
            ),
            None,
        )

    grad_query = lax.scan(advance, start_query, (key_blocks, value_blocks, allow_part))[0]
    seg_range = jnp.arange(seg_count, dtype=jnp.int32)
    every_reach = jax.vmap(lambda one_seg: ancestor_row(parent[0], one_seg, seg_count))(seg_range)
    sees_mine = every_reach[:, seg_index]
    own_live = lax.dynamic_index_in_dim(live_tokens, seg_index, 0, keepdims=False)
    total_all, delta_all = (
        lax.all_gather(jnp.transpose(log_total), "seq", axis=0, tiled=True),
        lax.all_gather(jnp.transpose(delta_rows), "seq", axis=0, tiled=True),
    )
    query_flat = query_rot.reshape(tok_rows, model_width)
    grad_key_acc = jnp.zeros((tok_rows, head_count, head_dim), jnp.float32)
    grad_value_acc = jnp.zeros((tok_rows, head_count, head_dim), jnp.float32)
    query_part = lax.all_gather(query_flat, "seq", axis=0, tiled=True)
    grad_part = lax.all_gather(grad_attended, "seq", axis=0, tiled=True)
    count_rows = query_part.shape[0]
    block_size = tok_rows
    block_count = count_rows // block_size
    row_seg = jnp.arange(count_rows, dtype=jnp.int32) // tok_rows
    row_ok = sees_mine[row_seg].reshape(block_count, block_size)
    total_part = total_all.reshape(block_count, block_size, head_count)
    delta_part = delta_all.reshape(block_count, block_size, head_count)
    query_blocks = query_part.reshape(block_count, block_size, head_count, head_dim)
    grad_blocks = grad_part.reshape(block_count, block_size, head_count, head_dim)

    def advance(acc_now, block_in):
        key_acc, value_acc = acc_now
        query_block, grad_block, total_block, delta_block, ok_block = block_in
        mask_wide = ok_block[None, :, None] & own_live[None, None, :]
        probs, grad_scores = score_grads(
            query_block,
            grad_block,
            jnp.transpose(total_block),
            jnp.transpose(delta_block),
            key_rot,
            value_rows,
            mask_wide,
            score_scale,
        )
        key_acc = (
            key_acc
            + jnp.einsum(
                "hqk,qhd->khd", grad_scores, query_block, preferred_element_type=jnp.float32
            )
            * score_scale
        )
        value_acc = value_acc + jnp.einsum(
            "hqk,qhd->khd",
            probs.astype(jnp.bfloat16),
            grad_block,
            preferred_element_type=jnp.float32,
        )
        return ((key_acc, value_acc), None)

    grad_key_rows, grad_value_heads = lax.scan(
        advance,
        (grad_key_acc, grad_value_acc),
        (query_blocks, grad_blocks, total_part, delta_part, row_ok),
    )[0]
    grad_value_rows = grad_value_heads.reshape(tok_rows, model_width)
    grad_query_pre = rotate_back(grad_query, cosine, sine).reshape(tok_rows, model_width)
    grad_key_pre = rotate_back(grad_key_rows, cosine, sine).reshape(tok_rows, model_width)
    grad_projected = jnp.concatenate(
        [grad_query_pre, grad_key_pre, grad_value_rows], axis=-1
    ).astype(jnp.bfloat16)
    grad_qkv = jnp.einsum("qi,qj->ij", hidden_a, grad_projected, preferred_element_type=jnp.float32)
    grad_hidden_a = jnp.einsum(
        "qj,ij->qi", grad_projected, qkv_back, preferred_element_type=jnp.float32
    )
    dshift_a = jnp.sum(grad_hidden_a, axis=0)
    dscale_a = jnp.sum(grad_hidden_a * normed_a, axis=0)
    norm_pull_a = jax.vjp(layer_norm, inputs_f)[1]
    grad_tokens = grad_middle + norm_pull_a(grad_hidden_a * (1.0 + scale_a))[0]
    grad_modulation = jnp.concatenate([dshift_a, dscale_a, dgate_a, dshift_b, dscale_b, dgate_b])
    sum_qkv, sum_out, sum_up, sum_down = (
        lax.psum_scatter(
            grad.astype(jnp.bfloat16), ("leaf", "seq"), scatter_dimension=0, tiled=True
        ).astype(jnp.float32)
        for grad in (grad_qkv, grad_out, grad_up, grad_down)
    )
    tree_grads = lax.psum(grad_modulation, "seq")
    tree_grads = lax.all_gather(tree_grads, "leaf", axis=0)
    sum_mod = jnp.einsum("tr,tc->rc", cond_rows.astype(jnp.float32), tree_grads, precision=lax.Precision.HIGHEST)
    return (layer_out[None], grad_tokens[None], sum_qkv, sum_out, sum_up, sum_down, sum_mod)


def solution(mesh):
    placed = (
        P("leaf", "seq", None),
        P("leaf", "seq", None),
        P(),
        P("leaf", None),
        P("leaf", "seq"),
        P("leaf", None, None),
        P(("leaf", "seq"), None),
        P(("leaf", "seq"), None),
        P(("leaf", "seq"), None),
        P(("leaf", "seq"), None),
        P(("leaf", "seq"), None),
    )
    return jax.shard_map(
        per_device,
        mesh=mesh,
        in_specs=placed,
        out_specs=(
            P("leaf", "seq", None),
            P("leaf", "seq", None),
            P(("leaf", "seq"), None),
            P(("leaf", "seq"), None),
            P(("leaf", "seq"), None),
            P(("leaf", "seq"), None),
            P(("leaf", "seq"), None),
        ),
        check_vma=False,
    )
```

```python
import functools, math
import jax, jax.numpy as jnp
from jax import lax
from jax.experimental import pallas as pl
from jax.experimental.pallas import tpu as pltpu
from jax.sharding import PartitionSpec as P

MESH = pl.DeviceIdType.MESH
HEADS = 12
EPSILON = 1e-06
NEGATIVE = -1e30
F32 = jnp.float32
BF16 = jnp.bfloat16
GELU_A = math.sqrt(2.0 / math.pi)
GELU_B = 0.044715


class Sems:
    def __init__(self, ref):
        self.ref, self.used = ref, 0

    def one(self):
        self.used += 1
        return self.ref.at[self.used - 1]


class Place:
    def __init__(self, leaf_count, seg_count):
        self.L, self.S = leaf_count, seg_count
        self.P = seg_count // 2
        self.l, self.s = lax.axis_index("leaf"), lax.axis_index("seq")
        self.c, self.p = lax.rem(self.s, 2), self.s // 2
        self.sib = self.s + 1 - 2 * self.c
        self.px = self.p + 1 - 2 * lax.rem(self.p, 2)
        self.py = lax.rem(self.p + 2, 4)
        self.pd = lax.rem(self.px + 2, 4)
        self.others = [self.px, self.py, self.pd]

    def at_leaf(self, k):
        return (lax.rem(self.l + k, self.L), self.s)

    def at_chip(self, q):
        return (self.l, 2 * q + self.c)

    def at_sib(self):
        return (self.l, self.sib)

    def barrier(self):
        sem = pltpu.get_barrier_semaphore()
        peers = [self.at_leaf(k) for k in range(1, self.L)]
        peers += [self.at_chip(q) for q in self.others] + [self.at_sib()]
        for peer in peers:
            pl.semaphore_signal(sem, inc=1, device_id=peer, device_id_type=MESH)
        pl.semaphore_wait(sem, len(peers))


class Wires:
    def __init__(self, send_sems, recv_sems, local_sems):
        self.send_sems, self.recv_sems, self.local_sems = Sems(send_sems), Sems(recv_sems), Sems(local_sems)
        self.open = []

    def make(self, src, dst, dev):
        return pltpu.make_async_remote_copy(
            src_ref=src, dst_ref=dst, send_sem=self.send_sems.one(), recv_sem=self.recv_sems.one(),
            device_id=dev, device_id_type=MESH)

    def send(self, src, dst, dev):
        copy = self.make(src, dst, dev)
        copy.start()
        self.open.append(copy)
        return copy

    def local(self, src, dst):
        copy = pltpu.make_async_copy(src, dst, self.local_sems.one())
        copy.start()
        return copy

    def drain(self):
        for copy in self.open:
            copy.wait_send()
        self.open = []


class Gather:
    def __init__(self, wires, at, shard, full, fine):
        self.w, self.at, self.shard, self.full, self.fine = wires, at, shard, full, fine
        count = shard.shape[0]
        self.rows = pl.ds(pl.multiple_of(at.c * count, 8), count)

    def begin(self):
        w, at = self.w, self.at
        mine = self.full.at[at.l, at.p, self.rows]
        self.own = w.local(self.shard, mine)
        self.z = [w.send(self.shard, mine, at.at_leaf(k)) for k in range(1, at.L)]
        self.sib = []
        self.plane = []

    def view(self, unit, chip):
        if self.fine:
            return self.full.at[lax.rem(self.at.l + self.at.L - unit, self.at.L), chip, self.rows]
        return self.full.at[:, chip, self.rows]

    def stage1(self, unit):
        w, at = self.w, self.at
        if self.fine:
            if unit:
                self.z[unit - 1].wait_recv()
        else:
            for copy in self.z:
                copy.wait_recv()
            self.own.wait()
        mine = self.view(unit, at.p)
        src = self.shard if self.fine and unit == 0 else mine
        self.plane.append([w.send(src, mine, at.at_chip(q)) for q in (at.px, at.py)])
        self.sib.append(w.send(src, mine, at.at_sib()))

    def stage2(self, unit):
        w, at = self.w, self.at
        half = at.L // 2
        self.diag = getattr(self, "diag", {})
        for i, (q, to) in enumerate(((at.px, at.py), (at.py, at.px))):
            self.plane[unit][i].wait_recv()
            theirs = self.view(unit, q)
            if self.fine:
                if unit % 2 == i:
                    self.diag[unit, i] = w.send(theirs, theirs, at.at_chip(to))
            else:
                part = self.full.at[pl.ds(i * half, half), q, self.rows]
                self.diag[unit, i] = w.send(part, part, at.at_chip(to))
            self.sib.append(w.send(theirs, theirs, at.at_sib()))

    def stage3(self, unit):
        w, at = self.w, self.at
        for i in range(2):
            if (unit, i) in self.diag:
                self.diag[unit, i].wait_recv()
        theirs = self.view(unit, at.pd)
        self.sib.append(w.send(theirs, theirs, at.at_sib()))

    def finish(self):
        if self.fine:
            self.own.wait()
        for copy in self.sib:
            copy.wait_recv()


def norm_rows(values):
    centred = values - jnp.mean(values, axis=-1, keepdims=True)
    variance = jnp.mean(centred * centred, axis=-1, keepdims=True)
    rstd = lax.rsqrt(variance + EPSILON)
    return centred * rstd, rstd


def dot(left, right):
    return jnp.dot(left, right, preferred_element_type=F32)


def dot_t(left, right):
    return lax.dot_general(left, right, (((1,), (1,)), ((), ())), preferred_element_type=F32)


def forward(at, w, R):
    L, S, PC = at.L, at.S, at.P
    T, D = R.tok.shape
    HD = D // HEADS
    HG = HEADS // PC
    GW = HG * HD
    gq = Gather(w, at, R.wq, R.Gq, True)
    go = Gather(w, at, R.wo, R.Go, False)
    gu = Gather(w, at, R.wu, R.Gu, False)
    gd = Gather(w, at, R.wd, R.Gd, False)
    at.barrier()
    gq.begin()
    gq.stage1(0)
    part = dot(R.cond[...], R.modw[...])
    for t in range(L):
        R.mpart[t] = part[t : t + 1, :]
    mz = [w.send(R.mpart.at[lax.rem(at.l + k, L)], R.mz.at[k - 1], at.at_leaf(k)) for k in range(1, L)]
    go.begin()
    gu.begin()
    gd.begin()
    tok = R.tok[...].astype(F32)
    normed, _ = norm_rows(tok)
    for u in range(1, L):
        gq.stage1(u)
    for copy in mz:
        copy.wait_recv()
    total = R.mpart[at.l]
    for k in range(L - 1):
        total = total + R.mz[k]
    R.m1[...] = total
    mp = [w.send(R.m1, R.mp.at[i], at.at_chip(q)) for i, q in enumerate(at.others)]
    gq.stage2(0)
    for copy in mp:
        copy.wait_recv()
    for i in range(3):
        total = total + R.mp[i]
    R.m2[...] = total
    ms = w.send(R.m2, R.ms, at.at_sib())
    for u in range(1, L):
        gq.stage2(u)
    ms.wait_recv()
    R.mod[...] = total + R.ms[...]
    shift_a, scale_a = R.mod[:, 0:D], R.mod[:, D : 2 * D]
    R.hidden_a[...] = (normed * (1.0 + scale_a) + shift_a).astype(BF16)
    R.haT2[0] = R.hidden_a[...].T
    sib_ha = w.send(R.haT2.at[0], R.haT2.at[1], at.at_sib())
    for u in range(L):
        gq.stage3(u)
    gq.finish()
    load = w.local(R.Gq.reshape(D, 3 * D), R.Wq)
    load.wait()
    cosine, sine = R.cos[...], R.sin[...]
    TN = 256
    for j in range(3 * D // TN):
        kind = j * TN // D
        rows = dot(R.hidden_a[...], R.Wq[:, j * TN : (j + 1) * TN]).T
        for i in range(TN // HD):
            head = (j * TN % D) // HD + i
            group, row = head // HG, (head % HG) * HD
            first, second = rows[i * HD : i * HD + HD // 2], rows[i * HD + HD // 2 : (i + 1) * HD]
            if kind < 2:
                first, second = first * cosine - second * sine, second * cosine + first * sine
            if kind == 0:
                first, second = first * HD**-0.5, second * HD**-0.5
            R.snd[group, kind, row : row + HD // 2] = first.astype(BF16)
            R.snd[group, kind, row + HD // 2 : row + HD] = second.astype(BF16)
    kv = [w.send(R.snd.at[q, 1:3], R.KVT.at[at.s], at.at_chip(q)) for q in at.others]
    own_kv = w.local(R.snd.at[at.p, 1:3], R.KVT.at[at.s])
    qs = [w.send(R.snd.at[q, 0], R.QT.at[at.p], at.at_chip(q)) for q in at.others]
    own_q = w.local(R.snd.at[at.p, 0], R.QT.at[at.p])
    go.stage1(0)
    gu.stage1(0)
    gd.stage1(0)
    own_kv.wait()
    sk = [w.send(R.KVT.at[at.s], R.KVT.at[at.s], at.at_sib())]
    for copy, q in zip(kv, at.others):
        copy.wait_recv()
        seg = 2 * q + at.c
        sk.append(w.send(R.KVT.at[seg], R.KVT.at[seg], at.at_sib()))
    own_q.wait()
    for copy in qs:
        copy.wait_recv()
    for copy in sk:
        copy.wait_recv()
    go.stage2(0)

    def flip(a, carry):
        for h in range(HG):
            R.kN[a, h] = R.KVT[a, 0, h * HD : (h + 1) * HD, :].T
        return carry

    lax.fori_loop(0, S, flip, 0)
    trunk = S // 2
    ret = []
    for i, q in enumerate([at.pd, at.px, at.py, at.p]):
        seg = 2 * q + at.c

        def block(j, state, q=q, seg=seg):
            a = jnp.where(j > trunk, seg, j)
            out = []
            for h in range(HG):
                m, t, o = state[3 * h : 3 * h + 3]
                score = dot(R.kN[a, h], R.QT[q, h * HD : (h + 1) * HD, :])
                nblk = R.btab.shape[1] // S
                bt = T // nblk
                score = jnp.concatenate(
                    [score[b * bt : (b + 1) * bt] + R.btab[seg, a * nblk + b] for b in range(nblk)], axis=0)
                m_new = jnp.maximum(m, jnp.max(score, axis=0, keepdims=True))
                alpha = jnp.exp(m - m_new)
                e = jnp.exp(score - m_new)
                t = t * alpha + jnp.sum(e, axis=0, keepdims=True)
                o = o * alpha + dot(R.KVT[a, 1, h * HD : (h + 1) * HD, :], e.astype(BF16))
                out += [m_new, t, o]
            return tuple(out)

        start = (jnp.full((1, T), NEGATIVE, F32), jnp.zeros((1, T), F32), jnp.zeros((HD, T), F32)) * HG
        count = jnp.minimum(seg, trunk) + 1 + jnp.where(seg > trunk, 1, 0)
        state = lax.fori_loop(0, count, block, start)
        for h in range(HG):
            m, t, o = state[3 * h : 3 * h + 3]
            o = o / t
            R.OT[q, h * HD : (h + 1) * HD, :] = o
            R.asnd[q, h * HD : (h + 1) * HD, :] = o.astype(BF16)
            R.lse[q, h : h + 1, :] = m + jnp.log(t)
        if i < 3:
            ret.append(w.send(R.asnd.at[q], R.attT2.at[0, at.p], at.at_chip(q)))
        else:
            own_att = w.local(R.asnd.at[q], R.attT2.at[0, at.p])
        if i == 1:
            go.stage3(0)
    gu.stage2(0)
    go.finish()
    load = w.local(R.Go.reshape(D, D), R.Wo)
    own_att.wait()
    for copy in ret:
        copy.wait_recv()
    load.wait()
    sib_att = w.send(R.attT2.at[0], R.attT2.at[1], at.at_sib())
    att = jnp.concatenate([R.attT2[0, g].T for g in range(PC)], axis=1)
    gate_a = R.mod[:, 2 * D : 3 * D]
    for j in range(0, D, 256):
        branch = dot(att, R.Wo[:, j : j + 256])
        R.br_a[:, j : j + 256] = branch
        R.middle[:, j : j + 256] = R.tok[:, j : j + 256].astype(F32) + gate_a[:, j : j + 256] * branch
    shift_b, scale_b, gate_b = (R.mod[:, i * D : (i + 1) * D] for i in (3, 4, 5))
    normed, _ = norm_rows(R.middle[...])
    R.hidden_b[...] = (normed * (1.0 + scale_b) + shift_b).astype(BF16)
    R.hbT2[0] = R.hidden_b[...].T
    sib_hb = w.send(R.hbT2.at[0], R.hbT2.at[1], at.at_sib())
    gu.stage3(0)
    gu.finish()
    load = w.local(R.Gu.reshape(D, R.Wu.shape[1]), R.Wu)
    gd.stage2(0)
    load.wait()
    FF = R.Wu.shape[1]

    def up(j, carry):
        at_j = pl.ds(pl.multiple_of(j * 256, 256), 256)
        u = dot(R.hidden_b[...], R.Wu[:, at_j])
        square = u * u
        tanh = jnp.tanh(GELU_A * (u + GELU_B * square * u))
        act = (0.5 * u * (1.0 + tanh)).astype(BF16)
        R.active[:, at_j] = act
        R.actT2[0, at_j, :] = act.T
        slope = 0.5 * (1.0 + tanh) + (0.5 * GELU_A) * u * (1.0 - tanh * tanh) * (1.0 + 3.0 * GELU_B * square)
        R.slope[:, at_j] = slope.astype(BF16)
        return carry

    lax.fori_loop(0, FF // 256, up, 0)
    sib_act = w.send(R.actT2.at[0], R.actT2.at[1], at.at_sib())
    gd.stage3(0)
    gd.finish()
    load = w.local(R.Gd.reshape(FF, D), R.Wd)
    load.wait()
    for j in range(0, D, 256):
        branch = dot(R.active[...], R.Wd[:, j : j + 256])
        R.br_b[:, j : j + 256] = branch
        R.lo[:, j : j + 256] = (R.middle[:, j : j + 256] + gate_b[:, j : j + 256] * branch).astype(BF16)
    for copy in (sib_ha, sib_att, sib_hb, sib_act):
        copy.wait_recv()


class Refs:
    def __init__(self, **refs):
        self.__dict__.update(refs)


def call_forward(L, S, tok, cond, modw, cosT, sinT, btab, wq, wo, wu, wd):
    T, D = tok.shape
    FF = wu.shape[1]
    PC = S // 2
    HG = HEADS // PC
    HD = D // HEADS
    GW = HG * HD
    ins = dict(tok=tok, cond=cond, modw=modw, cos=cosT, sin=sinT, btab=btab, wq=wq, wo=wo, wu=wu, wd=wd)
    sd = jax.ShapeDtypeStruct
    outs = dict(
        Gq=sd((L, PC, 2 * wq.shape[0], wq.shape[1]), BF16), Go=sd((L, PC, 2 * wo.shape[0], wo.shape[1]), BF16), Gu=sd((L, PC, 2 * wu.shape[0], wu.shape[1]), BF16), Gd=sd((L, PC, 2 * wd.shape[0], wd.shape[1]), BF16),
        lo=sd((T, D), BF16), mod=sd((1, 6 * D), F32), haT2=sd((2, D, T), BF16), attT2=sd((2, PC, GW, T), BF16),
        middle=sd((T, D), F32), br_a=sd((T, D), F32), hbT2=sd((2, D, T), BF16), actT2=sd((2, FF, T), BF16), slope=sd((T, FF), BF16),
        br_b=sd((T, D), F32), QT=sd((PC, GW, T), BF16), KVT=sd((S, 2, GW, T), BF16), OT=sd((PC, GW, T), F32), lse=sd((PC, 8, T), F32))
    NS = 160
    DM = pltpu.SemaphoreType.DMA
    V = pltpu.VMEM
    scr = dict(
        Wq=V((D, 3 * D), BF16), Wo=V((D, D), BF16), Wu=V((D, FF), BF16), Wd=V((FF, D), BF16),
        mpart=V((L, 1, 6 * D), F32), mz=V((L - 1, 1, 6 * D), F32), m1=V((1, 6 * D), F32), mp=V((3, 1, 6 * D), F32), m2=V((1, 6 * D), F32), ms=V((1, 6 * D), F32),
        hidden_a=V((T, D), BF16), hidden_b=V((T, D), BF16), active=V((T, FF), BF16), snd=V((PC, 3, GW, T), BF16),
        kN=V((S, HG, T, HD), BF16), asnd=V((PC, GW, T), BF16),
        send_sems=DM((NS,)), recv_sems=DM((NS,)), local_sems=DM((16,)))
    hbm = pl.BlockSpec(memory_space=pltpu.HBM)
    vm = pl.BlockSpec(memory_space=pltpu.VMEM)
    sm = pl.BlockSpec(memory_space=pltpu.SMEM)

    def kernel(*refs):
        names = list(ins) + list(outs) + list(scr)
        R = Refs(**dict(zip(names, refs)))
        at = Place(L, S)
        w = Wires(R.send_sems, R.recv_sems, R.local_sems)
        R.mp1 = None
        forward(at, w, R)
        w.drain()

    res = pl.pallas_call(
        kernel, out_shape=list(outs.values()),
        in_specs=[hbm if k in ("wq", "wo", "wu", "wd") else sm if k == "btab" else vm for k in ins],
        out_specs=[hbm if k in ("Gq", "Go", "Gu", "Gd") else vm for k in outs],
        scratch_shapes=list(scr.values()),
        compiler_params=pltpu.CompilerParams(collective_id=1, has_side_effects=True, vmem_limit_bytes=60 << 20),
    )(*ins.values())
    return dict(zip(outs, res))


def time_embed(step_values, model_width):
    half_width = model_width // 2
    freqs = jnp.exp(-math.log(10000.0) * jnp.arange(half_width, dtype=jnp.float32) / half_width)
    angles = step_values.astype(jnp.float32)[..., None] * freqs
    return jnp.concatenate([jnp.cos(angles), jnp.sin(angles)], axis=-1)

def tree_bias(parent_row, live):
    seg_count = parent_row.shape[0]
    seg_range = jnp.arange(seg_count, dtype=jnp.int32)
    step = (parent_row[:, None] == seg_range[None, :]).astype(F32)
    reach = jnp.eye(seg_count, dtype=F32)
    reach = jnp.minimum(reach + step, 1.0)
    hops = 1
    while hops < seg_count:
        reach = jnp.minimum(jnp.dot(reach, reach), 1.0)
        hops *= 2
    seen = (reach > 0.5)[:, :, None] & (live > 0)[None, :, :]
    return jnp.where(seen, 0.0, NEGATIVE).astype(F32).reshape(seg_count, -1)

def prepare(L, S, timesteps, parent, positions, block_live, mod_rows, model_width):
    l, s = lax.axis_index("leaf"), lax.axis_index("seq")
    condition = jax.nn.silu(time_embed(timesteps, model_width)).astype(BF16)
    first = (l * S + s) * mod_rows
    cond_rows = lax.dynamic_slice_in_dim(condition, first, mod_rows, 1)
    cond_pad = jnp.zeros((8, mod_rows), BF16).at[:L].set(cond_rows)
    head_dim = model_width // HEADS
    half_dim = head_dim // 2
    inverse = jnp.exp(-math.log(10000.0) * 2.0 * jnp.arange(half_dim, dtype=F32) / head_dim)
    angles = inverse[:, None] * positions[0].astype(F32)[None, :]
    return cond_rows, cond_pad, jnp.cos(angles), jnp.sin(angles), tree_bias(parent[0], block_live[0])


def add_to(ref, *others):
    total = ref[...].astype(F32)
    for other in others:
        total = total + other[...].astype(F32)
    ref[...] = total.astype(ref.dtype)


class Scatter:
    def __init__(self, wires, at, A, dg, xy, zr, fin, sibr, out):
        self.w, self.at, self.H = wires, at, at.L // 2
        self.A, self.dg, self.xy, self.zr, self.fin, self.sibr, self.out = A, dg, xy, zr, fin, sibr, out

    def step1(self):
        w, at, A, H = self.w, self.at, self.A, self.H
        lo, hi = pl.ds(0, H), pl.ds(H, H)
        self.d = [w.send(A.at[lo, at.pd], self.dg.at[0], at.at_chip(at.px)), w.send(A.at[hi, at.pd], self.dg.at[1], at.at_chip(at.py))]
        self.x = [w.send(A.at[lo, at.px], self.xy.at[0, lo], at.at_chip(at.px)), w.send(A.at[hi, at.py], self.xy.at[1, hi], at.at_chip(at.py))]

    def step2(self):
        w, at, A, H = self.w, self.at, self.A, self.H
        lo, hi = pl.ds(0, H), pl.ds(H, H)
        self.d[0].wait_recv()
        for i in range(H):
            add_to(A.at[i, at.py], self.dg.at[0, i])
        self.x.append(w.send(A.at[lo, at.py], self.xy.at[1, lo], at.at_chip(at.py)))
        self.d[1].wait_recv()
        for i in range(H):
            add_to(A.at[H + i, at.px], self.dg.at[1, i])
        self.x.append(w.send(A.at[hi, at.px], self.xy.at[0, hi], at.at_chip(at.px)))

    def step3(self):
        w, at, A = self.w, self.at, self.A
        for copy in self.x:
            copy.wait_recv()
        for i in range(at.L):
            add_to(A.at[i, at.p], self.xy.at[0, i], self.xy.at[1, i])
        self.z = []
        for k in range(1, at.L):
            leaf = lax.rem(at.l + k, at.L)
            self.z.append(w.send(A.at[leaf, at.p], self.zr.at[k - 1], at.at_leaf(k)))

    def step4(self):
        w, at = self.w, self.at
        for copy in self.z:
            copy.wait_recv()
        total = self.A[at.l, at.p].astype(F32)
        for k in range(at.L - 1):
            total = total + self.zr[k].astype(F32)
        self.fin[...] = total
        rows = self.fin.shape[0] // 2
        self.f = w.send(self.fin.at[pl.ds(pl.multiple_of(rows * (1 - at.c), 8), rows)], self.sibr, at.at_sib())

    def step5(self):
        at = self.at
        rows, half = self.sibr.shape
        mine = self.fin[pl.ds(pl.multiple_of(rows * at.c, 8), rows), :]
        self.out[:, pl.ds(pl.multiple_of(half * at.c, 128), half)] = mine
        self.f.wait_recv()
        self.out[:, pl.ds(pl.multiple_of(half * (1 - at.c), 128), half)] = self.sibr[...]


def norm_back(grad, normed, rstd):
    return rstd * (grad - jnp.mean(grad, axis=-1, keepdims=True) - normed * jnp.mean(grad * normed, axis=-1, keepdims=True))


def total_rows(values):
    return jnp.sum(values, axis=0, keepdims=True)


def backward(at, w, R):
    L, S, PC = at.L, at.S, at.P
    T, D = R.tok.shape
    HD = D // HEADS
    HG = HEADS // PC
    FF = R.Wu.shape[1]
    NB = R.btab.shape[1] // S
    at.barrier()
    load_d = w.local(R.Gd.reshape(FF, D), R.Wd)
    load_u = w.local(R.Gu.reshape(D, FF), R.Wu)
    load_o = w.local(R.Go.reshape(D, D), R.Wo)
    scat = {n: Scatter(w, at, *(getattr(R, x + n) for x in ("A", "dg", "xy", "zr", "fin", "sr", "o"))) for n in "qoud"}
    part = lambda i: slice(i * D, (i + 1) * D)
    gate_a, scale_b, gate_b, scale_a = R.mod[:, part(2)], R.mod[:, part(4)], R.mod[:, part(5)], R.mod[:, part(1)]
    g = R.g[...].astype(F32)
    dbb = (gate_b * g).astype(BF16)
    R.dbb[...] = dbb
    for h in range(2):
        R.dbbh[h] = dbb[:, h * D // 2 : (h + 1) * D // 2]
    sib_dbb = w.send(R.dbbh.at[1 - at.c], R.dbbs, at.at_sib())
    R.gm[:, part(5)] = total_rows(g * R.br_b[...])
    load_d.wait()
    HF = FF // 2
    for h in range(2):
        def act(j, carry, h=h):
            lanes = pl.ds(pl.multiple_of(j * 256, 256), 256)
            wide = pl.ds(pl.multiple_of(h * HF + j * 256, 256), 256)
            da = dot_t(R.dbb[...], R.Wd[wide, :])
            R.du[h, :, lanes] = (da * R.slope[:, wide].astype(F32)).astype(BF16)
            return carry

        lax.fori_loop(0, HF // 256, act, 0)
    sib_du = w.send(R.du.at[1 - at.c], R.dus, at.at_sib())
    load_u.wait()
    for j in range(0, D, 256):
        R.dh[:, j : j + 256] = dot_t(R.du[0], R.Wu[j : j + 256, 0:HF]) + dot_t(R.du[1], R.Wu[j : j + 256, HF:FF])
    load_q = w.local(R.Gq.reshape(D, 3 * D), R.Wq)
    dh = R.dh[...]
    normed, rstd = norm_rows(R.middle[...])
    R.gm[:, part(3)] = total_rows(dh)
    R.gm[:, part(4)] = total_rows(dh * normed)
    dmid = R.g[...].astype(F32) + norm_back(dh * (1.0 + scale_b), normed, rstd)
    R.dmid[...] = dmid
    R.gm[:, part(2)] = total_rows(dmid * R.br_a[...])
    dba = (gate_a * dmid).astype(BF16)
    R.dba[...] = dba
    for h in range(2):
        R.dbah[h] = dba[:, h * D // 2 : (h + 1) * D // 2]
    sib_dba = w.send(R.dbah.at[1 - at.c], R.dbas, at.at_sib())
    load_o.wait()
    GW = HG * HD
    for j in range(PC):
        R.dosnd[j] = dot_t(R.Wo[j * GW : (j + 1) * GW, :], R.dba[...]).astype(BF16)
    dos = [w.send(R.dosnd.at[q], R.dOT.at[at.p], at.at_chip(q)) for q in at.others]
    own_do = w.local(R.dosnd.at[at.p], R.dOT.at[at.p])
    sib_dbb.wait_recv()
    RB = FF // (L * PC)

    def down(i, carry):
        rows = pl.ds(pl.multiple_of(i * RB, RB), RB)
        block = dot(R.actT2[0, rows, :], R.dbbh[at.c]) + dot(R.actT2[1, rows, :], R.dbbs[...])
        R.Ad[i // PC, lax.rem(i, PC)] = block.astype(BF16)
        return carry

    lax.fori_loop(0, L * PC, down, 0)
    scat["d"].step1()
    RB2 = D // (L * PC)

    def split(A, lanes, block):
        for i in range(L * PC):
            A[i // PC, i % PC, :, lanes] = block[i * RB2 : (i + 1) * RB2].astype(BF16)

    sib_du.wait_recv()

    def up(j, carry):
        lanes = pl.ds(pl.multiple_of(j * 256, 256), 256)
        split(R.Au, lanes, dot(R.hbT2[0], R.du[at.c, :, lanes]) + dot(R.hbT2[1], R.dus[:, lanes]))
        return carry

    lax.fori_loop(0, HF // 256, up, 0)
    scat["u"].step1()
    sib_dba.wait_recv()
    attT = [R.attT2[i].reshape(D, T) for i in range(2)]
    split(R.Ao, slice(0, D // 2), dot(attT[0], R.dbah[at.c]) + dot(attT[1], R.dbas[...]))
    scat["o"].step1()

    def flip(a, carry):
        for h in range(HG):
            rows = slice(h * HD, (h + 1) * HD)
            R.kN[a, h] = R.KVT[a, 0, rows, :].T
            R.vN[a, h] = R.KVT[a, 1, rows, :].T
            R.acc[a, 0, rows, :] = jnp.zeros((HD, T), F32)
            R.acc[a, 1, rows, :] = jnp.zeros((HD, T), F32)
        return carry

    lax.fori_loop(0, S, flip, 0)
    trunk = S // 2
    own_do.wait()
    back_q = []
    order = [at.p, at.px, at.py, at.pd]
    for i, q in enumerate(order):
        seg = 2 * q + at.c
        if i:
            dos[i - 1].wait_recv()
        delta = [total_rows(R.dOT[q, h * HD : (h + 1) * HD, :].astype(F32) * R.OT[q, h * HD : (h + 1) * HD, :]) for h in range(HG)]

        def block(j, dqs, q=q, seg=seg, delta=delta):
            a = jnp.where(j > trunk, seg, j)
            out = []
            for h in range(HG):
                rows = slice(h * HD, (h + 1) * HD)
                qT, dO = R.QT[q, rows, :], R.dOT[q, rows, :]
                score = dot(R.kN[a, h], qT)
                bt = T // NB
                score = jnp.concatenate(
                    [score[b * bt : (b + 1) * bt] + R.btab[seg, a * NB + b] for b in range(NB)], axis=0)
                prob = jnp.exp(score - R.lse[q, h : h + 1, :])
                dprob = dot(R.vN[a, h], dO)
                ds = (prob * (dprob - delta[h])).astype(BF16)
                out.append(dqs[h] + dot(R.KVT[a, 0, rows, :], ds))
                R.acc[a, 0, rows, :] += dot_t(qT, ds)
                R.acc[a, 1, rows, :] += dot_t(dO, prob.astype(BF16))
            return tuple(out)

        count = jnp.minimum(seg, trunk) + 1 + jnp.where(seg > trunk, 1, 0)
        dqs = lax.fori_loop(0, count, block, (jnp.zeros((HD, T), F32),) * HG)
        for h in range(HG):
            R.bsnd[q, 0, h * HD : (h + 1) * HD, :] = dqs[h].astype(BF16)
        if i:
            back_q.append(w.send(R.bsnd.at[q, 0], R.brcv.at[at.p, 0], at.at_chip(q)))
        else:
            own_q = w.local(R.bsnd.at[q, 0], R.brcv.at[at.p, 0])
        if i == 0:
            scat["d"].step2()
        if i == 1:
            scat["u"].step2()
            scat["o"].step2()
        if i == 2:
            scat["d"].step3()
    NK = PC // 2 + 1
    sk = [w.send(R.acc.at[2 * k + 1 - at.c], R.acs.at[k], at.at_sib()) for k in range(NK)]
    for copy in sk:
        copy.wait_recv()
    for k in range(PC):
        for i in range(2):
            grad = R.acc[2 * k + at.c, i]
            if k < NK:
                grad = grad + R.acs[k, i]
            R.bsnd[k, 1 + i] = grad.astype(BF16)
    back_kv = [w.send(R.bsnd.at[q, 1:3], R.brcv.at[at.p, 1:3], at.at_chip(q)) for q in at.others]
    own_kv = w.local(R.bsnd.at[at.p, 1:3], R.brcv.at[at.p, 1:3])
    scat["u"].step3()
    scat["o"].step3()
    own_q.wait()
    own_kv.wait()
    for copy in back_q + back_kv:
        copy.wait_recv()
    cosine, sine = R.cos[...], R.sin[...]
    HP = 3 * D // 2
    for kind in range(3):
        for head in range(HEADS):
            row = (head % HG) * HD
            both = R.brcv[head // HG, kind, row : row + HD, :].astype(F32)
            if kind < 2:
                first, second = both[: HD // 2], both[HD // 2 :]
                first, second = first * cosine + second * sine, second * cosine - first * sine
                both = jnp.concatenate([first, second], axis=0)
            if kind == 0:
                both = both * HD**-0.5
            at_row = kind * D + head * HD
            R.dpT[at_row // HP, at_row % HP : at_row % HP + HD, :] = both.astype(BF16)
    sib_dp = w.send(R.dpT.at[1 - at.c], R.dps, at.at_sib())
    sib_dp.wait_recv()
    NW = 384
    def qkv(j, carry):
        lanes = pl.ds(pl.multiple_of(j * NW, 128), NW)
        split(R.Aq, lanes, dot_t(R.haT2[0], R.dpT[at.c, lanes, :]) + dot_t(R.haT2[1], R.dps[lanes, :]))
        return carry

    lax.fori_loop(0, HP // NW, qkv, 0)
    scat["q"].step1()
    load_q.wait()
    for j in range(0, D, 256):
        dhT = dot(R.Wq[j : j + 256, 0:HP], R.dpT[0]) + dot(R.Wq[j : j + 256, HP : 2 * HP], R.dpT[1])
        R.dh[:, j : j + 256] = dhT.T
    scat["q"].step2()
    dh = R.dh[...]
    normed, rstd = norm_rows(R.tok[...].astype(F32))
    R.gm[:, part(0)] = total_rows(dh)
    R.gm[:, part(1)] = total_rows(dh * normed)
    gsib = w.send(R.gm, R.gs, at.at_sib())
    R.gt[...] = R.dmid[...] + norm_back(dh * (1.0 + scale_a), normed, rstd)
    gsib.wait_recv()
    R.g1[...] = R.gm[...] + R.gs[...]
    gp = [w.send(R.g1, R.gp.at[i], at.at_chip(q)) for i, q in enumerate(at.others)]
    scat["q"].step3()
    for copy in gp:
        copy.wait_recv()
    total = R.g1[...]
    for i in range(3):
        total = total + R.gp[i]
    R.gtree[at.l] = total
    gz = [w.send(R.gtree.at[at.l], R.gtree.at[at.l], at.at_leaf(k)) for k in range(1, L)]
    for n in "duo":
        scat[n].step4()
    for n in "duo":
        scat[n].step5()
    for copy in gz:
        copy.wait_recv()
    total = R.condT[:, 0:1] * R.gtree[0]
    for t in range(1, L):
        total = total + R.condT[:, t : t + 1] * R.gtree[t]
    R.om[...] = total
    scat["q"].step4()
    scat["q"].step5()


def call_backward(L, S, g, tok, condT, cosT, sinT, btab, f):
    T, D = tok.shape
    FF = f["slope"].shape[1]
    PC, HD = S // 2, D // HEADS
    HG = HEADS // PC
    GW = HG * HD
    H = L // 2
    ins = dict(g=g, tok=tok, condT=condT, cos=cosT, sin=sinT, btab=btab)
    ins.update({k: v for k, v in f.items() if k != "lo"})
    sd = jax.ShapeDtypeStruct
    DM = pltpu.SemaphoreType.DMA
    V = pltpu.VMEM
    NM = L * S
    outs = dict(gt=sd((T, D), F32), oq=sd((D // NM, 3 * D), F32), oo=sd((D // NM, D), F32), ou=sd((D // NM, FF), F32),
                od=sd((FF // NM, D), F32), om=sd((D // NM, 6 * D), F32))
    scr = dict(
        Wd=V((FF, D), BF16), Wu=V((D, FF), BF16), Wo=V((D, D), BF16), Wq=V((D, 3 * D), BF16),
        dbb=V((T, D), BF16), dbbh=V((2, T, D // 2), BF16), dbbs=V((T, D // 2), BF16),
        du=V((2, T, FF // 2), BF16), dus=V((T, FF // 2), BF16), dh=V((T, D), F32), dmid=V((T, D), F32),
        dba=V((T, D), BF16), dbah=V((2, T, D // 2), BF16), dbas=V((T, D // 2), BF16),
        dosnd=V((PC, GW, T), BF16), dOT=V((PC, GW, T), BF16), kN=V((S, HG, T, HD), BF16), vN=V((S, HG, T, HD), BF16),
        acc=V((S, 2, GW, T), F32), acs=V((PC // 2 + 1, 2, GW, T), F32), bsnd=V((PC, 3, GW, T), BF16), brcv=V((PC, 3, GW, T), BF16),
        dpT=V((2, 3 * D // 2, T), BF16), dps=V((3 * D // 2, T), BF16),
        gm=V((1, 6 * D), F32), gs=V((1, 6 * D), F32), g1=V((1, 6 * D), F32), gp=V((3, 1, 6 * D), F32), gtree=V((L, 1, 6 * D), F32))
    for n, rows, cols in (("q", D, 3 * D), ("o", D, D), ("u", D, FF), ("d", FF, D)):
        rb, half = rows // (L * PC), cols // 2
        scr["A" + n] = V((L, PC, rb, half), BF16)
        scr["dg" + n] = V((2, H, rb, half), BF16)
        scr["xy" + n] = V((2, L, rb, half), BF16)
        scr["zr" + n] = V((L - 1, rb, half), BF16)
        scr["fin" + n] = V((rb, half), F32)
        scr["sr" + n] = V((rb // 2, half), F32)
    scr.update(send_sems=DM((120,)), recv_sems=DM((120,)), local_sems=DM((16,)))
    hbm = pl.BlockSpec(memory_space=pltpu.HBM)
    vm = pl.BlockSpec(memory_space=pltpu.VMEM)
    sm = pl.BlockSpec(memory_space=pltpu.SMEM)

    def kernel(*refs):
        R = Refs(**dict(zip(list(ins) + list(outs) + list(scr), refs)))
        w = Wires(R.send_sems, R.recv_sems, R.local_sems)
        backward(Place(L, S), w, R)
        w.drain()

    res = pl.pallas_call(
        kernel, out_shape=list(outs.values()),
        in_specs=[hbm if k in ("Gq", "Go", "Gu", "Gd") else sm if k == "btab" else vm for k in ins],
        out_specs=[vm for k in outs], scratch_shapes=list(scr.values()),
        compiler_params=pltpu.CompilerParams(collective_id=2, has_side_effects=True, vmem_limit_bytes=63 << 20),
    )(*ins.values())
    return dict(zip(outs, res))


def layer_norm(values):
    centred = values - jnp.mean(values, axis=-1, keepdims=True)
    variance = jnp.mean(centred * centred, axis=-1, keepdims=True)
    return centred * lax.rsqrt(variance + EPSILON)


def rope_tables(places, head_dim):
    half_dim = head_dim // 2
    inverse = jnp.exp(-math.log(10000.0) * 2.0 * jnp.arange(half_dim, dtype=jnp.float32) / head_dim)
    angles = places.astype(jnp.float32)[:, None] * inverse[None, :]
    return (jnp.cos(angles), jnp.sin(angles))


def rotate(values, cosine, sine):
    half_dim = values.shape[-1] // 2
    first = values[..., :half_dim]
    second = values[..., half_dim:]
    cos_wide = cosine[:, None, :]
    sin_wide = sine[:, None, :]
    return jnp.concatenate(
        [first * cos_wide - second * sin_wide, second * cos_wide + first * sin_wide], axis=-1
    )


def rotate_back(grads, cosine, sine):
    half_dim = grads.shape[-1] // 2
    first = grads[..., :half_dim]
    second = grads[..., half_dim:]
    cos_wide = cosine[:, None, :]
    sin_wide = sine[:, None, :]
    return jnp.concatenate(
        [first * cos_wide + second * sin_wide, second * cos_wide - first * sin_wide], axis=-1
    )


def ancestor_row(parent_row, seg_index, seg_count):
    seg_range = jnp.arange(seg_count, dtype=jnp.int32)

    def climb(step_index, state_now):
        current, reached = state_now
        current = parent_row[current]
        return (current, reached | (seg_range == current))

    return lax.fori_loop(0, seg_count, climb, (seg_index, seg_range == seg_index))[1]


def attend_keys(state_now, query_rot, key_block, value_block, key_ok, score_scale):
    maximum_old, total_old, accum_old = state_now
    scores = (
        jnp.einsum("qhd,khd->hqk", query_rot, key_block, preferred_element_type=jnp.float32)
        * score_scale
    )
    visible = key_ok[None, None, :]
    scores = jnp.where(visible, scores, NEGATIVE)
    maximum_new = jnp.maximum(maximum_old, jnp.max(scores, axis=-1))
    weights_p = jnp.where(visible, jnp.exp(scores - maximum_new[..., None]), 0.0)
    rescale = jnp.exp(maximum_old - maximum_new)
    total_new = total_old * rescale + jnp.sum(weights_p, axis=-1)
    accum_new = accum_old * rescale[..., None] + jnp.einsum(
        "hqk,khd->hqd",
        weights_p.astype(jnp.bfloat16),
        value_block,
        preferred_element_type=jnp.float32,
    )
    return (maximum_new, total_new, accum_new)


def score_grads(
    query_rot, grad_attended, log_total, delta_rows, key_block, value_block, mask_wide, score_scale
):
    scores = (
        jnp.einsum("qhd,khd->hqk", query_rot, key_block, preferred_element_type=jnp.float32)
        * score_scale
    )
    probs = jnp.where(mask_wide, jnp.exp(scores - log_total[..., None]), 0.0)
    grad_probs = jnp.einsum(
        "qhd,khd->hqk", grad_attended, value_block, preferred_element_type=jnp.float32
    )
    grad_scores = (probs * (grad_probs - delta_rows[..., None])).astype(jnp.bfloat16)
    return (probs, grad_scores)


def query_only(
    grad_query,
    query_rot,
    grad_attended,
    log_total,
    delta_rows,
    key_block,
    value_block,
    key_ok,
    score_scale,
):
    probs, grad_scores = score_grads(
        query_rot,
        grad_attended,
        log_total,
        delta_rows,
        key_block,
        value_block,
        key_ok[None, None, :],
        score_scale,
    )
    return (
        grad_query
        + jnp.einsum("hqk,khd->qhd", grad_scores, key_block, preferred_element_type=jnp.float32)
        * score_scale
    )


def layer_native(
    tokens,
    cotangent,
    timesteps,
    parent,
    positions,
    block_live,
    qkv_weight,
    out_weight,
    up_weight,
    down_weight,
    mod_weight,
):
    seg_count = lax.axis_size("seq")
    seg_index = lax.axis_index("seq")
    tree_index = lax.axis_index("leaf")
    tok_rows = tokens.shape[1]
    model_width = tokens.shape[2]
    head_count = HEADS
    head_dim = model_width // head_count
    score_scale = head_dim ** (-0.5)
    tree_rows = tok_rows * seg_count
    qkv_all, out_all, up_all, down_all = (
        lax.all_gather(qkv_weight, ("leaf", "seq"), axis=0, tiled=True),
        lax.all_gather(out_weight, ("leaf", "seq"), axis=0, tiled=True),
        lax.all_gather(up_weight, ("leaf", "seq"), axis=0, tiled=True),
        lax.all_gather(down_weight, ("leaf", "seq"), axis=0, tiled=True),
    )
    condition = jax.nn.silu(time_embed(timesteps, model_width)).astype(jnp.bfloat16)
    mod_all = lax.all_gather(mod_weight, ("leaf", "seq"), axis=0, tiled=True)
    cond_own = lax.dynamic_index_in_dim(condition, tree_index, 0, keepdims=False)
    modulation = jnp.dot(cond_own[None, :], mod_all, preferred_element_type=jnp.float32)[0]
    shift_a, scale_a, gate_a, shift_b, scale_b, gate_b = jnp.split(modulation, 6)
    inputs_f = tokens[0].astype(jnp.float32)
    normed_a = layer_norm(inputs_f)
    hidden_a = (normed_a * (1.0 + scale_a) + shift_a).astype(jnp.bfloat16)
    projected = jnp.dot(hidden_a, qkv_all, preferred_element_type=jnp.float32).reshape(
        tok_rows, 3, head_count, head_dim
    )
    cosine, sine = rope_tables(positions[0], head_dim)
    query_rot = rotate(projected[:, 0], cosine, sine).astype(jnp.bfloat16)
    key_rot = rotate(projected[:, 1], cosine, sine).astype(jnp.bfloat16)
    value_rows = projected[:, 2].astype(jnp.bfloat16)
    key_flat = key_rot.reshape(tok_rows, model_width)
    value_flat = value_rows.reshape(tok_rows, model_width)
    reached = ancestor_row(parent[0], seg_index, seg_count)
    live_blocks = block_live.shape[2]
    live_tokens = jnp.repeat(block_live[0] > 0, tok_rows // live_blocks, axis=1)
    key_allowed = (reached[:, None] & live_tokens).reshape(tree_rows)
    start_state = (
        jnp.full((head_count, tok_rows), NEGATIVE, jnp.float32),
        jnp.zeros((head_count, tok_rows), jnp.float32),
        jnp.zeros((head_count, tok_rows, head_dim), jnp.float32),
    )
    key_part = lax.all_gather(key_flat, "seq", axis=0, tiled=True)
    value_part = lax.all_gather(value_flat, "seq", axis=0, tiled=True)
    count_keys = key_part.shape[0]
    block_size = tok_rows
    block_count = count_keys // block_size
    allow_part = key_allowed.reshape(block_count, block_size)
    key_blocks = key_part.reshape(block_count, block_size, head_count, head_dim)
    value_blocks = value_part.reshape(block_count, block_size, head_count, head_dim)

    def advance(state_now, block_in):
        return (
            attend_keys(state_now, query_rot, block_in[0], block_in[1], block_in[2], score_scale),
            None,
        )

    maximum_run, total_run, accum_run = lax.scan(
        advance, start_state, (key_blocks, value_blocks, allow_part)
    )[0]
    attended_heads = jnp.transpose(accum_run / total_run[..., None], (1, 0, 2))
    log_total = maximum_run + jnp.log(total_run)
    attended = attended_heads.reshape(tok_rows, model_width).astype(jnp.bfloat16)
    branch_a = jnp.dot(attended, out_all, preferred_element_type=jnp.float32)
    middle = inputs_f + gate_a * branch_a
    normed_b = layer_norm(middle)
    hidden_b = (normed_b * (1.0 + scale_b) + shift_b).astype(jnp.bfloat16)
    upper = jnp.dot(hidden_b, up_all, preferred_element_type=jnp.float32)
    active = jax.nn.gelu(upper).astype(jnp.bfloat16)
    branch_b = jnp.dot(active, down_all, preferred_element_type=jnp.float32)
    layer_out = (middle + gate_b * branch_b).astype(jnp.bfloat16)
    qkv_back, out_back, up_back, down_back = (
        lax.all_gather(qkv_weight, ("leaf", "seq"), axis=0, tiled=True),
        lax.all_gather(out_weight, ("leaf", "seq"), axis=0, tiled=True),
        lax.all_gather(up_weight, ("leaf", "seq"), axis=0, tiled=True),
        lax.all_gather(down_weight, ("leaf", "seq"), axis=0, tiled=True),
    )
    grad_out_rows = cotangent[0].astype(jnp.float32)
    grad_branch_b = (gate_b * grad_out_rows).astype(jnp.bfloat16)
    dgate_b = jnp.sum(grad_out_rows * branch_b, axis=0)
    grad_down = jnp.einsum("qf,qd->fd", active, grad_branch_b, preferred_element_type=jnp.float32)
    grad_active = jnp.einsum(
        "qd,fd->qf", grad_branch_b, down_back, preferred_element_type=jnp.float32
    )
    gelu_pull = jax.vjp(jax.nn.gelu, upper)[1]
    grad_upper = gelu_pull(grad_active)[0].astype(jnp.bfloat16)
    grad_up = jnp.einsum("qd,qf->df", hidden_b, grad_upper, preferred_element_type=jnp.float32)
    grad_hidden_b = jnp.einsum("qf,df->qd", grad_upper, up_back, preferred_element_type=jnp.float32)
    dshift_b = jnp.sum(grad_hidden_b, axis=0)
    dscale_b = jnp.sum(grad_hidden_b * normed_b, axis=0)
    norm_pull_b = jax.vjp(layer_norm, middle)[1]
    grad_middle = grad_out_rows + norm_pull_b(grad_hidden_b * (1.0 + scale_b))[0]
    grad_branch_a = (gate_a * grad_middle).astype(jnp.bfloat16)
    dgate_a = jnp.sum(grad_middle * branch_a, axis=0)
    grad_out = jnp.einsum("qi,qd->id", attended, grad_branch_a, preferred_element_type=jnp.float32)
    grad_attended = jnp.einsum(
        "qd,id->qi", grad_branch_a, out_back, preferred_element_type=jnp.float32
    ).astype(jnp.bfloat16)
    grad_att_heads = grad_attended.reshape(tok_rows, head_count, head_dim)
    delta_rows = jnp.einsum("qhd,qhd->hq", grad_att_heads.astype(jnp.float32), attended_heads)
    start_query = jnp.zeros((tok_rows, head_count, head_dim), jnp.float32)
    key_part = lax.all_gather(key_flat, "seq", axis=0, tiled=True)
    value_part = lax.all_gather(value_flat, "seq", axis=0, tiled=True)
    count_keys = key_part.shape[0]
    block_size = tok_rows
    block_count = count_keys // block_size
    allow_part = key_allowed.reshape(block_count, block_size)
    key_blocks = key_part.reshape(block_count, block_size, head_count, head_dim)
    value_blocks = value_part.reshape(block_count, block_size, head_count, head_dim)

    def advance(grad_now, block_in):
        return (
            query_only(
                grad_now,
                query_rot,
                grad_att_heads,
                log_total,
                delta_rows,
                block_in[0],
                block_in[1],
                block_in[2],
                score_scale,
            ),
            None,
        )

    grad_query = lax.scan(advance, start_query, (key_blocks, value_blocks, allow_part))[0]
    seg_range = jnp.arange(seg_count, dtype=jnp.int32)
    every_reach = jax.vmap(lambda one_seg: ancestor_row(parent[0], one_seg, seg_count))(seg_range)
    sees_mine = every_reach[:, seg_index]
    own_live = lax.dynamic_index_in_dim(live_tokens, seg_index, 0, keepdims=False)
    total_all, delta_all = (
        lax.all_gather(jnp.transpose(log_total), "seq", axis=0, tiled=True),
        lax.all_gather(jnp.transpose(delta_rows), "seq", axis=0, tiled=True),
    )
    query_flat = query_rot.reshape(tok_rows, model_width)
    grad_key_acc = jnp.zeros((tok_rows, head_count, head_dim), jnp.float32)
    grad_value_acc = jnp.zeros((tok_rows, head_count, head_dim), jnp.float32)
    query_part = lax.all_gather(query_flat, "seq", axis=0, tiled=True)
    grad_part = lax.all_gather(grad_attended, "seq", axis=0, tiled=True)
    count_rows = query_part.shape[0]
    block_size = tok_rows
    block_count = count_rows // block_size
    row_seg = jnp.arange(count_rows, dtype=jnp.int32) // tok_rows
    row_ok = sees_mine[row_seg].reshape(block_count, block_size)
    total_part = total_all.reshape(block_count, block_size, head_count)
    delta_part = delta_all.reshape(block_count, block_size, head_count)
    query_blocks = query_part.reshape(block_count, block_size, head_count, head_dim)
    grad_blocks = grad_part.reshape(block_count, block_size, head_count, head_dim)

    def advance(acc_now, block_in):
        key_acc, value_acc = acc_now
        query_block, grad_block, total_block, delta_block, ok_block = block_in
        mask_wide = ok_block[None, :, None] & own_live[None, None, :]
        probs, grad_scores = score_grads(
            query_block,
            grad_block,
            jnp.transpose(total_block),
            jnp.transpose(delta_block),
            key_rot,
            value_rows,
            mask_wide,
            score_scale,
        )
        key_acc = (
            key_acc
            + jnp.einsum(
                "hqk,qhd->khd", grad_scores, query_block, preferred_element_type=jnp.float32
            )
            * score_scale
        )
        value_acc = value_acc + jnp.einsum(
            "hqk,qhd->khd",
            probs.astype(jnp.bfloat16),
            grad_block,
            preferred_element_type=jnp.float32,
        )
        return ((key_acc, value_acc), None)

    grad_key_rows, grad_value_heads = lax.scan(
        advance,
        (grad_key_acc, grad_value_acc),
        (query_blocks, grad_blocks, total_part, delta_part, row_ok),
    )[0]
    grad_value_rows = grad_value_heads.reshape(tok_rows, model_width)
    grad_query_pre = rotate_back(grad_query, cosine, sine).reshape(tok_rows, model_width)
    grad_key_pre = rotate_back(grad_key_rows, cosine, sine).reshape(tok_rows, model_width)
    grad_projected = jnp.concatenate(
        [grad_query_pre, grad_key_pre, grad_value_rows], axis=-1
    ).astype(jnp.bfloat16)
    grad_qkv = jnp.einsum("qi,qj->ij", hidden_a, grad_projected, preferred_element_type=jnp.float32)
    grad_hidden_a = jnp.einsum(
        "qj,ij->qi", grad_projected, qkv_back, preferred_element_type=jnp.float32
    )
    dshift_a = jnp.sum(grad_hidden_a, axis=0)
    dscale_a = jnp.sum(grad_hidden_a * normed_a, axis=0)
    norm_pull_a = jax.vjp(layer_norm, inputs_f)[1]
    grad_tokens = grad_middle + norm_pull_a(grad_hidden_a * (1.0 + scale_a))[0]
    grad_modulation = jnp.concatenate([dshift_a, dscale_a, dgate_a, dshift_b, dscale_b, dgate_b])
    sum_qkv, sum_out, sum_up, sum_down = (
        lax.psum_scatter(grad_qkv, ("leaf", "seq"), scatter_dimension=0, tiled=True),
        lax.psum_scatter(grad_out, ("leaf", "seq"), scatter_dimension=0, tiled=True),
        lax.psum_scatter(grad_up, ("leaf", "seq"), scatter_dimension=0, tiled=True),
        lax.psum_scatter(grad_down, ("leaf", "seq"), scatter_dimension=0, tiled=True),
    )
    mod_term = cond_own.astype(jnp.float32)[:, None] * grad_modulation[None, :]
    sum_mod = lax.psum_scatter(mod_term, ("leaf", "seq"), scatter_dimension=0, tiled=True)
    return (layer_out[None], grad_tokens[None], sum_qkv, sum_out, sum_up, sum_down, sum_mod)


def layer_kernels(
    tokens,
    cotangent,
    timesteps,
    parent,
    positions,
    block_live,
    qkv_weight,
    out_weight,
    up_weight,
    down_weight,
    mod_weight,
):
    L, S = lax.axis_size("leaf"), lax.axis_size("seq")
    cond_rows, cond_pad, cosine, sine, bias = prepare(
        L, S, timesteps, parent, positions, block_live, mod_weight.shape[0], tokens.shape[2]
    )
    f = call_forward(L, S, tokens[0], cond_pad, mod_weight, cosine, sine, bias, qkv_weight, out_weight, up_weight, down_weight)
    b = call_backward(L, S, cotangent[0], tokens[0], cond_rows.T.astype(F32), cosine, sine, bias, f)
    return (f["lo"][None], b["gt"][None], b["oq"], b["oo"], b["ou"], b["od"], b["om"])


def solution(mesh):
    rows = P("leaf", "seq", None)
    held = P(("leaf", "seq"), None)
    placed = (rows, rows, P(), P("leaf", None), P("leaf", "seq"), P("leaf", None, None), held, held, held, held, held)
    kernels = mesh.shape["seq"] == 8 and mesh.shape["leaf"] % 2 == 0
    return jax.shard_map(
        layer_kernels if kernels else layer_native,
        mesh=mesh,
        in_specs=placed,
        out_specs=(rows, rows, held, held, held, held, held),
        check_vma=False,
    )
```

```python
import functools, math
import jax, jax.numpy as jnp
from jax import lax
from jax.experimental import pallas as pl
from jax.experimental.pallas import tpu as pltpu
from jax.sharding import PartitionSpec as P

MESH = pl.DeviceIdType.MESH
HEADS = 12
EPSILON = 1e-06
NEGATIVE = -1e30
F32 = jnp.float32
BF16 = jnp.bfloat16
GELU_A = math.sqrt(2.0 / math.pi)
GELU_B = 0.044715


class Sems:
    def __init__(self, ref):
        self.ref, self.used = ref, 0

    def one(self):
        self.used += 1
        return self.ref.at[self.used - 1]


class Place:
    def __init__(self, leaf_count, seg_count):
        self.L, self.S = leaf_count, seg_count
        self.P = seg_count // 2
        self.l, self.s = lax.axis_index("leaf"), lax.axis_index("seq")
        self.c, self.p = lax.rem(self.s, 2), self.s // 2
        self.sib = self.s + 1 - 2 * self.c
        self.px = self.p + 1 - 2 * lax.rem(self.p, 2)
        self.py = lax.rem(self.p + 2, 4)
        self.pd = lax.rem(self.px + 2, 4)
        self.others = [self.px, self.py, self.pd]

    def at_leaf(self, k):
        return (lax.rem(self.l + k, self.L), self.s)

    def at_chip(self, q):
        return (self.l, 2 * q + self.c)

    def at_sib(self):
        return (self.l, self.sib)

    def barrier(self):
        sem = pltpu.get_barrier_semaphore()
        peers = [self.at_leaf(k) for k in range(1, self.L)]
        peers += [self.at_chip(q) for q in self.others] + [self.at_sib()]
        for peer in peers:
            pl.semaphore_signal(sem, inc=1, device_id=peer, device_id_type=MESH)
        pl.semaphore_wait(sem, len(peers))


class Wires:
    def __init__(self, send_sems, recv_sems, local_sems):
        self.send_sems, self.recv_sems, self.local_sems = Sems(send_sems), Sems(recv_sems), Sems(local_sems)
        self.open = []

    def make(self, src, dst, dev):
        return pltpu.make_async_remote_copy(
            src_ref=src, dst_ref=dst, send_sem=self.send_sems.one(), recv_sem=self.recv_sems.one(),
            device_id=dev, device_id_type=MESH)

    def send(self, src, dst, dev):
        copy = self.make(src, dst, dev)
        copy.start()
        self.open.append(copy)
        return copy

    def local(self, src, dst):
        copy = pltpu.make_async_copy(src, dst, self.local_sems.one())
        copy.start()
        return copy

    def sent(self, copies):
        for copy in copies:
            copy.wait_send()
        self.open = [copy for copy in self.open if all(copy is not other for other in copies)]

    def drain(self):
        for copy in self.open:
            copy.wait_send()
        self.open = []


class Gather:
    def __init__(self, wires, at, shard, full):
        self.w, self.at, self.shard, self.full = wires, at, shard, full
        count = shard.shape[0]
        self.rows = pl.ds(pl.multiple_of(at.c * count, 8), count)
        self.sib, self.plane, self.diag = [], {}, {}

    def begin(self):
        w, at = self.w, self.at
        mine = self.view(0, at.p)
        self.own = w.local(self.shard, mine)
        self.z = [w.send(self.shard, mine, at.at_leaf(k)) for k in range(1, at.L)]

    def view(self, unit, chip):
        return self.full.at[lax.rem(self.at.l + self.at.L - unit, self.at.L), chip, self.rows]

    def stage1(self, unit):
        w, at = self.w, self.at
        if unit:
            self.z[unit - 1].wait_recv()
        mine = self.view(unit, at.p)
        src = mine if unit else self.shard
        self.plane[unit] = [w.send(src, mine, at.at_chip(q)) for q in (at.px, at.py)]
        self.sib.append(w.send(src, mine, at.at_sib()))

    def stage2(self, unit):
        w, at = self.w, self.at
        for i, (q, to) in enumerate(((at.px, at.py), (at.py, at.px))):
            self.plane[unit][i].wait_recv()
            theirs = self.view(unit, q)
            if unit % 2 == i:
                self.diag[unit] = w.send(theirs, theirs, at.at_chip(to))
            self.sib.append(w.send(theirs, theirs, at.at_sib()))

    def stage3(self, unit):
        self.diag[unit].wait_recv()
        theirs = self.view(unit, self.at.pd)
        self.sib.append(self.w.send(theirs, theirs, self.at.at_sib()))

    def finish(self):
        self.own.wait()
        for copy in self.sib:
            copy.wait_recv()


def add_to(ref, *others):
    total = ref[...].astype(F32)
    for other in others:
        total = total + other[...].astype(F32)
    ref[...] = total.astype(ref.dtype)


class Scatter:
    def __init__(self, wires, at, A, dg, xy, zr, fin, sibr, out, first):
        self.w, self.at, self.H = wires, at, at.L // 2
        self.A, self.dg, self.xy, self.zr, self.fin, self.sibr, self.out, self.first = A, dg, xy, zr, fin, sibr, out, first

    def step1(self):
        w, at, A, H = self.w, self.at, self.A, self.H
        lo, hi = pl.ds(0, H), pl.ds(H, H)
        self.d = [w.send(A.at[lo, at.pd], self.dg.at[0], at.at_chip(at.px)), w.send(A.at[hi, at.pd], self.dg.at[1], at.at_chip(at.py))]
        self.x = [w.send(A.at[lo, at.px], self.xy.at[0, lo], at.at_chip(at.px)), w.send(A.at[hi, at.py], self.xy.at[1, hi], at.at_chip(at.py))]

    def step2(self):
        w, at, A, H = self.w, self.at, self.A, self.H
        lo, hi = pl.ds(0, H), pl.ds(H, H)
        self.d[0].wait_recv()
        for i in range(H):
            add_to(A.at[i, at.py], self.dg.at[0, i])
        self.x.append(w.send(A.at[lo, at.py], self.xy.at[1, lo], at.at_chip(at.py)))
        self.d[1].wait_recv()
        for i in range(H):
            add_to(A.at[H + i, at.px], self.dg.at[1, i])
        self.x.append(w.send(A.at[hi, at.px], self.xy.at[0, hi], at.at_chip(at.px)))

    def step3(self):
        w, at, A = self.w, self.at, self.A
        for copy in self.x:
            copy.wait_recv()
        self.z = []
        for k in range(1, at.L + 1):
            leaf = lax.rem(at.l + k, at.L)
            add_to(A.at[leaf, at.p], self.xy.at[0, leaf], self.xy.at[1, leaf])
            if k < at.L:
                self.z.append(w.send(A.at[leaf, at.p], self.zr.at[k - 1], at.at_leaf(k)))

    def step4(self):
        w, at = self.w, self.at
        for copy in self.z:
            copy.wait_recv()
        total = self.A[at.l, at.p].astype(F32)
        for k in range(at.L - 1):
            total = total + self.zr[k].astype(F32)
        self.fin[...] = total
        rows = self.fin.shape[0] // 2
        self.f = w.send(self.fin.at[pl.ds(pl.multiple_of(rows * (1 - at.c), 8), rows)], self.sibr, at.at_sib())

    def step5(self):
        at = self.at
        rows, half = self.sibr.shape
        mine = self.fin[pl.ds(pl.multiple_of(rows * at.c, 8), rows), :]
        self.out[:, pl.ds(pl.multiple_of(self.first + half * at.c, 128), half)] = mine
        self.f.wait_recv()
        self.out[:, pl.ds(pl.multiple_of(self.first + half * (1 - at.c), 128), half)] = self.sibr[...]


def norm_rows(values):
    centred = values - jnp.mean(values, axis=-1, keepdims=True)
    variance = jnp.mean(centred * centred, axis=-1, keepdims=True)
    rstd = lax.rsqrt(variance + EPSILON)
    return centred * rstd, rstd


def norm_back(grad, normed, rstd):
    return rstd * (grad - jnp.mean(grad, axis=-1, keepdims=True) - normed * jnp.mean(grad * normed, axis=-1, keepdims=True))


def total_rows(values):
    return jnp.sum(values, axis=0, keepdims=True)


def dot(left, right):
    return jnp.dot(left, right, preferred_element_type=F32)


def dot_t(left, right):
    return lax.dot_general(left, right, (((1,), (1,)), ((), ())), preferred_element_type=F32)


def tile(j, size):
    return pl.ds(pl.multiple_of(j * size, size), size)


def condition_column(at, timestep, count, width):
    half = width // 2
    row = (at.l * at.S + at.s) * count + lax.broadcasted_iota(jnp.int32, (count, 1), 0)
    index = jnp.where(row < half, row, row - half).astype(F32)
    angle = timestep.astype(F32) * jnp.exp(-math.log(10000.0) * index / half)
    value = jnp.where(row < half, jnp.cos(angle), jnp.sin(angle))
    return (value / (1.0 + jnp.exp(-value))).astype(BF16).astype(F32)


def fill_bias(at, R):
    _, seg_count, blocks = R.live.shape

    def fill(k, carry):
        seg = 2 * k + at.c
        current = seg
        reached = [jnp.where(seg == a, 1, 0) for a in range(seg_count)]
        for _ in range(seg_count):
            current = R.parent[0, current]
            reached = [jnp.where(current == a, 1, r) for a, r in enumerate(reached)]
        for a in range(seg_count):
            for b in range(blocks):
                R.bias[k, a * blocks + b] = jnp.where(reached[a] * R.live[0, a, b] > 0, 0.0, NEGATIVE)
        return carry

    lax.fori_loop(0, at.P, fill, 0)


def seen_scores(R, score, chip, a):
    blocks = R.live.shape[2]
    rows = score.shape[0] // blocks
    return jnp.concatenate(
        [score[b * rows : (b + 1) * rows] + R.bias[chip, a * blocks + b] for b in range(blocks)], axis=0)


def layer(at, w, R):
    L, S, PC = at.L, at.S, at.P
    T, D = R.tok.shape
    HD = D // HEADS
    HG = HEADS // PC
    GW = HG * HD
    FF = R.Wu.shape[1]
    HF, DH = FF // 2, D // 2
    trunk = S // 2
    part = lambda i: slice(i * D, (i + 1) * D)
    head_rows = lambda h: slice(h * HD, (h + 1) * HD)
    gq, go, gu, gd = (Gather(w, at, shard, full) for shard, full in ((R.wq, R.Gq), (R.wo, R.Go), (R.wu, R.Gu), (R.wd, R.Gd)))

    def key_count(seg):
        return jnp.minimum(seg, trunk) + 1 + jnp.where(seg > trunk, 1, 0)

    at.barrier()
    gq.begin()
    gq.stage1(0)
    modw = R.modw[...].astype(F32)
    for t in range(L):
        column = condition_column(at, R.time[t], modw.shape[0], D)
        R.cond[t] = column
        R.mpart[t] = total_rows(column * modw)
    mz = [w.send(R.mpart.at[lax.rem(at.l + k, L)], R.mz.at[k - 1], at.at_leaf(k)) for k in range(1, L)]
    go.stage1(0)
    gu.stage1(0)
    fill_bias(at, R)
    slow = jnp.exp(-math.log(10000.0) * 2.0 * lax.broadcasted_iota(jnp.int32, (HD // 2, 1), 0).astype(F32) / HD)
    angles = slow * R.pos[...].astype(F32)
    R.cos[...] = jnp.cos(angles)
    R.sin[...] = jnp.sin(angles)
    normed, _ = norm_rows(R.tok[...].astype(F32))
    R.dh[...] = normed
    for u in range(1, L):
        gq.stage1(u)
    go.begin()
    gu.begin()
    gd.begin()
    gd.stage1(0)
    for copy in mz:
        copy.wait_recv()
    total = R.mpart[at.l]
    for k in range(L - 1):
        total = total + R.mz[k]
    R.m1[...] = total
    mp = [w.send(R.m1, R.mp.at[i], at.at_chip(q)) for i, q in enumerate(at.others)]
    gq.stage2(0)
    for copy in mp:
        copy.wait_recv()
    for i in range(3):
        total = total + R.mp[i]
    R.m2[...] = total
    ms = w.send(R.m2, R.ms, at.at_sib())
    gq.stage2(1)
    ms.wait_recv()
    R.mod[...] = total + R.ms[...]
    shift_a, scale_a, gate_a, shift_b, scale_b, gate_b = (R.mod[:, part(i)] for i in range(6))
    hidden_a = (R.dh[...] * (1.0 + scale_a) + shift_a).astype(BF16)
    R.hidden_a[...] = hidden_a
    R.haT2[0] = hidden_a.T
    sib_ha = w.send(R.haT2.at[0], R.haT2.at[1], at.at_sib())
    dbb = (gate_b * R.g[...].astype(F32)).astype(BF16)
    R.dbb[...] = dbb
    for h in range(2):
        R.dbbh[h] = dbb[:, h * DH : (h + 1) * DH]
    sib_dbb = w.send(R.dbbh.at[1 - at.c], R.dbbs, at.at_sib())
    for u in range(2, L):
        gq.stage2(u)
    for u in range(L):
        gq.stage3(u)
    for u in range(1, L):
        go.stage1(u)
    gu.stage1(1)
    gq.finish()
    load = w.local(R.Gq.reshape(D, 3 * D), R.Wq)
    load.wait()
    cosine, sine = R.cos[...], R.sin[...]
    TN = 256
    for j in range(3 * D // TN):
        kind = j * TN // D
        rows = dot(R.hidden_a[...], R.Wq[:, j * TN : (j + 1) * TN]).T
        for i in range(TN // HD):
            head = (j * TN % D) // HD + i
            group, row = head // HG, (head % HG) * HD
            first, second = rows[i * HD : i * HD + HD // 2], rows[i * HD + HD // 2 : (i + 1) * HD]
            if kind < 2:
                first, second = first * cosine - second * sine, second * cosine + first * sine
            if kind == 0:
                first, second = first * HD**-0.5, second * HD**-0.5
            R.snd[group, kind, row : row + HD // 2] = first.astype(BF16)
            R.snd[group, kind, row + HD // 2 : row + HD] = second.astype(BF16)
    kv = [w.send(R.snd.at[q, 1:3], R.KVT.at[at.s], at.at_chip(q)) for q in at.others]
    qs = [w.send(R.snd.at[q, 0], R.QT.at[at.p], at.at_chip(q)) for q in at.others]
    own_kv = w.local(R.snd.at[at.p, 1:3], R.KVT.at[at.s])
    own_q = w.local(R.snd.at[at.p, 0], R.QT.at[at.p])
    for u in range(L):
        go.stage2(u)
    gu.stage1(2)
    gu.stage1(3)
    gu.stage2(0)
    own_kv.wait()
    sk = [w.send(R.KVT.at[at.s], R.KVT.at[at.s], at.at_sib())]
    for copy, q in zip(kv, at.others):
        copy.wait_recv()
        seg = 2 * q + at.c
        sk.append(w.send(R.KVT.at[seg], R.KVT.at[seg], at.at_sib()))
    own_q.wait()
    for copy in qs:
        copy.wait_recv()
    for copy in sk:
        copy.wait_recv()
    for u in range(L):
        go.stage3(u)
    gd.stage1(1)

    def flip_k(a, carry):
        for h in range(HG):
            R.kN[a, h] = R.KVT[a, 0, head_rows(h), :].T
        return carry

    lax.fori_loop(0, S, flip_k, 0)
    ret = []
    for i, q in enumerate([at.pd, at.px, at.py, at.p]):
        seg = 2 * q + at.c

        def block(j, state, q=q, seg=seg):
            a = jnp.where(j > trunk, seg, j)
            out = []
            for h in range(HG):
                m, t, o = state[3 * h : 3 * h + 3]
                score = seen_scores(R, dot(R.kN[a, h], R.QT[q, head_rows(h), :]), q, a)
                m_new = jnp.maximum(m, jnp.max(score, axis=0, keepdims=True))
                alpha = jnp.exp(m - m_new)
                e = jnp.exp(score - m_new)
                t = t * alpha + total_rows(e)
                o = o * alpha + dot(R.KVT[a, 1, head_rows(h), :], e.astype(BF16))
                out += [m_new, t, o]
            return tuple(out)

        start = (jnp.full((1, T), NEGATIVE, F32), jnp.zeros((1, T), F32), jnp.zeros((HD, T), F32)) * HG
        state = lax.fori_loop(0, key_count(seg), block, start)
        for h in range(HG):
            m, t, o = state[3 * h : 3 * h + 3]
            o = o / t
            R.OT[q, head_rows(h), :] = o
            R.hsnd[q, head_rows(h), :] = o.astype(BF16)
            R.lse[q, h : h + 1, :] = m + jnp.log(t)
        if i < 3:
            ret.append(w.send(R.hsnd.at[q], R.attT2.at[0, at.p], at.at_chip(q)))
            gu.stage2(i + 1)
            if i < 2:
                gd.stage1(i + 2)
        else:
            own_att = w.local(R.hsnd.at[q], R.attT2.at[0, at.p])
    go.finish()
    load = w.local(R.Go.reshape(D, D), R.Wo)
    own_att.wait()
    for u in range(L):
        gu.stage3(u)
    for copy in ret:
        copy.wait_recv()
    sib_att = w.send(R.attT2.at[0], R.attT2.at[1], at.at_sib())
    load.wait()
    att = jnp.concatenate([R.attT2[0, k].T for k in range(PC)], axis=1)
    for j in range(0, D, 256):
        lanes = slice(j, j + 256)
        branch = dot(att, R.Wo[:, lanes])
        R.br_a[:, lanes] = branch
        R.middle[:, lanes] = R.tok[:, lanes].astype(F32) + gate_a[:, lanes] * branch
    gd.stage2(0)
    normed, _ = norm_rows(R.middle[...])
    hidden_b = (normed * (1.0 + scale_b) + shift_b).astype(BF16)
    R.hidden_b[...] = hidden_b
    R.hbT2[0] = hidden_b.T
    sib_hb = w.send(R.hbT2.at[0], R.hbT2.at[1], at.at_sib())
    gd.stage2(1)
    gu.finish()
    load = w.local(R.Gu.reshape(D, FF), R.Wu)
    gd.stage2(2)
    gd.stage2(3)
    load.wait()
    for h in range(2):
        def up(j, carry, h=h):
            lanes, wide = tile(j, 256), tile(h * (HF // 256) + j, 256)
            u = dot(R.hidden_b[...], R.Wu[:, wide])
            square = u * u
            tanh = jnp.tanh(GELU_A * (u + GELU_B * square * u))
            act = (0.5 * u * (1.0 + tanh)).astype(BF16)
            R.active[:, wide] = act
            R.actT2[0, wide, :] = act.T
            slope = 0.5 * (1.0 + tanh) + (0.5 * GELU_A) * u * (1.0 - tanh * tanh) * (1.0 + 3.0 * GELU_B * square)
            R.du[h, :, lanes] = slope.astype(BF16)
            return carry

        lax.fori_loop(0, HF // 256, up, 0)
    sib_act = w.send(R.actT2.at[0], R.actT2.at[1], at.at_sib())
    for u in range(L):
        gd.stage3(u)
    sib_dbb.wait_recv()
    sib_act.wait_recv()

    def scatter(n, out, first):
        return Scatter(w, at, *(getattr(R, x + n) for x in ("A", "dg", "xy", "zr", "fin", "sr")), out, first)

    scat = {"o": scatter("o", R.oo, 0), "u": scatter("u", R.ou, 0), "d": scatter("d", R.od, 0)}
    for k in range(3):
        scat[k] = scatter("q%d" % k, R.oq, k * D)
    RB = FF // (L * PC)

    def down_grad(i, carry):
        block = dot(R.actT2[0, tile(i, RB), :], R.dbbh[at.c]) + dot(R.actT2[1, tile(i, RB), :], R.dbbs[...])
        R.Ad[i // PC, lax.rem(i, PC)] = block.astype(BF16)
        return carry

    lax.fori_loop(0, L * PC, down_grad, 0)
    scat["d"].step1()
    gd.finish()
    load = w.local(R.Gd.reshape(FF, D), R.Wd)
    load.wait()
    for h in range(2):
        def act_grad(j, carry, h=h):
            lanes, wide = tile(j, 256), tile(h * (HF // 256) + j, 256)
            da = dot_t(R.dbb[...], R.Wd[wide, :])
            R.du[h, :, lanes] = (da * R.du[h, :, lanes].astype(F32)).astype(BF16)
            return carry

        lax.fori_loop(0, HF // 256, act_grad, 0)
    sib_du = w.send(R.du.at[1 - at.c], R.dus, at.at_sib())
    for j in range(0, D, 256):
        R.dh[:, j : j + 256] = dot_t(R.du[0], R.Wu[j : j + 256, 0:HF]) + dot_t(R.du[1], R.Wu[j : j + 256, HF:FF])
    dh = R.dh[...]
    normed, rstd = norm_rows(R.middle[...])
    R.gm[:, part(3)] = total_rows(dh)
    R.gm[:, part(4)] = total_rows(dh * normed)
    dmid = R.g[...].astype(F32) + norm_back(dh * (1.0 + scale_b), normed, rstd)
    R.dmid[...] = dmid
    R.gm[:, part(2)] = total_rows(dmid * R.br_a[...])
    dba = (gate_a * dmid).astype(BF16)
    R.dba[...] = dba
    for h in range(2):
        R.dbah[h] = dba[:, h * DH : (h + 1) * DH]
    sib_dba = w.send(R.dbah.at[1 - at.c], R.dbas, at.at_sib())
    w.sent(ret)
    for j in range(PC):
        R.hsnd[j] = dot_t(R.Wo[j * GW : (j + 1) * GW, :], R.dba[...]).astype(BF16)
    dos = [w.send(R.hsnd.at[q], R.dOT.at[at.p], at.at_chip(q)) for q in at.others]
    own_do = w.local(R.hsnd.at[at.p], R.dOT.at[at.p])
    sib_du.wait_recv()
    RB2 = D // (L * PC)

    def split(A, lanes, block):
        for i in range(L * PC):
            A[i // PC, i % PC, :, lanes] = block[i * RB2 : (i + 1) * RB2].astype(BF16)

    sib_hb.wait_recv()

    def up_grad(j, carry):
        split(R.Au, tile(j, 256), dot(R.hbT2[0], R.du[at.c, :, tile(j, 256)]) + dot(R.hbT2[1], R.dus[:, tile(j, 256)]))
        return carry

    lax.fori_loop(0, HF // 256, up_grad, 0)
    scat["u"].step1()
    sib_dba.wait_recv()
    sib_att.wait_recv()
    attT = [R.attT2[i].reshape(D, T) for i in range(2)]
    split(R.Ao, slice(0, DH), dot(attT[0], R.dbah[at.c]) + dot(attT[1], R.dbas[...]))
    scat["o"].step1()
    dgate = []
    for j in range(0, D, 256):
        lanes = slice(j, j + 256)
        branch = dot(R.active[...], R.Wd[:, lanes])
        R.lo[:, lanes] = (R.middle[:, lanes] + gate_b[:, lanes] * branch).astype(BF16)
        R.gm[:, 5 * D + j : 5 * D + j + 256] = total_rows(R.g[:, lanes].astype(F32) * branch)

    def flip_v(a, carry):
        for h in range(HG):
            R.vN[a, h] = R.KVT[a, 1, head_rows(h), :].T
        R.acc[a] = jnp.zeros((2, GW, T), F32)
        return carry

    lax.fori_loop(0, S, flip_v, 0)
    own_do.wait()
    w.sent(kv + qs)
    back_q = []
    for i, q in enumerate([at.p, at.px, at.py, at.pd]):
        seg = 2 * q + at.c
        if i:
            dos[i - 1].wait_recv()
        delta = [total_rows(R.dOT[q, head_rows(h), :].astype(F32) * R.OT[q, head_rows(h), :]) for h in range(HG)]

        def block(j, dqs, q=q, seg=seg, delta=delta):
            a = jnp.where(j > trunk, seg, j)
            out = []
            for h in range(HG):
                rows = head_rows(h)
                qT, dO = R.QT[q, rows, :], R.dOT[q, rows, :]
                prob = jnp.exp(seen_scores(R, dot(R.kN[a, h], qT), q, a) - R.lse[q, h : h + 1, :])
                dprob = dot(R.vN[a, h], dO)
                ds = (prob * (dprob - delta[h])).astype(BF16)
                out.append(dqs[h] + dot(R.KVT[a, 0, rows, :], ds))
                R.acc[a, 0, rows, :] += dot_t(qT, ds)
                R.acc[a, 1, rows, :] += dot_t(dO, prob.astype(BF16))
            return tuple(out)

        dqs = lax.fori_loop(0, key_count(seg), block, (jnp.zeros((HD, T), F32),) * HG)
        for h in range(HG):
            R.snd[q, 0, head_rows(h), :] = dqs[h].astype(BF16)
        if i:
            back_q.append(w.send(R.snd.at[q, 0], R.brcv.at[at.p, 0], at.at_chip(q)))
        else:
            own_bq = w.local(R.snd.at[q, 0], R.brcv.at[at.p, 0])
        if i == 0:
            scat["d"].step2()
        if i == 1:
            scat["u"].step2()
            scat["o"].step2()
        if i == 2:
            scat["d"].step3()
    NK = PC // 2 + 1
    sk = [w.send(R.acc.at[2 * k + 1 - at.c], R.acs.at[k], at.at_sib()) for k in range(NK)]
    own_bkv = None
    for copy in sk:
        copy.wait_recv()
    for k in range(PC):
        for i in range(2):
            grad = R.acc[2 * k + at.c, i]
            if k < NK:
                grad = grad + R.acs[k, i]
            R.snd[k, 1 + i] = grad.astype(BF16)
    back_kv = [w.send(R.snd.at[q, 1:3], R.brcv.at[at.p, 1:3], at.at_chip(q)) for q in at.others]
    own_bkv = w.local(R.snd.at[at.p, 1:3], R.brcv.at[at.p, 1:3])
    cosine, sine = R.cos[...], R.sin[...]

    def turn(kind):
        for head in range(HEADS):
            row = (head % HG) * HD
            both = R.brcv[head // HG, kind, row : row + HD, :].astype(F32)
            if kind < 2:
                first, second = both[: HD // 2], both[HD // 2 :]
                first, second = first * cosine + second * sine, second * cosine - first * sine
                both = jnp.concatenate([first, second], axis=0)
            if kind == 0:
                both = both * HD**-0.5
            at_row = head * HD
            R.dpT[kind, at_row // DH, at_row % DH : at_row % DH + HD, :] = both.astype(BF16)
        return w.send(R.dpT.at[kind, 1 - at.c], R.dps.at[kind], at.at_sib())

    def proj_grad(kind):
        split(getattr(R, "Aq%d" % kind), slice(0, DH), dot_t(R.haT2[0], R.dpT[kind, at.c]) + dot_t(R.haT2[1], R.dps[kind]))
        scat[kind].step1()

    own_bq.wait()
    for copy in back_q:
        copy.wait_recv()
    sib_ha.wait_recv()
    sib_dp = turn(0)
    scat["u"].step3()
    sib_dp.wait_recv()
    proj_grad(0)
    scat["o"].step3()
    own_bkv.wait()
    for copy in back_kv:
        copy.wait_recv()
    sib_dp = [turn(1), turn(2)]
    scat[0].step2()
    for kind in (1, 2):
        sib_dp[kind - 1].wait_recv()
        proj_grad(kind)
    for j in range(0, D, 256):
        dhT = dot(R.Wq[j : j + 256, 0:D], R.dpT[0].reshape(D, T))
        for kind in (1, 2):
            dhT = dhT + dot(R.Wq[j : j + 256, kind * D : (kind + 1) * D], R.dpT[kind].reshape(D, T))
        R.dh[:, j : j + 256] = dhT.T
    scat[0].step3()
    scat[1].step2()
    scat[2].step2()
    dh = R.dh[...]
    normed, rstd = norm_rows(R.tok[...].astype(F32))
    R.gm[:, part(0)] = total_rows(dh)
    R.gm[:, part(1)] = total_rows(dh * normed)
    gsib = w.send(R.gm, R.gs, at.at_sib())
    R.gt[...] = R.dmid[...] + norm_back(dh * (1.0 + scale_a), normed, rstd)
    gsib.wait_recv()
    R.g1[...] = R.gm[...] + R.gs[...]
    gp = [w.send(R.g1, R.gp.at[i], at.at_chip(q)) for i, q in enumerate(at.others)]
    for n in "duo":
        scat[n].step4()
    scat[1].step3()
    for copy in gp:
        copy.wait_recv()
    total = R.g1[...]
    for i in range(3):
        total = total + R.gp[i]
    R.gtree[at.l] = total
    gz = [w.send(R.gtree.at[at.l], R.gtree.at[at.l], at.at_leaf(k)) for k in range(1, L)]
    scat[2].step3()
    for n in "duo":
        scat[n].step5()
    scat[0].step4()
    for copy in gz:
        copy.wait_recv()
    total = R.cond[0] * R.gtree[0]
    for t in range(1, L):
        total = total + R.cond[t] * R.gtree[t]
    R.om[...] = total
    scat[1].step4()
    scat[2].step4()
    for kind in range(3):
        scat[kind].step5()


class Refs:
    def __init__(self, **refs):
        self.__dict__.update(refs)


def call_layer(L, S, tok, g, time, parent, pos, live, wq, wo, wu, wd, modw):
    T, D = tok.shape
    FF = wu.shape[1]
    PC, HD = S // 2, D // HEADS
    HG = HEADS // PC
    GW = HG * HD
    NM, H = L * S, L // 2
    sd = jax.ShapeDtypeStruct
    DM, V = pltpu.SemaphoreType.DMA, pltpu.VMEM
    ins = dict(tok=tok, g=g, time=time, parent=parent, pos=pos, live=live, wq=wq, wo=wo, wu=wu, wd=wd, modw=modw)
    outs = {"G" + n: sd((L, PC, 2 * x.shape[0], x.shape[1]), BF16) for n, x in (("q", wq), ("o", wo), ("u", wu), ("d", wd))}
    outs.update(lo=sd((T, D), BF16), gt=sd((T, D), F32), oq=sd((D // NM, 3 * D), F32), oo=sd((D // NM, D), F32),
                ou=sd((D // NM, FF), F32), od=sd((FF // NM, D), F32), om=sd((D // NM, 6 * D), F32))
    M6 = 6 * D
    scr = dict(
        Wq=V((D, 3 * D), BF16), Wo=V((D, D), BF16), Wu=V((D, FF), BF16), Wd=V((FF, D), BF16),
        bias=pltpu.SMEM((PC, live.size), F32), cond=V((L, D // NM, 1), F32), cos=V((HD // 2, T), F32), sin=V((HD // 2, T), F32),
        mpart=V((L, 1, M6), F32), mz=V((L - 1, 1, M6), F32), m1=V((1, M6), F32), mp=V((3, 1, M6), F32), m2=V((1, M6), F32),
        ms=V((1, M6), F32), mod=V((1, M6), F32),
        hidden_a=V((T, D), BF16), haT2=V((2, D, T), BF16), snd=V((PC, 3, GW, T), BF16), QT=V((PC, GW, T), BF16),
        KVT=V((S, 2, GW, T), BF16), kN=V((S, HG, T, HD), BF16), OT=V((PC, GW, T), F32), lse=V((PC, 8, T), F32),
        hsnd=V((PC, GW, T), BF16), attT2=V((2, PC, GW, T), BF16), br_a=V((T, D), F32), middle=V((T, D), F32),
        hidden_b=V((T, D), BF16), hbT2=V((2, D, T), BF16), active=V((T, FF), BF16), actT2=V((2, FF, T), BF16),
        dbb=V((T, D), BF16), dbbh=V((2, T, D // 2), BF16), dbbs=V((T, D // 2), BF16),
        du=V((2, T, FF // 2), BF16), dus=V((T, FF // 2), BF16), dh=V((T, D), F32), dmid=V((T, D), F32),
        dba=V((T, D), BF16), dbah=V((2, T, D // 2), BF16), dbas=V((T, D // 2), BF16),
        dOT=V((PC, GW, T), BF16), vN=V((S, HG, T, HD), BF16),
        acc=V((S, 2, GW, T), F32), acs=V((PC // 2 + 1, 2, GW, T), F32), brcv=V((PC, 3, GW, T), BF16),
        dpT=V((3, 2, D // 2, T), BF16), dps=V((3, D // 2, T), BF16),
        gm=V((1, M6), F32), gs=V((1, M6), F32), g1=V((1, M6), F32), gp=V((3, 1, M6), F32), gtree=V((L, 1, M6), F32))
    for n, rows, cols in (("q0", D, D), ("q1", D, D), ("q2", D, D), ("o", D, D), ("u", D, FF), ("d", FF, D)):
        rb, half = rows // (L * PC), cols // 2
        scr["A" + n] = V((L, PC, rb, half), BF16)
        scr["dg" + n] = V((2, H, rb, half), BF16)
        scr["xy" + n] = V((2, L, rb, half), BF16)
        scr["zr" + n] = V((L - 1, rb, half), BF16)
        scr["fin" + n] = V((rb, half), F32)
        scr["sr" + n] = V((rb // 2, half), F32)
    scr.update(send_sems=DM((280,)), recv_sems=DM((280,)), local_sems=DM((24,)))
    space = dict(time=pltpu.SMEM, parent=pltpu.SMEM, live=pltpu.SMEM, wq=pltpu.HBM, wo=pltpu.HBM, wu=pltpu.HBM, wd=pltpu.HBM,
                 Gq=pltpu.HBM, Go=pltpu.HBM, Gu=pltpu.HBM, Gd=pltpu.HBM)
    spec = lambda k: pl.BlockSpec(memory_space=space.get(k, pltpu.VMEM))

    def kernel(*refs):
        R = Refs(**dict(zip(list(ins) + list(outs) + list(scr), refs)))
        w = Wires(R.send_sems, R.recv_sems, R.local_sems)
        layer(Place(L, S), w, R)
        w.drain()

    res = pl.pallas_call(
        kernel, out_shape=list(outs.values()), in_specs=[spec(k) for k in ins], out_specs=[spec(k) for k in outs],
        scratch_shapes=list(scr.values()),
        compiler_params=pltpu.CompilerParams(collective_id=1, has_side_effects=True, vmem_limit_bytes=64 << 20),
    )(*ins.values())
    return dict(zip(outs, res))


def hand_out(*arrays):
    count = len(arrays)

    def kernel(*refs):
        sources, targets, held, sems = refs[:count], refs[count : 2 * count], refs[2 * count : 3 * count], refs[-1]
        arrive = [pltpu.make_async_copy(x, y, sems.at[0, i]) for i, (x, y) in enumerate(zip(sources, held))]
        leave = [pltpu.make_async_copy(x, y, sems.at[1, i]) for i, (x, y) in enumerate(zip(held, targets))]
        for copy in arrive:
            copy.start()
        for first, second in zip(arrive, leave):
            first.wait()
            second.start()
        for copy in leave:
            copy.wait()

    hbm = pl.BlockSpec(memory_space=pltpu.HBM)
    return pl.pallas_call(
        kernel, out_shape=[jax.ShapeDtypeStruct(a.shape, a.dtype) for a in arrays],
        in_specs=[hbm] * count, out_specs=[hbm] * count,
        scratch_shapes=[pltpu.VMEM(a.shape, a.dtype) for a in arrays] + [pltpu.SemaphoreType.DMA((2, count))],
    )(*arrays)


def layer_kernels(
    tokens, cotangent, timesteps, parent, positions, block_live, qkv_weight, out_weight, up_weight, down_weight, mod_weight
):
    f = call_layer(
        lax.axis_size("leaf"), lax.axis_size("seq"), tokens[0], cotangent[0], timesteps, parent, positions, block_live,
        qkv_weight, out_weight, up_weight, down_weight, mod_weight,
    )
    lo, gt, *rest = hand_out(*(f[k] for k in ("lo", "gt", "oq", "oo", "ou", "od", "om")))
    return (lo[None], gt[None], *rest)


def layer_norm(values):
    centred = values - jnp.mean(values, axis=-1, keepdims=True)
    variance = jnp.mean(centred * centred, axis=-1, keepdims=True)
    return centred * lax.rsqrt(variance + EPSILON)


def time_embed(step_values, model_width):
    half_width = model_width // 2
    freqs = jnp.exp(-math.log(10000.0) * jnp.arange(half_width, dtype=jnp.float32) / half_width)
    angles = step_values.astype(jnp.float32)[..., None] * freqs
    return jnp.concatenate([jnp.cos(angles), jnp.sin(angles)], axis=-1)


def rope_tables(places, head_dim):
    half_dim = head_dim // 2
    inverse = jnp.exp(-math.log(10000.0) * 2.0 * jnp.arange(half_dim, dtype=jnp.float32) / head_dim)
    angles = places.astype(jnp.float32)[:, None] * inverse[None, :]
    return (jnp.cos(angles), jnp.sin(angles))


def rotate(values, cosine, sine):
    half_dim = values.shape[-1] // 2
    first = values[..., :half_dim]
    second = values[..., half_dim:]
    cos_wide = cosine[:, None, :]
    sin_wide = sine[:, None, :]
    return jnp.concatenate(
        [first * cos_wide - second * sin_wide, second * cos_wide + first * sin_wide], axis=-1
    )


def rotate_back(grads, cosine, sine):
    half_dim = grads.shape[-1] // 2
    first = grads[..., :half_dim]
    second = grads[..., half_dim:]
    cos_wide = cosine[:, None, :]
    sin_wide = sine[:, None, :]
    return jnp.concatenate(
        [first * cos_wide + second * sin_wide, second * cos_wide - first * sin_wide], axis=-1
    )


def ancestor_row(parent_row, seg_index, seg_count):
    seg_range = jnp.arange(seg_count, dtype=jnp.int32)

    def climb(step_index, state_now):
        current, reached = state_now
        current = parent_row[current]
        return (current, reached | (seg_range == current))

    return lax.fori_loop(0, seg_count, climb, (seg_index, seg_range == seg_index))[1]


def attend_keys(state_now, query_rot, key_block, value_block, key_ok, score_scale):
    maximum_old, total_old, accum_old = state_now
    scores = (
        jnp.einsum("qhd,khd->hqk", query_rot, key_block, preferred_element_type=jnp.float32)
        * score_scale
    )
    visible = key_ok[None, None, :]
    scores = jnp.where(visible, scores, NEGATIVE)
    maximum_new = jnp.maximum(maximum_old, jnp.max(scores, axis=-1))
    weights_p = jnp.where(visible, jnp.exp(scores - maximum_new[..., None]), 0.0)
    rescale = jnp.exp(maximum_old - maximum_new)
    total_new = total_old * rescale + jnp.sum(weights_p, axis=-1)
    accum_new = accum_old * rescale[..., None] + jnp.einsum(
        "hqk,khd->hqd",
        weights_p.astype(jnp.bfloat16),
        value_block,
        preferred_element_type=jnp.float32,
    )
    return (maximum_new, total_new, accum_new)


def score_grads(
    query_rot, grad_attended, log_total, delta_rows, key_block, value_block, mask_wide, score_scale
):
    scores = (
        jnp.einsum("qhd,khd->hqk", query_rot, key_block, preferred_element_type=jnp.float32)
        * score_scale
    )
    probs = jnp.where(mask_wide, jnp.exp(scores - log_total[..., None]), 0.0)
    grad_probs = jnp.einsum(
        "qhd,khd->hqk", grad_attended, value_block, preferred_element_type=jnp.float32
    )
    grad_scores = (probs * (grad_probs - delta_rows[..., None])).astype(jnp.bfloat16)
    return (probs, grad_scores)


def query_only(
    grad_query,
    query_rot,
    grad_attended,
    log_total,
    delta_rows,
    key_block,
    value_block,
    key_ok,
    score_scale,
):
    probs, grad_scores = score_grads(
        query_rot,
        grad_attended,
        log_total,
        delta_rows,
        key_block,
        value_block,
        key_ok[None, None, :],
        score_scale,
    )
    return (
        grad_query
        + jnp.einsum("hqk,khd->qhd", grad_scores, key_block, preferred_element_type=jnp.float32)
        * score_scale
    )


def layer_native(
    tokens,
    cotangent,
    timesteps,
    parent,
    positions,
    block_live,
    qkv_weight,
    out_weight,
    up_weight,
    down_weight,
    mod_weight,
):
    seg_count = lax.axis_size("seq")
    seg_index = lax.axis_index("seq")
    tree_index = lax.axis_index("leaf")
    tok_rows = tokens.shape[1]
    model_width = tokens.shape[2]
    head_count = HEADS
    head_dim = model_width // head_count
    score_scale = head_dim ** (-0.5)
    tree_rows = tok_rows * seg_count
    qkv_all, out_all, up_all, down_all = (
        lax.all_gather(qkv_weight, ("leaf", "seq"), axis=0, tiled=True),
        lax.all_gather(out_weight, ("leaf", "seq"), axis=0, tiled=True),
        lax.all_gather(up_weight, ("leaf", "seq"), axis=0, tiled=True),
        lax.all_gather(down_weight, ("leaf", "seq"), axis=0, tiled=True),
    )
    condition = jax.nn.silu(time_embed(timesteps, model_width)).astype(jnp.bfloat16)
    mod_all = lax.all_gather(mod_weight, ("leaf", "seq"), axis=0, tiled=True)
    cond_own = lax.dynamic_index_in_dim(condition, tree_index, 0, keepdims=False)
    modulation = jnp.dot(cond_own[None, :], mod_all, preferred_element_type=jnp.float32)[0]
    shift_a, scale_a, gate_a, shift_b, scale_b, gate_b = jnp.split(modulation, 6)
    inputs_f = tokens[0].astype(jnp.float32)
    normed_a = layer_norm(inputs_f)
    hidden_a = (normed_a * (1.0 + scale_a) + shift_a).astype(jnp.bfloat16)
    projected = jnp.dot(hidden_a, qkv_all, preferred_element_type=jnp.float32).reshape(
        tok_rows, 3, head_count, head_dim
    )
    cosine, sine = rope_tables(positions[0], head_dim)
    query_rot = rotate(projected[:, 0], cosine, sine).astype(jnp.bfloat16)
    key_rot = rotate(projected[:, 1], cosine, sine).astype(jnp.bfloat16)
    value_rows = projected[:, 2].astype(jnp.bfloat16)
    key_flat = key_rot.reshape(tok_rows, model_width)
    value_flat = value_rows.reshape(tok_rows, model_width)
    reached = ancestor_row(parent[0], seg_index, seg_count)
    live_blocks = block_live.shape[2]
    live_tokens = jnp.repeat(block_live[0] > 0, tok_rows // live_blocks, axis=1)
    key_allowed = (reached[:, None] & live_tokens).reshape(tree_rows)
    start_state = (
        jnp.full((head_count, tok_rows), NEGATIVE, jnp.float32),
        jnp.zeros((head_count, tok_rows), jnp.float32),
        jnp.zeros((head_count, tok_rows, head_dim), jnp.float32),
    )
    key_part = lax.all_gather(key_flat, "seq", axis=0, tiled=True)
    value_part = lax.all_gather(value_flat, "seq", axis=0, tiled=True)
    count_keys = key_part.shape[0]
    block_size = tok_rows
    block_count = count_keys // block_size
    allow_part = key_allowed.reshape(block_count, block_size)
    key_blocks = key_part.reshape(block_count, block_size, head_count, head_dim)
    value_blocks = value_part.reshape(block_count, block_size, head_count, head_dim)

    def advance(state_now, block_in):
        return (
            attend_keys(state_now, query_rot, block_in[0], block_in[1], block_in[2], score_scale),
            None,
        )

    maximum_run, total_run, accum_run = lax.scan(
        advance, start_state, (key_blocks, value_blocks, allow_part)
    )[0]
    attended_heads = jnp.transpose(accum_run / total_run[..., None], (1, 0, 2))
    log_total = maximum_run + jnp.log(total_run)
    attended = attended_heads.reshape(tok_rows, model_width).astype(jnp.bfloat16)
    branch_a = jnp.dot(attended, out_all, preferred_element_type=jnp.float32)
    middle = inputs_f + gate_a * branch_a
    normed_b = layer_norm(middle)
    hidden_b = (normed_b * (1.0 + scale_b) + shift_b).astype(jnp.bfloat16)
    upper = jnp.dot(hidden_b, up_all, preferred_element_type=jnp.float32)
    active = jax.nn.gelu(upper).astype(jnp.bfloat16)
    branch_b = jnp.dot(active, down_all, preferred_element_type=jnp.float32)
    layer_out = (middle + gate_b * branch_b).astype(jnp.bfloat16)
    qkv_back, out_back, up_back, down_back = (
        lax.all_gather(qkv_weight, ("leaf", "seq"), axis=0, tiled=True),
        lax.all_gather(out_weight, ("leaf", "seq"), axis=0, tiled=True),
        lax.all_gather(up_weight, ("leaf", "seq"), axis=0, tiled=True),
        lax.all_gather(down_weight, ("leaf", "seq"), axis=0, tiled=True),
    )
    grad_out_rows = cotangent[0].astype(jnp.float32)
    grad_branch_b = (gate_b * grad_out_rows).astype(jnp.bfloat16)
    dgate_b = jnp.sum(grad_out_rows * branch_b, axis=0)
    grad_down = jnp.einsum("qf,qd->fd", active, grad_branch_b, preferred_element_type=jnp.float32)
    grad_active = jnp.einsum(
        "qd,fd->qf", grad_branch_b, down_back, preferred_element_type=jnp.float32
    )
    gelu_pull = jax.vjp(jax.nn.gelu, upper)[1]
    grad_upper = gelu_pull(grad_active)[0].astype(jnp.bfloat16)
    grad_up = jnp.einsum("qd,qf->df", hidden_b, grad_upper, preferred_element_type=jnp.float32)
    grad_hidden_b = jnp.einsum("qf,df->qd", grad_upper, up_back, preferred_element_type=jnp.float32)
    dshift_b = jnp.sum(grad_hidden_b, axis=0)
    dscale_b = jnp.sum(grad_hidden_b * normed_b, axis=0)
    norm_pull_b = jax.vjp(layer_norm, middle)[1]
    grad_middle = grad_out_rows + norm_pull_b(grad_hidden_b * (1.0 + scale_b))[0]
    grad_branch_a = (gate_a * grad_middle).astype(jnp.bfloat16)
    dgate_a = jnp.sum(grad_middle * branch_a, axis=0)
    grad_out = jnp.einsum("qi,qd->id", attended, grad_branch_a, preferred_element_type=jnp.float32)
    grad_attended = jnp.einsum(
        "qd,id->qi", grad_branch_a, out_back, preferred_element_type=jnp.float32
    ).astype(jnp.bfloat16)
    grad_att_heads = grad_attended.reshape(tok_rows, head_count, head_dim)
    delta_rows = jnp.einsum("qhd,qhd->hq", grad_att_heads.astype(jnp.float32), attended_heads)
    start_query = jnp.zeros((tok_rows, head_count, head_dim), jnp.float32)
    key_part = lax.all_gather(key_flat, "seq", axis=0, tiled=True)
    value_part = lax.all_gather(value_flat, "seq", axis=0, tiled=True)
    count_keys = key_part.shape[0]
    block_size = tok_rows
    block_count = count_keys // block_size
    allow_part = key_allowed.reshape(block_count, block_size)
    key_blocks = key_part.reshape(block_count, block_size, head_count, head_dim)
    value_blocks = value_part.reshape(block_count, block_size, head_count, head_dim)

    def advance(grad_now, block_in):
        return (
            query_only(
                grad_now,
                query_rot,
                grad_att_heads,
                log_total,
                delta_rows,
                block_in[0],
                block_in[1],
                block_in[2],
                score_scale,
            ),
            None,
        )

    grad_query = lax.scan(advance, start_query, (key_blocks, value_blocks, allow_part))[0]
    seg_range = jnp.arange(seg_count, dtype=jnp.int32)
    every_reach = jax.vmap(lambda one_seg: ancestor_row(parent[0], one_seg, seg_count))(seg_range)
    sees_mine = every_reach[:, seg_index]
    own_live = lax.dynamic_index_in_dim(live_tokens, seg_index, 0, keepdims=False)
    total_all, delta_all = (
        lax.all_gather(jnp.transpose(log_total), "seq", axis=0, tiled=True),
        lax.all_gather(jnp.transpose(delta_rows), "seq", axis=0, tiled=True),
    )
    query_flat = query_rot.reshape(tok_rows, model_width)
    grad_key_acc = jnp.zeros((tok_rows, head_count, head_dim), jnp.float32)
    grad_value_acc = jnp.zeros((tok_rows, head_count, head_dim), jnp.float32)
    query_part = lax.all_gather(query_flat, "seq", axis=0, tiled=True)
    grad_part = lax.all_gather(grad_attended, "seq", axis=0, tiled=True)
    count_rows = query_part.shape[0]
    block_size = tok_rows
    block_count = count_rows // block_size
    row_seg = jnp.arange(count_rows, dtype=jnp.int32) // tok_rows
    row_ok = sees_mine[row_seg].reshape(block_count, block_size)
    total_part = total_all.reshape(block_count, block_size, head_count)
    delta_part = delta_all.reshape(block_count, block_size, head_count)
    query_blocks = query_part.reshape(block_count, block_size, head_count, head_dim)
    grad_blocks = grad_part.reshape(block_count, block_size, head_count, head_dim)

    def advance(acc_now, block_in):
        key_acc, value_acc = acc_now
        query_block, grad_block, total_block, delta_block, ok_block = block_in
        mask_wide = ok_block[None, :, None] & own_live[None, None, :]
        probs, grad_scores = score_grads(
            query_block,
            grad_block,
            jnp.transpose(total_block),
            jnp.transpose(delta_block),
            key_rot,
            value_rows,
            mask_wide,
            score_scale,
        )
        key_acc = (
            key_acc
            + jnp.einsum(
                "hqk,qhd->khd", grad_scores, query_block, preferred_element_type=jnp.float32
            )
            * score_scale
        )
        value_acc = value_acc + jnp.einsum(
            "hqk,qhd->khd",
            probs.astype(jnp.bfloat16),
            grad_block,
            preferred_element_type=jnp.float32,
        )
        return ((key_acc, value_acc), None)

    grad_key_rows, grad_value_heads = lax.scan(
        advance,
        (grad_key_acc, grad_value_acc),
        (query_blocks, grad_blocks, total_part, delta_part, row_ok),
    )[0]
    grad_value_rows = grad_value_heads.reshape(tok_rows, model_width)
    grad_query_pre = rotate_back(grad_query, cosine, sine).reshape(tok_rows, model_width)
    grad_key_pre = rotate_back(grad_key_rows, cosine, sine).reshape(tok_rows, model_width)
    grad_projected = jnp.concatenate(
        [grad_query_pre, grad_key_pre, grad_value_rows], axis=-1
    ).astype(jnp.bfloat16)
    grad_qkv = jnp.einsum("qi,qj->ij", hidden_a, grad_projected, preferred_element_type=jnp.float32)
    grad_hidden_a = jnp.einsum(
        "qj,ij->qi", grad_projected, qkv_back, preferred_element_type=jnp.float32
    )
    dshift_a = jnp.sum(grad_hidden_a, axis=0)
    dscale_a = jnp.sum(grad_hidden_a * normed_a, axis=0)
    norm_pull_a = jax.vjp(layer_norm, inputs_f)[1]
    grad_tokens = grad_middle + norm_pull_a(grad_hidden_a * (1.0 + scale_a))[0]
    grad_modulation = jnp.concatenate([dshift_a, dscale_a, dgate_a, dshift_b, dscale_b, dgate_b])
    sum_qkv, sum_out, sum_up, sum_down = (
        lax.psum_scatter(grad_qkv, ("leaf", "seq"), scatter_dimension=0, tiled=True),
        lax.psum_scatter(grad_out, ("leaf", "seq"), scatter_dimension=0, tiled=True),
        lax.psum_scatter(grad_up, ("leaf", "seq"), scatter_dimension=0, tiled=True),
        lax.psum_scatter(grad_down, ("leaf", "seq"), scatter_dimension=0, tiled=True),
    )
    mod_term = cond_own.astype(jnp.float32)[:, None] * grad_modulation[None, :]
    sum_mod = lax.psum_scatter(mod_term, ("leaf", "seq"), scatter_dimension=0, tiled=True)
    return (layer_out[None], grad_tokens[None], sum_qkv, sum_out, sum_up, sum_down, sum_mod)


def solution(mesh):
    rows = P("leaf", "seq", None)
    held = P(("leaf", "seq"), None)
    placed = (rows, rows, P(), P("leaf", None), P("leaf", "seq"), P("leaf", None, None), held, held, held, held, held)
    kernels = mesh.shape["seq"] == 8 and mesh.shape["leaf"] == 4
    return jax.shard_map(
        layer_kernels if kernels else layer_native,
        mesh=mesh,
        in_specs=placed,
        out_specs=(rows, rows, held, held, held, held, held),
        check_vma=False,
    )
```

```python
import functools, math
import jax, jax.numpy as jnp
from jax import lax
from jax.experimental import pallas as pl
from jax.experimental.pallas import tpu as pltpu
from jax.sharding import PartitionSpec as P

MESH = pl.DeviceIdType.MESH
HEADS = 12
EPSILON = 1e-06
NEGATIVE = -1e30
F32 = jnp.float32
BF16 = jnp.bfloat16
GELU_A = math.sqrt(2.0 / math.pi)
GELU_B = 0.044715


class Sems:
    def __init__(self, ref):
        self.ref, self.used = ref, 0

    def one(self):
        self.used += 1
        assert self.used <= self.ref.shape[0]
        return self.ref.at[self.used - 1]


class Place:
    def __init__(self, leaf_count, seg_count):
        self.L, self.S = leaf_count, seg_count
        self.P = seg_count // 2
        self.l, self.s = lax.axis_index("leaf"), lax.axis_index("seq")
        self.c, self.p = lax.rem(self.s, 2), self.s // 2
        self.sib = self.s + 1 - 2 * self.c
        self.inner = (self.l + 1) // 2 == 1
        self.px = self.p + 1 - 2 * lax.rem(self.p, 2)
        self.py = lax.rem(self.p + 2, 4)
        self.pd = lax.rem(self.px + 2, 4)
        self.others = [self.px, self.py, self.pd]

    def leaf(self, k):
        far = lax.rem(self.l + 2, 4) if k >= 2 else self.l
        return far + 1 - 2 * lax.rem(far, 2) if k % 2 else far

    def turn(self, k):
        return jnp.where(self.inner, 4 - k, k)

    def leaf_turn(self, k):
        return jnp.where(self.inner, self.leaf(4 - k), self.leaf(k))

    def at_leaf(self, k):
        return (self.leaf(k), self.s)

    def at_chip(self, q):
        return (self.l, 2 * q + self.c)

    def at_sib(self):
        return (self.l, self.sib)

    def barrier(self):
        sem = pltpu.get_barrier_semaphore()
        peers = [self.at_leaf(k) for k in range(1, self.L)]
        peers += [self.at_chip(q) for q in self.others] + [self.at_sib()]
        for peer in peers:
            pl.semaphore_signal(sem, inc=1, device_id=peer, device_id_type=MESH)
        pl.semaphore_wait(sem, len(peers))


class Wires:
    def __init__(self, at, send_sems, recv_sems, local_sems):
        self.at = at
        self.send_sems, self.recv_sems, self.local_sems = Sems(send_sems), Sems(recv_sems), Sems(local_sems)
        self.open = []

    def send(self, src, dst, dev):
        copy = pltpu.make_async_remote_copy(
            src_ref=src, dst_ref=dst, send_sem=self.send_sems.one(), recv_sem=self.recv_sems.one(),
            device_id=dev, device_id_type=MESH)
        copy.start()
        self.open.append(copy)
        return copy

    def group(self, whole):
        group = Group(self, whole)
        self.open.append(group)
        return group

    def local(self, src, dst):
        copy = pltpu.make_async_copy(src, dst, self.local_sems.one())
        copy.start()
        return copy

    def sent(self, copies):
        for copy in copies:
            copy.wait_send()
        self.open = [copy for copy in self.open if all(copy is not other for other in copies)]

    def drain(self):
        for copy in self.open:
            copy.wait_send()
        self.open = []


class Group:
    def __init__(self, wires, whole):
        self.at, self.whole = wires.at, whole
        self.send_sem, self.recv_sem = wires.send_sems.one(), wires.recv_sems.one()

    def make(self, src, dst, dev):
        return pltpu.make_async_remote_copy(
            src_ref=src, dst_ref=dst, send_sem=self.send_sem, recv_sem=self.recv_sem, device_id=dev, device_id_type=MESH)

    def send(self, src, dst, dev):
        self.make(src, dst, dev).start()
        return self

    def wait_recv(self):
        self.make(self.whole, self.whole, self.at.at_sib()).wait_recv()

    def wait_send(self):
        self.make(self.whole, self.whole, self.at.at_sib()).wait_send()


class Line:
    def __init__(self, wires, at, view, whole):
        self.w, self.at, self.view = wires, at, view
        self.first = wires.send_sems.one()
        self.onward = wires.send_sems.one()
        self.arrive = [None] + [wires.recv_sems.one() for _ in range(3)]
        self.whole = whole
        wires.open.append(self)

    def leaf(self, unit):
        at = self.at
        if unit < 2:
            return at.leaf(unit)
        return jnp.where(at.l < 2, unit, 3 - unit)

    def make(self, src, leaf, unit, to, sem):
        return pltpu.make_async_remote_copy(
            src_ref=src, dst_ref=self.view(leaf), send_sem=sem, recv_sem=self.arrive[unit], device_id=to, device_id_type=MESH)

    def begin(self, src):
        at = self.at
        self.make(src, at.l, 1, at.at_leaf(1), self.first).start()

        @pl.when(at.inner)
        def _():
            self.make(src, at.l, 2, at.at_leaf(3), self.onward).start()

    def early(self, unit):
        at = self.at
        leaf = self.leaf(unit)
        part = self.view(leaf)

        @pl.when(at.inner)
        def _():
            self.make(part, leaf, unit, at.at_sib(), self.first).wait_recv()
            if unit == 1:
                self.make(part, leaf, 3, at.at_leaf(3), self.onward).start()
            else:
                self.make(part, leaf, unit, at.at_leaf(1), self.onward).start()

    def late(self, unit):
        at = self.at
        leaf = self.leaf(unit)

        @pl.when(jnp.logical_not(at.inner))
        def _():
            self.make(self.view(leaf), leaf, unit, at.at_sib(), self.first).wait_recv()

    def wait_send(self):
        at = self.at
        part = self.view(at.l)
        self.make(part, at.l, 1, at.at_sib(), self.first).wait_send()

        @pl.when(at.inner)
        def _():
            pltpu.make_async_remote_copy(
                src_ref=self.whole, dst_ref=self.whole, send_sem=self.onward, recv_sem=self.arrive[1],
                device_id=at.at_sib(), device_id_type=MESH).wait_send()


class Gather:
    def __init__(self, wires, at, shard, full):
        self.w, self.at, self.shard, self.full = wires, at, shard, full
        count = shard.shape[0]
        self.rows = pl.ds(pl.multiple_of(at.c * count, 8), count)
        self.line = Line(wires, at, lambda leaf: full.at[leaf, at.p, self.rows], full.at[:, at.p, self.rows])
        self.pair = wires.group(full.at[:, :, self.rows])
        self.cross, self.relay = {}, {}
        self.sent_cross, self.sent_relay = wires.send_sems.one(), wires.send_sems.one()
        wires.open.append(self)

    def view(self, unit, chip):
        return self.full.at[self.line.leaf(unit), chip, self.rows]

    def make(self, src, dst, to, sem, recv):
        return pltpu.make_async_remote_copy(
            src_ref=src, dst_ref=dst, send_sem=sem, recv_sem=recv, device_id=self.at.at_chip(to), device_id_type=MESH)

    def begin(self):
        self.own = self.w.local(self.shard, self.view(0, self.at.p))
        self.line.begin(self.shard)

    def stage1(self, unit):
        at = self.at
        mine = self.view(unit, at.p)
        src = mine if unit else self.shard
        self.cross[unit] = [self.make(src, mine, q, self.sent_cross, self.w.recv_sems.one()) for q in (at.px, at.py)]
        for copy in self.cross[unit]:
            copy.start()
        self.pair.send(src, mine, at.at_sib())

    def stage2(self, unit):
        at = self.at
        for i, (q, to) in enumerate(((at.px, at.py), (at.py, at.px))):
            self.cross[unit][i].wait_recv()
            theirs = self.view(unit, q)
            if unit % 2 == i:
                self.relay[unit] = self.make(theirs, theirs, to, self.sent_relay, self.w.recv_sems.one())
                self.relay[unit].start()
            self.pair.send(theirs, theirs, at.at_sib())

    def stage3(self, unit):
        self.relay[unit].wait_recv()
        theirs = self.view(unit, self.at.pd)
        self.pair.send(theirs, theirs, self.at.at_sib())

    def finish(self):
        self.own.wait()
        self.pair.wait_recv()

    def wait_send(self):
        at = self.at
        two, one = self.full.at[:, 0:2, self.rows], self.full.at[:, 0, self.rows]
        spare = self.line.arrive[1]
        self.make(two, two, at.px, self.sent_cross, spare).wait_send()
        self.make(one, one, at.px, self.sent_relay, spare).wait_send()


def add_to(ref, *others):
    total = ref[...].astype(F32)
    for other in others:
        total = total + other[...].astype(F32)
    ref[...] = total.astype(ref.dtype)


class Scatter:
    def __init__(self, wires, at, A, sw, dg, xy, zr, fin, sibr, out):
        self.w, self.at = wires, at
        self.A, self.sw, self.dg, self.xy, self.zr, self.fin, self.sibr, self.out = A, sw, dg, xy, zr, fin, sibr, out

    def cross(self, unit, to, side):
        leaf = self.at.leaf(unit)
        self.x.send(self.A.at[leaf, to], self.xy.at[side, leaf], self.at.at_chip(to))

    def step0(self):
        at = self.at
        self.s = self.w.group(self.sw)
        for i in range(2):
            self.s.send(self.A.at[at.leaf(1 + 2 * i), at.pd], self.sw.at[i], at.at_leaf(1))
        self.x = self.w.group(self.xy)

    def step1(self, units):
        at = self.at
        for unit in units:
            if unit != 2:
                self.cross(unit, at.px, 0)
            if unit != 0:
                self.cross(unit, at.py, 1)

    def step1d(self):
        w, at, A = self.w, self.at, self.A
        self.s.wait_recv()
        self.d = []
        for i, to in enumerate((at.px, at.py)):
            add_to(A.at[at.leaf(2 * i), at.pd], self.sw.at[i])
            self.d.append(w.send(A.at[at.leaf(2 * i), at.pd], self.dg.at[i], at.at_chip(to)))

    def step2(self):
        at, A = self.at, self.A
        for i, to in enumerate((at.py, at.px)):
            self.d[i].wait_recv()
            add_to(A.at[at.leaf(2 * i), to], self.dg.at[i])
            self.cross(2 * i, to, 1 - i)

    def step3(self):
        w, at, A = self.w, self.at, self.A
        self.x.wait_recv()
        self.z = w.group(self.zr)
        for k in (1, 2, 3):
            leaf = at.leaf_turn(k)
            add_to(A.at[leaf, at.p], self.xy.at[0, leaf], self.xy.at[1, leaf])
            self.z.send(A.at[leaf, at.p], self.zr.at[at.turn(k) - 1], (leaf, at.s))
        add_to(A.at[at.l, at.p], self.xy.at[0, at.l], self.xy.at[1, at.l])

    def step4(self):
        w, at = self.w, self.at
        self.z.wait_recv()
        total = self.A[at.l, at.p].astype(F32)
        for k in range(at.L - 1):
            total = total + self.zr[k].astype(F32)
        self.fin[...] = total
        rows = self.fin.shape[0] // 2
        self.f = w.send(self.fin.at[pl.ds(pl.multiple_of(rows * (1 - at.c), 8), rows)], self.sibr, at.at_sib())

    def step5(self):
        at = self.at
        rows, half = self.sibr.shape
        mine = self.fin[pl.ds(pl.multiple_of(rows * at.c, 8), rows), :]
        self.out[:, pl.ds(pl.multiple_of(half * at.c, 128), half)] = mine
        self.f.wait_recv()
        self.out[:, pl.ds(pl.multiple_of(half * (1 - at.c), 128), half)] = self.sibr[...]


def norm_rows(values):
    centred = values - jnp.mean(values, axis=-1, keepdims=True)
    variance = jnp.mean(centred * centred, axis=-1, keepdims=True)
    rstd = lax.rsqrt(variance + EPSILON)
    return centred * rstd, rstd


def norm_back(grad, normed, rstd):
    return rstd * (grad - jnp.mean(grad, axis=-1, keepdims=True) - normed * jnp.mean(grad * normed, axis=-1, keepdims=True))


def total_rows(values):
    return jnp.sum(values, axis=0, keepdims=True)


def dot(left, right):
    return jnp.dot(left, right, preferred_element_type=F32)


def dot_t(left, right):
    return lax.dot_general(left, right, (((1,), (1,)), ((), ())), preferred_element_type=F32)


def tile(j, size):
    return pl.ds(pl.multiple_of(j * size, size), size)


def condition_column(at, timestep, count, width):
    half = width // 2
    row = (at.l * at.S + at.s) * count + lax.broadcasted_iota(jnp.int32, (count, 1), 0)
    index = jnp.where(row < half, row, row - half).astype(F32)
    angle = timestep.astype(F32) * jnp.exp(-math.log(10000.0) * index / half)
    value = jnp.where(row < half, jnp.cos(angle), jnp.sin(angle))
    return (value / (1.0 + jnp.exp(-value))).astype(BF16).astype(F32)


def fill_bias(at, R):
    _, seg_count, blocks = R.live.shape

    def fill(k, carry):
        seg = 2 * k + at.c
        current = seg
        reached = [jnp.where(seg == a, 1, 0) for a in range(seg_count)]
        for _ in range(seg_count):
            current = R.parent[0, current]
            reached = [jnp.where(current == a, 1, r) for a, r in enumerate(reached)]
        for a in range(seg_count):
            for b in range(blocks):
                R.bias[k, a * blocks + b] = jnp.where(reached[a] * R.live[0, a, b] > 0, 0.0, NEGATIVE)
        return carry

    lax.fori_loop(0, at.P, fill, 0)


def seen_scores(R, score, chip, a):
    blocks = R.live.shape[2]
    rows = score.shape[0] // blocks
    return jnp.concatenate(
        [score[b * rows : (b + 1) * rows] + R.bias[chip, a * blocks + b] for b in range(blocks)], axis=0)


def layer(at, w, R):
    L, S, PC = at.L, at.S, at.P
    T, D = R.tok.shape
    HD = D // HEADS
    HG = HEADS // PC
    GW = HG * HD
    CW = R.Wh.shape[1]
    FF = R.Wu.shape[1]
    HF, DH, TH = FF // 2, D // 2, T // 2
    MR = R.wq.shape[0]
    trunk = S // 2
    NK = PC // 2 + 1
    part = lambda i: slice(i * D, (i + 1) * D)
    head_rows = lambda h: slice(h * HD, (h + 1) * HD)
    go, gu, gd = (Gather(w, at, shard, full) for shard, full in ((R.wo, R.Go), (R.wu, R.Gu), (R.wd, R.Gd)))

    def key_count(seg):
        return jnp.minimum(seg, trunk) + 1 + jnp.where(seg > trunk, 1, 0)

    at.barrier()
    wq = R.wq[...].astype(F32)
    my_rows = pl.ds(pl.multiple_of(at.c * MR, 8), MR)
    for q in range(PC):
        pieces = [wq[:, k * D + q * GW : k * D + (q + 1) * GW] for k in range(3)]
        R.wqs[q] = jnp.concatenate(pieces + [jnp.zeros((MR, CW - 3 * GW), F32)], axis=1).astype(BF16)
    qp = w.group(R.Gh.at[0, 0:3, my_rows])
    for q in at.others:
        qp.send(R.wqs.at[q], R.Gh.at[at.l, at.p, my_rows], at.at_chip(q))
    own_wq = w.local(R.wqs.at[at.p], R.Gh.at[at.l, at.p, my_rows])
    modw = R.modw[...].astype(F32)
    for t in range(L):
        column = condition_column(at, R.time[t], modw.shape[0], D)
        R.cond[t] = column
        R.mpart[t] = total_rows(column * modw)
    mz = w.group(R.mz)
    for k in range(1, L):
        mz.send(R.mpart.at[at.leaf(k)], R.mz.at[k - 1], at.at_leaf(k))
    R.pos2[at.p] = R.pos[...].astype(F32)
    ps = w.group(R.pos2.at[0:3])
    for q in at.others:
        ps.send(R.pos2.at[at.p], R.pos2.at[at.p], at.at_chip(q))
    normed, _ = norm_rows(R.tok[...].astype(F32))
    R.dh[...] = normed
    qp.wait_recv()
    own_wq.wait()
    held = lambda leaf: R.Gh.at[leaf, :, my_rows]
    ql = Line(w, at, held, R.Gh.at[:, :, my_rows])
    ql.begin(held(at.l))
    qs = w.group(R.Gh.at[:, :, my_rows])
    qs.send(held(at.l), held(at.l), at.at_sib())

    def q_late(unit):
        ql.late(unit)
        qs.send(held(ql.leaf(unit)), held(ql.leaf(unit)), at.at_sib())

    mz.wait_recv()
    total = R.mpart[at.l]
    for k in range(L - 1):
        total = total + R.mz[k]
    R.m1[...] = total
    mp = w.group(R.mp)
    for i, q in enumerate(at.others):
        mp.send(R.m1, R.mp.at[i], at.at_chip(q))
    go.stage1(0)
    gu.stage1(0)
    fill_bias(at, R)
    mp.wait_recv()
    for i in range(3):
        total = total + R.mp[i]
    R.m2[...] = total
    ms = w.send(R.m2, R.ms, at.at_sib())
    ms.wait_recv()
    R.mod[...] = total + R.ms[...]
    shift_a, scale_a, gate_a, shift_b, scale_b, gate_b = (R.mod[:, part(i)] for i in range(6))
    R.hA[at.p] = (R.dh[...] * (1.0 + scale_a) + shift_a).astype(BF16)
    up_half, low_half = pl.ds(0, TH), pl.ds(TH, TH)
    ha = [w.send(R.hA.at[at.p, half], R.hA.at[at.p, half], at.at_chip(q))
          for half, q in ((up_half, at.px), (low_half, at.py), (low_half, at.px), (up_half, at.py))]
    ql.early(1)
    ql.early(2)
    q_late(1)
    slow = jnp.exp(-math.log(10000.0) * 2.0 * lax.broadcasted_iota(jnp.int32, (HD // 2, 1), 0).astype(F32) / HD)
    ps.wait_recv()
    for k in range(PC):
        angles = slow * R.pos2[k]
        R.cos[k] = jnp.cos(angles)
        R.sin[k] = jnp.sin(angles)
    dbb = (gate_b * R.g[...].astype(F32)).astype(BF16)
    R.dbb[...] = dbb
    for h in range(2):
        R.dbbh[h] = dbb[:, h * DH : (h + 1) * DH]
    sib_dbb = w.send(R.dbbh.at[1 - at.c], R.dbbs, at.at_sib())
    ql.early(3)
    go.begin()
    gu.begin()
    q_late(2)
    ha[0].wait_recv()
    relay = [w.send(R.hA.at[at.px, up_half], R.hA.at[at.px, up_half], at.at_chip(at.py))]
    ha[1].wait_recv()
    relay.append(w.send(R.hA.at[at.py, low_half], R.hA.at[at.py, low_half], at.at_chip(at.px)))
    go.line.early(1)
    go.line.early(2)
    gu.line.early(1)
    q_late(3)
    go.line.late(1)
    go.stage1(1)
    qs.wait_recv()
    load = w.local(R.Gh.reshape(D, CW), R.Wh)
    load.wait()

    def project(q):
        cosine, sine = R.cos[q], R.sin[q]
        hidden = R.hA[q]
        R.haT[q] = hidden.T
        for j in range(0, CW, 128):
            rows = dot(hidden, R.Wh[:, j : j + 128]).T
            for i in range(128 // HD):
                kind, h = divmod(j // HD + i, HG)
                if kind == 3:
                    continue
                first, second = rows[i * HD : i * HD + HD // 2], rows[i * HD + HD // 2 : (i + 1) * HD]
                if kind < 2:
                    first, second = first * cosine - second * sine, second * cosine + first * sine
                if kind == 0:
                    first, second = first * HD**-0.5, second * HD**-0.5
                low, high = pl.ds(h * HD, HD // 2), pl.ds(h * HD + HD // 2, HD // 2)
                if kind == 0:
                    R.QT[q, low, :] = first.astype(BF16)
                    R.QT[q, high, :] = second.astype(BF16)
                else:
                    R.KVT[2 * q + at.c, kind - 1, low, :] = first.astype(BF16)
                    R.KVT[2 * q + at.c, kind - 1, high, :] = second.astype(BF16)

    project(at.p)
    go.line.early(3)
    gu.line.early(2)
    ha[2].wait_recv()
    ha[3].wait_recv()
    project(at.px)
    project(at.py)
    gu.line.late(1)
    gu.stage1(1)
    go.line.late(2)
    go.stage1(2)
    gu.stage2(0)
    for copy in relay:
        copy.wait_recv()
    project(at.pd)
    sk = w.group(R.KVT.at[0:NK])
    for k in range(NK):
        sk.send(R.KVT.at[2 * k + at.c], R.KVT.at[2 * k + at.c], at.at_sib())
    gu.line.early(3)
    gd.begin()
    gu.line.late(2)
    gu.stage1(2)
    go.line.late(3)
    go.stage1(3)
    sk.wait_recv()

    def flip_k(a, carry):
        for h in range(HG):
            R.kN[a, h] = R.KVT[a, 0, head_rows(h), :].T
        return carry

    lax.fori_loop(0, S, flip_k, 0)
    ret = w.group(R.hsnd.at[0:3])
    for i, q in enumerate([at.pd, at.px, at.py, at.p]):
        seg = 2 * q + at.c

        def block(j, state, q=q, seg=seg):
            a = jnp.where(j > trunk, seg, j)
            out = []
            for h in range(HG):
                m, t, o = state[3 * h : 3 * h + 3]
                score = seen_scores(R, dot(R.kN[a, h], R.QT[q, head_rows(h), :]), q, a)
                m_new = jnp.maximum(m, jnp.max(score, axis=0, keepdims=True))
                alpha = jnp.exp(m - m_new)
                e = jnp.exp(score - m_new)
                t = t * alpha + total_rows(e)
                o = o * alpha + dot(R.KVT[a, 1, head_rows(h), :], e.astype(BF16))
                out += [m_new, t, o]
            return tuple(out)

        start = (jnp.full((1, T), NEGATIVE, F32), jnp.zeros((1, T), F32), jnp.zeros((HD, T), F32)) * HG
        state = lax.fori_loop(0, key_count(seg), block, start)
        for h in range(HG):
            m, t, o = state[3 * h : 3 * h + 3]
            o = o / t
            R.OT[q, head_rows(h), :] = o
            R.hsnd[q, head_rows(h), :] = o.astype(BF16)
            R.lse[q, h : h + 1, :] = m + jnp.log(t)
        if i < 3:
            ret.send(R.hsnd.at[q], R.attT2.at[0, at.p], at.at_chip(q))
        else:
            own_att = w.local(R.hsnd.at[q], R.attT2.at[0, at.p])
        if i == 0:
            gu.line.late(3)
            gu.stage1(3)
            gu.stage2(1)
            for u in range(L):
                go.stage2(u)
            gd.line.early(1)
            gd.line.early(2)
        if i == 1:
            gu.stage2(2)
            gd.line.late(1)
            gd.stage1(0)
        if i == 2:
            gu.stage2(3)
            gd.line.early(3)
            gd.stage1(1)
            for u in range(L):
                go.stage3(u)
    gd.line.late(2)
    gd.stage1(2)
    go.finish()
    load = w.local(R.Go.reshape(D, D), R.Wo)
    own_att.wait()
    ret.wait_recv()
    sib_att = w.send(R.attT2.at[0], R.attT2.at[1], at.at_sib())
    load.wait()
    att = jnp.concatenate([R.attT2[0, k].T for k in range(PC)], axis=1)
    for j in range(0, D, 256):
        lanes = slice(j, j + 256)
        branch = dot(att, R.Wo[:, lanes])
        R.br_a[:, lanes] = branch
        R.middle[:, lanes] = R.tok[:, lanes].astype(F32) + gate_a[:, lanes] * branch
    normed, _ = norm_rows(R.middle[...])
    hidden_b = (normed * (1.0 + scale_b) + shift_b).astype(BF16)
    R.hidden_b[...] = hidden_b
    R.hbT2[0] = hidden_b.T
    sib_hb = w.send(R.hbT2.at[0], R.hbT2.at[1], at.at_sib())
    gd.line.late(3)
    gd.stage1(3)
    for u in range(L):
        gu.stage3(u)
    gd.stage2(0)
    gu.finish()
    load = w.local(R.Gu.reshape(D, FF), R.Wu)
    load.wait()
    for h in range(2):
        def up(j, carry, h=h):
            lanes, wide = tile(j, 256), tile(h * (HF // 256) + j, 256)
            u = dot(R.hidden_b[...], R.Wu[:, wide])
            square = u * u
            tanh = jnp.tanh(GELU_A * (u + GELU_B * square * u))
            act = (0.5 * u * (1.0 + tanh)).astype(BF16)
            R.active[:, wide] = act
            R.actT2[0, wide, :] = act.T
            slope = 0.5 * (1.0 + tanh) + (0.5 * GELU_A) * u * (1.0 - tanh * tanh) * (1.0 + 3.0 * GELU_B * square)
            R.du[h, :, lanes] = slope.astype(BF16)
            return carry

        lax.fori_loop(0, HF // 256, up, 0)
        gd.stage2(1 + h)
    sib_act = w.send(R.actT2.at[0], R.actT2.at[1], at.at_sib())
    gd.stage2(3)
    gd.stage3(0)
    sib_dbb.wait_recv()
    sib_act.wait_recv()

    scat = {n: Scatter(w, at, *(getattr(R, x + n) for x in ("A", "sw", "dg", "xy", "zr", "fin", "sr", "v"))) for n in "oud"}
    RB = FF // (L * PC)

    def down_grad(i, carry):
        block = dot(R.actT2[0, tile(i, RB), :], R.dbbh[at.c]) + dot(R.actT2[1, tile(i, RB), :], R.dbbs[...])
        R.Ad[i // PC, lax.rem(i, PC)] = block.astype(BF16)
        return carry

    lax.fori_loop(0, L * PC, down_grad, 0)
    scat["d"].step0()
    for u in range(1, L):
        gd.stage3(u)
    scat["d"].step1d()
    scat["d"].step1((1, 3))
    gd.finish()
    load = w.local(R.Gd.reshape(FF, D), R.Wd)
    load.wait()
    for h in range(2):
        def act_grad(j, carry, h=h):
            lanes, wide = tile(j, 256), tile(h * (HF // 256) + j, 256)
            da = dot_t(R.dbb[...], R.Wd[wide, :])
            R.du[h, :, lanes] = (da * R.du[h, :, lanes].astype(F32)).astype(BF16)
            return carry

        lax.fori_loop(0, HF // 256, act_grad, 0)
    sib_du = w.send(R.du.at[1 - at.c], R.dus, at.at_sib())
    for j in range(0, D, 256):
        R.dh[:, j : j + 256] = dot_t(R.du[0], R.Wu[j : j + 256, 0:HF]) + dot_t(R.du[1], R.Wu[j : j + 256, HF:FF])
    scat["d"].step2()
    dh = R.dh[...]
    normed, rstd = norm_rows(R.middle[...])
    R.gm[:, part(3)] = total_rows(dh)
    R.gm[:, part(4)] = total_rows(dh * normed)
    dmid = R.g[...].astype(F32) + norm_back(dh * (1.0 + scale_b), normed, rstd)
    R.dmid[...] = dmid
    R.gm[:, part(2)] = total_rows(dmid * R.br_a[...])
    dba = (gate_a * dmid).astype(BF16)
    R.dba[...] = dba
    for h in range(2):
        R.dbah[h] = dba[:, h * DH : (h + 1) * DH]
    sib_dba = w.send(R.dbah.at[1 - at.c], R.dbas, at.at_sib())
    w.sent([ret])
    for j in range(PC):
        R.hsnd[j] = dot_t(R.Wo[j * GW : (j + 1) * GW, :], R.dba[...]).astype(BF16)
    dos = [w.send(R.hsnd.at[q], R.dOT.at[at.p], at.at_chip(q)) for q in at.others]
    own_do = w.local(R.hsnd.at[at.p], R.dOT.at[at.p])
    scat["d"].step1((0, 2))
    RB2 = D // (L * PC)

    def split(A, lanes, block):
        for i in range(L * PC):
            A[i // PC, i % PC, :, lanes] = block[i * RB2 : (i + 1) * RB2].astype(BF16)

    sib_du.wait_recv()
    sib_hb.wait_recv()

    def up_grad(j, carry):
        split(R.Au, tile(j, 256), dot(R.hbT2[0], R.du[at.c, :, tile(j, 256)]) + dot(R.hbT2[1], R.dus[:, tile(j, 256)]))
        return carry

    lax.fori_loop(0, HF // 256, up_grad, 0)
    scat["u"].step0()
    sib_dba.wait_recv()
    sib_att.wait_recv()
    attT = [R.attT2[i].reshape(D, T) for i in range(2)]
    split(R.Ao, slice(0, DH), dot(attT[0], R.dbah[at.c]) + dot(attT[1], R.dbas[...]))
    scat["o"].step0()
    for j in range(0, D, 256):
        lanes = slice(j, j + 256)
        branch = dot(R.active[...], R.Wd[:, lanes])
        R.vlo[:, lanes] = (R.middle[:, lanes] + gate_b[:, lanes] * branch).astype(BF16)
        R.gm[:, 5 * D + j : 5 * D + j + 256] = total_rows(R.g[:, lanes].astype(F32) * branch)
    results = [w.local(R.vlo, R.lo)]

    def flip_v(a, carry):
        for h in range(HG):
            R.vN[a, h] = R.KVT[a, 1, head_rows(h), :].T
        R.acc[a] = jnp.zeros((2, GW, T), F32)
        return carry

    lax.fori_loop(0, S, flip_v, 0)
    for k in range(PC):
        R.dpT[k, 3 * GW : CW, :] = jnp.zeros((CW - 3 * GW, T), BF16)
    own_do.wait()

    def unturn(first, second, q):
        cosine, sine = R.cos[q], R.sin[q]
        return jnp.concatenate([first * cosine + second * sine, second * cosine - first * sine], axis=0)

    for i, q in enumerate([at.p, at.px, at.py, at.pd]):
        seg = 2 * q + at.c
        if i:
            dos[i - 1].wait_recv()
        delta = [total_rows(R.dOT[q, head_rows(h), :].astype(F32) * R.OT[q, head_rows(h), :]) for h in range(HG)]

        def block(j, dqs, q=q, seg=seg, delta=delta):
            a = jnp.where(j > trunk, seg, j)
            out = []
            for h in range(HG):
                rows = head_rows(h)
                qT, dO = R.QT[q, rows, :], R.dOT[q, rows, :]
                prob = jnp.exp(seen_scores(R, dot(R.kN[a, h], qT), q, a) - R.lse[q, h : h + 1, :])
                dprob = dot(R.vN[a, h], dO)
                ds = (prob * (dprob - delta[h])).astype(BF16)
                out.append(dqs[h] + dot(R.KVT[a, 0, rows, :], ds))
                R.acc[a, 0, rows, :] += dot_t(qT, ds)
                R.acc[a, 1, rows, :] += dot_t(dO, prob.astype(BF16))
            return tuple(out)

        dqs = lax.fori_loop(0, key_count(seg), block, (jnp.zeros((HD, T), F32),) * HG)
        for h in range(HG):
            dq = dqs[h] * HD**-0.5
            R.dpT[q, head_rows(h), :] = unturn(dq[: HD // 2], dq[HD // 2 :], q).astype(BF16)
        if i == 0:
            scat["u"].step1d()
            scat["u"].step1((1, 3))
        if i == 1:
            scat["d"].step3()
            scat["u"].step1((0, 2))
            scat["o"].step1d()
            scat["o"].step1((1, 3, 0, 2))
        if i == 2:
            scat["u"].step2()
    sk = w.group(R.acs)
    for k in range(NK):
        sk.send(R.acc.at[2 * k + 1 - at.c], R.acs.at[k], at.at_sib())
    scat["o"].step2()
    sk.wait_recv()
    for k in range(PC):
        for i in range(2):
            grad = R.acc[2 * k + at.c, i]
            if k < NK:
                grad = grad + R.acs[k, i]
            for h in range(HG):
                one = grad[head_rows(h)]
                if i == 0:
                    one = unturn(one[: HD // 2], one[HD // 2 :], k)
                R.dpT[k, (i + 1) * GW + h * HD : (i + 1) * GW + (h + 1) * HD, :] = one.astype(BF16)
    for q in (at.pd, at.px, at.py, at.p):
        for i in range(2):
            R.dA[i, q] = dot(R.Wh[i * DH : (i + 1) * DH, :], R.dpT[q]).astype(BF16)
        if q is at.pd:
            dd = [w.send(R.dA.at[i, q], R.dAd.at[i], at.at_chip(to)) for i, to in enumerate((at.px, at.py))]
        if q is at.px:
            dx = w.group(R.dAx)
            dx.send(R.dA.at[0, q], R.dAx.at[0, 0], at.at_chip(q))
        if q is at.py:
            dx.send(R.dA.at[1, q], R.dAx.at[1, 1], at.at_chip(q))
    scat["u"].step3()
    def proj_grad(i, carry):
        total = dot_t(R.haT[0, tile(i, D // L), :], R.dpT[0])
        for k in range(1, PC):
            total = total + dot_t(R.haT[k, tile(i, D // L), :], R.dpT[k])
        for core in range(2):
            rows = [total[(2 * k + core) * MR : (2 * k + core + 1) * MR] for k in range(PC)]
            R.Aq[core, i] = jnp.concatenate(rows, axis=0).astype(BF16)
        return carry

    lax.fori_loop(0, L, proj_grad, 0)
    sib_q = w.send(R.Aq.at[1 - at.c], R.Aqs, at.at_sib())
    sib_q.wait_recv()
    qz = w.group(R.zrq)
    for k in (1, 2, 3):
        leaf = at.leaf_turn(k)
        add_to(R.Aq.at[at.c, leaf], R.Aqs.at[leaf])
        qz.send(R.Aq.at[at.c, leaf], R.zrq.at[at.turn(k) - 1], (leaf, at.s))
    add_to(R.Aq.at[at.c, at.l], R.Aqs.at[at.l])
    for i, to in enumerate((at.py, at.px)):
        dd[i].wait_recv()
        add_to(R.dA.at[i, to], R.dAd.at[i])
        dx.send(R.dA.at[i, to], R.dAx.at[1 - i, i], at.at_chip(to))
    scat["o"].step3()
    dx.wait_recv()
    dh = jnp.concatenate(
        [(R.dA[i, at.p].astype(F32) + R.dAx[0, i].astype(F32) + R.dAx[1, i].astype(F32)).T for i in range(2)], axis=1)
    normed, rstd = norm_rows(R.tok[...].astype(F32))
    R.gm[:, part(0)] = total_rows(dh)
    R.gm[:, part(1)] = total_rows(dh * normed)
    gsib = w.send(R.gm, R.gs, at.at_sib())
    R.vgt[...] = R.dmid[...] + norm_back(dh * (1.0 + scale_a), normed, rstd)
    results.append(w.local(R.vgt, R.gt))
    gsib.wait_recv()
    R.g1[...] = R.gm[...] + R.gs[...]
    gp = w.group(R.gp)
    for i, q in enumerate(at.others):
        gp.send(R.g1, R.gp.at[i], at.at_chip(q))
    scat["d"].step4()
    scat["d"].step5()
    results.append(w.local(R.vd, R.od))
    qz.wait_recv()
    total = R.Aq[at.c, at.l].astype(F32)
    for k in range(L - 1):
        total = total + R.zrq[k].astype(F32)
    R.finq[...] = total
    mine = lambda q: R.finq.at[pl.ds(pl.multiple_of(q * MR, 8), MR)]
    rq = w.group(R.rq.at[0:3])
    for q in at.others:
        rq.send(mine(q), R.rq.at[at.p], at.at_chip(q))
    own_rq = w.local(mine(at.p), R.rq.at[at.p])
    gp.wait_recv()
    total = R.g1[...]
    for i in range(3):
        total = total + R.gp[i]
    R.gtree[at.l] = total
    gz = w.group(R.gtree.at[0:3])
    for k in range(1, L):
        gz.send(R.gtree.at[at.l], R.gtree.at[at.l], at.at_leaf(k))
    scat["o"].step4()
    scat["u"].step4()
    scat["o"].step5()
    results.append(w.local(R.vo, R.oo))
    own_rq.wait()
    rq.wait_recv()
    R.vq[...] = jnp.concatenate([R.rq[q][:, k * GW : (k + 1) * GW] for k in range(3) for q in range(PC)], axis=1)
    results.append(w.local(R.vq, R.oq))
    scat["u"].step5()
    results.append(w.local(R.vu, R.ou))
    gz.wait_recv()
    total = R.cond[0] * R.gtree[0]
    for t in range(1, L):
        total = total + R.cond[t] * R.gtree[t]
    R.vm[...] = total
    results.append(w.local(R.vm, R.om))
    for copy in results:
        copy.wait()


class Refs:
    def __init__(self, **refs):
        self.__dict__.update(refs)


def call_layer(L, S, tok, g, time, parent, pos, live, wq, wo, wu, wd, modw):
    T, D = tok.shape
    FF = wu.shape[1]
    PC, HD = S // 2, D // HEADS
    HG = HEADS // PC
    GW = HG * HD
    CW = -(-3 * GW // 128) * 128
    NM, MR = L * S, wq.shape[0]
    sd = jax.ShapeDtypeStruct
    DM, V = pltpu.SemaphoreType.DMA, pltpu.VMEM
    ins = dict(tok=tok, g=g, time=time, parent=parent, pos=pos, live=live, wq=wq, wo=wo, wu=wu, wd=wd, modw=modw)
    outs = {"G" + n: sd((L, PC, 2 * x.shape[0], x.shape[1]), BF16) for n, x in (("o", wo), ("u", wu), ("d", wd))}
    outs["Gh"] = sd((L, PC, 2 * MR, CW), BF16)
    last = dict(lo=((T, D), BF16), gt=((T, D), F32), oq=((MR, 3 * D), F32), oo=((MR, D), F32),
                ou=((MR, FF), F32), od=((FF // NM, D), F32), om=((MR, 6 * D), F32))
    outs.update({k: sd(*v) for k, v in last.items()})
    M6 = 6 * D
    scr = dict(
        Wh=V((D, CW), BF16), Wo=V((D, D), BF16), Wu=V((D, FF), BF16), Wd=V((FF, D), BF16), wqs=V((PC, MR, CW), BF16),
        bias=pltpu.SMEM((PC, live.size), F32), cond=V((L, MR, 1), F32),
        pos2=V((PC, 1, T), F32), cos=V((PC, HD // 2, T), F32), sin=V((PC, HD // 2, T), F32),
        mpart=V((L, 1, M6), F32), mz=V((L - 1, 1, M6), F32), m1=V((1, M6), F32), mp=V((3, 1, M6), F32), m2=V((1, M6), F32),
        ms=V((1, M6), F32), mod=V((1, M6), F32),
        hA=V((PC, T, D), BF16), haT=V((PC, D, T), BF16), QT=V((PC, GW, T), BF16),
        KVT=V((S, 2, GW, T), BF16), kN=V((S, HG, T, HD), BF16), OT=V((PC, GW, T), F32), lse=V((PC, 8, T), F32),
        hsnd=V((PC, GW, T), BF16), attT2=V((2, PC, GW, T), BF16), br_a=V((T, D), F32), middle=V((T, D), F32),
        hidden_b=V((T, D), BF16), hbT2=V((2, D, T), BF16), active=V((T, FF), BF16), actT2=V((2, FF, T), BF16),
        dbb=V((T, D), BF16), dbbh=V((2, T, D // 2), BF16), dbbs=V((T, D // 2), BF16),
        du=V((2, T, FF // 2), BF16), dus=V((T, FF // 2), BF16), dh=V((T, D), F32), dmid=V((T, D), F32),
        dba=V((T, D), BF16), dbah=V((2, T, D // 2), BF16), dbas=V((T, D // 2), BF16),
        dOT=V((PC, GW, T), BF16), vN=V((S, HG, T, HD), BF16),
        acc=V((S, 2, GW, T), F32), acs=V((PC // 2 + 1, 2, GW, T), F32), dpT=V((PC, CW, T), BF16),
        dA=V((2, PC, D // 2, T), BF16), dAd=V((2, D // 2, T), BF16), dAx=V((2, 2, D // 2, T), BF16),
        Aq=V((2, L, PC * MR, CW), BF16), Aqs=V((L, PC * MR, CW), BF16), zrq=V((L - 1, PC * MR, CW), BF16),
        finq=V((PC * MR, CW), F32), rq=V((PC, MR, CW), F32),
        gm=V((1, M6), F32), gs=V((1, M6), F32), g1=V((1, M6), F32), gp=V((3, 1, M6), F32), gtree=V((L, 1, M6), F32))
    for n, rows, cols in (("o", D, D), ("u", D, FF), ("d", FF, D)):
        rb, half = rows // (L * PC), cols // 2
        scr["A" + n] = V((L, PC, rb, half), BF16)
        scr["sw" + n] = V((2, rb, half), BF16)
        scr["dg" + n] = V((2, rb, half), BF16)
        scr["xy" + n] = V((2, L, rb, half), BF16)
        scr["zr" + n] = V((L - 1, rb, half), BF16)
        scr["fin" + n] = V((rb, half), F32)
        scr["sr" + n] = V((rb // 2, half), F32)
    for k, v in last.items():
        scr["v" + k.removeprefix("o") if k != "lo" else "vlo"] = V(*v)
    scr.update(send_sems=DM((68,)), recv_sems=DM((102,)), local_sems=DM((18,)))
    space = dict.fromkeys(("time", "parent", "live"), pltpu.SMEM)
    space.update(dict.fromkeys(("wo", "wu", "wd", *outs), pltpu.HBM))
    spec = lambda k: pl.BlockSpec(memory_space=space.get(k, pltpu.VMEM))

    def kernel(*refs):
        R = Refs(**dict(zip(list(ins) + list(outs) + list(scr), refs)))
        at = Place(L, S)
        w = Wires(at, R.send_sems, R.recv_sems, R.local_sems)
        layer(at, w, R)
        w.drain()

    res = pl.pallas_call(
        kernel, out_shape=list(outs.values()), in_specs=[spec(k) for k in ins], out_specs=[spec(k) for k in outs],
        scratch_shapes=list(scr.values()),
        compiler_params=pltpu.CompilerParams(collective_id=1, has_side_effects=True, vmem_limit_bytes=64 << 20),
    )(*ins.values())
    return dict(zip(outs, res))


def hand_out(*arrays):
    count = len(arrays)

    def kernel(*refs):
        sources, targets, held, sems = refs[:count], refs[count : 2 * count], refs[2 * count : 3 * count], refs[-1]
        arrive = [pltpu.make_async_copy(x, y, sems.at[0, i]) for i, (x, y) in enumerate(zip(sources, held))]
        leave = [pltpu.make_async_copy(x, y, sems.at[1, i]) for i, (x, y) in enumerate(zip(held, targets))]
        for copy in arrive:
            copy.start()
        for first, second in zip(arrive, leave):
            first.wait()
            second.start()
        for copy in leave:
            copy.wait()

    hbm = pl.BlockSpec(memory_space=pltpu.HBM)
    return pl.pallas_call(
        kernel, out_shape=[jax.ShapeDtypeStruct(a.shape, a.dtype) for a in arrays],
        in_specs=[hbm] * count, out_specs=[hbm] * count,
        scratch_shapes=[pltpu.VMEM(a.shape, a.dtype) for a in arrays] + [pltpu.SemaphoreType.DMA((2, count))],
    )(*arrays)


def layer_kernels(
    tokens, cotangent, timesteps, parent, positions, block_live, qkv_weight, out_weight, up_weight, down_weight, mod_weight
):
    f = call_layer(
        lax.axis_size("leaf"), lax.axis_size("seq"), tokens[0], cotangent[0], timesteps, parent, positions, block_live,
        qkv_weight, out_weight, up_weight, down_weight, mod_weight,
    )
    lo, gt, *rest = hand_out(*(f[k] for k in ("lo", "gt", "oq", "oo", "ou", "od", "om")))
    return (lo[None], gt[None], *rest)


def layer_norm(values):
    centred = values - jnp.mean(values, axis=-1, keepdims=True)
    variance = jnp.mean(centred * centred, axis=-1, keepdims=True)
    return centred * lax.rsqrt(variance + EPSILON)


def time_embed(step_values, model_width):
    half_width = model_width // 2
    freqs = jnp.exp(-math.log(10000.0) * jnp.arange(half_width, dtype=jnp.float32) / half_width)
    angles = step_values.astype(jnp.float32)[..., None] * freqs
    return jnp.concatenate([jnp.cos(angles), jnp.sin(angles)], axis=-1)


def rope_tables(places, head_dim):
    half_dim = head_dim // 2
    inverse = jnp.exp(-math.log(10000.0) * 2.0 * jnp.arange(half_dim, dtype=jnp.float32) / head_dim)
    angles = places.astype(jnp.float32)[:, None] * inverse[None, :]
    return (jnp.cos(angles), jnp.sin(angles))


def rotate(values, cosine, sine):
    half_dim = values.shape[-1] // 2
    first = values[..., :half_dim]
    second = values[..., half_dim:]
    cos_wide = cosine[:, None, :]
    sin_wide = sine[:, None, :]
    return jnp.concatenate(
        [first * cos_wide - second * sin_wide, second * cos_wide + first * sin_wide], axis=-1
    )


def rotate_back(grads, cosine, sine):
    half_dim = grads.shape[-1] // 2
    first = grads[..., :half_dim]
    second = grads[..., half_dim:]
    cos_wide = cosine[:, None, :]
    sin_wide = sine[:, None, :]
    return jnp.concatenate(
        [first * cos_wide + second * sin_wide, second * cos_wide - first * sin_wide], axis=-1
    )


def ancestor_row(parent_row, seg_index, seg_count):
    seg_range = jnp.arange(seg_count, dtype=jnp.int32)

    def climb(step_index, state_now):
        current, reached = state_now
        current = parent_row[current]
        return (current, reached | (seg_range == current))

    return lax.fori_loop(0, seg_count, climb, (seg_index, seg_range == seg_index))[1]


def attend_keys(state_now, query_rot, key_block, value_block, key_ok, score_scale):
    maximum_old, total_old, accum_old = state_now
    scores = (
        jnp.einsum("qhd,khd->hqk", query_rot, key_block, preferred_element_type=jnp.float32)
        * score_scale
    )
    visible = key_ok[None, None, :]
    scores = jnp.where(visible, scores, NEGATIVE)
    maximum_new = jnp.maximum(maximum_old, jnp.max(scores, axis=-1))
    weights_p = jnp.where(visible, jnp.exp(scores - maximum_new[..., None]), 0.0)
    rescale = jnp.exp(maximum_old - maximum_new)
    total_new = total_old * rescale + jnp.sum(weights_p, axis=-1)
    accum_new = accum_old * rescale[..., None] + jnp.einsum(
        "hqk,khd->hqd",
        weights_p.astype(jnp.bfloat16),
        value_block,
        preferred_element_type=jnp.float32,
    )
    return (maximum_new, total_new, accum_new)


def score_grads(
    query_rot, grad_attended, log_total, delta_rows, key_block, value_block, mask_wide, score_scale
):
    scores = (
        jnp.einsum("qhd,khd->hqk", query_rot, key_block, preferred_element_type=jnp.float32)
        * score_scale
    )
    probs = jnp.where(mask_wide, jnp.exp(scores - log_total[..., None]), 0.0)
    grad_probs = jnp.einsum(
        "qhd,khd->hqk", grad_attended, value_block, preferred_element_type=jnp.float32
    )
    grad_scores = (probs * (grad_probs - delta_rows[..., None])).astype(jnp.bfloat16)
    return (probs, grad_scores)


def query_only(
    grad_query,
    query_rot,
    grad_attended,
    log_total,
    delta_rows,
    key_block,
    value_block,
    key_ok,
    score_scale,
):
    probs, grad_scores = score_grads(
        query_rot,
        grad_attended,
        log_total,
        delta_rows,
        key_block,
        value_block,
        key_ok[None, None, :],
        score_scale,
    )
    return (
        grad_query
        + jnp.einsum("hqk,khd->qhd", grad_scores, key_block, preferred_element_type=jnp.float32)
        * score_scale
    )


def layer_native(
    tokens,
    cotangent,
    timesteps,
    parent,
    positions,
    block_live,
    qkv_weight,
    out_weight,
    up_weight,
    down_weight,
    mod_weight,
):
    seg_count = lax.axis_size("seq")
    seg_index = lax.axis_index("seq")
    tree_index = lax.axis_index("leaf")
    tok_rows = tokens.shape[1]
    model_width = tokens.shape[2]
    head_count = HEADS
    head_dim = model_width // head_count
    score_scale = head_dim ** (-0.5)
    tree_rows = tok_rows * seg_count
    qkv_all, out_all, up_all, down_all = (
        lax.all_gather(qkv_weight, ("leaf", "seq"), axis=0, tiled=True),
        lax.all_gather(out_weight, ("leaf", "seq"), axis=0, tiled=True),
        lax.all_gather(up_weight, ("leaf", "seq"), axis=0, tiled=True),
        lax.all_gather(down_weight, ("leaf", "seq"), axis=0, tiled=True),
    )
    condition = jax.nn.silu(time_embed(timesteps, model_width)).astype(jnp.bfloat16)
    mod_all = lax.all_gather(mod_weight, ("leaf", "seq"), axis=0, tiled=True)
    cond_own = lax.dynamic_index_in_dim(condition, tree_index, 0, keepdims=False)
    modulation = jnp.dot(cond_own[None, :], mod_all, preferred_element_type=jnp.float32)[0]
    shift_a, scale_a, gate_a, shift_b, scale_b, gate_b = jnp.split(modulation, 6)
    inputs_f = tokens[0].astype(jnp.float32)
    normed_a = layer_norm(inputs_f)
    hidden_a = (normed_a * (1.0 + scale_a) + shift_a).astype(jnp.bfloat16)
    projected = jnp.dot(hidden_a, qkv_all, preferred_element_type=jnp.float32).reshape(
        tok_rows, 3, head_count, head_dim
    )
    cosine, sine = rope_tables(positions[0], head_dim)
    query_rot = rotate(projected[:, 0], cosine, sine).astype(jnp.bfloat16)
    key_rot = rotate(projected[:, 1], cosine, sine).astype(jnp.bfloat16)
    value_rows = projected[:, 2].astype(jnp.bfloat16)
    key_flat = key_rot.reshape(tok_rows, model_width)
    value_flat = value_rows.reshape(tok_rows, model_width)
    reached = ancestor_row(parent[0], seg_index, seg_count)
    live_blocks = block_live.shape[2]
    live_tokens = jnp.repeat(block_live[0] > 0, tok_rows // live_blocks, axis=1)
    key_allowed = (reached[:, None] & live_tokens).reshape(tree_rows)
    start_state = (
        jnp.full((head_count, tok_rows), NEGATIVE, jnp.float32),
        jnp.zeros((head_count, tok_rows), jnp.float32),
        jnp.zeros((head_count, tok_rows, head_dim), jnp.float32),
    )
    key_part = lax.all_gather(key_flat, "seq", axis=0, tiled=True)
    value_part = lax.all_gather(value_flat, "seq", axis=0, tiled=True)
    count_keys = key_part.shape[0]
    block_size = tok_rows
    block_count = count_keys // block_size
    allow_part = key_allowed.reshape(block_count, block_size)
    key_blocks = key_part.reshape(block_count, block_size, head_count, head_dim)
    value_blocks = value_part.reshape(block_count, block_size, head_count, head_dim)

    def advance(state_now, block_in):
        return (
            attend_keys(state_now, query_rot, block_in[0], block_in[1], block_in[2], score_scale),
            None,
        )

    maximum_run, total_run, accum_run = lax.scan(
        advance, start_state, (key_blocks, value_blocks, allow_part)
    )[0]
    attended_heads = jnp.transpose(accum_run / total_run[..., None], (1, 0, 2))
    log_total = maximum_run + jnp.log(total_run)
    attended = attended_heads.reshape(tok_rows, model_width).astype(jnp.bfloat16)
    branch_a = jnp.dot(attended, out_all, preferred_element_type=jnp.float32)
    middle = inputs_f + gate_a * branch_a
    normed_b = layer_norm(middle)
    hidden_b = (normed_b * (1.0 + scale_b) + shift_b).astype(jnp.bfloat16)
    upper = jnp.dot(hidden_b, up_all, preferred_element_type=jnp.float32)
    active = jax.nn.gelu(upper).astype(jnp.bfloat16)
    branch_b = jnp.dot(active, down_all, preferred_element_type=jnp.float32)
    layer_out = (middle + gate_b * branch_b).astype(jnp.bfloat16)
    qkv_back, out_back, up_back, down_back = (
        lax.all_gather(qkv_weight, ("leaf", "seq"), axis=0, tiled=True),
        lax.all_gather(out_weight, ("leaf", "seq"), axis=0, tiled=True),
        lax.all_gather(up_weight, ("leaf", "seq"), axis=0, tiled=True),
        lax.all_gather(down_weight, ("leaf", "seq"), axis=0, tiled=True),
    )
    grad_out_rows = cotangent[0].astype(jnp.float32)
    grad_branch_b = (gate_b * grad_out_rows).astype(jnp.bfloat16)
    dgate_b = jnp.sum(grad_out_rows * branch_b, axis=0)
    grad_down = jnp.einsum("qf,qd->fd", active, grad_branch_b, preferred_element_type=jnp.float32)
    grad_active = jnp.einsum(
        "qd,fd->qf", grad_branch_b, down_back, preferred_element_type=jnp.float32
    )
    gelu_pull = jax.vjp(jax.nn.gelu, upper)[1]
    grad_upper = gelu_pull(grad_active)[0].astype(jnp.bfloat16)
    grad_up = jnp.einsum("qd,qf->df", hidden_b, grad_upper, preferred_element_type=jnp.float32)
    grad_hidden_b = jnp.einsum("qf,df->qd", grad_upper, up_back, preferred_element_type=jnp.float32)
    dshift_b = jnp.sum(grad_hidden_b, axis=0)
    dscale_b = jnp.sum(grad_hidden_b * normed_b, axis=0)
    norm_pull_b = jax.vjp(layer_norm, middle)[1]
    grad_middle = grad_out_rows + norm_pull_b(grad_hidden_b * (1.0 + scale_b))[0]
    grad_branch_a = (gate_a * grad_middle).astype(jnp.bfloat16)
    dgate_a = jnp.sum(grad_middle * branch_a, axis=0)
    grad_out = jnp.einsum("qi,qd->id", attended, grad_branch_a, preferred_element_type=jnp.float32)
    grad_attended = jnp.einsum(
        "qd,id->qi", grad_branch_a, out_back, preferred_element_type=jnp.float32
    ).astype(jnp.bfloat16)
    grad_att_heads = grad_attended.reshape(tok_rows, head_count, head_dim)
    delta_rows = jnp.einsum("qhd,qhd->hq", grad_att_heads.astype(jnp.float32), attended_heads)
    start_query = jnp.zeros((tok_rows, head_count, head_dim), jnp.float32)
    key_part = lax.all_gather(key_flat, "seq", axis=0, tiled=True)
    value_part = lax.all_gather(value_flat, "seq", axis=0, tiled=True)
    count_keys = key_part.shape[0]
    block_size = tok_rows
    block_count = count_keys // block_size
    allow_part = key_allowed.reshape(block_count, block_size)
    key_blocks = key_part.reshape(block_count, block_size, head_count, head_dim)
    value_blocks = value_part.reshape(block_count, block_size, head_count, head_dim)

    def advance(grad_now, block_in):
        return (
            query_only(
                grad_now,
                query_rot,
                grad_att_heads,
                log_total,
                delta_rows,
                block_in[0],
                block_in[1],
                block_in[2],
                score_scale,
            ),
            None,
        )

    grad_query = lax.scan(advance, start_query, (key_blocks, value_blocks, allow_part))[0]
    seg_range = jnp.arange(seg_count, dtype=jnp.int32)
    every_reach = jax.vmap(lambda one_seg: ancestor_row(parent[0], one_seg, seg_count))(seg_range)
    sees_mine = every_reach[:, seg_index]
    own_live = lax.dynamic_index_in_dim(live_tokens, seg_index, 0, keepdims=False)
    total_all, delta_all = (
        lax.all_gather(jnp.transpose(log_total), "seq", axis=0, tiled=True),
        lax.all_gather(jnp.transpose(delta_rows), "seq", axis=0, tiled=True),
    )
    query_flat = query_rot.reshape(tok_rows, model_width)
    grad_key_acc = jnp.zeros((tok_rows, head_count, head_dim), jnp.float32)
    grad_value_acc = jnp.zeros((tok_rows, head_count, head_dim), jnp.float32)
    query_part = lax.all_gather(query_flat, "seq", axis=0, tiled=True)
    grad_part = lax.all_gather(grad_attended, "seq", axis=0, tiled=True)
    count_rows = query_part.shape[0]
    block_size = tok_rows
    block_count = count_rows // block_size
    row_seg = jnp.arange(count_rows, dtype=jnp.int32) // tok_rows
    row_ok = sees_mine[row_seg].reshape(block_count, block_size)
    total_part = total_all.reshape(block_count, block_size, head_count)
    delta_part = delta_all.reshape(block_count, block_size, head_count)
    query_blocks = query_part.reshape(block_count, block_size, head_count, head_dim)
    grad_blocks = grad_part.reshape(block_count, block_size, head_count, head_dim)

    def advance(acc_now, block_in):
        key_acc, value_acc = acc_now
        query_block, grad_block, total_block, delta_block, ok_block = block_in
        mask_wide = ok_block[None, :, None] & own_live[None, None, :]
        probs, grad_scores = score_grads(
            query_block,
            grad_block,
            jnp.transpose(total_block),
            jnp.transpose(delta_block),
            key_rot,
            value_rows,
            mask_wide,
            score_scale,
        )
        key_acc = (
            key_acc
            + jnp.einsum(
                "hqk,qhd->khd", grad_scores, query_block, preferred_element_type=jnp.float32
            )
            * score_scale
        )
        value_acc = value_acc + jnp.einsum(
            "hqk,qhd->khd",
            probs.astype(jnp.bfloat16),
            grad_block,
            preferred_element_type=jnp.float32,
        )
        return ((key_acc, value_acc), None)

    grad_key_rows, grad_value_heads = lax.scan(
        advance,
        (grad_key_acc, grad_value_acc),
        (query_blocks, grad_blocks, total_part, delta_part, row_ok),
    )[0]
    grad_value_rows = grad_value_heads.reshape(tok_rows, model_width)
    grad_query_pre = rotate_back(grad_query, cosine, sine).reshape(tok_rows, model_width)
    grad_key_pre = rotate_back(grad_key_rows, cosine, sine).reshape(tok_rows, model_width)
    grad_projected = jnp.concatenate(
        [grad_query_pre, grad_key_pre, grad_value_rows], axis=-1
    ).astype(jnp.bfloat16)
    grad_qkv = jnp.einsum("qi,qj->ij", hidden_a, grad_projected, preferred_element_type=jnp.float32)
    grad_hidden_a = jnp.einsum(
        "qj,ij->qi", grad_projected, qkv_back, preferred_element_type=jnp.float32
    )
    dshift_a = jnp.sum(grad_hidden_a, axis=0)
    dscale_a = jnp.sum(grad_hidden_a * normed_a, axis=0)
    norm_pull_a = jax.vjp(layer_norm, inputs_f)[1]
    grad_tokens = grad_middle + norm_pull_a(grad_hidden_a * (1.0 + scale_a))[0]
    grad_modulation = jnp.concatenate([dshift_a, dscale_a, dgate_a, dshift_b, dscale_b, dgate_b])
    sum_qkv, sum_out, sum_up, sum_down = (
        lax.psum_scatter(grad_qkv, ("leaf", "seq"), scatter_dimension=0, tiled=True),
        lax.psum_scatter(grad_out, ("leaf", "seq"), scatter_dimension=0, tiled=True),
        lax.psum_scatter(grad_up, ("leaf", "seq"), scatter_dimension=0, tiled=True),
        lax.psum_scatter(grad_down, ("leaf", "seq"), scatter_dimension=0, tiled=True),
    )
    mod_term = cond_own.astype(jnp.float32)[:, None] * grad_modulation[None, :]
    sum_mod = lax.psum_scatter(mod_term, ("leaf", "seq"), scatter_dimension=0, tiled=True)
    return (layer_out[None], grad_tokens[None], sum_qkv, sum_out, sum_up, sum_down, sum_mod)


def solution(mesh):
    rows = P("leaf", "seq", None)
    held = P(("leaf", "seq"), None)
    placed = (rows, rows, P(), P("leaf", None), P("leaf", "seq"), P("leaf", None, None), held, held, held, held, held)
    kernels = mesh.shape["seq"] == 8 and mesh.shape["leaf"] == 4
    return jax.shard_map(
        layer_kernels if kernels else layer_native,
        mesh=mesh,
        in_specs=placed,
        out_specs=(rows, rows, held, held, held, held, held),
        check_vma=False,
    )
```

```python
import functools, math
import jax, jax.numpy as jnp
from jax import lax
from jax.experimental import pallas as pl
from jax.experimental.pallas import tpu as pltpu
from jax.sharding import PartitionSpec as P

MESH = pl.DeviceIdType.MESH
HEADS = 12
EPSILON = 1e-06
NEGATIVE = -1e30
F32 = jnp.float32
BF16 = jnp.bfloat16
GELU_A = math.sqrt(2.0 / math.pi)
GELU_B = 0.044715


class Sems:
    def __init__(self, ref):
        self.ref, self.used = ref, 0

    def one(self):
        self.used += 1
        assert self.used <= self.ref.shape[0]
        return self.ref.at[self.used - 1]


class Place:
    def __init__(self, leaf_count, seg_count):
        self.L, self.S = leaf_count, seg_count
        self.P = seg_count // 2
        self.l, self.s = lax.axis_index("leaf"), lax.axis_index("seq")
        self.c, self.p = lax.rem(self.s, 2), self.s // 2
        self.sib = self.s + 1 - 2 * self.c
        self.inner = (self.l + 1) // 2 == 1
        self.px = self.p + 1 - 2 * lax.rem(self.p, 2)
        self.py = lax.rem(self.p + 2, 4)
        self.pd = lax.rem(self.px + 2, 4)
        self.others = [self.px, self.py, self.pd]

    def leaf(self, k):
        far = lax.rem(self.l + 2, 4) if k >= 2 else self.l
        return far + 1 - 2 * lax.rem(far, 2) if k % 2 else far

    def turn(self, k):
        return jnp.where(self.inner, 4 - k, k)

    def leaf_turn(self, k):
        return jnp.where(self.inner, self.leaf(4 - k), self.leaf(k))

    def at_leaf(self, k):
        return (self.leaf(k), self.s)

    def at_chip(self, q):
        return (self.l, 2 * q + self.c)

    def at_sib(self):
        return (self.l, self.sib)

    def barrier(self):
        sem = pltpu.get_barrier_semaphore()
        peers = [self.at_leaf(k) for k in range(1, self.L)]
        peers += [self.at_chip(q) for q in self.others] + [self.at_sib()]
        for peer in peers:
            pl.semaphore_signal(sem, inc=1, device_id=peer, device_id_type=MESH)
        pl.semaphore_wait(sem, len(peers))


class Wires:
    def __init__(self, at, send_sems, recv_sems, local_sems):
        self.at = at
        self.send_sems, self.recv_sems, self.local_sems = Sems(send_sems), Sems(recv_sems), Sems(local_sems)
        self.open = []

    def send(self, src, dst, dev):
        copy = pltpu.make_async_remote_copy(
            src_ref=src, dst_ref=dst, send_sem=self.send_sems.one(), recv_sem=self.recv_sems.one(),
            device_id=dev, device_id_type=MESH)
        copy.start()
        self.open.append(copy)
        return copy

    def group(self, whole):
        group = Group(self, whole)
        self.open.append(group)
        return group

    def local(self, src, dst):
        copy = pltpu.make_async_copy(src, dst, self.local_sems.one())
        copy.start()
        return copy

    def sent(self, copies):
        for copy in copies:
            copy.wait_send()
        self.open = [copy for copy in self.open if all(copy is not other for other in copies)]

    def drain(self):
        for copy in self.open:
            copy.wait_send()
        self.open = []


class Group:
    def __init__(self, wires, whole):
        self.at, self.whole = wires.at, whole
        self.send_sem, self.recv_sem = wires.send_sems.one(), wires.recv_sems.one()

    def make(self, src, dst, dev):
        return pltpu.make_async_remote_copy(
            src_ref=src, dst_ref=dst, send_sem=self.send_sem, recv_sem=self.recv_sem, device_id=dev, device_id_type=MESH)

    def send(self, src, dst, dev):
        self.make(src, dst, dev).start()
        return self

    def wait_recv(self):
        self.make(self.whole, self.whole, self.at.at_sib()).wait_recv()

    def wait_send(self):
        self.make(self.whole, self.whole, self.at.at_sib()).wait_send()


class Line:
    def __init__(self, wires, at, view, whole):
        self.w, self.at, self.view = wires, at, view
        self.first = wires.send_sems.one()
        self.onward = wires.send_sems.one()
        self.arrive = [None] + [wires.recv_sems.one() for _ in range(3)]
        self.whole = whole
        wires.open.append(self)

    def leaf(self, unit):
        at = self.at
        if unit < 2:
            return at.leaf(unit)
        return jnp.where(at.l < 2, unit, 3 - unit)

    def make(self, src, leaf, unit, to, sem):
        return pltpu.make_async_remote_copy(
            src_ref=src, dst_ref=self.view(leaf), send_sem=sem, recv_sem=self.arrive[unit], device_id=to, device_id_type=MESH)

    def begin(self, src):
        at = self.at
        self.make(src, at.l, 1, at.at_leaf(1), self.first).start()

        @pl.when(at.inner)
        def _():
            self.make(src, at.l, 2, at.at_leaf(3), self.onward).start()

    def early(self, unit):
        at = self.at
        leaf = self.leaf(unit)
        part = self.view(leaf)

        @pl.when(at.inner)
        def _():
            self.make(part, leaf, unit, at.at_sib(), self.first).wait_recv()
            if unit == 1:
                self.make(part, leaf, 3, at.at_leaf(3), self.onward).start()
            else:
                self.make(part, leaf, unit, at.at_leaf(1), self.onward).start()

    def late(self, unit):
        at = self.at
        leaf = self.leaf(unit)

        @pl.when(jnp.logical_not(at.inner))
        def _():
            self.make(self.view(leaf), leaf, unit, at.at_sib(), self.first).wait_recv()

    def wait_send(self):
        at = self.at
        part = self.view(at.l)
        self.make(part, at.l, 1, at.at_sib(), self.first).wait_send()

        @pl.when(at.inner)
        def _():
            pltpu.make_async_remote_copy(
                src_ref=self.whole, dst_ref=self.whole, send_sem=self.onward, recv_sem=self.arrive[1],
                device_id=at.at_sib(), device_id_type=MESH).wait_send()


class Gather:
    def __init__(self, wires, at, shard, full):
        self.w, self.at, self.shard, self.full = wires, at, shard, full
        count = shard.shape[0]
        self.rows = pl.ds(pl.multiple_of(at.c * count, 8), count)
        self.line = Line(wires, at, lambda leaf: full.at[leaf, at.p, self.rows], full.at[:, at.p, self.rows])
        self.pair = wires.group(full.at[:, :, self.rows])
        self.cross, self.relay = {}, {}
        self.sent_cross, self.sent_relay = wires.send_sems.one(), wires.send_sems.one()
        wires.open.append(self)

    def view(self, unit, chip):
        return self.full.at[self.line.leaf(unit), chip, self.rows]

    def make(self, src, dst, to, sem, recv):
        return pltpu.make_async_remote_copy(
            src_ref=src, dst_ref=dst, send_sem=sem, recv_sem=recv, device_id=self.at.at_chip(to), device_id_type=MESH)

    def begin(self):
        self.own = self.w.local(self.shard, self.view(0, self.at.p))
        self.line.begin(self.shard)

    def stage1(self, unit):
        at = self.at
        mine = self.view(unit, at.p)
        src = mine if unit else self.shard
        self.cross[unit] = [self.make(src, mine, q, self.sent_cross, self.w.recv_sems.one()) for q in (at.px, at.py)]
        for copy in self.cross[unit]:
            copy.start()
        self.pair.send(src, mine, at.at_sib())

    def stage2(self, unit):
        at = self.at
        for i, (q, to) in enumerate(((at.px, at.py), (at.py, at.px))):
            self.cross[unit][i].wait_recv()
            theirs = self.view(unit, q)
            if unit % 2 == i:
                self.relay[unit] = self.make(theirs, theirs, to, self.sent_relay, self.w.recv_sems.one())
                self.relay[unit].start()
            self.pair.send(theirs, theirs, at.at_sib())

    def stage3(self, unit):
        self.relay[unit].wait_recv()
        theirs = self.view(unit, self.at.pd)
        self.pair.send(theirs, theirs, self.at.at_sib())

    def finish(self):
        self.own.wait()
        self.pair.wait_recv()

    def wait_send(self):
        at = self.at
        two, one = self.full.at[:, 0:2, self.rows], self.full.at[:, 0, self.rows]
        spare = self.line.arrive[1]
        self.make(two, two, at.px, self.sent_cross, spare).wait_send()
        self.make(one, one, at.px, self.sent_relay, spare).wait_send()


def add_to(ref, *others):
    total = ref[...].astype(F32)
    for other in others:
        total = total + other[...].astype(F32)
    ref[...] = total.astype(ref.dtype)


class Scatter:
    def __init__(self, wires, at, A, sw, dg, xy, zr, fin, sibr, out):
        self.w, self.at = wires, at
        self.A, self.sw, self.dg, self.xy, self.zr, self.fin, self.sibr, self.out = A, sw, dg, xy, zr, fin, sibr, out

    def cross(self, unit, to, side):
        leaf = self.at.leaf(unit)
        self.x.send(self.A.at[leaf, to], self.xy.at[side, leaf], self.at.at_chip(to))

    def step0(self):
        at = self.at
        self.s = self.w.group(self.sw)
        for i in range(2):
            self.s.send(self.A.at[at.leaf(1 + 2 * i), at.pd], self.sw.at[i], at.at_leaf(1))
        self.x = self.w.group(self.xy)

    def step1(self, units):
        at = self.at
        for unit in units:
            if unit != 2:
                self.cross(unit, at.px, 0)
            if unit != 0:
                self.cross(unit, at.py, 1)

    def step1d(self):
        w, at, A = self.w, self.at, self.A
        self.s.wait_recv()
        self.d = []
        for i, to in enumerate((at.px, at.py)):
            add_to(A.at[at.leaf(2 * i), at.pd], self.sw.at[i])
            self.d.append(w.send(A.at[at.leaf(2 * i), at.pd], self.dg.at[i], at.at_chip(to)))

    def step2(self):
        at, A = self.at, self.A
        for i, to in enumerate((at.py, at.px)):
            self.d[i].wait_recv()
            add_to(A.at[at.leaf(2 * i), to], self.dg.at[i])
            self.cross(2 * i, to, 1 - i)

    def step3(self):
        w, at, A = self.w, self.at, self.A
        self.x.wait_recv()
        self.z = w.group(self.zr)
        for k in (1, 2, 3):
            leaf = at.leaf_turn(k)
            add_to(A.at[leaf, at.p], self.xy.at[0, leaf], self.xy.at[1, leaf])
            self.z.send(A.at[leaf, at.p], self.zr.at[at.turn(k) - 1], (leaf, at.s))
        add_to(A.at[at.l, at.p], self.xy.at[0, at.l], self.xy.at[1, at.l])

    def step4(self):
        w, at = self.w, self.at
        self.z.wait_recv()
        total = self.A[at.l, at.p].astype(F32)
        for k in range(at.L - 1):
            total = total + self.zr[k].astype(F32)
        self.fin[...] = total
        rows = self.fin.shape[0] // 2
        self.f = w.send(self.fin.at[pl.ds(pl.multiple_of(rows * (1 - at.c), 8), rows)], self.sibr, at.at_sib())

    def step5(self):
        at = self.at
        rows, half = self.sibr.shape
        mine = self.fin[pl.ds(pl.multiple_of(rows * at.c, 8), rows), :]
        self.out[:, pl.ds(pl.multiple_of(half * at.c, 128), half)] = mine
        self.f.wait_recv()
        self.out[:, pl.ds(pl.multiple_of(half * (1 - at.c), 128), half)] = self.sibr[...]


class PlaneGather:
    def __init__(self, wires, at, buf):
        self.w, self.at, self.buf = wires, at, buf
        rows = buf.shape[1] // 2
        self.halves = pl.ds(0, rows), pl.ds(rows, rows)

    def start(self):
        at, (up, low) = self.at, self.halves
        self.own = [self.w.send(self.buf.at[at.p, half], self.buf.at[at.p, half], at.at_chip(q))
                    for half, q in ((up, at.px), (low, at.py), (low, at.px), (up, at.py))]

    def relay(self):
        at = self.at
        self.passed = []
        for half, copy, q, to in zip(self.halves, self.own, (at.px, at.py), (at.py, at.px)):
            copy.wait_recv()
            theirs = self.buf.at[q, half]
            self.passed.append(self.w.send(theirs, theirs, at.at_chip(to)))

    def near(self):
        for copy in self.own[2:]:
            copy.wait_recv()

    def far(self):
        for copy in self.passed:
            copy.wait_recv()


class PlaneSum:
    def __init__(self, wires, at, A, Ad, Ax):
        self.w, self.at, self.A, self.Ad, self.Ax = wires, at, A, Ad, Ax

    def far(self):
        at = self.at
        self.d = [self.w.send(self.A.at[i, at.pd], self.Ad.at[i], at.at_chip(to)) for i, to in enumerate((at.px, at.py))]
        self.x = self.w.group(self.Ax)

    def near(self, i):
        at = self.at
        to = (at.px, at.py)[i]
        self.x.send(self.A.at[i, to], self.Ax.at[i, i], at.at_chip(to))

    def relay(self):
        at = self.at
        for i, to in enumerate((at.py, at.px)):
            self.d[i].wait_recv()
            add_to(self.A.at[i, to], self.Ad.at[i])
            self.x.send(self.A.at[i, to], self.Ax.at[1 - i, i], at.at_chip(to))

    def total(self):
        self.x.wait_recv()
        return [self.A[i, self.at.p].astype(F32) + self.Ax[0, i].astype(F32) + self.Ax[1, i].astype(F32) for i in range(2)]


class LineSum:
    def __init__(self, wires, at, A, As, zr):
        self.w, self.at, self.A, self.As, self.zr = wires, at, A, As, zr

    def pair(self):
        self.s = self.w.send(self.A.at[1 - self.at.c], self.As, self.at.at_sib())

    def line(self):
        at, A = self.at, self.A
        self.s.wait_recv()
        self.z = self.w.group(self.zr)
        for k in (1, 2, 3):
            leaf = at.leaf_turn(k)
            add_to(A.at[at.c, leaf], self.As.at[leaf])
            self.z.send(A.at[at.c, leaf], self.zr.at[at.turn(k) - 1], (leaf, at.s))
        add_to(A.at[at.c, at.l], self.As.at[at.l])

    def total(self):
        self.z.wait_recv()
        total = self.A[self.at.c, self.at.l].astype(F32)
        for k in range(self.at.L - 1):
            total = total + self.zr[k].astype(F32)
        return total


class Columns:
    def __init__(self, wires, at, full):
        self.w, self.at, self.full = wires, at, full
        count = full.shape[2] // 2
        self.rows = pl.ds(pl.multiple_of(at.c * count, 8), count)
        self.first = wires.group(full.at[0, 0:3, self.rows])
        self.line = Line(wires, at, self.held, full.at[:, :, self.rows])
        self.pair = wires.group(full.at[:, :, self.rows])

    def held(self, leaf):
        return self.full.at[leaf, :, self.rows]

    def start(self, parts):
        at = self.at
        mine = self.full.at[at.l, at.p, self.rows]
        for q in at.others:
            self.first.send(parts.at[q], mine, at.at_chip(q))
        self.own = self.w.local(parts.at[at.p], mine)

    def begin(self):
        at = self.at
        self.first.wait_recv()
        self.own.wait()
        self.line.begin(self.held(at.l))
        self.pair.send(self.held(at.l), self.held(at.l), at.at_sib())

    def late(self, unit):
        self.line.late(unit)
        part = self.held(self.line.leaf(unit))
        self.pair.send(part, part, self.at.at_sib())


class Rows:
    def __init__(self, wires, at, shard, full):
        self.w, self.at, self.shard, self.full = wires, at, shard, full
        count = shard.shape[0]
        self.rows = pl.ds(pl.multiple_of(at.c * count, 8), count)
        self.line = Line(wires, at, self.held, full.at[:, self.rows])
        self.pair = wires.group(full.at[:, self.rows])

    def held(self, leaf):
        return self.full.at[leaf, self.rows]

    def begin(self):
        at = self.at
        self.own = self.w.local(self.shard, self.held(at.l))
        self.line.begin(self.shard)
        self.pair.send(self.shard, self.held(at.l), at.at_sib())

    def late(self, unit):
        self.line.late(unit)
        part = self.held(self.line.leaf(unit))
        self.pair.send(part, part, self.at.at_sib())


def norm_rows(values):
    centred = values - jnp.mean(values, axis=-1, keepdims=True)
    variance = jnp.mean(centred * centred, axis=-1, keepdims=True)
    rstd = lax.rsqrt(variance + EPSILON)
    return centred * rstd, rstd


def norm_back(grad, normed, rstd):
    return rstd * (grad - jnp.mean(grad, axis=-1, keepdims=True) - normed * jnp.mean(grad * normed, axis=-1, keepdims=True))


def total_rows(values):
    return jnp.sum(values, axis=0, keepdims=True)


def dot(left, right):
    return jnp.dot(left, right, preferred_element_type=F32)


def dot_t(left, right):
    return lax.dot_general(left, right, (((1,), (1,)), ((), ())), preferred_element_type=F32)


def tile(j, size):
    return pl.ds(pl.multiple_of(j * size, size), size)


def condition_column(at, timestep, count, width):
    half = width // 2
    row = (at.l * at.S + at.s) * count + lax.broadcasted_iota(jnp.int32, (count, 1), 0)
    index = jnp.where(row < half, row, row - half).astype(F32)
    angle = timestep.astype(F32) * jnp.exp(-math.log(10000.0) * index / half)
    value = jnp.where(row < half, jnp.cos(angle), jnp.sin(angle))
    return (value / (1.0 + jnp.exp(-value))).astype(BF16).astype(F32)


def fill_bias(at, R):
    _, seg_count, blocks = R.live.shape

    def fill(k, carry):
        seg = 2 * k + at.c
        current = seg
        reached = [jnp.where(seg == a, 1, 0) for a in range(seg_count)]
        for _ in range(seg_count):
            current = R.parent[0, current]
            reached = [jnp.where(current == a, 1, r) for a, r in enumerate(reached)]
        for a in range(seg_count):
            for b in range(blocks):
                R.bias[k, a * blocks + b] = jnp.where(reached[a] * R.live[0, a, b] > 0, 0.0, NEGATIVE)
        return carry

    lax.fori_loop(0, at.P, fill, 0)


def seen_scores(R, score, chip, a):
    blocks = R.live.shape[2]
    rows = score.shape[0] // blocks
    return jnp.concatenate(
        [score[b * rows : (b + 1) * rows] + R.bias[chip, a * blocks + b] for b in range(blocks)], axis=0)


def layer(at, w, R):
    L, S, PC = at.L, at.S, at.P
    T, D = R.tok.shape
    HD = D // HEADS
    HG = HEADS // PC
    GW = HG * HD
    CW = R.Wh.shape[1]
    HU = R.Wu.shape[1]
    DH, TH = D // 2, T // 2
    MR = R.wq.shape[0]
    HB = HU // L
    trunk = S // 2
    NK = PC // 2 + 1
    part = lambda i: slice(i * D, (i + 1) * D)
    head_rows = lambda h: slice(h * HD, (h + 1) * HD)
    go = Gather(w, at, R.wo, R.Go)
    cq, cu = Columns(w, at, R.Gh), Columns(w, at, R.Gu)
    rd = Rows(w, at, R.wd, R.Gd)

    def key_count(seg):
        return jnp.minimum(seg, trunk) + 1 + jnp.where(seg > trunk, 1, 0)

    at.barrier()
    wq, wu = R.wq[...].astype(F32), R.wu[...].astype(F32)
    for q in range(PC):
        pieces = [wq[:, k * D + q * GW : k * D + (q + 1) * GW] for k in range(3)]
        R.wqs[q] = jnp.concatenate(pieces + [jnp.zeros((MR, CW - 3 * GW), F32)], axis=1).astype(BF16)
    cq.start(R.wqs)
    for q in range(PC):
        R.wus[q] = jnp.concatenate([wu[:, k * HU + q * HB : k * HU + (q + 1) * HB] for k in range(L)], axis=1).astype(BF16)
    modw = R.modw[...].astype(F32)
    for t in range(L):
        column = condition_column(at, R.time[t], modw.shape[0], D)
        R.cond[t] = column
        R.mpart[t] = total_rows(column * modw)
    mz = w.group(R.mz)
    for k in range(1, L):
        mz.send(R.mpart.at[at.leaf(k)], R.mz.at[k - 1], at.at_leaf(k))
    R.pos2[at.p] = R.pos[...].astype(F32)
    ps = w.group(R.pos2.at[0:3])
    for q in at.others:
        ps.send(R.pos2.at[at.p], R.pos2.at[at.p], at.at_chip(q))
    normed, _ = norm_rows(R.tok[...].astype(F32))
    R.dh[...] = normed
    cu.start(R.wus)
    cq.begin()
    mz.wait_recv()
    total = R.mpart[at.l]
    for k in range(L - 1):
        total = total + R.mz[k]
    R.m1[...] = total
    mp = w.group(R.mp)
    for i, q in enumerate(at.others):
        mp.send(R.m1, R.mp.at[i], at.at_chip(q))
    go.stage1(0)
    fill_bias(at, R)
    mp.wait_recv()
    for i in range(3):
        total = total + R.mp[i]
    R.m2[...] = total
    ms = w.send(R.m2, R.ms, at.at_sib())
    ms.wait_recv()
    R.mod[...] = total + R.ms[...]
    shift_a, scale_a, gate_a, shift_b, scale_b, gate_b = (R.mod[:, part(i)] for i in range(6))
    R.hA[at.p] = (R.dh[...] * (1.0 + scale_a) + shift_a).astype(BF16)
    ha = PlaneGather(w, at, R.hA)
    ha.start()
    cq.line.early(1)
    cq.line.early(2)
    cq.late(1)
    slow = jnp.exp(-math.log(10000.0) * 2.0 * lax.broadcasted_iota(jnp.int32, (HD // 2, 1), 0).astype(F32) / HD)
    ps.wait_recv()
    for k in range(PC):
        angles = slow * R.pos2[k]
        R.cos[k] = jnp.cos(angles)
        R.sin[k] = jnp.sin(angles)
    R.dbb[at.p] = (gate_b * R.g[...].astype(F32)).astype(BF16)
    db = PlaneGather(w, at, R.dbb)
    cq.line.early(3)
    go.begin()
    cu.begin()
    cq.late(2)
    ha.relay()
    go.line.early(1)
    go.line.early(2)
    cu.line.early(1)
    cq.late(3)
    go.line.late(1)
    go.stage1(1)
    db.start()
    cq.pair.wait_recv()
    load = w.local(R.Gh.reshape(D, CW), R.Wh)
    load.wait()

    def project(q):
        cosine, sine = R.cos[q], R.sin[q]
        hidden = R.hA[q]
        R.haT[q] = hidden.T
        for j in range(0, CW, 128):
            rows = dot(hidden, R.Wh[:, j : j + 128]).T
            for i in range(128 // HD):
                kind, h = divmod(j // HD + i, HG)
                if kind == 3:
                    continue
                first, second = rows[i * HD : i * HD + HD // 2], rows[i * HD + HD // 2 : (i + 1) * HD]
                if kind < 2:
                    first, second = first * cosine - second * sine, second * cosine + first * sine
                if kind == 0:
                    first, second = first * HD**-0.5, second * HD**-0.5
                low, high = pl.ds(h * HD, HD // 2), pl.ds(h * HD + HD // 2, HD // 2)
                if kind == 0:
                    R.QT[q, low, :] = first.astype(BF16)
                    R.QT[q, high, :] = second.astype(BF16)
                else:
                    R.KVT[2 * q + at.c, kind - 1, low, :] = first.astype(BF16)
                    R.KVT[2 * q + at.c, kind - 1, high, :] = second.astype(BF16)

    project(at.p)
    go.line.early(3)
    cu.line.early(2)
    rd.begin()
    ha.near()
    project(at.px)
    project(at.py)
    go.line.late(2)
    go.stage1(2)
    cu.late(1)
    ha.far()
    project(at.pd)
    sk = w.group(R.KVT.at[0:NK])
    for k in range(NK):
        sk.send(R.KVT.at[2 * k + at.c], R.KVT.at[2 * k + at.c], at.at_sib())
    go.line.late(3)
    go.stage1(3)
    cu.line.early(3)
    sk.wait_recv()

    def flip_k(a, carry):
        for h in range(HG):
            R.kN[a, h] = R.KVT[a, 0, head_rows(h), :].T
        return carry

    lax.fori_loop(0, S, flip_k, 0)
    ret = w.group(R.hsnd.at[0:3])
    for i, q in enumerate([at.pd, at.px, at.py, at.p]):
        seg = 2 * q + at.c

        def block(j, state, q=q, seg=seg):
            a = jnp.where(j > trunk, seg, j)
            out = []
            for h in range(HG):
                m, t, o = state[3 * h : 3 * h + 3]
                score = seen_scores(R, dot(R.kN[a, h], R.QT[q, head_rows(h), :]), q, a)
                m_new = jnp.maximum(m, jnp.max(score, axis=0, keepdims=True))
                alpha = jnp.exp(m - m_new)
                e = jnp.exp(score - m_new)
                t = t * alpha + total_rows(e)
                o = o * alpha + dot(R.KVT[a, 1, head_rows(h), :], e.astype(BF16))
                out += [m_new, t, o]
            return tuple(out)

        start = (jnp.full((1, T), NEGATIVE, F32), jnp.zeros((1, T), F32), jnp.zeros((HD, T), F32)) * HG
        state = lax.fori_loop(0, key_count(seg), block, start)
        for h in range(HG):
            m, t, o = state[3 * h : 3 * h + 3]
            o = o / t
            R.OT[q, head_rows(h), :] = o
            R.hsnd[q, head_rows(h), :] = o.astype(BF16)
            R.lse[q, h : h + 1, :] = m + jnp.log(t)
        if i < 3:
            ret.send(R.hsnd.at[q], R.attT2.at[0, at.p], at.at_chip(q))
        else:
            own_att = w.local(R.hsnd.at[q], R.attT2.at[0, at.p])
        if i == 0:
            for u in range(L):
                go.stage2(u)
            db.relay()
            cu.late(2)
            rd.line.early(1)
            rd.line.early(2)
        if i == 1:
            cu.late(3)
            rd.late(1)
        if i == 2:
            for u in range(L):
                go.stage3(u)
            rd.line.early(3)
    go.finish()
    load = w.local(R.Go.reshape(D, D), R.Wo)
    own_att.wait()
    ret.wait_recv()
    sib_att = w.send(R.attT2.at[0], R.attT2.at[1], at.at_sib())
    load.wait()
    att = jnp.concatenate([R.attT2[0, k].T for k in range(PC)], axis=1)
    for j in range(0, D, 256):
        lanes = slice(j, j + 256)
        branch = dot(att, R.Wo[:, lanes])
        R.br_a[:, lanes] = branch
        R.middle[:, lanes] = R.tok[:, lanes].astype(F32) + gate_a[:, lanes] * branch
    normed, _ = norm_rows(R.middle[...])
    R.hB[at.p] = (normed * (1.0 + scale_b) + shift_b).astype(BF16)
    hb = PlaneGather(w, at, R.hB)
    hb.start()
    rd.late(2)
    rd.late(3)
    cu.pair.wait_recv()
    loads = [w.local(R.Gu.reshape(D, HU), R.Wu)]
    rd.own.wait()
    rd.pair.wait_recv()
    loads.append(w.local(R.Gd.reshape(HU, D), R.Wd))
    for load in loads:
        load.wait()
    db.near()
    db.far()

    def feed(k):
        hidden = R.hB[k]
        R.hBT[k] = hidden.T
        for j in range(0, HU, 256):
            lanes = slice(j, j + 256)
            u = dot(hidden, R.Wu[:, lanes])
            square = u * u
            tanh = jnp.tanh(GELU_A * (u + GELU_B * square * u))
            act = (0.5 * u * (1.0 + tanh)).astype(BF16)
            R.active[k, :, lanes] = act
            R.actT[k, lanes, :] = act.T
            slope = 0.5 * (1.0 + tanh) + (0.5 * GELU_A) * u * (1.0 - tanh * tanh) * (1.0 + 3.0 * GELU_B * square)
            R.du[k, :, lanes] = (dot_t(R.dbb[k], R.Wd[lanes, :]) * slope).astype(BF16)

    def feed_back(k):
        for i in range(2):
            R.dB[i, k] = dot_t(R.du[k, i * TH : (i + 1) * TH, :], R.Wu[...]).astype(BF16)

    feed(at.p)
    hb.relay()
    hb.near()
    feed(at.px)
    feed(at.py)
    hb.far()
    feed(at.pd)
    scat = {"o": Scatter(w, at, *(getattr(R, x + "o") for x in ("A", "sw", "dg", "xy", "zr", "fin", "sr", "v")))}
    sb = PlaneSum(w, at, R.dB, R.dBd, R.dBx)
    feed_back(at.pd)
    sb.far()
    feed_back(at.px)
    sb.near(0)
    feed_back(at.py)
    sb.near(1)
    feed_back(at.p)
    RD = HU // L
    ld, lu, lq = (LineSum(w, at, *(getattr(R, x + n) for x in ("A", "As", "zr"))) for n in ("d", "u", "q"))

    def down_grad(i, carry):
        total = dot(R.actT[0, tile(i, RD), :], R.dbb[0])
        for k in range(1, PC):
            total = total + dot(R.actT[k, tile(i, RD), :], R.dbb[k])
        for core in range(2):
            R.Ad[core, i] = total[core * (RD // 2) : (core + 1) * (RD // 2)].astype(BF16)
        return carry

    lax.fori_loop(0, L, down_grad, 0)
    ld.pair()
    sb.relay()

    def by_core(A, i, total):
        for core in range(2):
            rows = [total[(2 * k + core) * MR : (2 * k + core + 1) * MR] for k in range(PC)]
            A[core, i] = jnp.concatenate(rows, axis=0).astype(BF16)

    def up_grad(i, carry):
        total = dot(R.hBT[0, tile(i, D // L), :], R.du[0])
        for k in range(1, PC):
            total = total + dot(R.hBT[k, tile(i, D // L), :], R.du[k])
        by_core(R.Au, i, total)
        return carry

    lax.fori_loop(0, L, up_grad, 0)
    lu.pair()
    ld.line()
    lu.line()
    dh = jnp.concatenate(sb.total(), axis=0)
    normed, rstd = norm_rows(R.middle[...])
    R.gm[:, part(3)] = total_rows(dh)
    R.gm[:, part(4)] = total_rows(dh * normed)
    dmid = R.g[...].astype(F32) + norm_back(dh * (1.0 + scale_b), normed, rstd)
    R.dmid[...] = dmid
    R.gm[:, part(2)] = total_rows(dmid * R.br_a[...])
    dba = (gate_a * dmid).astype(BF16)
    R.dba[...] = dba
    for h in range(2):
        R.dbah[h] = dba[:, h * DH : (h + 1) * DH]
    sib_dba = w.send(R.dbah.at[1 - at.c], R.dbas, at.at_sib())
    w.sent([ret])
    for j in range(PC):
        R.hsnd[j] = dot_t(R.Wo[j * GW : (j + 1) * GW, :], R.dba[...]).astype(BF16)
    dos = [w.send(R.hsnd.at[q], R.dOT.at[at.p], at.at_chip(q)) for q in at.others]
    own_do = w.local(R.hsnd.at[at.p], R.dOT.at[at.p])
    RB2 = D // (L * PC)
    sib_dba.wait_recv()
    sib_att.wait_recv()
    attT = [R.attT2[i].reshape(D, T) for i in range(2)]
    block = dot(attT[0], R.dbah[at.c]) + dot(attT[1], R.dbas[...])
    for i in range(L * PC):
        R.Ao[i // PC, i % PC] = block[i * RB2 : (i + 1) * RB2].astype(BF16)
    scat["o"].step0()
    sc = PlaneSum(w, at, R.bB, R.bBd, R.bBx)
    for k in (at.pd, at.px, at.py, at.p):
        for i in range(2):
            R.bB[i, k] = dot(R.active[k, i * TH : (i + 1) * TH, :], R.Wd[...]).astype(BF16)
    sc.far()
    sc.near(0)
    sc.near(1)

    def flip_v(a, carry):
        for h in range(HG):
            R.vN[a, h] = R.KVT[a, 1, head_rows(h), :].T
        R.acc[a] = jnp.zeros((2, GW, T), F32)
        return carry

    lax.fori_loop(0, S, flip_v, 0)
    for k in range(PC):
        R.dpT[k, 3 * GW : CW, :] = jnp.zeros((CW - 3 * GW, T), BF16)
    own_do.wait()

    def unturn(first, second, q):
        cosine, sine = R.cos[q], R.sin[q]
        return jnp.concatenate([first * cosine + second * sine, second * cosine - first * sine], axis=0)

    for i, q in enumerate([at.p, at.px, at.py, at.pd]):
        seg = 2 * q + at.c
        if i:
            dos[i - 1].wait_recv()
        delta = [total_rows(R.dOT[q, head_rows(h), :].astype(F32) * R.OT[q, head_rows(h), :]) for h in range(HG)]

        def block(j, dqs, q=q, seg=seg, delta=delta):
            a = jnp.where(j > trunk, seg, j)
            out = []
            for h in range(HG):
                rows = head_rows(h)
                qT, dO = R.QT[q, rows, :], R.dOT[q, rows, :]
                prob = jnp.exp(seen_scores(R, dot(R.kN[a, h], qT), q, a) - R.lse[q, h : h + 1, :])
                dprob = dot(R.vN[a, h], dO)
                ds = (prob * (dprob - delta[h])).astype(BF16)
                out.append(dqs[h] + dot(R.KVT[a, 0, rows, :], ds))
                R.acc[a, 0, rows, :] += dot_t(qT, ds)
                R.acc[a, 1, rows, :] += dot_t(dO, prob.astype(BF16))
            return tuple(out)

        dqs = lax.fori_loop(0, key_count(seg), block, (jnp.zeros((HD, T), F32),) * HG)
        for h in range(HG):
            dq = dqs[h] * HD**-0.5
            R.dpT[q, head_rows(h), :] = unturn(dq[: HD // 2], dq[HD // 2 :], q).astype(BF16)
        if i == 0:
            sc.relay()
            scat["o"].step1d()
            scat["o"].step1((1, 3, 0, 2))
        if i == 2:
            scat["o"].step2()
    sk = w.group(R.acs)
    for k in range(NK):
        sk.send(R.acc.at[2 * k + 1 - at.c], R.acs.at[k], at.at_sib())
    branch = sc.total()
    for i in range(2):
        rows = slice(i * TH, (i + 1) * TH)
        R.vlo[rows, :] = (R.middle[rows, :] + gate_b * branch[i]).astype(BF16)
    R.gm[:, part(5)] = total_rows(R.g[...].astype(F32) * jnp.concatenate(branch, axis=0))
    results = [w.local(R.vlo, R.lo)]
    sk.wait_recv()
    for k in range(PC):
        for i in range(2):
            grad = R.acc[2 * k + at.c, i]
            if k < NK:
                grad = grad + R.acs[k, i]
            for h in range(HG):
                one = grad[head_rows(h)]
                if i == 0:
                    one = unturn(one[: HD // 2], one[HD // 2 :], k)
                R.dpT[k, (i + 1) * GW + h * HD : (i + 1) * GW + (h + 1) * HD, :] = one.astype(BF16)
    sa = PlaneSum(w, at, R.dA, R.dAd, R.dAx)
    for n, q in enumerate((at.pd, at.px, at.py, at.p)):
        for i in range(2):
            R.dA[i, q] = dot(R.Wh[i * DH : (i + 1) * DH, :], R.dpT[q]).astype(BF16)
        if n == 0:
            sa.far()
        elif n < 3:
            sa.near(n - 1)
    scat["o"].step3()
    def proj_grad(i, carry):
        total = dot_t(R.haT[0, tile(i, D // L), :], R.dpT[0])
        for k in range(1, PC):
            total = total + dot_t(R.haT[k, tile(i, D // L), :], R.dpT[k])
        by_core(R.Aq, i, total)
        return carry

    lax.fori_loop(0, L, proj_grad, 0)
    lq.pair()
    lq.line()
    sa.relay()
    R.vd[...] = ld.total()
    results.append(w.local(R.vd, R.od))

    def to_chips(fin, buf):
        group = w.group(buf.at[0:3])
        mine = lambda q: fin.at[pl.ds(pl.multiple_of(q * MR, 8), MR)]
        for q in at.others:
            group.send(mine(q), buf.at[at.p], at.at_chip(q))
        return group, w.local(mine(at.p), buf.at[at.p])

    R.finu[...] = lu.total()
    ru = to_chips(R.finu, R.ru)
    dh = jnp.concatenate([half.T for half in sa.total()], axis=1)
    normed, rstd = norm_rows(R.tok[...].astype(F32))
    R.gm[:, part(0)] = total_rows(dh)
    R.gm[:, part(1)] = total_rows(dh * normed)
    gsib = w.send(R.gm, R.gs, at.at_sib())
    R.vgt[...] = R.dmid[...] + norm_back(dh * (1.0 + scale_a), normed, rstd)
    results.append(w.local(R.vgt, R.gt))
    gsib.wait_recv()
    R.g1[...] = R.gm[...] + R.gs[...]
    gp = w.group(R.gp)
    for i, q in enumerate(at.others):
        gp.send(R.g1, R.gp.at[i], at.at_chip(q))
    for copy in ru:
        (copy.wait_recv if copy is ru[0] else copy.wait)()
    R.vu[...] = jnp.concatenate([R.ru[q][:, k * HB : (k + 1) * HB] for k in range(L) for q in range(PC)], axis=1)
    results.append(w.local(R.vu, R.ou))
    R.finq[...] = lq.total()
    rq = to_chips(R.finq, R.rq)
    gp.wait_recv()
    total = R.g1[...]
    for i in range(3):
        total = total + R.gp[i]
    R.gtree[at.l] = total
    gz = w.group(R.gtree.at[0:3])
    for k in range(1, L):
        gz.send(R.gtree.at[at.l], R.gtree.at[at.l], at.at_leaf(k))
    scat["o"].step4()
    scat["o"].step5()
    results.append(w.local(R.vo, R.oo))
    rq[1].wait()
    rq[0].wait_recv()
    R.vq[...] = jnp.concatenate([R.rq[q][:, k * GW : (k + 1) * GW] for k in range(3) for q in range(PC)], axis=1)
    results.append(w.local(R.vq, R.oq))
    gz.wait_recv()
    total = R.cond[0] * R.gtree[0]
    for t in range(1, L):
        total = total + R.cond[t] * R.gtree[t]
    R.vm[...] = total
    results.append(w.local(R.vm, R.om))
    for copy in results:
        copy.wait()


class Refs:
    def __init__(self, **refs):
        self.__dict__.update(refs)


def call_layer(L, S, tok, g, time, parent, pos, live, wq, wo, wu, wd, modw):
    T, D = tok.shape
    FF = wu.shape[1]
    PC, HD = S // 2, D // HEADS
    HG = HEADS // PC
    GW = HG * HD
    CW = -(-3 * GW // 128) * 128
    NM, MR = L * S, wq.shape[0]
    sd = jax.ShapeDtypeStruct
    DM, V = pltpu.SemaphoreType.DMA, pltpu.VMEM
    ins = dict(tok=tok, g=g, time=time, parent=parent, pos=pos, live=live, wq=wq, wo=wo, wu=wu, wd=wd, modw=modw)
    HU = FF // PC
    outs = dict(Go=sd((L, PC, 2 * MR, D), BF16), Gh=sd((L, PC, 2 * MR, CW), BF16), Gu=sd((L, PC, 2 * MR, HU), BF16),
                Gd=sd((L, 2 * wd.shape[0], D), BF16))
    last = dict(lo=((T, D), BF16), gt=((T, D), F32), oq=((MR, 3 * D), F32), oo=((MR, D), F32),
                ou=((MR, FF), F32), od=((FF // NM, D), F32), om=((MR, 6 * D), F32))
    outs.update({k: sd(*v) for k, v in last.items()})
    M6 = 6 * D
    scr = dict(
        Wh=V((D, CW), BF16), Wo=V((D, D), BF16), Wu=V((D, HU), BF16), Wd=V((HU, D), BF16), wqs=V((PC, MR, CW), BF16), wus=V((PC, MR, HU), BF16),
        bias=pltpu.SMEM((PC, live.size), F32), cond=V((L, MR, 1), F32),
        pos2=V((PC, 1, T), F32), cos=V((PC, HD // 2, T), F32), sin=V((PC, HD // 2, T), F32),
        mpart=V((L, 1, M6), F32), mz=V((L - 1, 1, M6), F32), m1=V((1, M6), F32), mp=V((3, 1, M6), F32), m2=V((1, M6), F32),
        ms=V((1, M6), F32), mod=V((1, M6), F32),
        hA=V((PC, T, D), BF16), haT=V((PC, D, T), BF16), QT=V((PC, GW, T), BF16),
        KVT=V((S, 2, GW, T), BF16), kN=V((S, HG, T, HD), BF16), OT=V((PC, GW, T), F32), lse=V((PC, 8, T), F32),
        hsnd=V((PC, GW, T), BF16), attT2=V((2, PC, GW, T), BF16), br_a=V((T, D), F32), middle=V((T, D), F32),
        hB=V((PC, T, D), BF16), hBT=V((PC, D, T), BF16), active=V((PC, T, HU), BF16), actT=V((PC, HU, T), BF16),
        dbb=V((PC, T, D), BF16), du=V((PC, T, HU), BF16), dh=V((T, D), F32), dmid=V((T, D), F32),
        dB=V((2, PC, T // 2, D), BF16), dBd=V((2, T // 2, D), BF16), dBx=V((2, 2, T // 2, D), BF16),
        bB=V((2, PC, T // 2, D), BF16), bBd=V((2, T // 2, D), BF16), bBx=V((2, 2, T // 2, D), BF16),
        Au=V((2, L, PC * MR, HU), BF16), Asu=V((L, PC * MR, HU), BF16), zru=V((L - 1, PC * MR, HU), BF16),
        finu=V((PC * MR, HU), F32), ru=V((PC, MR, HU), F32),
        Ad=V((2, L, HU // L // 2, D), BF16), Asd=V((L, HU // L // 2, D), BF16), zrd=V((L - 1, HU // L // 2, D), BF16),
        dba=V((T, D), BF16), dbah=V((2, T, D // 2), BF16), dbas=V((T, D // 2), BF16),
        dOT=V((PC, GW, T), BF16), vN=V((S, HG, T, HD), BF16),
        acc=V((S, 2, GW, T), F32), acs=V((PC // 2 + 1, 2, GW, T), F32), dpT=V((PC, CW, T), BF16),
        dA=V((2, PC, D // 2, T), BF16), dAd=V((2, D // 2, T), BF16), dAx=V((2, 2, D // 2, T), BF16),
        Aq=V((2, L, PC * MR, CW), BF16), Asq=V((L, PC * MR, CW), BF16), zrq=V((L - 1, PC * MR, CW), BF16),
        finq=V((PC * MR, CW), F32), rq=V((PC, MR, CW), F32),
        gm=V((1, M6), F32), gs=V((1, M6), F32), g1=V((1, M6), F32), gp=V((3, 1, M6), F32), gtree=V((L, 1, M6), F32))
    for n, rows, cols in (("o", D, D),):
        rb, half = rows // (L * PC), cols // 2
        scr["A" + n] = V((L, PC, rb, half), BF16)
        scr["sw" + n] = V((2, rb, half), BF16)
        scr["dg" + n] = V((2, rb, half), BF16)
        scr["xy" + n] = V((2, L, rb, half), BF16)
        scr["zr" + n] = V((L - 1, rb, half), BF16)
        scr["fin" + n] = V((rb, half), F32)
        scr["sr" + n] = V((rb // 2, half), F32)
    for k, v in last.items():
        scr["v" + k.removeprefix("o") if k != "lo" else "vlo"] = V(*v)
    scr.update(send_sems=DM((72,)), recv_sems=DM((86,)), local_sems=DM((19,)))
    space = dict.fromkeys(("time", "parent", "live"), pltpu.SMEM)
    space.update(dict.fromkeys(("wo", "wd", *outs), pltpu.HBM))
    spec = lambda k: pl.BlockSpec(memory_space=space.get(k, pltpu.VMEM))

    def kernel(*refs):
        R = Refs(**dict(zip(list(ins) + list(outs) + list(scr), refs)))
        at = Place(L, S)
        w = Wires(at, R.send_sems, R.recv_sems, R.local_sems)
        layer(at, w, R)
        w.drain()

    res = pl.pallas_call(
        kernel, out_shape=list(outs.values()), in_specs=[spec(k) for k in ins], out_specs=[spec(k) for k in outs],
        scratch_shapes=list(scr.values()),
        compiler_params=pltpu.CompilerParams(collective_id=1, has_side_effects=True, vmem_limit_bytes=64 << 20),
    )(*ins.values())
    return dict(zip(outs, res))


def hand_out(*arrays):
    count = len(arrays)

    def kernel(*refs):
        sources, targets, held, sems = refs[:count], refs[count : 2 * count], refs[2 * count : 3 * count], refs[-1]
        arrive = [pltpu.make_async_copy(x, y, sems.at[0, i]) for i, (x, y) in enumerate(zip(sources, held))]
        leave = [pltpu.make_async_copy(x, y, sems.at[1, i]) for i, (x, y) in enumerate(zip(held, targets))]
        for copy in arrive:
            copy.start()
        for first, second in zip(arrive, leave):
            first.wait()
            second.start()
        for copy in leave:
            copy.wait()

    hbm = pl.BlockSpec(memory_space=pltpu.HBM)
    return pl.pallas_call(
        kernel, out_shape=[jax.ShapeDtypeStruct(a.shape, a.dtype) for a in arrays],
        in_specs=[hbm] * count, out_specs=[hbm] * count,
        scratch_shapes=[pltpu.VMEM(a.shape, a.dtype) for a in arrays] + [pltpu.SemaphoreType.DMA((2, count))],
    )(*arrays)


def layer_kernels(
    tokens, cotangent, timesteps, parent, positions, block_live, qkv_weight, out_weight, up_weight, down_weight, mod_weight
):
    f = call_layer(
        lax.axis_size("leaf"), lax.axis_size("seq"), tokens[0], cotangent[0], timesteps, parent, positions, block_live,
        qkv_weight, out_weight, up_weight, down_weight, mod_weight,
    )
    lo, gt, *rest = hand_out(*(f[k] for k in ("lo", "gt", "oq", "oo", "ou", "od", "om")))
    return (lo[None], gt[None], *rest)


def layer_norm(values):
    centred = values - jnp.mean(values, axis=-1, keepdims=True)
    variance = jnp.mean(centred * centred, axis=-1, keepdims=True)
    return centred * lax.rsqrt(variance + EPSILON)


def time_embed(step_values, model_width):
    half_width = model_width // 2
    freqs = jnp.exp(-math.log(10000.0) * jnp.arange(half_width, dtype=jnp.float32) / half_width)
    angles = step_values.astype(jnp.float32)[..., None] * freqs
    return jnp.concatenate([jnp.cos(angles), jnp.sin(angles)], axis=-1)


def rope_tables(places, head_dim):
    half_dim = head_dim // 2
    inverse = jnp.exp(-math.log(10000.0) * 2.0 * jnp.arange(half_dim, dtype=jnp.float32) / head_dim)
    angles = places.astype(jnp.float32)[:, None] * inverse[None, :]
    return (jnp.cos(angles), jnp.sin(angles))


def rotate(values, cosine, sine):
    half_dim = values.shape[-1] // 2
    first = values[..., :half_dim]
    second = values[..., half_dim:]
    cos_wide = cosine[:, None, :]
    sin_wide = sine[:, None, :]
    return jnp.concatenate(
        [first * cos_wide - second * sin_wide, second * cos_wide + first * sin_wide], axis=-1
    )


def rotate_back(grads, cosine, sine):
    half_dim = grads.shape[-1] // 2
    first = grads[..., :half_dim]
    second = grads[..., half_dim:]
    cos_wide = cosine[:, None, :]
    sin_wide = sine[:, None, :]
    return jnp.concatenate(
        [first * cos_wide + second * sin_wide, second * cos_wide - first * sin_wide], axis=-1
    )


def ancestor_row(parent_row, seg_index, seg_count):
    seg_range = jnp.arange(seg_count, dtype=jnp.int32)

    def climb(step_index, state_now):
        current, reached = state_now
        current = parent_row[current]
        return (current, reached | (seg_range == current))

    return lax.fori_loop(0, seg_count, climb, (seg_index, seg_range == seg_index))[1]


def attend_keys(state_now, query_rot, key_block, value_block, key_ok, score_scale):
    maximum_old, total_old, accum_old = state_now
    scores = (
        jnp.einsum("qhd,khd->hqk", query_rot, key_block, preferred_element_type=jnp.float32)
        * score_scale
    )
    visible = key_ok[None, None, :]
    scores = jnp.where(visible, scores, NEGATIVE)
    maximum_new = jnp.maximum(maximum_old, jnp.max(scores, axis=-1))
    weights_p = jnp.where(visible, jnp.exp(scores - maximum_new[..., None]), 0.0)
    rescale = jnp.exp(maximum_old - maximum_new)
    total_new = total_old * rescale + jnp.sum(weights_p, axis=-1)
    accum_new = accum_old * rescale[..., None] + jnp.einsum(
        "hqk,khd->hqd",
        weights_p.astype(jnp.bfloat16),
        value_block,
        preferred_element_type=jnp.float32,
    )
    return (maximum_new, total_new, accum_new)


def score_grads(
    query_rot, grad_attended, log_total, delta_rows, key_block, value_block, mask_wide, score_scale
):
    scores = (
        jnp.einsum("qhd,khd->hqk", query_rot, key_block, preferred_element_type=jnp.float32)
        * score_scale
    )
    probs = jnp.where(mask_wide, jnp.exp(scores - log_total[..., None]), 0.0)
    grad_probs = jnp.einsum(
        "qhd,khd->hqk", grad_attended, value_block, preferred_element_type=jnp.float32
    )
    grad_scores = (probs * (grad_probs - delta_rows[..., None])).astype(jnp.bfloat16)
    return (probs, grad_scores)


def query_only(
    grad_query,
    query_rot,
    grad_attended,
    log_total,
    delta_rows,
    key_block,
    value_block,
    key_ok,
    score_scale,
):
    probs, grad_scores = score_grads(
        query_rot,
        grad_attended,
        log_total,
        delta_rows,
        key_block,
        value_block,
        key_ok[None, None, :],
        score_scale,
    )
    return (
        grad_query
        + jnp.einsum("hqk,khd->qhd", grad_scores, key_block, preferred_element_type=jnp.float32)
        * score_scale
    )


def layer_native(
    tokens,
    cotangent,
    timesteps,
    parent,
    positions,
    block_live,
    qkv_weight,
    out_weight,
    up_weight,
    down_weight,
    mod_weight,
):
    seg_count = lax.axis_size("seq")
    seg_index = lax.axis_index("seq")
    tree_index = lax.axis_index("leaf")
    tok_rows = tokens.shape[1]
    model_width = tokens.shape[2]
    head_count = HEADS
    head_dim = model_width // head_count
    score_scale = head_dim ** (-0.5)
    tree_rows = tok_rows * seg_count
    qkv_all, out_all, up_all, down_all = (
        lax.all_gather(qkv_weight, ("leaf", "seq"), axis=0, tiled=True),
        lax.all_gather(out_weight, ("leaf", "seq"), axis=0, tiled=True),
        lax.all_gather(up_weight, ("leaf", "seq"), axis=0, tiled=True),
        lax.all_gather(down_weight, ("leaf", "seq"), axis=0, tiled=True),
    )
    condition = jax.nn.silu(time_embed(timesteps, model_width)).astype(jnp.bfloat16)
    mod_all = lax.all_gather(mod_weight, ("leaf", "seq"), axis=0, tiled=True)
    cond_own = lax.dynamic_index_in_dim(condition, tree_index, 0, keepdims=False)
    modulation = jnp.dot(cond_own[None, :], mod_all, preferred_element_type=jnp.float32)[0]
    shift_a, scale_a, gate_a, shift_b, scale_b, gate_b = jnp.split(modulation, 6)
    inputs_f = tokens[0].astype(jnp.float32)
    normed_a = layer_norm(inputs_f)
    hidden_a = (normed_a * (1.0 + scale_a) + shift_a).astype(jnp.bfloat16)
    projected = jnp.dot(hidden_a, qkv_all, preferred_element_type=jnp.float32).reshape(
        tok_rows, 3, head_count, head_dim
    )
    cosine, sine = rope_tables(positions[0], head_dim)
    query_rot = rotate(projected[:, 0], cosine, sine).astype(jnp.bfloat16)
    key_rot = rotate(projected[:, 1], cosine, sine).astype(jnp.bfloat16)
    value_rows = projected[:, 2].astype(jnp.bfloat16)
    key_flat = key_rot.reshape(tok_rows, model_width)
    value_flat = value_rows.reshape(tok_rows, model_width)
    reached = ancestor_row(parent[0], seg_index, seg_count)
    live_blocks = block_live.shape[2]
    live_tokens = jnp.repeat(block_live[0] > 0, tok_rows // live_blocks, axis=1)
    key_allowed = (reached[:, None] & live_tokens).reshape(tree_rows)
    start_state = (
        jnp.full((head_count, tok_rows), NEGATIVE, jnp.float32),
        jnp.zeros((head_count, tok_rows), jnp.float32),
        jnp.zeros((head_count, tok_rows, head_dim), jnp.float32),
    )
    key_part = lax.all_gather(key_flat, "seq", axis=0, tiled=True)
    value_part = lax.all_gather(value_flat, "seq", axis=0, tiled=True)
    count_keys = key_part.shape[0]
    block_size = tok_rows
    block_count = count_keys // block_size
    allow_part = key_allowed.reshape(block_count, block_size)
    key_blocks = key_part.reshape(block_count, block_size, head_count, head_dim)
    value_blocks = value_part.reshape(block_count, block_size, head_count, head_dim)

    def advance(state_now, block_in):
        return (
            attend_keys(state_now, query_rot, block_in[0], block_in[1], block_in[2], score_scale),
            None,
        )

    maximum_run, total_run, accum_run = lax.scan(
        advance, start_state, (key_blocks, value_blocks, allow_part)
    )[0]
    attended_heads = jnp.transpose(accum_run / total_run[..., None], (1, 0, 2))
    log_total = maximum_run + jnp.log(total_run)
    attended = attended_heads.reshape(tok_rows, model_width).astype(jnp.bfloat16)
    branch_a = jnp.dot(attended, out_all, preferred_element_type=jnp.float32)
    middle = inputs_f + gate_a * branch_a
    normed_b = layer_norm(middle)
    hidden_b = (normed_b * (1.0 + scale_b) + shift_b).astype(jnp.bfloat16)
    upper = jnp.dot(hidden_b, up_all, preferred_element_type=jnp.float32)
    active = jax.nn.gelu(upper).astype(jnp.bfloat16)
    branch_b = jnp.dot(active, down_all, preferred_element_type=jnp.float32)
    layer_out = (middle + gate_b * branch_b).astype(jnp.bfloat16)
    qkv_back, out_back, up_back, down_back = (
        lax.all_gather(qkv_weight, ("leaf", "seq"), axis=0, tiled=True),
        lax.all_gather(out_weight, ("leaf", "seq"), axis=0, tiled=True),
        lax.all_gather(up_weight, ("leaf", "seq"), axis=0, tiled=True),
        lax.all_gather(down_weight, ("leaf", "seq"), axis=0, tiled=True),
    )
    grad_out_rows = cotangent[0].astype(jnp.float32)
    grad_branch_b = (gate_b * grad_out_rows).astype(jnp.bfloat16)
    dgate_b = jnp.sum(grad_out_rows * branch_b, axis=0)
    grad_down = jnp.einsum("qf,qd->fd", active, grad_branch_b, preferred_element_type=jnp.float32)
    grad_active = jnp.einsum(
        "qd,fd->qf", grad_branch_b, down_back, preferred_element_type=jnp.float32
    )
    gelu_pull = jax.vjp(jax.nn.gelu, upper)[1]
    grad_upper = gelu_pull(grad_active)[0].astype(jnp.bfloat16)
    grad_up = jnp.einsum("qd,qf->df", hidden_b, grad_upper, preferred_element_type=jnp.float32)
    grad_hidden_b = jnp.einsum("qf,df->qd", grad_upper, up_back, preferred_element_type=jnp.float32)
    dshift_b = jnp.sum(grad_hidden_b, axis=0)
    dscale_b = jnp.sum(grad_hidden_b * normed_b, axis=0)
    norm_pull_b = jax.vjp(layer_norm, middle)[1]
    grad_middle = grad_out_rows + norm_pull_b(grad_hidden_b * (1.0 + scale_b))[0]
    grad_branch_a = (gate_a * grad_middle).astype(jnp.bfloat16)
    dgate_a = jnp.sum(grad_middle * branch_a, axis=0)
    grad_out = jnp.einsum("qi,qd->id", attended, grad_branch_a, preferred_element_type=jnp.float32)
    grad_attended = jnp.einsum(
        "qd,id->qi", grad_branch_a, out_back, preferred_element_type=jnp.float32
    ).astype(jnp.bfloat16)
    grad_att_heads = grad_attended.reshape(tok_rows, head_count, head_dim)
    delta_rows = jnp.einsum("qhd,qhd->hq", grad_att_heads.astype(jnp.float32), attended_heads)
    start_query = jnp.zeros((tok_rows, head_count, head_dim), jnp.float32)
    key_part = lax.all_gather(key_flat, "seq", axis=0, tiled=True)
    value_part = lax.all_gather(value_flat, "seq", axis=0, tiled=True)
    count_keys = key_part.shape[0]
    block_size = tok_rows
    block_count = count_keys // block_size
    allow_part = key_allowed.reshape(block_count, block_size)
    key_blocks = key_part.reshape(block_count, block_size, head_count, head_dim)
    value_blocks = value_part.reshape(block_count, block_size, head_count, head_dim)

    def advance(grad_now, block_in):
        return (
            query_only(
                grad_now,
                query_rot,
                grad_att_heads,
                log_total,
                delta_rows,
                block_in[0],
                block_in[1],
                block_in[2],
                score_scale,
            ),
            None,
        )

    grad_query = lax.scan(advance, start_query, (key_blocks, value_blocks, allow_part))[0]
    seg_range = jnp.arange(seg_count, dtype=jnp.int32)
    every_reach = jax.vmap(lambda one_seg: ancestor_row(parent[0], one_seg, seg_count))(seg_range)
    sees_mine = every_reach[:, seg_index]
    own_live = lax.dynamic_index_in_dim(live_tokens, seg_index, 0, keepdims=False)
    total_all, delta_all = (
        lax.all_gather(jnp.transpose(log_total), "seq", axis=0, tiled=True),
        lax.all_gather(jnp.transpose(delta_rows), "seq", axis=0, tiled=True),
    )
    query_flat = query_rot.reshape(tok_rows, model_width)
    grad_key_acc = jnp.zeros((tok_rows, head_count, head_dim), jnp.float32)
    grad_value_acc = jnp.zeros((tok_rows, head_count, head_dim), jnp.float32)
    query_part = lax.all_gather(query_flat, "seq", axis=0, tiled=True)
    grad_part = lax.all_gather(grad_attended, "seq", axis=0, tiled=True)
    count_rows = query_part.shape[0]
    block_size = tok_rows
    block_count = count_rows // block_size
    row_seg = jnp.arange(count_rows, dtype=jnp.int32) // tok_rows
    row_ok = sees_mine[row_seg].reshape(block_count, block_size)
    total_part = total_all.reshape(block_count, block_size, head_count)
    delta_part = delta_all.reshape(block_count, block_size, head_count)
    query_blocks = query_part.reshape(block_count, block_size, head_count, head_dim)
    grad_blocks = grad_part.reshape(block_count, block_size, head_count, head_dim)

    def advance(acc_now, block_in):
        key_acc, value_acc = acc_now
        query_block, grad_block, total_block, delta_block, ok_block = block_in
        mask_wide = ok_block[None, :, None] & own_live[None, None, :]
        probs, grad_scores = score_grads(
            query_block,
            grad_block,
            jnp.transpose(total_block),
            jnp.transpose(delta_block),
            key_rot,
            value_rows,
            mask_wide,
            score_scale,
        )
        key_acc = (
            key_acc
            + jnp.einsum(
                "hqk,qhd->khd", grad_scores, query_block, preferred_element_type=jnp.float32
            )
            * score_scale
        )
        value_acc = value_acc + jnp.einsum(
            "hqk,qhd->khd",
            probs.astype(jnp.bfloat16),
            grad_block,
            preferred_element_type=jnp.float32,
        )
        return ((key_acc, value_acc), None)

    grad_key_rows, grad_value_heads = lax.scan(
        advance,
        (grad_key_acc, grad_value_acc),
        (query_blocks, grad_blocks, total_part, delta_part, row_ok),
    )[0]
    grad_value_rows = grad_value_heads.reshape(tok_rows, model_width)
    grad_query_pre = rotate_back(grad_query, cosine, sine).reshape(tok_rows, model_width)
    grad_key_pre = rotate_back(grad_key_rows, cosine, sine).reshape(tok_rows, model_width)
    grad_projected = jnp.concatenate(
        [grad_query_pre, grad_key_pre, grad_value_rows], axis=-1
    ).astype(jnp.bfloat16)
    grad_qkv = jnp.einsum("qi,qj->ij", hidden_a, grad_projected, preferred_element_type=jnp.float32)
    grad_hidden_a = jnp.einsum(
        "qj,ij->qi", grad_projected, qkv_back, preferred_element_type=jnp.float32
    )
    dshift_a = jnp.sum(grad_hidden_a, axis=0)
    dscale_a = jnp.sum(grad_hidden_a * normed_a, axis=0)
    norm_pull_a = jax.vjp(layer_norm, inputs_f)[1]
    grad_tokens = grad_middle + norm_pull_a(grad_hidden_a * (1.0 + scale_a))[0]
    grad_modulation = jnp.concatenate([dshift_a, dscale_a, dgate_a, dshift_b, dscale_b, dgate_b])
    sum_qkv, sum_out, sum_up, sum_down = (
        lax.psum_scatter(grad_qkv, ("leaf", "seq"), scatter_dimension=0, tiled=True),
        lax.psum_scatter(grad_out, ("leaf", "seq"), scatter_dimension=0, tiled=True),
        lax.psum_scatter(grad_up, ("leaf", "seq"), scatter_dimension=0, tiled=True),
        lax.psum_scatter(grad_down, ("leaf", "seq"), scatter_dimension=0, tiled=True),
    )
    mod_term = cond_own.astype(jnp.float32)[:, None] * grad_modulation[None, :]
    sum_mod = lax.psum_scatter(mod_term, ("leaf", "seq"), scatter_dimension=0, tiled=True)
    return (layer_out[None], grad_tokens[None], sum_qkv, sum_out, sum_up, sum_down, sum_mod)


def solution(mesh):
    rows = P("leaf", "seq", None)
    held = P(("leaf", "seq"), None)
    placed = (rows, rows, P(), P("leaf", None), P("leaf", "seq"), P("leaf", None, None), held, held, held, held, held)
    kernels = mesh.shape["seq"] == 8 and mesh.shape["leaf"] == 4
    return jax.shard_map(
        layer_kernels if kernels else layer_native,
        mesh=mesh,
        in_specs=placed,
        out_specs=(rows, rows, held, held, held, held, held),
        check_vma=False,
    )
```

```python
import functools, math
import jax, jax.numpy as jnp
from jax import lax
from jax.experimental import pallas as pl
from jax.experimental.pallas import tpu as pltpu
from jax.sharding import PartitionSpec as P

MESH = pl.DeviceIdType.MESH
HEADS = 12
EPSILON = 1e-06
NEGATIVE = -1e30
F32 = jnp.float32
BF16 = jnp.bfloat16
GELU_A = math.sqrt(2.0 / math.pi)
GELU_B = 0.044715


class Sems:
    def __init__(self, ref):
        self.ref, self.used = ref, 0

    def one(self):
        self.used += 1
        assert self.used <= self.ref.shape[0]
        return self.ref.at[self.used - 1]


class Place:
    def __init__(self, leaf_count, seg_count):
        self.L, self.S = leaf_count, seg_count
        self.P = seg_count // 2
        self.l, self.s = lax.axis_index("leaf"), lax.axis_index("seq")
        self.c, self.p = lax.rem(self.s, 2), self.s // 2
        self.sib = self.s + 1 - 2 * self.c
        self.inner = (self.l + 1) // 2 == 1
        self.px = self.p + 1 - 2 * lax.rem(self.p, 2)
        self.py = lax.rem(self.p + 2, 4)
        self.pd = lax.rem(self.px + 2, 4)
        self.others = [self.px, self.py, self.pd]
        self.tree = [(self.l, 2 * q + core) for core in (self.c, 1 - self.c) for q in self.others] + [(self.l, self.sib)]

    def leaf(self, k):
        far = lax.rem(self.l + 2, 4) if k >= 2 else self.l
        return far + 1 - 2 * lax.rem(far, 2) if k % 2 else far

    def turn(self, k):
        return jnp.where(self.inner, 4 - k, k)

    def leaf_turn(self, k):
        return jnp.where(self.inner, self.leaf(4 - k), self.leaf(k))

    def at_leaf(self, k):
        return (self.leaf(k), self.s)

    def at_chip(self, q):
        return (self.l, 2 * q + self.c)

    def at_sib(self):
        return (self.l, self.sib)

    def barrier(self):
        sem = pltpu.get_barrier_semaphore()
        peers = [self.at_leaf(k) for k in range(1, self.L)]
        peers += self.tree
        for peer in peers:
            pl.semaphore_signal(sem, inc=1, device_id=peer, device_id_type=MESH)
        pl.semaphore_wait(sem, len(peers))


class Wires:
    def __init__(self, at, send_sems, recv_sems, local_sems):
        self.at = at
        self.send_sems, self.recv_sems, self.local_sems = Sems(send_sems), Sems(recv_sems), Sems(local_sems)
        self.open = []

    def send(self, src, dst, dev):
        copy = pltpu.make_async_remote_copy(
            src_ref=src, dst_ref=dst, send_sem=self.send_sems.one(), recv_sem=self.recv_sems.one(),
            device_id=dev, device_id_type=MESH)
        copy.start()
        self.open.append(copy)
        return copy

    def group(self, whole):
        group = Group(self, whole)
        self.open.append(group)
        return group

    def local(self, src, dst):
        copy = pltpu.make_async_copy(src, dst, self.local_sems.one())
        copy.start()
        return copy

    def sent(self, copies):
        for copy in copies:
            copy.wait_send()
        self.open = [copy for copy in self.open if all(copy is not other for other in copies)]

    def drain(self):
        for copy in self.open:
            copy.wait_send()
        self.open = []


class Group:
    def __init__(self, wires, whole):
        self.at, self.whole = wires.at, whole
        self.send_sem, self.recv_sem = wires.send_sems.one(), wires.recv_sems.one()

    def make(self, src, dst, dev):
        return pltpu.make_async_remote_copy(
            src_ref=src, dst_ref=dst, send_sem=self.send_sem, recv_sem=self.recv_sem, device_id=dev, device_id_type=MESH)

    def send(self, src, dst, dev):
        self.make(src, dst, dev).start()
        return self

    def wait_recv(self):
        self.make(self.whole, self.whole, self.at.at_sib()).wait_recv()

    def wait_send(self):
        self.make(self.whole, self.whole, self.at.at_sib()).wait_send()


class Line:
    def __init__(self, wires, at, view, whole):
        self.w, self.at, self.view = wires, at, view
        self.first = wires.send_sems.one()
        self.onward = wires.send_sems.one()
        self.arrive = [None] + [wires.recv_sems.one() for _ in range(3)]
        self.whole = whole
        wires.open.append(self)

    def leaf(self, unit):
        at = self.at
        if unit < 2:
            return at.leaf(unit)
        return jnp.where(at.l < 2, unit, 3 - unit)

    def make(self, src, leaf, unit, to, sem):
        return pltpu.make_async_remote_copy(
            src_ref=src, dst_ref=self.view(leaf), send_sem=sem, recv_sem=self.arrive[unit], device_id=to, device_id_type=MESH)

    def begin(self, src):
        at = self.at
        self.make(src, at.l, 1, at.at_leaf(1), self.first).start()

        @pl.when(at.inner)
        def _():
            self.make(src, at.l, 2, at.at_leaf(3), self.onward).start()

    def early(self, unit):
        at = self.at
        leaf = self.leaf(unit)
        part = self.view(leaf)

        @pl.when(at.inner)
        def _():
            self.make(part, leaf, unit, at.at_sib(), self.first).wait_recv()
            if unit == 1:
                self.make(part, leaf, 3, at.at_leaf(3), self.onward).start()
            else:
                self.make(part, leaf, unit, at.at_leaf(1), self.onward).start()

    def late(self, unit):
        at = self.at
        leaf = self.leaf(unit)

        @pl.when(jnp.logical_not(at.inner))
        def _():
            self.make(self.view(leaf), leaf, unit, at.at_sib(), self.first).wait_recv()

    def wait_send(self):
        at = self.at
        part = self.view(at.l)
        self.make(part, at.l, 1, at.at_sib(), self.first).wait_send()

        @pl.when(at.inner)
        def _():
            pltpu.make_async_remote_copy(
                src_ref=self.whole, dst_ref=self.whole, send_sem=self.onward, recv_sem=self.arrive[1],
                device_id=at.at_sib(), device_id_type=MESH).wait_send()


class Gather:
    def __init__(self, wires, at, shard, full):
        self.w, self.at, self.shard, self.full = wires, at, shard, full
        count = shard.shape[0]
        self.rows = pl.ds(pl.multiple_of(at.c * count, 8), count)
        self.line = Line(wires, at, lambda leaf: full.at[leaf, at.p, self.rows], full.at[:, at.p, self.rows])
        self.pair = wires.group(full.at[:, :, self.rows])
        self.cross, self.relay = {}, {}
        self.sent_cross, self.sent_relay = wires.send_sems.one(), wires.send_sems.one()
        wires.open.append(self)

    def view(self, unit, chip):
        return self.full.at[self.line.leaf(unit), chip, self.rows]

    def make(self, src, dst, to, sem, recv):
        return pltpu.make_async_remote_copy(
            src_ref=src, dst_ref=dst, send_sem=sem, recv_sem=recv, device_id=self.at.at_chip(to), device_id_type=MESH)

    def begin(self):
        self.own = self.w.local(self.shard, self.view(0, self.at.p))
        self.line.begin(self.shard)

    def stage1(self, unit):
        at = self.at
        mine = self.view(unit, at.p)
        src = mine if unit else self.shard
        self.cross[unit] = [self.make(src, mine, q, self.sent_cross, self.w.recv_sems.one()) for q in (at.px, at.py)]
        for copy in self.cross[unit]:
            copy.start()
        self.pair.send(src, mine, at.at_sib())

    def stage2(self, unit):
        at = self.at
        for i, (q, to) in enumerate(((at.px, at.py), (at.py, at.px))):
            self.cross[unit][i].wait_recv()
            theirs = self.view(unit, q)
            if unit % 2 == i:
                self.relay[unit] = self.make(theirs, theirs, to, self.sent_relay, self.w.recv_sems.one())
                self.relay[unit].start()
            self.pair.send(theirs, theirs, at.at_sib())

    def stage3(self, unit):
        self.relay[unit].wait_recv()
        theirs = self.view(unit, self.at.pd)
        self.pair.send(theirs, theirs, self.at.at_sib())

    def finish(self):
        self.own.wait()
        self.pair.wait_recv()

    def wait_send(self):
        at = self.at
        two, one = self.full.at[:, 0:2, self.rows], self.full.at[:, 0, self.rows]
        spare = self.line.arrive[1]
        self.make(two, two, at.px, self.sent_cross, spare).wait_send()
        self.make(one, one, at.px, self.sent_relay, spare).wait_send()


def add_to(ref, *others):
    total = ref[...].astype(F32)
    for other in others:
        total = total + other[...].astype(F32)
    ref[...] = total.astype(ref.dtype)


class Scatter:
    def __init__(self, wires, at, A, sw, dg, xy, zr, fin, sibr, out):
        self.w, self.at = wires, at
        self.A, self.sw, self.dg, self.xy, self.zr, self.fin, self.sibr, self.out = A, sw, dg, xy, zr, fin, sibr, out

    def cross(self, unit, to, side):
        leaf = self.at.leaf(unit)
        self.x.send(self.A.at[leaf, to], self.xy.at[side, leaf], self.at.at_chip(to))

    def step0(self):
        at = self.at
        self.s = self.w.group(self.sw)
        for i in range(2):
            self.s.send(self.A.at[at.leaf(1 + 2 * i), at.pd], self.sw.at[i], at.at_leaf(1))
        self.x = self.w.group(self.xy)

    def step1(self, units):
        at = self.at
        for unit in units:
            if unit != 2:
                self.cross(unit, at.px, 0)
            if unit != 0:
                self.cross(unit, at.py, 1)

    def step1d(self):
        w, at, A = self.w, self.at, self.A
        self.s.wait_recv()
        self.d = []
        for i, to in enumerate((at.px, at.py)):
            add_to(A.at[at.leaf(2 * i), at.pd], self.sw.at[i])
            self.d.append(w.send(A.at[at.leaf(2 * i), at.pd], self.dg.at[i], at.at_chip(to)))

    def step2(self):
        at, A = self.at, self.A
        for i, to in enumerate((at.py, at.px)):
            self.d[i].wait_recv()
            add_to(A.at[at.leaf(2 * i), to], self.dg.at[i])
            self.cross(2 * i, to, 1 - i)

    def step3(self):
        w, at, A = self.w, self.at, self.A
        self.x.wait_recv()
        self.z = w.group(self.zr)
        for k in (1, 2, 3):
            leaf = at.leaf_turn(k)
            add_to(A.at[leaf, at.p], self.xy.at[0, leaf], self.xy.at[1, leaf])
            self.z.send(A.at[leaf, at.p], self.zr.at[at.turn(k) - 1], (leaf, at.s))
        add_to(A.at[at.l, at.p], self.xy.at[0, at.l], self.xy.at[1, at.l])

    def step4(self):
        w, at = self.w, self.at
        self.z.wait_recv()
        total = self.A[at.l, at.p].astype(F32)
        for k in range(at.L - 1):
            total = total + self.zr[k].astype(F32)
        self.fin[...] = total
        rows = self.fin.shape[0] // 2
        self.f = w.send(self.fin.at[pl.ds(pl.multiple_of(rows * (1 - at.c), 8), rows)], self.sibr, at.at_sib())

    def step5(self):
        at = self.at
        rows, half = self.sibr.shape
        mine = self.fin[pl.ds(pl.multiple_of(rows * at.c, 8), rows), :]
        self.out[:, pl.ds(pl.multiple_of(half * at.c, 128), half)] = mine
        self.f.wait_recv()
        self.out[:, pl.ds(pl.multiple_of(half * (1 - at.c), 128), half)] = self.sibr[...]


class PlaneGather:
    def __init__(self, wires, at, buf):
        self.w, self.at, self.buf = wires, at, buf
        rows = buf.shape[1] // 2
        self.halves = pl.ds(0, rows), pl.ds(rows, rows)

    def send(self, half, q):
        mine = self.buf.at[self.at.p, half]
        return self.w.send(mine, mine, self.at.at_chip(q))

    def first(self):
        at, (up, low) = self.at, self.halves
        self.own = [self.send(up, at.px), self.send(low, at.py)]

    def second(self):
        at, (up, low) = self.at, self.halves
        self.own += [self.send(low, at.px), self.send(up, at.py)]

    def start(self):
        self.first()
        self.second()

    def relay(self):
        at = self.at
        self.passed = []
        for half, copy, q, to in zip(self.halves, self.own, (at.px, at.py), (at.py, at.px)):
            copy.wait_recv()
            theirs = self.buf.at[q, half]
            self.passed.append(self.w.send(theirs, theirs, at.at_chip(to)))

    def near(self):
        for copy in self.own[2:]:
            copy.wait_recv()

    def far(self):
        for copy in self.passed:
            copy.wait_recv()


class PlaneSum:
    def __init__(self, wires, at, A, Ad, Ax):
        self.w, self.at, self.A, self.Ad, self.Ax = wires, at, A, Ad, Ax
        self.x = wires.group(Ax)

    def far(self):
        at = self.at
        self.d = [self.w.send(self.A.at[i, at.pd], self.Ad.at[i], at.at_chip(to)) for i, to in enumerate((at.px, at.py))]

    def near(self, i):
        at = self.at
        to = (at.px, at.py)[i]
        self.x.send(self.A.at[i, to], self.Ax.at[i, i], at.at_chip(to))

    def relay(self):
        at = self.at
        for i, to in enumerate((at.py, at.px)):
            self.d[i].wait_recv()
            add_to(self.A.at[i, to], self.Ad.at[i])
            self.x.send(self.A.at[i, to], self.Ax.at[1 - i, i], at.at_chip(to))

    def total(self):
        self.x.wait_recv()
        return [self.A[i, self.at.p].astype(F32) + self.Ax[0, i].astype(F32) + self.Ax[1, i].astype(F32) for i in range(2)]


class LineSum:
    def __init__(self, wires, at, A, As, zr):
        self.w, self.at, self.A, self.As, self.zr = wires, at, A, As, zr

    def pair(self):
        self.s = self.w.send(self.A.at[1 - self.at.c], self.As, self.at.at_sib())

    def line(self):
        at, A = self.at, self.A
        self.s.wait_recv()
        self.z = self.w.group(self.zr)
        for k in (1, 2, 3):
            leaf = at.leaf_turn(k)
            add_to(A.at[at.c, leaf], self.As.at[leaf])
            self.z.send(A.at[at.c, leaf], self.zr.at[at.turn(k) - 1], (leaf, at.s))
        add_to(A.at[at.c, at.l], self.As.at[at.l])

    def total(self):
        self.z.wait_recv()
        total = self.A[self.at.c, self.at.l].astype(F32)
        for k in range(self.at.L - 1):
            total = total + self.zr[k].astype(F32)
        return total


class Columns:
    def __init__(self, wires, at, full, parts):
        self.w, self.at, self.full = wires, at, full
        count = full.shape[2] // 2
        self.rows = pl.ds(pl.multiple_of(at.c * count, 8), count)
        self.first = wires.group(full.at[0, 0:3, self.rows])
        size = at.P // parts
        self.lines = []
        for i in range(parts):
            some = pl.ds(i * size, size)
            held = lambda leaf, some=some: full.at[leaf, some, self.rows]
            self.lines.append(Line(wires, at, held, full.at[:, some, self.rows]))
        self.pair = wires.group(full.at[:, :, self.rows])

    def start(self, parts):
        at = self.at
        mine = self.full.at[at.l, at.p, self.rows]
        for q in at.others:
            self.first.send(parts.at[q], mine, at.at_chip(q))
        self.own = self.w.local(parts.at[at.p], mine)

    def begin(self):
        at = self.at
        self.first.wait_recv()
        self.own.wait()
        for line in self.lines:
            line.begin(line.view(at.l))
        for line in self.lines:
            self.pair.send(line.view(at.l), line.view(at.l), at.at_sib())

    def early(self, unit):
        for line in self.lines:
            line.early(unit)

    def late(self, unit):
        for line in self.lines:
            line.late(unit)
            part = line.view(line.leaf(unit))
            self.pair.send(part, part, self.at.at_sib())


class Rows:
    def __init__(self, wires, at, shard, full):
        self.w, self.at, self.shard, self.full = wires, at, shard, full
        count = shard.shape[0]
        self.rows = pl.ds(pl.multiple_of(at.c * count, 8), count)
        self.line = Line(wires, at, self.held, full.at[:, self.rows])
        self.pair = wires.group(full.at[:, self.rows])

    def held(self, leaf):
        return self.full.at[leaf, self.rows]

    def begin(self):
        at = self.at
        self.own = self.w.local(self.shard, self.held(at.l))
        self.line.begin(self.shard)
        self.pair.send(self.shard, self.held(at.l), at.at_sib())

    def late(self, unit):
        self.line.late(unit)
        part = self.held(self.line.leaf(unit))
        self.pair.send(part, part, self.at.at_sib())


def norm_rows(values):
    centred = values - jnp.mean(values, axis=-1, keepdims=True)
    variance = jnp.mean(centred * centred, axis=-1, keepdims=True)
    rstd = lax.rsqrt(variance + EPSILON)
    return centred * rstd, rstd


def norm_back(grad, normed, rstd):
    return rstd * (grad - jnp.mean(grad, axis=-1, keepdims=True) - normed * jnp.mean(grad * normed, axis=-1, keepdims=True))


def total_rows(values):
    return jnp.sum(values, axis=0, keepdims=True)


def dot(left, right):
    return jnp.dot(left, right, preferred_element_type=F32)


def dot_t(left, right):
    return lax.dot_general(left, right, (((1,), (1,)), ((), ())), preferred_element_type=F32)


def tile(j, size):
    return pl.ds(pl.multiple_of(j * size, size), size)


def condition_column(at, timestep, count, width):
    half = width // 2
    row = (at.l * at.S + at.s) * count + lax.broadcasted_iota(jnp.int32, (count, 1), 0)
    index = jnp.where(row < half, row, row - half).astype(F32)
    angle = timestep.astype(F32) * jnp.exp(-math.log(10000.0) * index / half)
    value = jnp.where(row < half, jnp.cos(angle), jnp.sin(angle))
    return (value / (1.0 + jnp.exp(-value))).astype(BF16).astype(F32)


def fill_bias(at, R):
    _, seg_count, blocks = R.live.shape

    def fill(k, carry):
        seg = 2 * k + at.c
        current = seg
        reached = [jnp.where(seg == a, 1, 0) for a in range(seg_count)]
        for _ in range(seg_count):
            current = R.parent[0, current]
            reached = [jnp.where(current == a, 1, r) for a, r in enumerate(reached)]
        for a in range(seg_count):
            for b in range(blocks):
                R.bias[k, a * blocks + b] = jnp.where(reached[a] * R.live[0, a, b] > 0, 0.0, NEGATIVE)
        return carry

    lax.fori_loop(0, at.P, fill, 0)


def by_blocks(R, score, chip, a):
    blocks = R.live.shape[2]
    rows = score.shape[0] // blocks
    return [(score[b * rows : (b + 1) * rows], R.bias[chip, a * blocks + b]) for b in range(blocks)]


def layer(at, w, R):
    L, S, PC = at.L, at.S, at.P
    T, D = R.tok.shape
    HD = D // HEADS
    HG = HEADS // PC
    GW = HG * HD
    CW = R.Wh.shape[1]
    HU = R.Wu.shape[1]
    DH, TH = D // 2, T // 2
    MR = R.wq.shape[0]
    HB = HU // L
    trunk = S // 2
    NK = PC // 2 + 1
    part = lambda i: slice(i * D, (i + 1) * D)
    head_rows = lambda h: slice(h * HD, (h + 1) * HD)
    go = Gather(w, at, R.wo, R.Go)
    cq, cu = Columns(w, at, R.Gh, 2), Columns(w, at, R.Gu, 1)
    ta, ga = PlaneGather(w, at, R.tX), PlaneGather(w, at, R.gX)
    rd = Rows(w, at, R.wd, R.Gd)

    def key_count(seg):
        return jnp.minimum(seg, trunk) + 1 + jnp.where(seg > trunk, 1, 0)

    at.barrier()
    wq, wu = R.wq[...].astype(F32), R.wu[...].astype(F32)
    for q in range(PC):
        pieces = [wq[:, k * D + q * GW : k * D + (q + 1) * GW] for k in range(3)]
        R.wqs[q] = jnp.concatenate(pieces + [jnp.zeros((MR, CW - 3 * GW), F32)], axis=1).astype(BF16)
    cq.start(R.wqs)
    R.tX[at.p] = R.tok[...]
    ta.first()
    R.gX[at.p] = R.g[...]
    for q in range(PC):
        R.wus[q] = jnp.concatenate([wu[:, k * HU + q * HB : k * HU + (q + 1) * HB] for k in range(L)], axis=1).astype(BF16)
    modw = R.modw[...].astype(F32)
    for t in range(L):
        column = condition_column(at, R.time[t], modw.shape[0], D)
        R.cond[t] = column
        R.mpart[t] = total_rows(column * modw)
    mz = w.group(R.mz)
    for k in range(1, L):
        mz.send(R.mpart.at[at.leaf(k)], R.mz.at[k - 1], at.at_leaf(k))
    R.pos2[at.p] = R.pos[...].astype(F32)
    ps = w.group(R.pos2.at[0:3])
    for q in at.others:
        ps.send(R.pos2.at[at.p], R.pos2.at[at.p], at.at_chip(q))
    cu.start(R.wus)
    cq.begin()
    mz.wait_recv()
    total = R.mpart[at.l]
    for k in range(L - 1):
        total = total + R.mz[k]
    R.m1[...] = total
    mp = w.group(R.mp)
    for i, peer in enumerate(at.tree):
        mp.send(R.m1, R.mp.at[i], peer)
    ta.second()
    ta.relay()
    go.stage1(0)
    fill_bias(at, R)
    cq.early(1)
    cq.early(2)
    cq.late(1)
    mp.wait_recv()
    for i in range(S - 1):
        total = total + R.mp[i]
    R.mod[...] = total
    shift_a, scale_a, gate_a, shift_b, scale_b, gate_b = (R.mod[:, part(i)] for i in range(6))

    def modulate(k):
        normed, _ = norm_rows(R.tX[k].astype(F32))
        hidden = (normed * (1.0 + scale_a) + shift_a).astype(BF16)
        R.hA[k] = hidden

    modulate(at.p)
    ga.first()
    slow = jnp.exp(-math.log(10000.0) * 2.0 * lax.broadcasted_iota(jnp.int32, (HD // 2, 1), 0).astype(F32) / HD)
    ps.wait_recv()
    for k in range(PC):
        angles = slow * R.pos2[k]
        R.cos[k] = jnp.cos(angles)
        R.sin[k] = jnp.sin(angles)
    cq.early(3)
    go.begin()
    cu.begin()
    cq.late(2)
    ta.near()
    cq.late(3)
    modulate(at.px)
    modulate(at.py)
    ta.far()
    modulate(at.pd)
    go.line.early(1)
    go.line.early(2)
    cu.early(1)
    go.line.late(1)
    go.stage1(1)
    cq.pair.wait_recv()
    load = w.local(R.Gh.reshape(D, CW), R.Wh)
    load.wait()

    def project(q):
        cosine, sine = R.cos[q], R.sin[q]
        hidden = R.hA[q]
        for j in range(0, CW, 128):
            rows = dot(hidden, R.Wh[:, j : j + 128]).T
            for i in range(128 // HD):
                kind, h = divmod(j // HD + i, HG)
                if kind == 3:
                    continue
                first, second = rows[i * HD : i * HD + HD // 2], rows[i * HD + HD // 2 : (i + 1) * HD]
                if kind < 2:
                    first, second = first * cosine - second * sine, second * cosine + first * sine
                if kind == 0:
                    first, second = first * HD**-0.5, second * HD**-0.5
                low, high = pl.ds(h * HD, HD // 2), pl.ds(h * HD + HD // 2, HD // 2)
                if kind == 0:
                    R.QT[q, low, :] = first.astype(BF16)
                    R.QT[q, high, :] = second.astype(BF16)
                else:
                    R.KVT[2 * q + at.c, kind - 1, low, :] = first.astype(BF16)
                    R.KVT[2 * q + at.c, kind - 1, high, :] = second.astype(BF16)

    project(at.p)
    go.line.early(3)
    cu.early(2)
    rd.begin()
    project(at.px)
    project(at.py)
    go.line.late(2)
    go.stage1(2)
    cu.late(1)
    project(at.pd)
    sk = w.group(R.KVT.at[0:NK])
    for k in range(NK):
        sk.send(R.KVT.at[2 * k + at.c], R.KVT.at[2 * k + at.c], at.at_sib())
    go.line.late(3)
    go.stage1(3)
    ga.second()
    cu.early(3)
    sk.wait_recv()

    def flip_k(a, carry):
        for h in range(HG):
            R.kN[a, h] = R.KVT[a, 0, head_rows(h), :].T
        return carry

    lax.fori_loop(0, S, flip_k, 0)
    ret = w.group(R.hsnd.at[0:3])
    for i, q in enumerate([at.pd, at.px, at.py, at.p]):
        seg = 2 * q + at.c

        def block(j, state, q=q, seg=seg):
            a = jnp.where(j > trunk, seg, j)
            out = []
            raw = [dot(R.kN[a, h], R.QT[q, head_rows(h), :]) for h in range(HG)]
            for h in range(HG):
                m, t, o = state[3 * h : 3 * h + 3]
                score = by_blocks(R, raw[h], q, a)
                m_new = m
                for one, bias in score:
                    m_new = jnp.maximum(m_new, jnp.max(one, axis=0, keepdims=True) + bias)
                alpha = jnp.exp(m - m_new)
                e = jnp.concatenate([jnp.exp(one - (m_new - bias)) for one, bias in score], axis=0)
                out.append((m_new, t * alpha + total_rows(e), o * alpha, e.astype(BF16)))
            out = [(m, t, o + dot(R.KVT[a, 1, head_rows(h), :], e)) for h, (m, t, o, e) in enumerate(out)]
            return tuple(x for one in out for x in one)

        start = (jnp.full((1, T), NEGATIVE, F32), jnp.zeros((1, T), F32), jnp.zeros((HD, T), F32)) * HG
        state = lax.fori_loop(0, key_count(seg), block, start)
        for h in range(HG):
            m, t, o = state[3 * h : 3 * h + 3]
            o = o / t
            R.OT[q, head_rows(h), :] = o
            R.hsnd[q, head_rows(h), :] = o.astype(BF16)
            R.lse[q, h : h + 1, :] = m + jnp.log(t)
        if i < 3:
            ret.send(R.hsnd.at[q], R.attT2.at[0, at.p], at.at_chip(q))
        else:
            own_att = w.local(R.hsnd.at[q], R.attT2.at[0, at.p])
        if i == 0:
            cu.late(2)
            for u in range(L):
                go.stage2(u)
            rd.line.early(1)
            rd.line.early(2)
        if i == 1:
            ga.relay()
            cu.late(3)
            rd.late(1)
            rd.line.early(3)
        if i == 2:
            rd.late(2)
            for u in range(L):
                go.stage3(u)
    go.finish()
    load = w.local(R.Go.reshape(D, D), R.Wo)
    own_att.wait()
    ret.wait_recv()
    sib_att = w.send(R.attT2.at[0], R.attT2.at[1], at.at_sib())
    load.wait()
    att = jnp.concatenate([R.attT2[0, k].T for k in range(PC)], axis=1)
    for j in range(0, D, 256):
        lanes = slice(j, j + 256)
        branch = dot(att, R.Wo[:, lanes])
        R.br_a[:, lanes] = branch
        R.middle[:, lanes] = R.tok[:, lanes].astype(F32) + gate_a[:, lanes] * branch
    normed, _ = norm_rows(R.middle[...])
    R.hB[at.p] = (normed * (1.0 + scale_b) + shift_b).astype(BF16)
    hb = PlaneGather(w, at, R.hB)
    hb.start()
    rd.late(3)
    cu.pair.wait_recv()
    loads = [w.local(R.Gu.reshape(D, HU), R.Wu)]
    rd.own.wait()
    rd.pair.wait_recv()
    loads.append(w.local(R.Gd.reshape(HU, D), R.Wd))
    for load in loads:
        load.wait()
    ga.near()
    ga.far()

    def feed(k):
        hidden = R.hB[k]
        dbb = (gate_b * R.gX[k].astype(F32)).astype(BF16)
        R.dbb[k] = dbb
        lanes = [slice(j, j + 256) for j in range(0, HU, 256)]
        uppers = [dot(hidden, R.Wu[:, some]) for some in lanes]
        grads = [dot_t(dbb, R.Wd[some, :]) for some in lanes]
        for some, u, grad in zip(lanes, uppers, grads):
            square = u * u
            tanh = jnp.tanh(GELU_A * (u + GELU_B * square * u))
            act = (0.5 * u * (1.0 + tanh)).astype(BF16)
            R.active[k, :, some] = act
            slope = 0.5 * (1.0 + tanh) + (0.5 * GELU_A) * u * (1.0 - tanh * tanh) * (1.0 + 3.0 * GELU_B * square)
            R.du[k, :, some] = (grad * slope).astype(BF16)

    def feed_back(k):
        for i in range(2):
            R.dB[i, k] = dot_t(R.du[k, i * TH : (i + 1) * TH, :], R.Wu[...]).astype(BF16)

    sb = PlaneSum(w, at, R.dB, R.dBd, R.dBx)
    feed(at.p)
    for k in range(PC):
        R.haT[k] = R.hA[k].T
    hb.relay()
    hb.near()
    feed(at.px)
    feed_back(at.px)
    sb.near(0)
    feed(at.py)
    feed_back(at.py)
    sb.near(1)
    hb.far()
    feed(at.pd)
    feed_back(at.pd)
    sb.far()
    feed_back(at.p)
    scat = {"o": Scatter(w, at, *(getattr(R, x + "o") for x in ("A", "sw", "dg", "xy", "zr", "fin", "sr", "v")))}

    RD = HU // L
    ld, lu, lq = (LineSum(w, at, *(getattr(R, x + n) for x in ("A", "As", "zr"))) for n in ("d", "u", "q"))

    def down_grad(i, carry):
        total = dot(R.actT[0, tile(i, RD), :], R.dbb[0])
        for k in range(1, PC):
            total = total + dot(R.actT[k, tile(i, RD), :], R.dbb[k])
        for core in range(2):
            R.Ad[core, i] = total[core * (RD // 2) : (core + 1) * (RD // 2)].astype(BF16)
        return carry

    for k in range(PC):
        R.actT[k] = R.active[k].T
    lax.fori_loop(0, L, down_grad, 0)
    ld.pair()
    sb.relay()

    def by_core(A, i, total):
        for core in range(2):
            rows = [total[(2 * k + core) * MR : (2 * k + core + 1) * MR] for k in range(PC)]
            A[core, i] = jnp.concatenate(rows, axis=0).astype(BF16)

    def up_grad(i, carry):
        total = dot(R.hBT[0, tile(i, D // L), :], R.du[0])
        for k in range(1, PC):
            total = total + dot(R.hBT[k, tile(i, D // L), :], R.du[k])
        by_core(R.Au, i, total)
        return carry

    for k in range(PC):
        R.hBT[k] = R.hB[k].T
    lax.fori_loop(0, L, up_grad, 0)
    lu.pair()
    ld.line()
    lu.line()
    dh = jnp.concatenate(sb.total(), axis=0)
    normed, rstd = norm_rows(R.middle[...])
    R.gm[:, part(3)] = total_rows(dh)
    R.gm[:, part(4)] = total_rows(dh * normed)
    dmid = R.g[...].astype(F32) + norm_back(dh * (1.0 + scale_b), normed, rstd)
    R.dmid[...] = dmid
    R.gm[:, part(2)] = total_rows(dmid * R.br_a[...])
    dba = (gate_a * dmid).astype(BF16)
    R.dba[...] = dba
    for h in range(2):
        R.dbah[h] = dba[:, h * DH : (h + 1) * DH]
    sib_dba = w.send(R.dbah.at[1 - at.c], R.dbas, at.at_sib())
    w.sent([ret])
    for j in range(PC):
        R.hsnd[j] = dot_t(R.Wo[j * GW : (j + 1) * GW, :], R.dba[...]).astype(BF16)
    dos = [w.send(R.hsnd.at[q], R.dOT.at[at.p], at.at_chip(q)) for q in at.others]
    own_do = w.local(R.hsnd.at[at.p], R.dOT.at[at.p])
    RB2 = D // (L * PC)
    sib_dba.wait_recv()
    sib_att.wait_recv()
    attT = [R.attT2[i].reshape(D, T) for i in range(2)]
    block = dot(attT[0], R.dbah[at.c]) + dot(attT[1], R.dbas[...])
    for i in range(L * PC):
        R.Ao[i // PC, i % PC] = block[i * RB2 : (i + 1) * RB2].astype(BF16)
    scat["o"].step0()
    sc = PlaneSum(w, at, R.bB, R.bBd, R.bBx)
    for k in (at.pd, at.px, at.py, at.p):
        for i in range(2):
            R.bB[i, k] = dot(R.active[k, i * TH : (i + 1) * TH, :], R.Wd[...]).astype(BF16)
    sc.far()
    sc.near(0)
    sc.near(1)

    def flip_v(a, carry):
        for h in range(HG):
            R.vN[a, h] = R.KVT[a, 1, head_rows(h), :].T
        R.acc[a] = jnp.zeros((2, GW, T), F32)
        return carry

    lax.fori_loop(0, S, flip_v, 0)
    for k in range(PC):
        R.dpT[k, 3 * GW : CW, :] = jnp.zeros((CW - 3 * GW, T), BF16)
    own_do.wait()

    def unturn(first, second, q):
        cosine, sine = R.cos[q], R.sin[q]
        return jnp.concatenate([first * cosine + second * sine, second * cosine - first * sine], axis=0)

    for i, q in enumerate([at.p, at.px, at.py, at.pd]):
        seg = 2 * q + at.c
        if i:
            dos[i - 1].wait_recv()
        delta = [total_rows(R.dOT[q, head_rows(h), :].astype(F32) * R.OT[q, head_rows(h), :]) for h in range(HG)]

        def block(j, dqs, q=q, seg=seg, delta=delta):
            a = jnp.where(j > trunk, seg, j)
            out = []
            raw = [dot(R.kN[a, h], R.QT[q, head_rows(h), :]) for h in range(HG)]
            draw = [dot(R.vN[a, h], R.dOT[q, head_rows(h), :]) for h in range(HG)]
            pairs = []
            for h in range(HG):
                lse = R.lse[q, h : h + 1, :]
                prob = jnp.concatenate([jnp.exp(one - (lse - bias)) for one, bias in by_blocks(R, raw[h], q, a)], axis=0)
                pairs.append((prob.astype(BF16), (prob * (draw[h] - delta[h])).astype(BF16)))
            for h, (prob, ds) in enumerate(pairs):
                rows = head_rows(h)
                out.append(dqs[h] + dot(R.KVT[a, 0, rows, :], ds))
                R.acc[a, 0, rows, :] += dot_t(R.QT[q, rows, :], ds)
                R.acc[a, 1, rows, :] += dot_t(R.dOT[q, rows, :], prob)
            return tuple(out)

        dqs = lax.fori_loop(0, key_count(seg), block, (jnp.zeros((HD, T), F32),) * HG)
        for h in range(HG):
            dq = dqs[h] * HD**-0.5
            R.dpT[q, head_rows(h), :] = unturn(dq[: HD // 2], dq[HD // 2 :], q).astype(BF16)
        if i == 0:
            scat["o"].step1((1, 3, 0, 2))
        if i == 2:
            sc.relay()
    sk = w.group(R.acs)
    for k in range(NK):
        sk.send(R.acc.at[2 * k + 1 - at.c], R.acs.at[k], at.at_sib())
    sk.wait_recv()
    for k in range(PC):
        for i in range(2):
            grad = R.acc[2 * k + at.c, i]
            if k < NK:
                grad = grad + R.acs[k, i]
            for h in range(HG):
                one = grad[head_rows(h)]
                if i == 0:
                    one = unturn(one[: HD // 2], one[HD // 2 :], k)
                R.dpT[k, (i + 1) * GW + h * HD : (i + 1) * GW + (h + 1) * HD, :] = one.astype(BF16)
    scat["o"].step1d()
    sa = PlaneSum(w, at, R.dA, R.dAd, R.dAx)
    for n, q in enumerate((at.pd, at.px, at.py, at.p)):
        for i in range(2):
            R.dA[i, q] = dot(R.Wh[i * DH : (i + 1) * DH, :], R.dpT[q]).astype(BF16)
        if n == 0:
            sa.far()
        elif n < 3:
            sa.near(n - 1)
    branch = sc.total()
    for i in range(2):
        rows = slice(i * TH, (i + 1) * TH)
        R.vlo[rows, :] = (R.middle[rows, :] + gate_b * branch[i]).astype(BF16)
    R.gm[:, part(5)] = total_rows(R.g[...].astype(F32) * jnp.concatenate(branch, axis=0))
    results = [w.local(R.vlo, R.lo)]
    def proj_grad(i, carry):
        total = dot_t(R.haT[0, tile(i, D // L), :], R.dpT[0])
        for k in range(1, PC):
            total = total + dot_t(R.haT[k, tile(i, D // L), :], R.dpT[k])
        by_core(R.Aq, i, total)
        return carry

    lax.fori_loop(0, L, proj_grad, 0)
    lq.pair()
    lq.line()
    sa.relay()
    scat["o"].step2()
    R.vd[...] = ld.total()
    results.append(w.local(R.vd, R.od))

    def to_chips(fin, buf):
        group = w.group(buf.at[0:3])
        mine = lambda q: fin.at[pl.ds(pl.multiple_of(q * MR, 8), MR)]
        for q in at.others:
            group.send(mine(q), buf.at[at.p], at.at_chip(q))
        return group, w.local(mine(at.p), buf.at[at.p])

    R.finu[...] = lu.total()
    ru = to_chips(R.finu, R.ru)
    dh = jnp.concatenate([half.T for half in sa.total()], axis=1)
    normed, rstd = norm_rows(R.tok[...].astype(F32))
    R.gm[:, part(0)] = total_rows(dh)
    R.gm[:, part(1)] = total_rows(dh * normed)
    gp = w.group(R.gp)
    for i, peer in enumerate(at.tree):
        gp.send(R.gm, R.gp.at[i], peer)
    scat["o"].step3()
    R.vgt[...] = R.dmid[...] + norm_back(dh * (1.0 + scale_a), normed, rstd)
    results.append(w.local(R.vgt, R.gt))
    for copy in ru:
        (copy.wait_recv if copy is ru[0] else copy.wait)()
    R.vu[...] = jnp.concatenate([R.ru[q][:, k * HB : (k + 1) * HB] for k in range(L) for q in range(PC)], axis=1)
    results.append(w.local(R.vu, R.ou))
    gp.wait_recv()
    total = R.gm[...]
    for i in range(S - 1):
        total = total + R.gp[i]
    R.gtree[at.l] = total
    gz = w.group(R.gtree.at[0:3])
    for k in range(1, L):
        gz.send(R.gtree.at[at.l], R.gtree.at[at.l], at.at_leaf(k))
    R.finq[...] = lq.total()
    rq = to_chips(R.finq, R.rq)
    scat["o"].step4()
    scat["o"].step5()
    results.append(w.local(R.vo, R.oo))
    rq[1].wait()
    rq[0].wait_recv()
    R.vq[...] = jnp.concatenate([R.rq[q][:, k * GW : (k + 1) * GW] for k in range(3) for q in range(PC)], axis=1)
    results.append(w.local(R.vq, R.oq))
    gz.wait_recv()
    total = R.cond[0] * R.gtree[0]
    for t in range(1, L):
        total = total + R.cond[t] * R.gtree[t]
    R.vm[...] = total
    results.append(w.local(R.vm, R.om))
    for copy in results:
        copy.wait()


class Refs:
    def __init__(self, **refs):
        self.__dict__.update(refs)


def call_layer(L, S, tok, g, time, parent, pos, live, wq, wo, wu, wd, modw):
    T, D = tok.shape
    FF = wu.shape[1]
    PC, HD = S // 2, D // HEADS
    HG = HEADS // PC
    GW = HG * HD
    CW = -(-3 * GW // 128) * 128
    NM, MR = L * S, wq.shape[0]
    sd = jax.ShapeDtypeStruct
    DM, V = pltpu.SemaphoreType.DMA, pltpu.VMEM
    ins = dict(tok=tok, g=g, time=time, parent=parent, pos=pos, live=live, wq=wq, wo=wo, wu=wu, wd=wd, modw=modw)
    HU = FF // PC
    outs = dict(Go=sd((L, PC, 2 * MR, D), BF16), Gh=sd((L, PC, 2 * MR, CW), BF16), Gu=sd((L, PC, 2 * MR, HU), BF16),
                Gd=sd((L, 2 * wd.shape[0], D), BF16))
    last = dict(lo=((T, D), BF16), gt=((T, D), F32), oq=((MR, 3 * D), F32), oo=((MR, D), F32),
                ou=((MR, FF), F32), od=((FF // NM, D), F32), om=((MR, 6 * D), F32))
    outs.update({k: sd(*v) for k, v in last.items()})
    M6 = 6 * D
    scr = dict(
        Wh=V((D, CW), BF16), Wo=V((D, D), BF16), Wu=V((D, HU), BF16), Wd=V((HU, D), BF16), wqs=V((PC, MR, CW), BF16), wus=V((PC, MR, HU), BF16),
        bias=pltpu.SMEM((PC, live.size), F32), cond=V((L, MR, 1), F32),
        pos2=V((PC, 1, T), F32), cos=V((PC, HD // 2, T), F32), sin=V((PC, HD // 2, T), F32),
        mpart=V((L, 1, M6), F32), mz=V((L - 1, 1, M6), F32), m1=V((1, M6), F32), mp=V((S - 1, 1, M6), F32),
        mod=V((1, M6), F32),
        tX=V((PC, T, D), BF16), gX=V((PC, T, D), BF16), hA=V((PC, T, D), BF16), haT=V((PC, D, T), BF16), QT=V((PC, GW, T), BF16),
        KVT=V((S, 2, GW, T), BF16), kN=V((S, HG, T, HD), BF16), OT=V((PC, GW, T), F32), lse=V((PC, 8, T), F32),
        hsnd=V((PC, GW, T), BF16), attT2=V((2, PC, GW, T), BF16), br_a=V((T, D), F32), middle=V((T, D), F32),
        hB=V((PC, T, D), BF16), hBT=V((PC, D, T), BF16), active=V((PC, T, HU), BF16), actT=V((PC, HU, T), BF16),
        dbb=V((PC, T, D), BF16), du=V((PC, T, HU), BF16), dh=V((T, D), F32), dmid=V((T, D), F32),
        dB=V((2, PC, T // 2, D), BF16), dBd=V((2, T // 2, D), BF16), dBx=V((2, 2, T // 2, D), BF16),
        bB=V((2, PC, T // 2, D), BF16), bBd=V((2, T // 2, D), BF16), bBx=V((2, 2, T // 2, D), BF16),
        Au=V((2, L, PC * MR, HU), BF16), Asu=V((L, PC * MR, HU), BF16), zru=V((L - 1, PC * MR, HU), BF16),
        finu=V((PC * MR, HU), F32), ru=V((PC, MR, HU), F32),
        Ad=V((2, L, HU // L // 2, D), BF16), Asd=V((L, HU // L // 2, D), BF16), zrd=V((L - 1, HU // L // 2, D), BF16),
        dba=V((T, D), BF16), dbah=V((2, T, D // 2), BF16), dbas=V((T, D // 2), BF16),
        dOT=V((PC, GW, T), BF16), vN=V((S, HG, T, HD), BF16),
        acc=V((S, 2, GW, T), F32), acs=V((PC // 2 + 1, 2, GW, T), F32), dpT=V((PC, CW, T), BF16),
        dA=V((2, PC, D // 2, T), BF16), dAd=V((2, D // 2, T), BF16), dAx=V((2, 2, D // 2, T), BF16),
        Aq=V((2, L, PC * MR, CW), BF16), Asq=V((L, PC * MR, CW), BF16), zrq=V((L - 1, PC * MR, CW), BF16),
        finq=V((PC * MR, CW), F32), rq=V((PC, MR, CW), F32),
        gm=V((1, M6), F32), gp=V((S - 1, 1, M6), F32), gtree=V((L, 1, M6), F32))
    for n, rows, cols in (("o", D, D),):
        rb, half = rows // (L * PC), cols // 2
        scr["A" + n] = V((L, PC, rb, half), BF16)
        scr["sw" + n] = V((2, rb, half), BF16)
        scr["dg" + n] = V((2, rb, half), BF16)
        scr["xy" + n] = V((2, L, rb, half), BF16)
        scr["zr" + n] = V((L - 1, rb, half), BF16)
        scr["fin" + n] = V((rb, half), F32)
        scr["sr" + n] = V((rb // 2, half), F32)
    for k, v in last.items():
        scr["v" + k.removeprefix("o") if k != "lo" else "vlo"] = V(*v)
    scr.update(send_sems=DM((72,)), recv_sems=DM((87,)), local_sems=DM((19,)))
    space = dict.fromkeys(("time", "parent", "live"), pltpu.SMEM)
    space.update(dict.fromkeys(("wo", "wd", *outs), pltpu.HBM))
    spec = lambda k: pl.BlockSpec(memory_space=space.get(k, pltpu.VMEM))

    def kernel(*refs):
        R = Refs(**dict(zip(list(ins) + list(outs) + list(scr), refs)))
        at = Place(L, S)
        w = Wires(at, R.send_sems, R.recv_sems, R.local_sems)
        layer(at, w, R)
        w.drain()

    res = pl.pallas_call(
        kernel, out_shape=list(outs.values()), in_specs=[spec(k) for k in ins], out_specs=[spec(k) for k in outs],
        scratch_shapes=list(scr.values()),
        compiler_params=pltpu.CompilerParams(collective_id=1, has_side_effects=True, vmem_limit_bytes=64 << 20),
    )(*ins.values())
    return dict(zip(outs, res))


def hand_out(*arrays):
    count = len(arrays)

    def kernel(*refs):
        sources, targets, held, sems = refs[:count], refs[count : 2 * count], refs[2 * count : 3 * count], refs[-1]
        arrive = [pltpu.make_async_copy(x, y, sems.at[0, i]) for i, (x, y) in enumerate(zip(sources, held))]
        leave = [pltpu.make_async_copy(x, y, sems.at[1, i]) for i, (x, y) in enumerate(zip(held, targets))]
        for copy in arrive:
            copy.start()
        for first, second in zip(arrive, leave):
            first.wait()
            second.start()
        for copy in leave:
            copy.wait()

    hbm = pl.BlockSpec(memory_space=pltpu.HBM)
    return pl.pallas_call(
        kernel, out_shape=[jax.ShapeDtypeStruct(a.shape, a.dtype) for a in arrays],
        in_specs=[hbm] * count, out_specs=[hbm] * count,
        scratch_shapes=[pltpu.VMEM(a.shape, a.dtype) for a in arrays] + [pltpu.SemaphoreType.DMA((2, count))],
    )(*arrays)


def layer_kernels(
    tokens, cotangent, timesteps, parent, positions, block_live, qkv_weight, out_weight, up_weight, down_weight, mod_weight
):
    f = call_layer(
        lax.axis_size("leaf"), lax.axis_size("seq"), tokens[0], cotangent[0], timesteps, parent, positions, block_live,
        qkv_weight, out_weight, up_weight, down_weight, mod_weight,
    )
    lo, gt, *rest = hand_out(*(f[k] for k in ("lo", "gt", "oq", "oo", "ou", "od", "om")))
    return (lo[None], gt[None], *rest)


def layer_norm(values):
    centred = values - jnp.mean(values, axis=-1, keepdims=True)
    variance = jnp.mean(centred * centred, axis=-1, keepdims=True)
    return centred * lax.rsqrt(variance + EPSILON)


def time_embed(step_values, model_width):
    half_width = model_width // 2
    freqs = jnp.exp(-math.log(10000.0) * jnp.arange(half_width, dtype=jnp.float32) / half_width)
    angles = step_values.astype(jnp.float32)[..., None] * freqs
    return jnp.concatenate([jnp.cos(angles), jnp.sin(angles)], axis=-1)


def rope_tables(places, head_dim):
    half_dim = head_dim // 2
    inverse = jnp.exp(-math.log(10000.0) * 2.0 * jnp.arange(half_dim, dtype=jnp.float32) / head_dim)
    angles = places.astype(jnp.float32)[:, None] * inverse[None, :]
    return (jnp.cos(angles), jnp.sin(angles))


def rotate(values, cosine, sine):
    half_dim = values.shape[-1] // 2
    first = values[..., :half_dim]
    second = values[..., half_dim:]
    cos_wide = cosine[:, None, :]
    sin_wide = sine[:, None, :]
    return jnp.concatenate(
        [first * cos_wide - second * sin_wide, second * cos_wide + first * sin_wide], axis=-1
    )


def rotate_back(grads, cosine, sine):
    half_dim = grads.shape[-1] // 2
    first = grads[..., :half_dim]
    second = grads[..., half_dim:]
    cos_wide = cosine[:, None, :]
    sin_wide = sine[:, None, :]
    return jnp.concatenate(
        [first * cos_wide + second * sin_wide, second * cos_wide - first * sin_wide], axis=-1
    )


def ancestor_row(parent_row, seg_index, seg_count):
    seg_range = jnp.arange(seg_count, dtype=jnp.int32)

    def climb(step_index, state_now):
        current, reached = state_now
        current = parent_row[current]
        return (current, reached | (seg_range == current))

    return lax.fori_loop(0, seg_count, climb, (seg_index, seg_range == seg_index))[1]


def attend_keys(state_now, query_rot, key_block, value_block, key_ok, score_scale):
    maximum_old, total_old, accum_old = state_now
    scores = (
        jnp.einsum("qhd,khd->hqk", query_rot, key_block, preferred_element_type=jnp.float32)
        * score_scale
    )
    visible = key_ok[None, None, :]
    scores = jnp.where(visible, scores, NEGATIVE)
    maximum_new = jnp.maximum(maximum_old, jnp.max(scores, axis=-1))
    weights_p = jnp.where(visible, jnp.exp(scores - maximum_new[..., None]), 0.0)
    rescale = jnp.exp(maximum_old - maximum_new)
    total_new = total_old * rescale + jnp.sum(weights_p, axis=-1)
    accum_new = accum_old * rescale[..., None] + jnp.einsum(
        "hqk,khd->hqd",
        weights_p.astype(jnp.bfloat16),
        value_block,
        preferred_element_type=jnp.float32,
    )
    return (maximum_new, total_new, accum_new)


def score_grads(
    query_rot, grad_attended, log_total, delta_rows, key_block, value_block, mask_wide, score_scale
):
    scores = (
        jnp.einsum("qhd,khd->hqk", query_rot, key_block, preferred_element_type=jnp.float32)
        * score_scale
    )
    probs = jnp.where(mask_wide, jnp.exp(scores - log_total[..., None]), 0.0)
    grad_probs = jnp.einsum(
        "qhd,khd->hqk", grad_attended, value_block, preferred_element_type=jnp.float32
    )
    grad_scores = (probs * (grad_probs - delta_rows[..., None])).astype(jnp.bfloat16)
    return (probs, grad_scores)


def query_only(
    grad_query,
    query_rot,
    grad_attended,
    log_total,
    delta_rows,
    key_block,
    value_block,
    key_ok,
    score_scale,
):
    probs, grad_scores = score_grads(
        query_rot,
        grad_attended,
        log_total,
        delta_rows,
        key_block,
        value_block,
        key_ok[None, None, :],
        score_scale,
    )
    return (
        grad_query
        + jnp.einsum("hqk,khd->qhd", grad_scores, key_block, preferred_element_type=jnp.float32)
        * score_scale
    )


def layer_native(
    tokens,
    cotangent,
    timesteps,
    parent,
    positions,
    block_live,
    qkv_weight,
    out_weight,
    up_weight,
    down_weight,
    mod_weight,
):
    seg_count = lax.axis_size("seq")
    seg_index = lax.axis_index("seq")
    tree_index = lax.axis_index("leaf")
    tok_rows = tokens.shape[1]
    model_width = tokens.shape[2]
    head_count = HEADS
    head_dim = model_width // head_count
    score_scale = head_dim ** (-0.5)
    tree_rows = tok_rows * seg_count
    qkv_all, out_all, up_all, down_all = (
        lax.all_gather(qkv_weight, ("leaf", "seq"), axis=0, tiled=True),
        lax.all_gather(out_weight, ("leaf", "seq"), axis=0, tiled=True),
        lax.all_gather(up_weight, ("leaf", "seq"), axis=0, tiled=True),
        lax.all_gather(down_weight, ("leaf", "seq"), axis=0, tiled=True),
    )
    condition = jax.nn.silu(time_embed(timesteps, model_width)).astype(jnp.bfloat16)
    mod_all = lax.all_gather(mod_weight, ("leaf", "seq"), axis=0, tiled=True)
    cond_own = lax.dynamic_index_in_dim(condition, tree_index, 0, keepdims=False)
    modulation = jnp.dot(cond_own[None, :], mod_all, preferred_element_type=jnp.float32)[0]
    shift_a, scale_a, gate_a, shift_b, scale_b, gate_b = jnp.split(modulation, 6)
    inputs_f = tokens[0].astype(jnp.float32)
    normed_a = layer_norm(inputs_f)
    hidden_a = (normed_a * (1.0 + scale_a) + shift_a).astype(jnp.bfloat16)
    projected = jnp.dot(hidden_a, qkv_all, preferred_element_type=jnp.float32).reshape(
        tok_rows, 3, head_count, head_dim
    )
    cosine, sine = rope_tables(positions[0], head_dim)
    query_rot = rotate(projected[:, 0], cosine, sine).astype(jnp.bfloat16)
    key_rot = rotate(projected[:, 1], cosine, sine).astype(jnp.bfloat16)
    value_rows = projected[:, 2].astype(jnp.bfloat16)
    key_flat = key_rot.reshape(tok_rows, model_width)
    value_flat = value_rows.reshape(tok_rows, model_width)
    reached = ancestor_row(parent[0], seg_index, seg_count)
    live_blocks = block_live.shape[2]
    live_tokens = jnp.repeat(block_live[0] > 0, tok_rows // live_blocks, axis=1)
    key_allowed = (reached[:, None] & live_tokens).reshape(tree_rows)
    start_state = (
        jnp.full((head_count, tok_rows), NEGATIVE, jnp.float32),
        jnp.zeros((head_count, tok_rows), jnp.float32),
        jnp.zeros((head_count, tok_rows, head_dim), jnp.float32),
    )
    key_part = lax.all_gather(key_flat, "seq", axis=0, tiled=True)
    value_part = lax.all_gather(value_flat, "seq", axis=0, tiled=True)
    count_keys = key_part.shape[0]
    block_size = tok_rows
    block_count = count_keys // block_size
    allow_part = key_allowed.reshape(block_count, block_size)
    key_blocks = key_part.reshape(block_count, block_size, head_count, head_dim)
    value_blocks = value_part.reshape(block_count, block_size, head_count, head_dim)

    def advance(state_now, block_in):
        return (
            attend_keys(state_now, query_rot, block_in[0], block_in[1], block_in[2], score_scale),
            None,
        )

    maximum_run, total_run, accum_run = lax.scan(
        advance, start_state, (key_blocks, value_blocks, allow_part)
    )[0]
    attended_heads = jnp.transpose(accum_run / total_run[..., None], (1, 0, 2))
    log_total = maximum_run + jnp.log(total_run)
    attended = attended_heads.reshape(tok_rows, model_width).astype(jnp.bfloat16)
    branch_a = jnp.dot(attended, out_all, preferred_element_type=jnp.float32)
    middle = inputs_f + gate_a * branch_a
    normed_b = layer_norm(middle)
    hidden_b = (normed_b * (1.0 + scale_b) + shift_b).astype(jnp.bfloat16)
    upper = jnp.dot(hidden_b, up_all, preferred_element_type=jnp.float32)
    active = jax.nn.gelu(upper).astype(jnp.bfloat16)
    branch_b = jnp.dot(active, down_all, preferred_element_type=jnp.float32)
    layer_out = (middle + gate_b * branch_b).astype(jnp.bfloat16)
    qkv_back, out_back, up_back, down_back = (
        lax.all_gather(qkv_weight, ("leaf", "seq"), axis=0, tiled=True),
        lax.all_gather(out_weight, ("leaf", "seq"), axis=0, tiled=True),
        lax.all_gather(up_weight, ("leaf", "seq"), axis=0, tiled=True),
        lax.all_gather(down_weight, ("leaf", "seq"), axis=0, tiled=True),
    )
    grad_out_rows = cotangent[0].astype(jnp.float32)
    grad_branch_b = (gate_b * grad_out_rows).astype(jnp.bfloat16)
    dgate_b = jnp.sum(grad_out_rows * branch_b, axis=0)
    grad_down = jnp.einsum("qf,qd->fd", active, grad_branch_b, preferred_element_type=jnp.float32)
    grad_active = jnp.einsum(
        "qd,fd->qf", grad_branch_b, down_back, preferred_element_type=jnp.float32
    )
    gelu_pull = jax.vjp(jax.nn.gelu, upper)[1]
    grad_upper = gelu_pull(grad_active)[0].astype(jnp.bfloat16)
    grad_up = jnp.einsum("qd,qf->df", hidden_b, grad_upper, preferred_element_type=jnp.float32)
    grad_hidden_b = jnp.einsum("qf,df->qd", grad_upper, up_back, preferred_element_type=jnp.float32)
    dshift_b = jnp.sum(grad_hidden_b, axis=0)
    dscale_b = jnp.sum(grad_hidden_b * normed_b, axis=0)
    norm_pull_b = jax.vjp(layer_norm, middle)[1]
    grad_middle = grad_out_rows + norm_pull_b(grad_hidden_b * (1.0 + scale_b))[0]
    grad_branch_a = (gate_a * grad_middle).astype(jnp.bfloat16)
    dgate_a = jnp.sum(grad_middle * branch_a, axis=0)
    grad_out = jnp.einsum("qi,qd->id", attended, grad_branch_a, preferred_element_type=jnp.float32)
    grad_attended = jnp.einsum(
        "qd,id->qi", grad_branch_a, out_back, preferred_element_type=jnp.float32
    ).astype(jnp.bfloat16)
    grad_att_heads = grad_attended.reshape(tok_rows, head_count, head_dim)
    delta_rows = jnp.einsum("qhd,qhd->hq", grad_att_heads.astype(jnp.float32), attended_heads)
    start_query = jnp.zeros((tok_rows, head_count, head_dim), jnp.float32)
    key_part = lax.all_gather(key_flat, "seq", axis=0, tiled=True)
    value_part = lax.all_gather(value_flat, "seq", axis=0, tiled=True)
    count_keys = key_part.shape[0]
    block_size = tok_rows
    block_count = count_keys // block_size
    allow_part = key_allowed.reshape(block_count, block_size)
    key_blocks = key_part.reshape(block_count, block_size, head_count, head_dim)
    value_blocks = value_part.reshape(block_count, block_size, head_count, head_dim)

    def advance(grad_now, block_in):
        return (
            query_only(
                grad_now,
                query_rot,
                grad_att_heads,
                log_total,
                delta_rows,
                block_in[0],
                block_in[1],
                block_in[2],
                score_scale,
            ),
            None,
        )

    grad_query = lax.scan(advance, start_query, (key_blocks, value_blocks, allow_part))[0]
    seg_range = jnp.arange(seg_count, dtype=jnp.int32)
    every_reach = jax.vmap(lambda one_seg: ancestor_row(parent[0], one_seg, seg_count))(seg_range)
    sees_mine = every_reach[:, seg_index]
    own_live = lax.dynamic_index_in_dim(live_tokens, seg_index, 0, keepdims=False)
    total_all, delta_all = (
        lax.all_gather(jnp.transpose(log_total), "seq", axis=0, tiled=True),
        lax.all_gather(jnp.transpose(delta_rows), "seq", axis=0, tiled=True),
    )
    query_flat = query_rot.reshape(tok_rows, model_width)
    grad_key_acc = jnp.zeros((tok_rows, head_count, head_dim), jnp.float32)
    grad_value_acc = jnp.zeros((tok_rows, head_count, head_dim), jnp.float32)
    query_part = lax.all_gather(query_flat, "seq", axis=0, tiled=True)
    grad_part = lax.all_gather(grad_attended, "seq", axis=0, tiled=True)
    count_rows = query_part.shape[0]
    block_size = tok_rows
    block_count = count_rows // block_size
    row_seg = jnp.arange(count_rows, dtype=jnp.int32) // tok_rows
    row_ok = sees_mine[row_seg].reshape(block_count, block_size)
    total_part = total_all.reshape(block_count, block_size, head_count)
    delta_part = delta_all.reshape(block_count, block_size, head_count)
    query_blocks = query_part.reshape(block_count, block_size, head_count, head_dim)
    grad_blocks = grad_part.reshape(block_count, block_size, head_count, head_dim)

    def advance(acc_now, block_in):
        key_acc, value_acc = acc_now
        query_block, grad_block, total_block, delta_block, ok_block = block_in
        mask_wide = ok_block[None, :, None] & own_live[None, None, :]
        probs, grad_scores = score_grads(
            query_block,
            grad_block,
            jnp.transpose(total_block),
            jnp.transpose(delta_block),
            key_rot,
            value_rows,
            mask_wide,
            score_scale,
        )
        key_acc = (
            key_acc
            + jnp.einsum(
                "hqk,qhd->khd", grad_scores, query_block, preferred_element_type=jnp.float32
            )
            * score_scale
        )
        value_acc = value_acc + jnp.einsum(
            "hqk,qhd->khd",
            probs.astype(jnp.bfloat16),
            grad_block,
            preferred_element_type=jnp.float32,
        )
        return ((key_acc, value_acc), None)

    grad_key_rows, grad_value_heads = lax.scan(
        advance,
        (grad_key_acc, grad_value_acc),
        (query_blocks, grad_blocks, total_part, delta_part, row_ok),
    )[0]
    grad_value_rows = grad_value_heads.reshape(tok_rows, model_width)
    grad_query_pre = rotate_back(grad_query, cosine, sine).reshape(tok_rows, model_width)
    grad_key_pre = rotate_back(grad_key_rows, cosine, sine).reshape(tok_rows, model_width)
    grad_projected = jnp.concatenate(
        [grad_query_pre, grad_key_pre, grad_value_rows], axis=-1
    ).astype(jnp.bfloat16)
    grad_qkv = jnp.einsum("qi,qj->ij", hidden_a, grad_projected, preferred_element_type=jnp.float32)
    grad_hidden_a = jnp.einsum(
        "qj,ij->qi", grad_projected, qkv_back, preferred_element_type=jnp.float32
    )
    dshift_a = jnp.sum(grad_hidden_a, axis=0)
    dscale_a = jnp.sum(grad_hidden_a * normed_a, axis=0)
    norm_pull_a = jax.vjp(layer_norm, inputs_f)[1]
    grad_tokens = grad_middle + norm_pull_a(grad_hidden_a * (1.0 + scale_a))[0]
    grad_modulation = jnp.concatenate([dshift_a, dscale_a, dgate_a, dshift_b, dscale_b, dgate_b])
    sum_qkv, sum_out, sum_up, sum_down = (
        lax.psum_scatter(grad_qkv, ("leaf", "seq"), scatter_dimension=0, tiled=True),
        lax.psum_scatter(grad_out, ("leaf", "seq"), scatter_dimension=0, tiled=True),
        lax.psum_scatter(grad_up, ("leaf", "seq"), scatter_dimension=0, tiled=True),
        lax.psum_scatter(grad_down, ("leaf", "seq"), scatter_dimension=0, tiled=True),
    )
    mod_term = cond_own.astype(jnp.float32)[:, None] * grad_modulation[None, :]
    sum_mod = lax.psum_scatter(mod_term, ("leaf", "seq"), scatter_dimension=0, tiled=True)
    return (layer_out[None], grad_tokens[None], sum_qkv, sum_out, sum_up, sum_down, sum_mod)


def solution(mesh):
    rows = P("leaf", "seq", None)
    held = P(("leaf", "seq"), None)
    placed = (rows, rows, P(), P("leaf", None), P("leaf", "seq"), P("leaf", None, None), held, held, held, held, held)
    kernels = mesh.shape["seq"] == 8 and mesh.shape["leaf"] == 4
    return jax.shard_map(
        layer_kernels if kernels else layer_native,
        mesh=mesh,
        in_specs=placed,
        out_specs=(rows, rows, held, held, held, held, held),
        check_vma=False,
    )
```

```python
import functools, math
import jax, jax.numpy as jnp
from jax import lax
from jax.experimental import pallas as pl
from jax.experimental.pallas import tpu as pltpu
from jax.sharding import PartitionSpec as P

MESH = pl.DeviceIdType.MESH
HEADS = 12
EPSILON = 1e-06
NEGATIVE = -1e30
F32 = jnp.float32
BF16 = jnp.bfloat16
GELU_A = math.sqrt(2.0 / math.pi)
GELU_B = 0.044715


class Sems:
    def __init__(self, ref):
        self.ref, self.used = ref, 0

    def one(self):
        self.used += 1
        assert self.used <= self.ref.shape[0]
        return self.ref.at[self.used - 1]


class Place:
    def __init__(self, leaf_count, seg_count):
        self.L, self.S = leaf_count, seg_count
        self.P = seg_count // 2
        self.l, self.s = lax.axis_index("leaf"), lax.axis_index("seq")
        self.c, self.p = lax.rem(self.s, 2), self.s // 2
        self.sib = self.s + 1 - 2 * self.c
        self.inner = (self.l + 1) // 2 == 1
        self.px = self.p + 1 - 2 * lax.rem(self.p, 2)
        self.py = lax.rem(self.p + 2, 4)
        self.pd = lax.rem(self.px + 2, 4)
        self.others = [self.px, self.py, self.pd]
        self.tree = [(self.l, 2 * q + core) for core in (self.c, 1 - self.c) for q in self.others] + [(self.l, self.sib)]

    def leaf(self, k):
        far = lax.rem(self.l + 2, 4) if k >= 2 else self.l
        return far + 1 - 2 * lax.rem(far, 2) if k % 2 else far

    def turn(self, k):
        return jnp.where(self.inner, 4 - k, k)

    def leaf_turn(self, k):
        return jnp.where(self.inner, self.leaf(4 - k), self.leaf(k))

    def at_leaf(self, k):
        return (self.leaf(k), self.s)

    def at_chip(self, q):
        return (self.l, 2 * q + self.c)

    def at_sib(self):
        return (self.l, self.sib)

    def greet(self):
        self.sem = pltpu.get_barrier_semaphore()
        self.peers = [self.at_leaf(k) for k in range(1, self.L)] + self.tree
        for peer in self.peers:
            pl.semaphore_signal(self.sem, inc=1, device_id=peer, device_id_type=MESH)

    def meet(self):
        pl.semaphore_wait(self.sem, len(self.peers))


class Wires:
    def __init__(self, at, send_sems, recv_sems, local_sems):
        self.at = at
        self.send_sems, self.recv_sems, self.local_sems = Sems(send_sems), Sems(recv_sems), Sems(local_sems)
        self.open = []

    def send(self, src, dst, dev):
        copy = pltpu.make_async_remote_copy(
            src_ref=src, dst_ref=dst, send_sem=self.send_sems.one(), recv_sem=self.recv_sems.one(),
            device_id=dev, device_id_type=MESH)
        copy.start()
        self.open.append(copy)
        return copy

    def group(self, whole):
        group = Group(self, whole)
        self.open.append(group)
        return group

    def local(self, src, dst):
        copy = pltpu.make_async_copy(src, dst, self.local_sems.one())
        copy.start()
        return copy

    def sent(self, copies):
        for copy in copies:
            copy.wait_send()
        self.open = [copy for copy in self.open if all(copy is not other for other in copies)]

    def drain(self):
        for copy in self.open:
            copy.wait_send()
        self.open = []


class Group:
    def __init__(self, wires, whole):
        self.at, self.whole = wires.at, whole
        self.send_sem, self.recv_sem = wires.send_sems.one(), wires.recv_sems.one()

    def make(self, src, dst, dev):
        return pltpu.make_async_remote_copy(
            src_ref=src, dst_ref=dst, send_sem=self.send_sem, recv_sem=self.recv_sem, device_id=dev, device_id_type=MESH)

    def send(self, src, dst, dev):
        self.make(src, dst, dev).start()
        return self

    def wait_recv(self):
        self.make(self.whole, self.whole, self.at.at_sib()).wait_recv()

    def wait_send(self):
        self.make(self.whole, self.whole, self.at.at_sib()).wait_send()


class Line:
    def __init__(self, wires, at, view, whole):
        self.w, self.at, self.view = wires, at, view
        self.first = wires.send_sems.one()
        self.onward = wires.send_sems.one()
        self.arrive = [None] + [wires.recv_sems.one() for _ in range(3)]
        self.whole = whole
        wires.open.append(self)

    def leaf(self, unit):
        at = self.at
        if unit < 2:
            return at.leaf(unit)
        return jnp.where(at.l < 2, unit, 3 - unit)

    def make(self, src, leaf, unit, to, sem):
        return pltpu.make_async_remote_copy(
            src_ref=src, dst_ref=self.view(leaf), send_sem=sem, recv_sem=self.arrive[unit], device_id=to, device_id_type=MESH)

    def begin(self, src):
        at = self.at
        self.make(src, at.l, 1, at.at_leaf(1), self.first).start()

        @pl.when(at.inner)
        def _():
            self.make(src, at.l, 2, at.at_leaf(3), self.onward).start()

    def early(self, unit):
        at = self.at
        leaf = self.leaf(unit)
        part = self.view(leaf)

        @pl.when(at.inner)
        def _():
            self.make(part, leaf, unit, at.at_sib(), self.first).wait_recv()
            if unit == 1:
                self.make(part, leaf, 3, at.at_leaf(3), self.onward).start()
            else:
                self.make(part, leaf, unit, at.at_leaf(1), self.onward).start()

    def late(self, unit):
        at = self.at
        leaf = self.leaf(unit)

        @pl.when(jnp.logical_not(at.inner))
        def _():
            self.make(self.view(leaf), leaf, unit, at.at_sib(), self.first).wait_recv()

    def wait_send(self):
        at = self.at
        part = self.view(at.l)
        self.make(part, at.l, 1, at.at_sib(), self.first).wait_send()

        @pl.when(at.inner)
        def _():
            pltpu.make_async_remote_copy(
                src_ref=self.whole, dst_ref=self.whole, send_sem=self.onward, recv_sem=self.arrive[1],
                device_id=at.at_sib(), device_id_type=MESH).wait_send()


class Gather:
    def __init__(self, wires, at, shard, full):
        self.w, self.at, self.shard, self.full = wires, at, shard, full
        count = shard.shape[0]
        self.rows = pl.ds(pl.multiple_of(at.c * count, 8), count)
        self.line = Line(wires, at, lambda leaf: full.at[leaf, at.p, self.rows], full.at[:, at.p, self.rows])
        self.pair = wires.group(full.at[:, :, self.rows])
        self.cross, self.relay = {}, {}
        self.sent_cross, self.sent_relay = wires.send_sems.one(), wires.send_sems.one()
        wires.open.append(self)

    def view(self, unit, chip):
        return self.full.at[self.line.leaf(unit), chip, self.rows]

    def make(self, src, dst, to, sem, recv):
        return pltpu.make_async_remote_copy(
            src_ref=src, dst_ref=dst, send_sem=sem, recv_sem=recv, device_id=self.at.at_chip(to), device_id_type=MESH)

    def begin(self):
        self.own = self.w.local(self.shard, self.view(0, self.at.p))
        self.line.begin(self.shard)

    def stage1(self, unit):
        at = self.at
        mine = self.view(unit, at.p)
        src = mine if unit else self.shard
        self.cross[unit] = [self.make(src, mine, q, self.sent_cross, self.w.recv_sems.one()) for q in (at.px, at.py)]
        for copy in self.cross[unit]:
            copy.start()
        self.pair.send(src, mine, at.at_sib())

    def stage2(self, unit):
        at = self.at
        for i, (q, to) in enumerate(((at.px, at.py), (at.py, at.px))):
            self.cross[unit][i].wait_recv()
            theirs = self.view(unit, q)
            if unit % 2 == i:
                self.relay[unit] = self.make(theirs, theirs, to, self.sent_relay, self.w.recv_sems.one())
                self.relay[unit].start()
            self.pair.send(theirs, theirs, at.at_sib())

    def stage3(self, unit):
        self.relay[unit].wait_recv()
        theirs = self.view(unit, self.at.pd)
        self.pair.send(theirs, theirs, self.at.at_sib())

    def finish(self):
        self.own.wait()
        self.pair.wait_recv()

    def wait_send(self):
        at = self.at
        two, one = self.full.at[:, 0:2, self.rows], self.full.at[:, 0, self.rows]
        spare = self.line.arrive[1]
        self.make(two, two, at.px, self.sent_cross, spare).wait_send()
        self.make(one, one, at.px, self.sent_relay, spare).wait_send()


def add_to(ref, *others):
    total = ref[...].astype(F32)
    for other in others:
        total = total + other[...].astype(F32)
    ref[...] = total.astype(ref.dtype)


class Scatter:
    def __init__(self, wires, at, A, sw, dg, xy, zr, fin, sibr, out):
        self.w, self.at = wires, at
        self.A, self.sw, self.dg, self.xy, self.zr, self.fin, self.sibr, self.out = A, sw, dg, xy, zr, fin, sibr, out

    def cross(self, unit, to, side):
        leaf = self.at.leaf(unit)
        self.x.send(self.A.at[leaf, to], self.xy.at[side, leaf], self.at.at_chip(to))

    def step0(self):
        at = self.at
        self.s = self.w.group(self.sw)
        for i in range(2):
            self.s.send(self.A.at[at.leaf(1 + 2 * i), at.pd], self.sw.at[i], at.at_leaf(1))
        self.x = self.w.group(self.xy)

    def step1(self, units):
        at = self.at
        for unit in units:
            if unit != 2:
                self.cross(unit, at.px, 0)
            if unit != 0:
                self.cross(unit, at.py, 1)

    def step1d(self):
        w, at, A = self.w, self.at, self.A
        self.s.wait_recv()
        self.d = []
        for i, to in enumerate((at.px, at.py)):
            add_to(A.at[at.leaf(2 * i), at.pd], self.sw.at[i])
            self.d.append(w.send(A.at[at.leaf(2 * i), at.pd], self.dg.at[i], at.at_chip(to)))

    def step2(self):
        at, A = self.at, self.A
        for i, to in enumerate((at.py, at.px)):
            self.d[i].wait_recv()
            add_to(A.at[at.leaf(2 * i), to], self.dg.at[i])
            self.cross(2 * i, to, 1 - i)

    def step3(self):
        w, at, A = self.w, self.at, self.A
        self.x.wait_recv()
        self.z = w.group(self.zr)
        for k in (1, 2, 3):
            leaf = at.leaf_turn(k)
            add_to(A.at[leaf, at.p], self.xy.at[0, leaf], self.xy.at[1, leaf])
            self.z.send(A.at[leaf, at.p], self.zr.at[at.turn(k) - 1], (leaf, at.s))
        add_to(A.at[at.l, at.p], self.xy.at[0, at.l], self.xy.at[1, at.l])

    def step4(self):
        w, at = self.w, self.at
        self.z.wait_recv()
        total = self.A[at.l, at.p].astype(F32)
        for k in range(at.L - 1):
            total = total + self.zr[k].astype(F32)
        self.fin[...] = total
        rows = self.fin.shape[0] // 2
        self.f = w.send(self.fin.at[pl.ds(pl.multiple_of(rows * (1 - at.c), 8), rows)], self.sibr, at.at_sib())

    def step5(self):
        at = self.at
        rows, half = self.sibr.shape
        mine = self.fin[pl.ds(pl.multiple_of(rows * at.c, 8), rows), :]
        self.out[:, pl.ds(pl.multiple_of(half * at.c, 128), half)] = mine
        self.f.wait_recv()
        self.out[:, pl.ds(pl.multiple_of(half * (1 - at.c), 128), half)] = self.sibr[...]


class PlaneGather:
    def __init__(self, wires, at, buf):
        self.w, self.at, self.buf = wires, at, buf
        rows = buf.shape[1] // 2
        self.halves = pl.ds(0, rows), pl.ds(rows, rows)

    def send(self, half, q):
        mine = self.buf.at[self.at.p, half]
        return self.w.send(mine, mine, self.at.at_chip(q))

    def first(self):
        at, (up, low) = self.at, self.halves
        self.own = [self.send(up, at.px), self.send(low, at.py)]

    def second(self):
        at, (up, low) = self.at, self.halves
        self.own += [self.send(low, at.px), self.send(up, at.py)]

    def start(self):
        self.first()
        self.second()

    def relay(self):
        at = self.at
        self.passed = []
        for half, copy, q, to in zip(self.halves, self.own, (at.px, at.py), (at.py, at.px)):
            copy.wait_recv()
            theirs = self.buf.at[q, half]
            self.passed.append(self.w.send(theirs, theirs, at.at_chip(to)))

    def near(self):
        for copy in self.own[2:]:
            copy.wait_recv()

    def far(self):
        for copy in self.passed:
            copy.wait_recv()


class PlaneSum:
    def __init__(self, wires, at, A, Ad, Ax):
        self.w, self.at, self.A, self.Ad, self.Ax = wires, at, A, Ad, Ax
        self.x = wires.group(Ax)

    def far(self):
        at = self.at
        self.d = [self.w.send(self.A.at[i, at.pd], self.Ad.at[i], at.at_chip(to)) for i, to in enumerate((at.px, at.py))]

    def near(self, i):
        at = self.at
        to = (at.px, at.py)[i]
        self.x.send(self.A.at[i, to], self.Ax.at[i, i], at.at_chip(to))

    def relay(self):
        at = self.at
        for i, to in enumerate((at.py, at.px)):
            self.d[i].wait_recv()
            add_to(self.A.at[i, to], self.Ad.at[i])
            self.x.send(self.A.at[i, to], self.Ax.at[1 - i, i], at.at_chip(to))

    def total(self):
        self.x.wait_recv()
        return [self.A[i, self.at.p].astype(F32) + self.Ax[0, i].astype(F32) + self.Ax[1, i].astype(F32) for i in range(2)]


class LineSum:
    def __init__(self, wires, at, A, As, zr):
        self.w, self.at, self.A, self.As, self.zr = wires, at, A, As, zr

    def pair(self):
        self.s = self.w.send(self.A.at[1 - self.at.c], self.As, self.at.at_sib())

    def line(self):
        at, A = self.at, self.A
        self.s.wait_recv()
        self.z = self.w.group(self.zr)
        for k in (1, 2, 3):
            leaf = at.leaf_turn(k)
            add_to(A.at[at.c, leaf], self.As.at[leaf])
            self.z.send(A.at[at.c, leaf], self.zr.at[at.turn(k) - 1], (leaf, at.s))
        add_to(A.at[at.c, at.l], self.As.at[at.l])

    def total(self):
        self.z.wait_recv()
        total = self.A[self.at.c, self.at.l].astype(F32)
        for k in range(self.at.L - 1):
            total = total + self.zr[k].astype(F32)
        return total


class Columns:
    def __init__(self, wires, at, full, parts):
        self.w, self.at, self.full = wires, at, full
        count = full.shape[2] // 2
        self.rows = pl.ds(pl.multiple_of(at.c * count, 8), count)
        self.first = wires.group(full.at[0, 0:3, self.rows])
        size = at.P // parts
        self.lines = []
        for i in range(parts):
            some = pl.ds(i * size, size)
            held = lambda leaf, some=some: full.at[leaf, some, self.rows]
            self.lines.append(Line(wires, at, held, full.at[:, some, self.rows]))
        self.pair = wires.group(full.at[:, :, self.rows])

    def start(self, parts):
        at = self.at
        mine = self.full.at[at.l, at.p, self.rows]
        for q in at.others:
            self.first.send(parts.at[q], mine, at.at_chip(q))
        self.own = self.w.local(parts.at[at.p], mine)

    def begin(self):
        at = self.at
        self.first.wait_recv()
        self.own.wait()
        for line in self.lines:
            line.begin(line.view(at.l))
        for line in self.lines:
            self.pair.send(line.view(at.l), line.view(at.l), at.at_sib())

    def early(self, unit):
        for line in self.lines:
            line.early(unit)

    def late(self, unit):
        for line in self.lines:
            line.late(unit)
            part = line.view(line.leaf(unit))
            self.pair.send(part, part, self.at.at_sib())


class Rows:
    def __init__(self, wires, at, shard, full):
        self.w, self.at, self.shard, self.full = wires, at, shard, full
        count = shard.shape[0]
        self.rows = pl.ds(pl.multiple_of(at.c * count, 8), count)
        self.line = Line(wires, at, self.held, full.at[:, self.rows])
        self.pair = wires.group(full.at[:, self.rows])

    def held(self, leaf):
        return self.full.at[leaf, self.rows]

    def begin(self):
        at = self.at
        self.own = self.w.local(self.shard, self.held(at.l))
        self.line.begin(self.shard)
        self.pair.send(self.shard, self.held(at.l), at.at_sib())

    def late(self, unit):
        self.line.late(unit)
        part = self.held(self.line.leaf(unit))
        self.pair.send(part, part, self.at.at_sib())


def norm_rows(values):
    centred = values - jnp.mean(values, axis=-1, keepdims=True)
    variance = jnp.mean(centred * centred, axis=-1, keepdims=True)
    rstd = lax.rsqrt(variance + EPSILON)
    return centred * rstd, rstd


def norm_back(grad, normed, rstd):
    return rstd * (grad - jnp.mean(grad, axis=-1, keepdims=True) - normed * jnp.mean(grad * normed, axis=-1, keepdims=True))


def total_rows(values):
    return jnp.sum(values, axis=0, keepdims=True)


def dot(left, right):
    return jnp.dot(left, right, preferred_element_type=F32)


def dot_t(left, right):
    return lax.dot_general(left, right, (((1,), (1,)), ((), ())), preferred_element_type=F32)


def tile(j, size):
    return pl.ds(pl.multiple_of(j * size, size), size)


def condition_column(at, timestep, count, width):
    half = width // 2
    row = (at.l * at.S + at.s) * count + lax.broadcasted_iota(jnp.int32, (count, 1), 0)
    index = jnp.where(row < half, row, row - half).astype(F32)
    angle = timestep.astype(F32) * jnp.exp(-math.log(10000.0) * index / half)
    value = jnp.where(row < half, jnp.cos(angle), jnp.sin(angle))
    return (value / (1.0 + jnp.exp(-value))).astype(BF16).astype(F32)


def fill_bias(at, R):
    _, blocks, seg_count = R.live.shape
    live = R.live[0]
    live = [[live[b, a] for b in range(blocks)] for a in range(seg_count)]

    def fill(k, carry):
        seg = 2 * k + at.c
        current = seg
        reached = [jnp.where(seg == a, 1, 0) for a in range(seg_count)]
        for _ in range(seg_count):
            current = R.parent[0, current]
            reached = [jnp.where(current == a, 1, r) for a, r in enumerate(reached)]
        for a in range(seg_count):
            for b in range(blocks):
                R.bias[k, a * blocks + b] = jnp.where(reached[a] * live[a][b] > 0, 0.0, NEGATIVE)
        return carry

    lax.fori_loop(0, at.P, fill, 0)


def by_blocks(R, score, chip, a):
    blocks = R.live.shape[1]
    rows = score.shape[0] // blocks
    return [(score[b * rows : (b + 1) * rows], R.bias[chip, a * blocks + b]) for b in range(blocks)]


def layer(at, w, R):
    L, S, PC = at.L, at.S, at.P
    T, D = R.tok.shape
    HD = D // HEADS
    HG = HEADS // PC
    GW = HG * HD
    CW = R.Wh.shape[1]
    HU = R.Wu.shape[1]
    DH, TH = D // 2, T // 2
    MR = R.wq.shape[0]
    HB = HU // L
    trunk = S // 2
    NK = PC // 2 + 1
    part = lambda i: slice(i * D, (i + 1) * D)
    head_rows = lambda h: slice(h * HD, (h + 1) * HD)
    go = Gather(w, at, R.wo, R.Go)
    cq, cu = Columns(w, at, R.Gh, 2), Columns(w, at, R.Gu, 1)
    ta, ga = PlaneGather(w, at, R.tX), PlaneGather(w, at, R.gX)
    rd = Rows(w, at, R.wd, R.Gd)

    def key_count(seg):
        return jnp.minimum(seg, trunk) + 1 + jnp.where(seg > trunk, 1, 0)

    at.greet()
    entry = {k: w.local(getattr(R, "in_" + k), getattr(R, k)) for k in ("wq", "modw", "tok", "pos", "wu", "g", "live")}
    for k in ("wq", "modw", "tok", "pos"):
        entry[k].wait()
    wq = R.wq[...].astype(F32)
    for q in range(PC):
        pieces = [wq[:, k * D + q * GW : k * D + (q + 1) * GW] for k in range(3)]
        R.wqs[q] = jnp.concatenate(pieces + [jnp.zeros((MR, CW - 3 * GW), F32)], axis=1).astype(BF16)
    R.tX[at.p] = R.tok[...]
    R.pos2[at.p] = R.pos[...].astype(F32)
    modw = R.modw[...].astype(F32)
    for t in range(L):
        column = condition_column(at, R.time[t], modw.shape[0], D)
        R.cond[t] = column
        R.mpart[t] = total_rows(column * modw)
    at.meet()
    cq.start(R.wqs)
    ta.first()
    mz = w.group(R.mz)
    for k in range(1, L):
        mz.send(R.mpart.at[at.leaf(k)], R.mz.at[k - 1], at.at_leaf(k))
    ps = w.group(R.pos2.at[0:3])
    for q in at.others:
        ps.send(R.pos2.at[at.p], R.pos2.at[at.p], at.at_chip(q))
    for k in ("wu", "g", "live"):
        entry[k].wait()
    R.gX[at.p] = R.g[...]
    wu = R.wu[...].astype(F32)
    for q in range(PC):
        R.wus[q] = jnp.concatenate([wu[:, k * HU + q * HB : k * HU + (q + 1) * HB] for k in range(L)], axis=1).astype(BF16)
    cu.start(R.wus)
    fill_bias(at, R)
    cq.begin()
    mz.wait_recv()
    total = R.mpart[at.l]
    for k in range(L - 1):
        total = total + R.mz[k]
    R.m1[...] = total
    ta.second()
    mp = w.group(R.mp)
    for i, peer in enumerate(at.tree):
        mp.send(R.m1, R.mp.at[i], peer)
    ta.relay()
    go.stage1(0)
    cq.early(1)
    cq.early(2)
    cq.late(1)
    cq.early(3)
    go.begin()
    cu.begin()
    mp.wait_recv()
    for i in range(S - 1):
        total = total + R.mp[i]
    R.mod[...] = total
    shift_a, scale_a, gate_a, shift_b, scale_b, gate_b = (R.mod[:, part(i)] for i in range(6))

    def modulate(k):
        normed, _ = norm_rows(R.tX[k].astype(F32))
        hidden = (normed * (1.0 + scale_a) + shift_a).astype(BF16)
        R.hA[k] = hidden

    modulate(at.p)
    ga.first()
    slow = jnp.exp(-math.log(10000.0) * 2.0 * lax.broadcasted_iota(jnp.int32, (HD // 2, 1), 0).astype(F32) / HD)
    ps.wait_recv()
    for k in range(PC):
        angles = slow * R.pos2[k]
        R.cos[k] = jnp.cos(angles)
        R.sin[k] = jnp.sin(angles)
    cq.late(2)
    ta.near()
    cq.late(3)
    modulate(at.px)
    modulate(at.py)
    ta.far()
    modulate(at.pd)
    go.line.early(1)
    go.line.early(2)
    cu.early(1)
    rd.begin()
    go.line.late(1)
    go.stage1(1)
    cq.pair.wait_recv()
    load = w.local(R.Gh.reshape(D, CW), R.Wh)
    load.wait()

    def project(q):
        cosine, sine = R.cos[q], R.sin[q]
        hidden = R.hA[q]
        for j in range(0, CW, 128):
            rows = dot(hidden, R.Wh[:, j : j + 128]).T
            for i in range(128 // HD):
                kind, h = divmod(j // HD + i, HG)
                if kind == 3:
                    continue
                first, second = rows[i * HD : i * HD + HD // 2], rows[i * HD + HD // 2 : (i + 1) * HD]
                if kind < 2:
                    first, second = first * cosine - second * sine, second * cosine + first * sine
                if kind == 0:
                    first, second = first * HD**-0.5, second * HD**-0.5
                low, high = pl.ds(h * HD, HD // 2), pl.ds(h * HD + HD // 2, HD // 2)
                if kind == 0:
                    R.QT[q, low, :] = first.astype(BF16)
                    R.QT[q, high, :] = second.astype(BF16)
                else:
                    R.KVT[2 * q + at.c, kind - 1, low, :] = first.astype(BF16)
                    R.KVT[2 * q + at.c, kind - 1, high, :] = second.astype(BF16)

    project(at.p)
    go.line.early(3)
    cu.early(2)
    project(at.px)
    project(at.py)
    go.line.late(2)
    go.stage1(2)
    cu.late(1)
    ga.relay()
    project(at.pd)
    sk = w.group(R.KVT.at[0:NK])
    for k in range(NK):
        sk.send(R.KVT.at[2 * k + at.c], R.KVT.at[2 * k + at.c], at.at_sib())
    cu.early(3)
    sk.wait_recv()

    def flip_k(a, carry):
        for h in range(HG):
            R.kN[a, h] = R.KVT[a, 0, head_rows(h), :].T
        return carry

    lax.fori_loop(0, S, flip_k, 0)
    go.line.late(3)
    go.stage1(3)
    ret = w.group(R.hsnd.at[0:3])
    for i, q in enumerate([at.pd, at.px, at.py, at.p]):
        seg = 2 * q + at.c

        def block(j, state, q=q, seg=seg):
            a = jnp.where(j > trunk, seg, j)
            out = []
            raw = [dot(R.kN[a, h], R.QT[q, head_rows(h), :]) for h in range(HG)]
            for h in range(HG):
                m, t, o = state[3 * h : 3 * h + 3]
                score = by_blocks(R, raw[h], q, a)
                m_new = m
                for one, bias in score:
                    m_new = jnp.maximum(m_new, jnp.max(one, axis=0, keepdims=True) + bias)
                alpha = jnp.exp(m - m_new)
                e = jnp.concatenate([jnp.exp(one - (m_new - bias)) for one, bias in score], axis=0)
                out.append((m_new, t * alpha + total_rows(e), o * alpha, e.astype(BF16)))
            out = [(m, t, o + dot(R.KVT[a, 1, head_rows(h), :], e)) for h, (m, t, o, e) in enumerate(out)]
            return tuple(x for one in out for x in one)

        start = (jnp.full((1, T), NEGATIVE, F32), jnp.zeros((1, T), F32), jnp.zeros((HD, T), F32)) * HG
        state = lax.fori_loop(0, key_count(seg), block, start)
        for h in range(HG):
            m, t, o = state[3 * h : 3 * h + 3]
            o = o / t
            R.OT[q, head_rows(h), :] = o
            R.hsnd[q, head_rows(h), :] = o.astype(BF16)
            R.lse[q, h : h + 1, :] = m + jnp.log(t)
        if i < 3:
            ret.send(R.hsnd.at[q], R.attT2.at[0, at.p], at.at_chip(q))
        else:
            own_att = w.local(R.hsnd.at[q], R.attT2.at[0, at.p])
        if i == 0:
            rd.line.early(1)
            rd.line.early(2)
            cu.late(2)
            for u in range(L):
                go.stage2(u)
        if i == 1:
            cu.late(3)
            rd.late(1)
        if i == 2:
            ga.second()
            rd.line.early(3)
            for u in range(L):
                go.stage3(u)
    go.finish()
    load = w.local(R.Go.reshape(D, D), R.Wo)
    own_att.wait()
    ret.wait_recv()
    sib_att = w.send(R.attT2.at[0], R.attT2.at[1], at.at_sib())
    load.wait()
    att = jnp.concatenate([R.attT2[0, k].T for k in range(PC)], axis=1)
    for j in range(0, D, 256):
        lanes = slice(j, j + 256)
        branch = dot(att, R.Wo[:, lanes])
        R.br_a[:, lanes] = branch
        R.middle[:, lanes] = R.tok[:, lanes].astype(F32) + gate_a[:, lanes] * branch
    normed, _ = norm_rows(R.middle[...])
    R.hB[at.p] = (normed * (1.0 + scale_b) + shift_b).astype(BF16)
    hb = PlaneGather(w, at, R.hB)
    hb.start()
    rd.late(2)
    rd.late(3)
    cu.pair.wait_recv()
    loads = [w.local(R.Gu.reshape(D, HU), R.Wu)]
    rd.own.wait()
    rd.pair.wait_recv()
    loads.append(w.local(R.Gd.reshape(HU, D), R.Wd))
    for load in loads:
        load.wait()

    def feed(k):
        hidden = R.hB[k]
        dbb = (gate_b * R.gX[k].astype(F32)).astype(BF16)
        R.dbb[k] = dbb
        lanes = [slice(j, j + 256) for j in range(0, HU, 256)]
        uppers = [dot(hidden, R.Wu[:, some]) for some in lanes]
        grads = [dot_t(dbb, R.Wd[some, :]) for some in lanes]
        for some, u, grad in zip(lanes, uppers, grads):
            square = u * u
            tanh = jnp.tanh(GELU_A * (u + GELU_B * square * u))
            act = (0.5 * u * (1.0 + tanh)).astype(BF16)
            R.active[k, :, some] = act
            slope = 0.5 * (1.0 + tanh) + (0.5 * GELU_A) * u * (1.0 - tanh * tanh) * (1.0 + 3.0 * GELU_B * square)
            R.du[k, :, some] = (grad * slope).astype(BF16)

    def feed_back(k):
        for i in range(2):
            R.dB[i, k] = dot_t(R.du[k, i * TH : (i + 1) * TH, :], R.Wu[...]).astype(BF16)

    sb = PlaneSum(w, at, R.dB, R.dBd, R.dBx)
    feed(at.p)
    for k in range(PC):
        R.haT[k] = R.hA[k].T
    hb.relay()
    hb.near()
    ga.near()
    feed(at.px)
    feed_back(at.px)
    sb.near(0)
    feed(at.py)
    feed_back(at.py)
    sb.near(1)
    hb.far()
    ga.far()
    feed(at.pd)
    feed_back(at.pd)
    sb.far()
    feed_back(at.p)
    scat = {"o": Scatter(w, at, *(getattr(R, x + "o") for x in ("A", "sw", "dg", "xy", "zr", "fin", "sr", "v")))}

    RD = HU // L
    ld, lu, lq = (LineSum(w, at, *(getattr(R, x + n) for x in ("A", "As", "zr"))) for n in ("d", "u", "q"))

    def down_grad(i, carry):
        total = dot(R.actT[0, tile(i, RD), :], R.dbb[0])
        for k in range(1, PC):
            total = total + dot(R.actT[k, tile(i, RD), :], R.dbb[k])
        for core in range(2):
            R.Ad[core, i] = total[core * (RD // 2) : (core + 1) * (RD // 2)].astype(BF16)
        return carry

    for k in range(PC):
        R.actT[k] = R.active[k].T
    lax.fori_loop(0, L, down_grad, 0)
    ld.pair()
    def flip_v(a, carry):
        for h in range(HG):
            R.vN[a, h] = R.KVT[a, 1, head_rows(h), :].T
        R.acc[a] = jnp.zeros((2, GW, T), F32)
        return carry

    lax.fori_loop(0, S, flip_v, 0)
    for k in range(PC):
        R.dpT[k, 3 * GW : CW, :] = jnp.zeros((CW - 3 * GW, T), BF16)
    sb.relay()

    def by_core(A, i, total):
        for core in range(2):
            rows = [total[(2 * k + core) * MR : (2 * k + core + 1) * MR] for k in range(PC)]
            A[core, i] = jnp.concatenate(rows, axis=0).astype(BF16)

    def up_grad(i, carry):
        total = dot(R.hBT[0, tile(i, D // L), :], R.du[0])
        for k in range(1, PC):
            total = total + dot(R.hBT[k, tile(i, D // L), :], R.du[k])
        by_core(R.Au, i, total)
        return carry

    for k in range(PC):
        R.hBT[k] = R.hB[k].T
    lax.fori_loop(0, L, up_grad, 0)
    lu.pair()
    ld.line()
    sc = PlaneSum(w, at, R.bB, R.bBd, R.bBx)
    for k in (at.pd, at.px, at.py, at.p):
        for i in range(2):
            R.bB[i, k] = dot(R.active[k, i * TH : (i + 1) * TH, :], R.Wd[...]).astype(BF16)
    lu.line()
    dh = jnp.concatenate(sb.total(), axis=0)
    normed, rstd = norm_rows(R.middle[...])
    R.gm[:, part(3)] = total_rows(dh)
    R.gm[:, part(4)] = total_rows(dh * normed)
    dmid = R.g[...].astype(F32) + norm_back(dh * (1.0 + scale_b), normed, rstd)
    R.dmid[...] = dmid
    R.gm[:, part(2)] = total_rows(dmid * R.br_a[...])
    dba = (gate_a * dmid).astype(BF16)
    R.dba[...] = dba
    for h in range(2):
        R.dbah[h] = dba[:, h * DH : (h + 1) * DH]
    sib_dba = w.send(R.dbah.at[1 - at.c], R.dbas, at.at_sib())
    w.sent([ret])
    for j in range(PC):
        R.hsnd[j] = dot_t(R.Wo[j * GW : (j + 1) * GW, :], R.dba[...]).astype(BF16)
    dos = [w.send(R.hsnd.at[q], R.dOT.at[at.p], at.at_chip(q)) for q in at.others]
    own_do = w.local(R.hsnd.at[at.p], R.dOT.at[at.p])
    sc.far()
    sc.near(0)
    sc.near(1)
    own_do.wait()

    def unturn(first, second, q):
        cosine, sine = R.cos[q], R.sin[q]
        return jnp.concatenate([first * cosine + second * sine, second * cosine - first * sine], axis=0)

    for i, q in enumerate([at.p, at.px, at.py, at.pd]):
        seg = 2 * q + at.c
        if i:
            dos[i - 1].wait_recv()
        delta = [total_rows(R.dOT[q, head_rows(h), :].astype(F32) * R.OT[q, head_rows(h), :]) for h in range(HG)]

        def block(j, dqs, q=q, seg=seg, delta=delta):
            a = jnp.where(j > trunk, seg, j)
            out = []
            raw = [dot(R.kN[a, h], R.QT[q, head_rows(h), :]) for h in range(HG)]
            draw = [dot(R.vN[a, h], R.dOT[q, head_rows(h), :]) for h in range(HG)]
            pairs = []
            for h in range(HG):
                lse = R.lse[q, h : h + 1, :]
                prob = jnp.concatenate([jnp.exp(one - (lse - bias)) for one, bias in by_blocks(R, raw[h], q, a)], axis=0)
                pairs.append((prob.astype(BF16), (prob * (draw[h] - delta[h])).astype(BF16)))
            for h, (prob, ds) in enumerate(pairs):
                rows = head_rows(h)
                out.append(dqs[h] + dot(R.KVT[a, 0, rows, :], ds))
                R.acc[a, 0, rows, :] += dot_t(R.QT[q, rows, :], ds)
                R.acc[a, 1, rows, :] += dot_t(R.dOT[q, rows, :], prob)
            return tuple(out)

        dqs = lax.fori_loop(0, key_count(seg), block, (jnp.zeros((HD, T), F32),) * HG)
        for h in range(HG):
            dq = dqs[h] * HD**-0.5
            R.dpT[q, head_rows(h), :] = unturn(dq[: HD // 2], dq[HD // 2 :], q).astype(BF16)
        if i == 0:
            RB2 = D // (L * PC)
            sib_dba.wait_recv()
            sib_att.wait_recv()
            attT = [R.attT2[i].reshape(D, T) for i in range(2)]
            block = dot(attT[0], R.dbah[at.c]) + dot(attT[1], R.dbas[...])
            for i in range(L * PC):
                R.Ao[i // PC, i % PC] = block[i * RB2 : (i + 1) * RB2].astype(BF16)
            scat["o"].step0()
            scat["o"].step1((1, 3, 0, 2))
        if i == 2:
            sc.relay()
    sk = w.group(R.acs)
    for k in range(NK):
        sk.send(R.acc.at[2 * k + 1 - at.c], R.acs.at[k], at.at_sib())
    sk.wait_recv()
    for k in range(PC):
        for i in range(2):
            grad = R.acc[2 * k + at.c, i]
            if k < NK:
                grad = grad + R.acs[k, i]
            for h in range(HG):
                one = grad[head_rows(h)]
                if i == 0:
                    one = unturn(one[: HD // 2], one[HD // 2 :], k)
                R.dpT[k, (i + 1) * GW + h * HD : (i + 1) * GW + (h + 1) * HD, :] = one.astype(BF16)
    scat["o"].step1d()
    sa = PlaneSum(w, at, R.dA, R.dAd, R.dAx)
    for n, q in enumerate((at.pd, at.px, at.py, at.p)):
        for i in range(2):
            R.dA[i, q] = dot(R.Wh[i * DH : (i + 1) * DH, :], R.dpT[q]).astype(BF16)
        if n == 0:
            sa.far()
        elif n < 3:
            sa.near(n - 1)
    scat["o"].step2()
    def proj_grad(i, carry):
        total = dot_t(R.haT[0, tile(i, D // L), :], R.dpT[0])
        for k in range(1, PC):
            total = total + dot_t(R.haT[k, tile(i, D // L), :], R.dpT[k])
        by_core(R.Aq, i, total)
        return carry

    lax.fori_loop(0, L, proj_grad, 0)
    lq.pair()
    lq.line()
    sa.relay()
    branch = sc.total()
    for i in range(2):
        rows = slice(i * TH, (i + 1) * TH)
        R.vlo[rows, :] = (R.middle[rows, :] + gate_b * branch[i]).astype(BF16)
    R.gm[:, part(5)] = total_rows(R.g[...].astype(F32) * jnp.concatenate(branch, axis=0))
    results = [w.local(R.vlo, R.lo)]
    R.vd[...] = ld.total()
    results.append(w.local(R.vd, R.od))

    def to_chips(fin, buf):
        group = w.group(buf.at[0:3])
        mine = lambda q: fin.at[pl.ds(pl.multiple_of(q * MR, 8), MR)]
        for q in at.others:
            group.send(mine(q), buf.at[at.p], at.at_chip(q))
        return group, w.local(mine(at.p), buf.at[at.p])

    R.finu[...] = lu.total()
    ru = to_chips(R.finu, R.ru)
    scat["o"].step3()
    dh = jnp.concatenate([half.T for half in sa.total()], axis=1)
    normed, rstd = norm_rows(R.tok[...].astype(F32))
    R.gm[:, part(0)] = total_rows(dh)
    R.gm[:, part(1)] = total_rows(dh * normed)
    gp = w.group(R.gp)
    for i, peer in enumerate(at.tree):
        gp.send(R.gm, R.gp.at[i], peer)
    R.vgt[...] = R.dmid[...] + norm_back(dh * (1.0 + scale_a), normed, rstd)
    results.append(w.local(R.vgt, R.gt))
    R.finq[...] = lq.total()
    rq = to_chips(R.finq, R.rq)
    gp.wait_recv()
    total = R.gm[...]
    for i in range(S - 1):
        total = total + R.gp[i]
    R.gtree[at.l] = total
    gz = w.group(R.gtree.at[0:3])
    for k in range(1, L):
        gz.send(R.gtree.at[at.l], R.gtree.at[at.l], at.at_leaf(k))
    for copy in ru:
        (copy.wait_recv if copy is ru[0] else copy.wait)()
    R.vu[...] = jnp.concatenate([R.ru[q][:, k * HB : (k + 1) * HB] for k in range(L) for q in range(PC)], axis=1)
    results.append(w.local(R.vu, R.ou))
    scat["o"].step4()
    scat["o"].step5()
    results.append(w.local(R.vo, R.oo))
    rq[1].wait()
    rq[0].wait_recv()
    R.vq[...] = jnp.concatenate([R.rq[q][:, k * GW : (k + 1) * GW] for k in range(3) for q in range(PC)], axis=1)
    results.append(w.local(R.vq, R.oq))
    gz.wait_recv()
    total = R.cond[0] * R.gtree[0]
    for t in range(1, L):
        total = total + R.cond[t] * R.gtree[t]
    R.vm[...] = total
    results.append(w.local(R.vm, R.om))
    for copy in results:
        copy.wait()


class Refs:
    def __init__(self, **refs):
        self.__dict__.update(refs)


def call_layer(L, S, tok, g, time, parent, pos, live, wq, wo, wu, wd, modw):
    T, D = tok.shape
    FF = wu.shape[1]
    PC, HD = S // 2, D // HEADS
    HG = HEADS // PC
    GW = HG * HD
    CW = -(-3 * GW // 128) * 128
    NM, MR = L * S, wq.shape[0]
    sd = jax.ShapeDtypeStruct
    DM, V = pltpu.SemaphoreType.DMA, pltpu.VMEM
    entry = dict(wq=wq, modw=modw, tok=tok, pos=pos, wu=wu, g=g, live=live)
    ins = dict(time=time, parent=parent, wo=wo, wd=wd)
    ins.update({"in_" + k: v for k, v in entry.items()})
    HU = FF // PC
    outs = dict(Go=sd((L, PC, 2 * MR, D), BF16), Gh=sd((L, PC, 2 * MR, CW), BF16), Gu=sd((L, PC, 2 * MR, HU), BF16),
                Gd=sd((L, 2 * wd.shape[0], D), BF16))
    last = dict(lo=((T, D), BF16), gt=((T, D), F32), oq=((MR, 3 * D), F32), oo=((MR, D), F32),
                ou=((MR, FF), F32), od=((FF // NM, D), F32), om=((MR, 6 * D), F32))
    outs.update({k: sd(*v) for k, v in last.items()})
    M6 = 6 * D
    scr = dict(
        Wh=V((D, CW), BF16), Wo=V((D, D), BF16), Wu=V((D, HU), BF16), Wd=V((HU, D), BF16), wqs=V((PC, MR, CW), BF16), wus=V((PC, MR, HU), BF16),
        bias=pltpu.SMEM((PC, live.size), F32), cond=V((L, MR, 1), F32),
        pos2=V((PC, 1, T), F32), cos=V((PC, HD // 2, T), F32), sin=V((PC, HD // 2, T), F32),
        mpart=V((L, 1, M6), F32), mz=V((L - 1, 1, M6), F32), m1=V((1, M6), F32), mp=V((S - 1, 1, M6), F32),
        mod=V((1, M6), F32),
        tX=V((PC, T, D), BF16), gX=V((PC, T, D), BF16), hA=V((PC, T, D), BF16), haT=V((PC, D, T), BF16), QT=V((PC, GW, T), BF16),
        KVT=V((S, 2, GW, T), BF16), kN=V((S, HG, T, HD), BF16), OT=V((PC, GW, T), F32), lse=V((PC, 8, T), F32),
        hsnd=V((PC, GW, T), BF16), attT2=V((2, PC, GW, T), BF16), br_a=V((T, D), F32), middle=V((T, D), F32),
        hB=V((PC, T, D), BF16), hBT=V((PC, D, T), BF16), active=V((PC, T, HU), BF16), actT=V((PC, HU, T), BF16),
        dbb=V((PC, T, D), BF16), du=V((PC, T, HU), BF16), dh=V((T, D), F32), dmid=V((T, D), F32),
        dB=V((2, PC, T // 2, D), BF16), dBd=V((2, T // 2, D), BF16), dBx=V((2, 2, T // 2, D), BF16),
        bB=V((2, PC, T // 2, D), BF16), bBd=V((2, T // 2, D), BF16), bBx=V((2, 2, T // 2, D), BF16),
        Au=V((2, L, PC * MR, HU), BF16), Asu=V((L, PC * MR, HU), BF16), zru=V((L - 1, PC * MR, HU), BF16),
        finu=V((PC * MR, HU), F32), ru=V((PC, MR, HU), F32),
        Ad=V((2, L, HU // L // 2, D), BF16), Asd=V((L, HU // L // 2, D), BF16), zrd=V((L - 1, HU // L // 2, D), BF16),
        dba=V((T, D), BF16), dbah=V((2, T, D // 2), BF16), dbas=V((T, D // 2), BF16),
        dOT=V((PC, GW, T), BF16), vN=V((S, HG, T, HD), BF16),
        acc=V((S, 2, GW, T), F32), acs=V((PC // 2 + 1, 2, GW, T), F32), dpT=V((PC, CW, T), BF16),
        dA=V((2, PC, D // 2, T), BF16), dAd=V((2, D // 2, T), BF16), dAx=V((2, 2, D // 2, T), BF16),
        Aq=V((2, L, PC * MR, CW), BF16), Asq=V((L, PC * MR, CW), BF16), zrq=V((L - 1, PC * MR, CW), BF16),
        finq=V((PC * MR, CW), F32), rq=V((PC, MR, CW), F32),
        gm=V((1, M6), F32), gp=V((S - 1, 1, M6), F32), gtree=V((L, 1, M6), F32))
    for n, rows, cols in (("o", D, D),):
        rb, half = rows // (L * PC), cols // 2
        scr["A" + n] = V((L, PC, rb, half), BF16)
        scr["sw" + n] = V((2, rb, half), BF16)
        scr["dg" + n] = V((2, rb, half), BF16)
        scr["xy" + n] = V((2, L, rb, half), BF16)
        scr["zr" + n] = V((L - 1, rb, half), BF16)
        scr["fin" + n] = V((rb, half), F32)
        scr["sr" + n] = V((rb // 2, half), F32)
    scr.update({k: V(v.shape, v.dtype) for k, v in entry.items()})
    for k, v in last.items():
        scr["v" + k.removeprefix("o") if k != "lo" else "vlo"] = V(*v)
    scr.update(send_sems=DM((72,)), recv_sems=DM((87,)), local_sems=DM((26,)))
    space = dict.fromkeys((*ins, *outs), pltpu.HBM)
    space.update(dict.fromkeys(("time", "parent"), pltpu.SMEM))
    spec = lambda k: pl.BlockSpec(memory_space=space.get(k, pltpu.VMEM))

    def kernel(*refs):
        R = Refs(**dict(zip(list(ins) + list(outs) + list(scr), refs)))
        at = Place(L, S)
        w = Wires(at, R.send_sems, R.recv_sems, R.local_sems)
        layer(at, w, R)
        w.drain()

    res = pl.pallas_call(
        kernel, out_shape=list(outs.values()), in_specs=[spec(k) for k in ins], out_specs=[spec(k) for k in outs],
        scratch_shapes=list(scr.values()),
        compiler_params=pltpu.CompilerParams(collective_id=1, has_side_effects=True, vmem_limit_bytes=64 << 20),
    )(*ins.values())
    return dict(zip(outs, res))


def hand_out(*arrays):
    count = len(arrays)

    def kernel(*refs):
        sources, targets, held, sems = refs[:count], refs[count : 2 * count], refs[2 * count : 3 * count], refs[-1]
        arrive = [pltpu.make_async_copy(x, y, sems.at[0, i]) for i, (x, y) in enumerate(zip(sources, held))]
        leave = [pltpu.make_async_copy(x, y, sems.at[1, i]) for i, (x, y) in enumerate(zip(held, targets))]
        for copy in arrive:
            copy.start()
        for first, second in zip(arrive, leave):
            first.wait()
            second.start()
        for copy in leave:
            copy.wait()

    hbm = pl.BlockSpec(memory_space=pltpu.HBM)
    return pl.pallas_call(
        kernel, out_shape=[jax.ShapeDtypeStruct(a.shape, a.dtype) for a in arrays],
        in_specs=[hbm] * count, out_specs=[hbm] * count,
        scratch_shapes=[pltpu.VMEM(a.shape, a.dtype) for a in arrays] + [pltpu.SemaphoreType.DMA((2, count))],
    )(*arrays)


def layer_kernels(
    tokens, cotangent, timesteps, parent, positions, block_live, qkv_weight, out_weight, up_weight, down_weight, mod_weight
):
    f = call_layer(
        lax.axis_size("leaf"), lax.axis_size("seq"), tokens[0], cotangent[0], timesteps, parent, positions, jnp.swapaxes(block_live, 1, 2),
        qkv_weight, out_weight, up_weight, down_weight, mod_weight,
    )
    lo, gt, *rest = hand_out(*(f[k] for k in ("lo", "gt", "oq", "oo", "ou", "od", "om")))
    return (lo[None], gt[None], *rest)


def layer_norm(values):
    centred = values - jnp.mean(values, axis=-1, keepdims=True)
    variance = jnp.mean(centred * centred, axis=-1, keepdims=True)
    return centred * lax.rsqrt(variance + EPSILON)


def time_embed(step_values, model_width):
    half_width = model_width // 2
    freqs = jnp.exp(-math.log(10000.0) * jnp.arange(half_width, dtype=jnp.float32) / half_width)
    angles = step_values.astype(jnp.float32)[..., None] * freqs
    return jnp.concatenate([jnp.cos(angles), jnp.sin(angles)], axis=-1)


def rope_tables(places, head_dim):
    half_dim = head_dim // 2
    inverse = jnp.exp(-math.log(10000.0) * 2.0 * jnp.arange(half_dim, dtype=jnp.float32) / head_dim)
    angles = places.astype(jnp.float32)[:, None] * inverse[None, :]
    return (jnp.cos(angles), jnp.sin(angles))


def rotate(values, cosine, sine):
    half_dim = values.shape[-1] // 2
    first = values[..., :half_dim]
    second = values[..., half_dim:]
    cos_wide = cosine[:, None, :]
    sin_wide = sine[:, None, :]
    return jnp.concatenate(
        [first * cos_wide - second * sin_wide, second * cos_wide + first * sin_wide], axis=-1
    )


def rotate_back(grads, cosine, sine):
    half_dim = grads.shape[-1] // 2
    first = grads[..., :half_dim]
    second = grads[..., half_dim:]
    cos_wide = cosine[:, None, :]
    sin_wide = sine[:, None, :]
    return jnp.concatenate(
        [first * cos_wide + second * sin_wide, second * cos_wide - first * sin_wide], axis=-1
    )


def ancestor_row(parent_row, seg_index, seg_count):
    seg_range = jnp.arange(seg_count, dtype=jnp.int32)

    def climb(step_index, state_now):
        current, reached = state_now
        current = parent_row[current]
        return (current, reached | (seg_range == current))

    return lax.fori_loop(0, seg_count, climb, (seg_index, seg_range == seg_index))[1]


def attend_keys(state_now, query_rot, key_block, value_block, key_ok, score_scale):
    maximum_old, total_old, accum_old = state_now
    scores = (
        jnp.einsum("qhd,khd->hqk", query_rot, key_block, preferred_element_type=jnp.float32)
        * score_scale
    )
    visible = key_ok[None, None, :]
    scores = jnp.where(visible, scores, NEGATIVE)
    maximum_new = jnp.maximum(maximum_old, jnp.max(scores, axis=-1))
    weights_p = jnp.where(visible, jnp.exp(scores - maximum_new[..., None]), 0.0)
    rescale = jnp.exp(maximum_old - maximum_new)
    total_new = total_old * rescale + jnp.sum(weights_p, axis=-1)
    accum_new = accum_old * rescale[..., None] + jnp.einsum(
        "hqk,khd->hqd",
        weights_p.astype(jnp.bfloat16),
        value_block,
        preferred_element_type=jnp.float32,
    )
    return (maximum_new, total_new, accum_new)


def score_grads(
    query_rot, grad_attended, log_total, delta_rows, key_block, value_block, mask_wide, score_scale
):
    scores = (
        jnp.einsum("qhd,khd->hqk", query_rot, key_block, preferred_element_type=jnp.float32)
        * score_scale
    )
    probs = jnp.where(mask_wide, jnp.exp(scores - log_total[..., None]), 0.0)
    grad_probs = jnp.einsum(
        "qhd,khd->hqk", grad_attended, value_block, preferred_element_type=jnp.float32
    )
    grad_scores = (probs * (grad_probs - delta_rows[..., None])).astype(jnp.bfloat16)
    return (probs, grad_scores)


def query_only(
    grad_query,
    query_rot,
    grad_attended,
    log_total,
    delta_rows,
    key_block,
    value_block,
    key_ok,
    score_scale,
):
    probs, grad_scores = score_grads(
        query_rot,
        grad_attended,
        log_total,
        delta_rows,
        key_block,
        value_block,
        key_ok[None, None, :],
        score_scale,
    )
    return (
        grad_query
        + jnp.einsum("hqk,khd->qhd", grad_scores, key_block, preferred_element_type=jnp.float32)
        * score_scale
    )


def layer_native(
    tokens,
    cotangent,
    timesteps,
    parent,
    positions,
    block_live,
    qkv_weight,
    out_weight,
    up_weight,
    down_weight,
    mod_weight,
):
    seg_count = lax.axis_size("seq")
    seg_index = lax.axis_index("seq")
    tree_index = lax.axis_index("leaf")
    tok_rows = tokens.shape[1]
    model_width = tokens.shape[2]
    head_count = HEADS
    head_dim = model_width // head_count
    score_scale = head_dim ** (-0.5)
    tree_rows = tok_rows * seg_count
    qkv_all, out_all, up_all, down_all = (
        lax.all_gather(qkv_weight, ("leaf", "seq"), axis=0, tiled=True),
        lax.all_gather(out_weight, ("leaf", "seq"), axis=0, tiled=True),
        lax.all_gather(up_weight, ("leaf", "seq"), axis=0, tiled=True),
        lax.all_gather(down_weight, ("leaf", "seq"), axis=0, tiled=True),
    )
    condition = jax.nn.silu(time_embed(timesteps, model_width)).astype(jnp.bfloat16)
    mod_all = lax.all_gather(mod_weight, ("leaf", "seq"), axis=0, tiled=True)
    cond_own = lax.dynamic_index_in_dim(condition, tree_index, 0, keepdims=False)
    modulation = jnp.dot(cond_own[None, :], mod_all, preferred_element_type=jnp.float32)[0]
    shift_a, scale_a, gate_a, shift_b, scale_b, gate_b = jnp.split(modulation, 6)
    inputs_f = tokens[0].astype(jnp.float32)
    normed_a = layer_norm(inputs_f)
    hidden_a = (normed_a * (1.0 + scale_a) + shift_a).astype(jnp.bfloat16)
    projected = jnp.dot(hidden_a, qkv_all, preferred_element_type=jnp.float32).reshape(
        tok_rows, 3, head_count, head_dim
    )
    cosine, sine = rope_tables(positions[0], head_dim)
    query_rot = rotate(projected[:, 0], cosine, sine).astype(jnp.bfloat16)
    key_rot = rotate(projected[:, 1], cosine, sine).astype(jnp.bfloat16)
    value_rows = projected[:, 2].astype(jnp.bfloat16)
    key_flat = key_rot.reshape(tok_rows, model_width)
    value_flat = value_rows.reshape(tok_rows, model_width)
    reached = ancestor_row(parent[0], seg_index, seg_count)
    live_blocks = block_live.shape[2]
    live_tokens = jnp.repeat(block_live[0] > 0, tok_rows // live_blocks, axis=1)
    key_allowed = (reached[:, None] & live_tokens).reshape(tree_rows)
    start_state = (
        jnp.full((head_count, tok_rows), NEGATIVE, jnp.float32),
        jnp.zeros((head_count, tok_rows), jnp.float32),
        jnp.zeros((head_count, tok_rows, head_dim), jnp.float32),
    )
    key_part = lax.all_gather(key_flat, "seq", axis=0, tiled=True)
    value_part = lax.all_gather(value_flat, "seq", axis=0, tiled=True)
    count_keys = key_part.shape[0]
    block_size = tok_rows
    block_count = count_keys // block_size
    allow_part = key_allowed.reshape(block_count, block_size)
    key_blocks = key_part.reshape(block_count, block_size, head_count, head_dim)
    value_blocks = value_part.reshape(block_count, block_size, head_count, head_dim)

    def advance(state_now, block_in):
        return (
            attend_keys(state_now, query_rot, block_in[0], block_in[1], block_in[2], score_scale),
            None,
        )

    maximum_run, total_run, accum_run = lax.scan(
        advance, start_state, (key_blocks, value_blocks, allow_part)
    )[0]
    attended_heads = jnp.transpose(accum_run / total_run[..., None], (1, 0, 2))
    log_total = maximum_run + jnp.log(total_run)
    attended = attended_heads.reshape(tok_rows, model_width).astype(jnp.bfloat16)
    branch_a = jnp.dot(attended, out_all, preferred_element_type=jnp.float32)
    middle = inputs_f + gate_a * branch_a
    normed_b = layer_norm(middle)
    hidden_b = (normed_b * (1.0 + scale_b) + shift_b).astype(jnp.bfloat16)
    upper = jnp.dot(hidden_b, up_all, preferred_element_type=jnp.float32)
    active = jax.nn.gelu(upper).astype(jnp.bfloat16)
    branch_b = jnp.dot(active, down_all, preferred_element_type=jnp.float32)
    layer_out = (middle + gate_b * branch_b).astype(jnp.bfloat16)
    qkv_back, out_back, up_back, down_back = (
        lax.all_gather(qkv_weight, ("leaf", "seq"), axis=0, tiled=True),
        lax.all_gather(out_weight, ("leaf", "seq"), axis=0, tiled=True),
        lax.all_gather(up_weight, ("leaf", "seq"), axis=0, tiled=True),
        lax.all_gather(down_weight, ("leaf", "seq"), axis=0, tiled=True),
    )
    grad_out_rows = cotangent[0].astype(jnp.float32)
    grad_branch_b = (gate_b * grad_out_rows).astype(jnp.bfloat16)
    dgate_b = jnp.sum(grad_out_rows * branch_b, axis=0)
    grad_down = jnp.einsum("qf,qd->fd", active, grad_branch_b, preferred_element_type=jnp.float32)
    grad_active = jnp.einsum(
        "qd,fd->qf", grad_branch_b, down_back, preferred_element_type=jnp.float32
    )
    gelu_pull = jax.vjp(jax.nn.gelu, upper)[1]
    grad_upper = gelu_pull(grad_active)[0].astype(jnp.bfloat16)
    grad_up = jnp.einsum("qd,qf->df", hidden_b, grad_upper, preferred_element_type=jnp.float32)
    grad_hidden_b = jnp.einsum("qf,df->qd", grad_upper, up_back, preferred_element_type=jnp.float32)
    dshift_b = jnp.sum(grad_hidden_b, axis=0)
    dscale_b = jnp.sum(grad_hidden_b * normed_b, axis=0)
    norm_pull_b = jax.vjp(layer_norm, middle)[1]
    grad_middle = grad_out_rows + norm_pull_b(grad_hidden_b * (1.0 + scale_b))[0]
    grad_branch_a = (gate_a * grad_middle).astype(jnp.bfloat16)
    dgate_a = jnp.sum(grad_middle * branch_a, axis=0)
    grad_out = jnp.einsum("qi,qd->id", attended, grad_branch_a, preferred_element_type=jnp.float32)
    grad_attended = jnp.einsum(
        "qd,id->qi", grad_branch_a, out_back, preferred_element_type=jnp.float32
    ).astype(jnp.bfloat16)
    grad_att_heads = grad_attended.reshape(tok_rows, head_count, head_dim)
    delta_rows = jnp.einsum("qhd,qhd->hq", grad_att_heads.astype(jnp.float32), attended_heads)
    start_query = jnp.zeros((tok_rows, head_count, head_dim), jnp.float32)
    key_part = lax.all_gather(key_flat, "seq", axis=0, tiled=True)
    value_part = lax.all_gather(value_flat, "seq", axis=0, tiled=True)
    count_keys = key_part.shape[0]
    block_size = tok_rows
    block_count = count_keys // block_size
    allow_part = key_allowed.reshape(block_count, block_size)
    key_blocks = key_part.reshape(block_count, block_size, head_count, head_dim)
    value_blocks = value_part.reshape(block_count, block_size, head_count, head_dim)

    def advance(grad_now, block_in):
        return (
            query_only(
                grad_now,
                query_rot,
                grad_att_heads,
                log_total,
                delta_rows,
                block_in[0],
                block_in[1],
                block_in[2],
                score_scale,
            ),
            None,
        )

    grad_query = lax.scan(advance, start_query, (key_blocks, value_blocks, allow_part))[0]
    seg_range = jnp.arange(seg_count, dtype=jnp.int32)
    every_reach = jax.vmap(lambda one_seg: ancestor_row(parent[0], one_seg, seg_count))(seg_range)
    sees_mine = every_reach[:, seg_index]
    own_live = lax.dynamic_index_in_dim(live_tokens, seg_index, 0, keepdims=False)
    total_all, delta_all = (
        lax.all_gather(jnp.transpose(log_total), "seq", axis=0, tiled=True),
        lax.all_gather(jnp.transpose(delta_rows), "seq", axis=0, tiled=True),
    )
    query_flat = query_rot.reshape(tok_rows, model_width)
    grad_key_acc = jnp.zeros((tok_rows, head_count, head_dim), jnp.float32)
    grad_value_acc = jnp.zeros((tok_rows, head_count, head_dim), jnp.float32)
    query_part = lax.all_gather(query_flat, "seq", axis=0, tiled=True)
    grad_part = lax.all_gather(grad_attended, "seq", axis=0, tiled=True)
    count_rows = query_part.shape[0]
    block_size = tok_rows
    block_count = count_rows // block_size
    row_seg = jnp.arange(count_rows, dtype=jnp.int32) // tok_rows
    row_ok = sees_mine[row_seg].reshape(block_count, block_size)
    total_part = total_all.reshape(block_count, block_size, head_count)
    delta_part = delta_all.reshape(block_count, block_size, head_count)
    query_blocks = query_part.reshape(block_count, block_size, head_count, head_dim)
    grad_blocks = grad_part.reshape(block_count, block_size, head_count, head_dim)

    def advance(acc_now, block_in):
        key_acc, value_acc = acc_now
        query_block, grad_block, total_block, delta_block, ok_block = block_in
        mask_wide = ok_block[None, :, None] & own_live[None, None, :]
        probs, grad_scores = score_grads(
            query_block,
            grad_block,
            jnp.transpose(total_block),
            jnp.transpose(delta_block),
            key_rot,
            value_rows,
            mask_wide,
            score_scale,
        )
        key_acc = (
            key_acc
            + jnp.einsum(
                "hqk,qhd->khd", grad_scores, query_block, preferred_element_type=jnp.float32
            )
            * score_scale
        )
        value_acc = value_acc + jnp.einsum(
            "hqk,qhd->khd",
            probs.astype(jnp.bfloat16),
            grad_block,
            preferred_element_type=jnp.float32,
        )
        return ((key_acc, value_acc), None)

    grad_key_rows, grad_value_heads = lax.scan(
        advance,
        (grad_key_acc, grad_value_acc),
        (query_blocks, grad_blocks, total_part, delta_part, row_ok),
    )[0]
    grad_value_rows = grad_value_heads.reshape(tok_rows, model_width)
    grad_query_pre = rotate_back(grad_query, cosine, sine).reshape(tok_rows, model_width)
    grad_key_pre = rotate_back(grad_key_rows, cosine, sine).reshape(tok_rows, model_width)
    grad_projected = jnp.concatenate(
        [grad_query_pre, grad_key_pre, grad_value_rows], axis=-1
    ).astype(jnp.bfloat16)
    grad_qkv = jnp.einsum("qi,qj->ij", hidden_a, grad_projected, preferred_element_type=jnp.float32)
    grad_hidden_a = jnp.einsum(
        "qj,ij->qi", grad_projected, qkv_back, preferred_element_type=jnp.float32
    )
    dshift_a = jnp.sum(grad_hidden_a, axis=0)
    dscale_a = jnp.sum(grad_hidden_a * normed_a, axis=0)
    norm_pull_a = jax.vjp(layer_norm, inputs_f)[1]
    grad_tokens = grad_middle + norm_pull_a(grad_hidden_a * (1.0 + scale_a))[0]
    grad_modulation = jnp.concatenate([dshift_a, dscale_a, dgate_a, dshift_b, dscale_b, dgate_b])
    sum_qkv, sum_out, sum_up, sum_down = (
        lax.psum_scatter(grad_qkv, ("leaf", "seq"), scatter_dimension=0, tiled=True),
        lax.psum_scatter(grad_out, ("leaf", "seq"), scatter_dimension=0, tiled=True),
        lax.psum_scatter(grad_up, ("leaf", "seq"), scatter_dimension=0, tiled=True),
        lax.psum_scatter(grad_down, ("leaf", "seq"), scatter_dimension=0, tiled=True),
    )
    mod_term = cond_own.astype(jnp.float32)[:, None] * grad_modulation[None, :]
    sum_mod = lax.psum_scatter(mod_term, ("leaf", "seq"), scatter_dimension=0, tiled=True)
    return (layer_out[None], grad_tokens[None], sum_qkv, sum_out, sum_up, sum_down, sum_mod)


def solution(mesh):
    rows = P("leaf", "seq", None)
    held = P(("leaf", "seq"), None)
    placed = (rows, rows, P(), P("leaf", None), P("leaf", "seq"), P("leaf", None, None), held, held, held, held, held)
    kernels = mesh.shape["seq"] == 8 and mesh.shape["leaf"] == 4
    return jax.shard_map(
        layer_kernels if kernels else layer_native,
        mesh=mesh,
        in_specs=placed,
        out_specs=(rows, rows, held, held, held, held, held),
        check_vma=False,
    )
```

```python
import functools, math
import jax, jax.numpy as jnp
from jax import lax
from jax.experimental import pallas as pl
from jax.experimental.pallas import tpu as pltpu
from jax.sharding import PartitionSpec as P

MESH = pl.DeviceIdType.MESH
HEADS = 12
EPSILON = 1e-06
NEGATIVE = -1e30
F32 = jnp.float32
BF16 = jnp.bfloat16
GELU_A = math.sqrt(2.0 / math.pi)
GELU_B = 0.044715


class Sems:
    def __init__(self, ref):
        self.ref, self.used = ref, 0

    def one(self):
        self.used += 1
        assert self.used <= self.ref.shape[0]
        return self.ref.at[self.used - 1]


class Place:
    def __init__(self, leaf_count, seg_count):
        self.L, self.S = leaf_count, seg_count
        self.P = seg_count // 2
        self.l, self.s = lax.axis_index("leaf"), lax.axis_index("seq")
        self.c, self.p = lax.rem(self.s, 2), self.s // 2
        self.sib = self.s + 1 - 2 * self.c
        self.inner = (self.l + 1) // 2 == 1
        self.px = self.p + 1 - 2 * lax.rem(self.p, 2)
        self.py = lax.rem(self.p + 2, 4)
        self.pd = lax.rem(self.px + 2, 4)
        self.others = [self.px, self.py, self.pd]
        self.tree = [(self.l, 2 * q + core) for core in (self.c, 1 - self.c) for q in self.others] + [(self.l, self.sib)]

    def leaf(self, k):
        far = lax.rem(self.l + 2, 4) if k >= 2 else self.l
        return far + 1 - 2 * lax.rem(far, 2) if k % 2 else far

    def turn(self, k):
        return jnp.where(self.inner, 4 - k, k)

    def leaf_turn(self, k):
        return jnp.where(self.inner, self.leaf(4 - k), self.leaf(k))

    def at_leaf(self, k):
        return (self.leaf(k), self.s)

    def at_chip(self, q):
        return (self.l, 2 * q + self.c)

    def at_sib(self):
        return (self.l, self.sib)

    def greet(self):
        self.sem = pltpu.get_barrier_semaphore()
        self.peers = [self.at_leaf(k) for k in range(1, self.L)] + self.tree
        for peer in self.peers:
            pl.semaphore_signal(self.sem, inc=1, device_id=peer, device_id_type=MESH)

    def meet(self):
        pl.semaphore_wait(self.sem, len(self.peers))


class Wires:
    def __init__(self, at, send_sems, recv_sems, local_sems):
        self.at = at
        self.send_sems, self.recv_sems, self.local_sems = Sems(send_sems), Sems(recv_sems), Sems(local_sems)
        self.open = []

    def send(self, src, dst, dev):
        copy = pltpu.make_async_remote_copy(
            src_ref=src, dst_ref=dst, send_sem=self.send_sems.one(), recv_sem=self.recv_sems.one(),
            device_id=dev, device_id_type=MESH)
        copy.start()
        self.open.append(copy)
        return copy

    def group(self, whole):
        group = Group(self, whole)
        self.open.append(group)
        return group

    def local(self, src, dst):
        copy = pltpu.make_async_copy(src, dst, self.local_sems.one())
        copy.start()
        return copy

    def sent(self, copies):
        for copy in copies:
            copy.wait_send()
        self.open = [copy for copy in self.open if all(copy is not other for other in copies)]

    def drain(self):
        for copy in self.open:
            copy.wait_send()
        self.open = []


class Group:
    def __init__(self, wires, whole):
        self.at, self.whole = wires.at, whole
        self.send_sem, self.recv_sem = wires.send_sems.one(), wires.recv_sems.one()

    def make(self, src, dst, dev):
        return pltpu.make_async_remote_copy(
            src_ref=src, dst_ref=dst, send_sem=self.send_sem, recv_sem=self.recv_sem, device_id=dev, device_id_type=MESH)

    def send(self, src, dst, dev):
        self.make(src, dst, dev).start()
        return self

    def wait_recv(self):
        self.make(self.whole, self.whole, self.at.at_sib()).wait_recv()

    def wait_send(self):
        self.make(self.whole, self.whole, self.at.at_sib()).wait_send()


class Line:
    def __init__(self, wires, at, view, whole):
        self.w, self.at, self.view = wires, at, view
        self.first = wires.send_sems.one()
        self.onward = wires.send_sems.one()
        self.arrive = [None] + [wires.recv_sems.one() for _ in range(3)]
        self.whole = whole
        wires.open.append(self)

    def leaf(self, unit):
        at = self.at
        if unit < 2:
            return at.leaf(unit)
        return jnp.where(at.l < 2, unit, 3 - unit)

    def make(self, src, leaf, unit, to, sem):
        return pltpu.make_async_remote_copy(
            src_ref=src, dst_ref=self.view(leaf), send_sem=sem, recv_sem=self.arrive[unit], device_id=to, device_id_type=MESH)

    def begin(self, src):
        at = self.at
        self.make(src, at.l, 1, at.at_leaf(1), self.first).start()

        @pl.when(at.inner)
        def _():
            self.make(src, at.l, 2, at.at_leaf(3), self.onward).start()

    def early(self, unit):
        at = self.at
        leaf = self.leaf(unit)
        part = self.view(leaf)

        @pl.when(at.inner)
        def _():
            self.make(part, leaf, unit, at.at_sib(), self.first).wait_recv()
            if unit == 1:
                self.make(part, leaf, 3, at.at_leaf(3), self.onward).start()
            else:
                self.make(part, leaf, unit, at.at_leaf(1), self.onward).start()

    def late(self, unit):
        at = self.at
        leaf = self.leaf(unit)

        @pl.when(jnp.logical_not(at.inner))
        def _():
            self.make(self.view(leaf), leaf, unit, at.at_sib(), self.first).wait_recv()

    def wait_send(self):
        at = self.at
        part = self.view(at.l)
        self.make(part, at.l, 1, at.at_sib(), self.first).wait_send()

        @pl.when(at.inner)
        def _():
            pltpu.make_async_remote_copy(
                src_ref=self.whole, dst_ref=self.whole, send_sem=self.onward, recv_sem=self.arrive[1],
                device_id=at.at_sib(), device_id_type=MESH).wait_send()


class Gather:
    def __init__(self, wires, at, shard, full):
        self.w, self.at, self.shard, self.full = wires, at, shard, full
        count = shard.shape[0]
        self.rows = pl.ds(pl.multiple_of(at.c * count, 8), count)
        self.line = Line(wires, at, lambda leaf: full.at[leaf, at.p, self.rows], full.at[:, at.p, self.rows])
        self.pair = wires.group(full.at[:, :, self.rows])
        self.cross, self.relay = {}, {}
        self.sent_cross, self.sent_relay = wires.send_sems.one(), wires.send_sems.one()
        wires.open.append(self)

    def view(self, unit, chip):
        return self.full.at[self.line.leaf(unit), chip, self.rows]

    def make(self, src, dst, to, sem, recv):
        return pltpu.make_async_remote_copy(
            src_ref=src, dst_ref=dst, send_sem=sem, recv_sem=recv, device_id=self.at.at_chip(to), device_id_type=MESH)

    def begin(self):
        self.own = self.w.local(self.shard, self.view(0, self.at.p))
        self.line.begin(self.shard)

    def stage1(self, unit):
        at = self.at
        mine = self.view(unit, at.p)
        src = mine if unit else self.shard
        self.cross[unit] = [self.make(src, mine, q, self.sent_cross, self.w.recv_sems.one()) for q in (at.px, at.py)]
        for copy in self.cross[unit]:
            copy.start()
        self.pair.send(src, mine, at.at_sib())

    def stage2(self, unit):
        at = self.at
        for i, (q, to) in enumerate(((at.px, at.py), (at.py, at.px))):
            self.cross[unit][i].wait_recv()
            theirs = self.view(unit, q)
            if unit % 2 == i:
                self.relay[unit] = self.make(theirs, theirs, to, self.sent_relay, self.w.recv_sems.one())
                self.relay[unit].start()
            self.pair.send(theirs, theirs, at.at_sib())

    def stage3(self, unit):
        self.relay[unit].wait_recv()
        theirs = self.view(unit, self.at.pd)
        self.pair.send(theirs, theirs, self.at.at_sib())

    def finish(self):
        self.own.wait()
        self.pair.wait_recv()

    def wait_send(self):
        at = self.at
        two, one = self.full.at[:, 0:2, self.rows], self.full.at[:, 0, self.rows]
        spare = self.line.arrive[1]
        self.make(two, two, at.px, self.sent_cross, spare).wait_send()
        self.make(one, one, at.px, self.sent_relay, spare).wait_send()


def add_to(ref, *others):
    total = ref[...].astype(F32)
    for other in others:
        total = total + other[...].astype(F32)
    ref[...] = total.astype(ref.dtype)


class Scatter:
    def __init__(self, wires, at, A, sw, dg, xy, zr, fin, sibr, out):
        self.w, self.at = wires, at
        self.A, self.sw, self.dg, self.xy, self.zr, self.fin, self.sibr, self.out = A, sw, dg, xy, zr, fin, sibr, out

    def cross(self, unit, to, side):
        leaf = self.at.leaf(unit)
        self.x.send(self.A.at[leaf, to], self.xy.at[side, leaf], self.at.at_chip(to))

    def step0(self):
        at = self.at
        self.s = self.w.group(self.sw)
        for i in range(2):
            self.s.send(self.A.at[at.leaf(1 + 2 * i), at.pd], self.sw.at[i], at.at_leaf(1))
        self.x = self.w.group(self.xy)

    def step1(self, units):
        at = self.at
        for unit in units:
            if unit != 2:
                self.cross(unit, at.px, 0)
            if unit != 0:
                self.cross(unit, at.py, 1)

    def step1d(self):
        w, at, A = self.w, self.at, self.A
        self.s.wait_recv()
        self.d = []
        for i, to in enumerate((at.px, at.py)):
            add_to(A.at[at.leaf(2 * i), at.pd], self.sw.at[i])
            self.d.append(w.send(A.at[at.leaf(2 * i), at.pd], self.dg.at[i], at.at_chip(to)))

    def step2(self):
        at, A = self.at, self.A
        for i, to in enumerate((at.py, at.px)):
            self.d[i].wait_recv()
            add_to(A.at[at.leaf(2 * i), to], self.dg.at[i])
            self.cross(2 * i, to, 1 - i)

    def step3(self):
        w, at, A = self.w, self.at, self.A
        self.x.wait_recv()
        self.z = w.group(self.zr)
        for k in (1, 2, 3):
            leaf = at.leaf_turn(k)
            add_to(A.at[leaf, at.p], self.xy.at[0, leaf], self.xy.at[1, leaf])
            self.z.send(A.at[leaf, at.p], self.zr.at[at.turn(k) - 1], (leaf, at.s))
        add_to(A.at[at.l, at.p], self.xy.at[0, at.l], self.xy.at[1, at.l])

    def step4(self):
        w, at = self.w, self.at
        self.z.wait_recv()
        total = self.A[at.l, at.p].astype(F32)
        for k in range(at.L - 1):
            total = total + self.zr[k].astype(F32)
        self.fin[...] = total
        rows = self.fin.shape[0] // 2
        self.f = w.send(self.fin.at[pl.ds(pl.multiple_of(rows * (1 - at.c), 8), rows)], self.sibr, at.at_sib())

    def step5(self):
        at = self.at
        rows, half = self.sibr.shape
        mine = self.fin[pl.ds(pl.multiple_of(rows * at.c, 8), rows), :]
        self.out[:, pl.ds(pl.multiple_of(half * at.c, 128), half)] = mine
        self.f.wait_recv()
        self.out[:, pl.ds(pl.multiple_of(half * (1 - at.c), 128), half)] = self.sibr[...]


class PlaneGather:
    def __init__(self, wires, at, buf):
        self.w, self.at, self.buf = wires, at, buf
        rows = buf.shape[1] // 2
        self.halves = pl.ds(0, rows), pl.ds(rows, rows)

    def send(self, half, q):
        mine = self.buf.at[self.at.p, half]
        return self.w.send(mine, mine, self.at.at_chip(q))

    def first(self):
        at, (up, low) = self.at, self.halves
        self.own = [self.send(up, at.px), self.send(low, at.py)]

    def second(self, parts=(0, 1)):
        at = self.at
        rows = self.buf.shape[1] // 4
        for i in parts:
            self.own += [self.send(pl.ds((2 + i) * rows, rows), at.px), self.send(pl.ds(i * rows, rows), at.py)]

    def start(self):
        self.first()
        self.second()

    def relay(self):
        at = self.at
        self.passed = []
        for half, copy, q, to in zip(self.halves, self.own, (at.px, at.py), (at.py, at.px)):
            copy.wait_recv()
            theirs = self.buf.at[q, half]
            self.passed.append(self.w.send(theirs, theirs, at.at_chip(to)))

    def near(self):
        for copy in self.own[2:]:
            copy.wait_recv()

    def far(self):
        for copy in self.passed:
            copy.wait_recv()


class PlaneSum:
    def __init__(self, wires, at, A, Ad, Ax):
        self.w, self.at, self.A, self.Ad, self.Ax = wires, at, A, Ad, Ax
        self.x = wires.group(Ax)

    def far(self):
        at = self.at
        self.d = [self.w.send(self.A.at[i, at.pd], self.Ad.at[i], at.at_chip(to)) for i, to in enumerate((at.px, at.py))]

    def near(self, i):
        at = self.at
        to = (at.px, at.py)[i]
        self.x.send(self.A.at[i, to], self.Ax.at[i, i], at.at_chip(to))

    def relay(self):
        at = self.at
        for i, to in enumerate((at.py, at.px)):
            self.d[i].wait_recv()
            add_to(self.A.at[i, to], self.Ad.at[i])
            self.x.send(self.A.at[i, to], self.Ax.at[1 - i, i], at.at_chip(to))

    def total(self):
        self.x.wait_recv()
        return [self.A[i, self.at.p].astype(F32) + self.Ax[0, i].astype(F32) + self.Ax[1, i].astype(F32) for i in range(2)]


class LineSum:
    def __init__(self, wires, at, A, As, zr):
        self.w, self.at, self.A, self.As, self.zr = wires, at, A, As, zr

    def pair(self):
        self.s = self.w.send(self.A.at[1 - self.at.c], self.As, self.at.at_sib())

    def line(self):
        at, A = self.at, self.A
        self.s.wait_recv()
        self.z = self.w.group(self.zr)
        for k in (1, 2, 3):
            leaf = at.leaf_turn(k)
            add_to(A.at[at.c, leaf], self.As.at[leaf])
            self.z.send(A.at[at.c, leaf], self.zr.at[at.turn(k) - 1], (leaf, at.s))
        add_to(A.at[at.c, at.l], self.As.at[at.l])

    def total(self):
        self.z.wait_recv()
        total = self.A[self.at.c, self.at.l].astype(F32)
        for k in range(self.at.L - 1):
            total = total + self.zr[k].astype(F32)
        return total


class Columns:
    def __init__(self, wires, at, full, parts):
        self.w, self.at, self.full = wires, at, full
        count = full.shape[2] // 2
        self.rows = pl.ds(pl.multiple_of(at.c * count, 8), count)
        self.first = wires.group(full.at[0, 0:3, self.rows])
        size = at.P // parts
        self.lines = []
        for i in range(parts):
            some = pl.ds(i * size, size)
            held = lambda leaf, some=some: full.at[leaf, some, self.rows]
            self.lines.append(Line(wires, at, held, full.at[:, some, self.rows]))
        self.pair = wires.group(full.at[:, :, self.rows])

    def start(self, parts):
        at = self.at
        mine = self.full.at[at.l, at.p, self.rows]
        for q in at.others:
            self.first.send(parts.at[q], mine, at.at_chip(q))
        self.own = self.w.local(parts.at[at.p], mine)

    def begin(self):
        at = self.at
        self.first.wait_recv()
        self.own.wait()
        for line in self.lines:
            line.begin(line.view(at.l))
        for line in self.lines:
            self.pair.send(line.view(at.l), line.view(at.l), at.at_sib())

    def early(self, unit):
        for line in self.lines:
            line.early(unit)

    def late(self, unit):
        for line in self.lines:
            line.late(unit)
            part = line.view(line.leaf(unit))
            self.pair.send(part, part, self.at.at_sib())


class Rows:
    def __init__(self, wires, at, shard, full):
        self.w, self.at, self.shard, self.full = wires, at, shard, full
        count = shard.shape[0]
        self.rows = pl.ds(pl.multiple_of(at.c * count, 8), count)
        self.line = Line(wires, at, self.held, full.at[:, self.rows])
        self.pair = wires.group(full.at[:, self.rows])

    def held(self, leaf):
        return self.full.at[leaf, self.rows]

    def begin(self):
        at = self.at
        self.own = self.w.local(self.shard, self.held(at.l))
        self.line.begin(self.shard)
        self.pair.send(self.shard, self.held(at.l), at.at_sib())

    def late(self, unit):
        self.line.late(unit)
        part = self.held(self.line.leaf(unit))
        self.pair.send(part, part, self.at.at_sib())


def norm_rows(values):
    centred = values - jnp.mean(values, axis=-1, keepdims=True)
    variance = jnp.mean(centred * centred, axis=-1, keepdims=True)
    rstd = lax.rsqrt(variance + EPSILON)
    return centred * rstd, rstd


def norm_back(grad, normed, rstd):
    return rstd * (grad - jnp.mean(grad, axis=-1, keepdims=True) - normed * jnp.mean(grad * normed, axis=-1, keepdims=True))


def total_rows(values):
    return jnp.sum(values, axis=0, keepdims=True)


def dot(left, right):
    return jnp.dot(left, right, preferred_element_type=F32)


def dot_t(left, right):
    return lax.dot_general(left, right, (((1,), (1,)), ((), ())), preferred_element_type=F32)


def tile(j, size):
    return pl.ds(pl.multiple_of(j * size, size), size)


def condition_column(at, timestep, count, width):
    half = width // 2
    row = (at.l * at.S + at.s) * count + lax.broadcasted_iota(jnp.int32, (count, 1), 0)
    index = jnp.where(row < half, row, row - half).astype(F32)
    angle = timestep.astype(F32) * jnp.exp(-math.log(10000.0) * index / half)
    value = jnp.where(row < half, jnp.cos(angle), jnp.sin(angle))
    return (value / (1.0 + jnp.exp(-value))).astype(BF16).astype(F32)


def fill_bias(at, R):
    _, blocks, seg_count = R.live.shape
    live = R.live[0]
    live = [[live[b, a] for b in range(blocks)] for a in range(seg_count)]

    def fill(k, carry):
        seg = 2 * k + at.c
        current = seg
        reached = [jnp.where(seg == a, 1, 0) for a in range(seg_count)]
        for _ in range(seg_count):
            current = R.parent[0, current]
            reached = [jnp.where(current == a, 1, r) for a, r in enumerate(reached)]
        for a in range(seg_count):
            for b in range(blocks):
                R.bias[k, a * blocks + b] = jnp.where(reached[a] * live[a][b] > 0, 0.0, NEGATIVE)
        return carry

    lax.fori_loop(0, at.P, fill, 0)


def by_blocks(R, score, chip, a):
    blocks = R.live.shape[1]
    rows = score.shape[0] // blocks
    return [(score[b * rows : (b + 1) * rows], R.bias[chip, a * blocks + b]) for b in range(blocks)]


def layer(at, w, R):
    L, S, PC = at.L, at.S, at.P
    T, D = R.tok.shape
    HD = D // HEADS
    HG = HEADS // PC
    GW = HG * HD
    CW = R.Wh.shape[1]
    HU = R.Wu.shape[1]
    DH, TH = D // 2, T // 2
    MR = R.wq.shape[0]
    HB = HU // L
    trunk = S // 2
    NK = PC // 2 + 1
    part = lambda i: slice(i * D, (i + 1) * D)
    head_rows = lambda h: slice(h * HD, (h + 1) * HD)
    go = Gather(w, at, R.wo, R.Go)
    cq, cu = Columns(w, at, R.Gh, 2), Columns(w, at, R.Gu, 1)
    ta, ga = PlaneGather(w, at, R.tX), PlaneGather(w, at, R.gX)
    rd = Rows(w, at, R.wd, R.Gd)

    def key_count(seg):
        return jnp.minimum(seg, trunk) + 1 + jnp.where(seg > trunk, 1, 0)

    at.greet()
    entry = {k: w.local(getattr(R, "in_" + k), getattr(R, k)) for k in ("wq", "modw", "tok", "pos", "wu", "g", "live")}
    for k in ("wq", "modw", "tok", "pos"):
        entry[k].wait()
    wq = R.wq[...].astype(F32)
    for q in range(PC):
        pieces = [wq[:, k * D + q * GW : k * D + (q + 1) * GW] for k in range(3)]
        R.wqs[q] = jnp.concatenate(pieces + [jnp.zeros((MR, CW - 3 * GW), F32)], axis=1).astype(BF16)
    R.tX[at.p] = R.tok[...]
    R.pos2[at.p] = R.pos[...].astype(F32)
    modw = R.modw[...].astype(F32)
    for t in range(L):
        column = condition_column(at, R.time[t], modw.shape[0], D)
        R.cond[t] = column
        R.mpart[t] = total_rows(column * modw)
    at.meet()
    cq.start(R.wqs)
    ta.first()
    mz = w.group(R.mz)
    for k in range(1, L):
        mz.send(R.mpart.at[at.leaf(k)], R.mz.at[k - 1], at.at_leaf(k))
    ps = w.group(R.pos2.at[0:3])
    for q in at.others:
        ps.send(R.pos2.at[at.p], R.pos2.at[at.p], at.at_chip(q))
    for k in ("wu", "g", "live"):
        entry[k].wait()
    R.gX[at.p] = R.g[...]
    wu = R.wu[...].astype(F32)
    for q in range(PC):
        R.wus[q] = jnp.concatenate([wu[:, k * HU + q * HB : k * HU + (q + 1) * HB] for k in range(L)], axis=1).astype(BF16)
    fill_bias(at, R)
    cq.begin()
    mz.wait_recv()
    total = R.mpart[at.l]
    for k in range(L - 1):
        total = total + R.mz[k]
    R.m1[...] = total
    ta.second()
    mp = w.group(R.mp)
    for i, peer in enumerate(at.tree):
        mp.send(R.m1, R.mp.at[i], peer)
    ta.relay()
    cu.start(R.wus)
    go.stage1(0)
    cq.early(1)
    cq.early(2)
    cq.late(1)
    cq.early(3)
    go.begin()
    mp.wait_recv()
    for i in range(S - 1):
        total = total + R.mp[i]
    R.mod[...] = total
    shift_a, scale_a, gate_a, shift_b, scale_b, gate_b = (R.mod[:, part(i)] for i in range(6))

    def modulate(k):
        normed, _ = norm_rows(R.tX[k].astype(F32))
        hidden = (normed * (1.0 + scale_a) + shift_a).astype(BF16)
        R.hA[k] = hidden

    modulate(at.p)
    ga.first()
    slow = jnp.exp(-math.log(10000.0) * 2.0 * lax.broadcasted_iota(jnp.int32, (HD // 2, 1), 0).astype(F32) / HD)
    ps.wait_recv()
    for k in range(PC):
        angles = slow * R.pos2[k]
        R.cos[k] = jnp.cos(angles)
        R.sin[k] = jnp.sin(angles)
    cq.late(2)
    ta.near()
    cq.late(3)
    modulate(at.px)
    modulate(at.py)
    ta.far()
    modulate(at.pd)
    go.line.early(1)
    go.line.early(2)
    cu.begin()
    rd.begin()
    go.line.late(1)
    go.stage1(1)
    cq.pair.wait_recv()
    load = w.local(R.Gh.reshape(D, CW), R.Wh)
    load.wait()

    def project(q):
        cosine, sine = R.cos[q], R.sin[q]
        hidden = R.hA[q]
        for j in range(0, CW, 128):
            rows = dot(hidden, R.Wh[:, j : j + 128]).T
            for i in range(128 // HD):
                kind, h = divmod(j // HD + i, HG)
                if kind == 3:
                    continue
                first, second = rows[i * HD : i * HD + HD // 2], rows[i * HD + HD // 2 : (i + 1) * HD]
                if kind < 2:
                    first, second = first * cosine - second * sine, second * cosine + first * sine
                if kind == 0:
                    first, second = first * HD**-0.5, second * HD**-0.5
                low, high = pl.ds(h * HD, HD // 2), pl.ds(h * HD + HD // 2, HD // 2)
                if kind == 0:
                    R.QT[q, low, :] = first.astype(BF16)
                    R.QT[q, high, :] = second.astype(BF16)
                else:
                    R.KVT[2 * q + at.c, kind - 1, low, :] = first.astype(BF16)
                    R.KVT[2 * q + at.c, kind - 1, high, :] = second.astype(BF16)

    project(at.p)
    go.line.early(3)
    project(at.px)
    project(at.py)
    go.line.late(2)
    go.stage1(2)
    ga.relay()
    project(at.pd)
    sk = w.group(R.KVT.at[0:NK])
    for k in range(NK):
        sk.send(R.KVT.at[2 * k + at.c], R.KVT.at[2 * k + at.c], at.at_sib())
    cu.early(1)
    cu.early(2)
    cu.late(1)

    def flip_k(a, carry):
        for h in range(HG):
            R.kN[a, h] = R.KVT[a, 0, head_rows(h), :].T
        return carry

    for k in range(PC):
        flip_k(2 * k + at.c, 0)
    sk.wait_recv()

    for k in range(NK):
        flip_k(2 * k + 1 - at.c, 0)
    go.line.late(3)
    go.stage1(3)
    ret = w.group(R.hsnd.at[0:3])
    for i, q in enumerate([at.pd, at.px, at.py, at.p]):
        seg = 2 * q + at.c

        def block(j, state, q=q, seg=seg):
            a = jnp.where(j > trunk, seg, j)
            out = []
            raw = [dot(R.kN[a, h], R.QT[q, head_rows(h), :]) for h in range(HG)]
            for h in range(HG):
                m, t, o = state[3 * h : 3 * h + 3]
                score = by_blocks(R, raw[h], q, a)
                m_new = m
                for one, bias in score:
                    m_new = jnp.maximum(m_new, jnp.max(one, axis=0, keepdims=True) + bias)
                alpha = jnp.exp(m - m_new)
                e = jnp.concatenate([jnp.exp(one - (m_new - bias)) for one, bias in score], axis=0)
                out.append((m_new, t * alpha + total_rows(e), o * alpha, e.astype(BF16)))
            out = [(m, t, o + dot(R.KVT[a, 1, head_rows(h), :], e)) for h, (m, t, o, e) in enumerate(out)]
            return tuple(x for one in out for x in one)

        start = (jnp.full((1, T), NEGATIVE, F32), jnp.zeros((1, T), F32), jnp.zeros((HD, T), F32)) * HG
        state = lax.fori_loop(0, key_count(seg), block, start)
        for h in range(HG):
            m, t, o = state[3 * h : 3 * h + 3]
            o = o / t
            R.OT[q, head_rows(h), :] = o
            R.hsnd[q, head_rows(h), :] = o.astype(BF16)
            R.lse[q, h : h + 1, :] = m + jnp.log(t)
        if i < 3:
            ret.send(R.hsnd.at[q], R.attT2.at[0, at.p], at.at_chip(q))
        else:
            own_att = w.local(R.hsnd.at[q], R.attT2.at[0, at.p])
        if i == 0:
            cu.early(3)
            rd.line.early(1)
            rd.line.early(2)
            cu.late(2)
            for u in range(L):
                go.stage2(u)
        if i == 1:
            rd.late(1)
        if i == 2:
            ga.second()
            rd.line.early(3)
            for u in range(L):
                go.stage3(u)
    go.finish()
    load = w.local(R.Go.reshape(D, D), R.Wo)
    own_att.wait()
    ret.wait_recv()
    sib_att = w.send(R.attT2.at[0], R.attT2.at[1], at.at_sib())
    load.wait()
    att = jnp.concatenate([R.attT2[0, k].T for k in range(PC)], axis=1)
    for j in range(0, D, 256):
        lanes = slice(j, j + 256)
        branch = dot(att, R.Wo[:, lanes])
        R.br_a[:, lanes] = branch
        R.middle[:, lanes] = R.tok[:, lanes].astype(F32) + gate_a[:, lanes] * branch
    normed, _ = norm_rows(R.middle[...])
    R.hB[at.p] = (normed * (1.0 + scale_b) + shift_b).astype(BF16)
    hb = PlaneGather(w, at, R.hB)
    hb.start()
    cu.late(3)
    rd.late(2)
    rd.late(3)
    cu.pair.wait_recv()
    loads = [w.local(R.Gu.reshape(D, HU), R.Wu)]
    rd.own.wait()
    rd.pair.wait_recv()
    loads.append(w.local(R.Gd.reshape(HU, D), R.Wd))
    for load in loads:
        load.wait()

    def feed(k):
        hidden = R.hB[k]
        dbb = (gate_b * R.gX[k].astype(F32)).astype(BF16)
        R.dbb[k] = dbb
        lanes = [slice(j, j + 256) for j in range(0, HU, 256)]
        uppers = [dot(hidden, R.Wu[:, some]) for some in lanes]
        grads = [dot_t(dbb, R.Wd[some, :]) for some in lanes]
        for some, u, grad in zip(lanes, uppers, grads):
            square = u * u
            tanh = jnp.tanh(GELU_A * (u + GELU_B * square * u))
            act = (0.5 * u * (1.0 + tanh)).astype(BF16)
            R.active[k, :, some] = act
            slope = 0.5 * (1.0 + tanh) + (0.5 * GELU_A) * u * (1.0 - tanh * tanh) * (1.0 + 3.0 * GELU_B * square)
            R.du[k, :, some] = (grad * slope).astype(BF16)

    def feed_back(k):
        for i in range(2):
            R.dB[i, k] = dot_t(R.du[k, i * TH : (i + 1) * TH, :], R.Wu[...]).astype(BF16)

    sb = PlaneSum(w, at, R.dB, R.dBd, R.dBx)
    feed(at.p)
    for k in range(PC):
        R.haT[k] = R.hA[k].T
    hb.relay()
    hb.near()
    ga.near()
    feed(at.px)
    feed_back(at.px)
    sb.near(0)
    feed(at.py)
    feed_back(at.py)
    sb.near(1)
    hb.far()
    ga.far()
    feed(at.pd)
    feed_back(at.pd)
    sb.far()
    feed_back(at.p)
    scat = {"o": Scatter(w, at, *(getattr(R, x + "o") for x in ("A", "sw", "dg", "xy", "zr", "fin", "sr", "v")))}

    RD = HU // L
    ld, lu, lq = (LineSum(w, at, *(getattr(R, x + n) for x in ("A", "As", "zr"))) for n in ("d", "u", "q"))

    def down_grad(i, carry):
        total = dot(R.actT[0, tile(i, RD), :], R.dbb[0])
        for k in range(1, PC):
            total = total + dot(R.actT[k, tile(i, RD), :], R.dbb[k])
        for core in range(2):
            R.Ad[core, i] = total[core * (RD // 2) : (core + 1) * (RD // 2)].astype(BF16)
        return carry

    for k in range(PC):
        R.actT[k] = R.active[k].T
    lax.fori_loop(0, L, down_grad, 0)
    ld.pair()
    def flip_v(a, carry):
        for h in range(HG):
            R.vN[a, h] = R.KVT[a, 1, head_rows(h), :].T
        R.acc[a] = jnp.zeros((2, GW, T), F32)
        return carry

    lax.fori_loop(0, S, flip_v, 0)
    for k in range(PC):
        R.dpT[k, 3 * GW : CW, :] = jnp.zeros((CW - 3 * GW, T), BF16)
    sb.relay()

    def by_core(A, i, total):
        for core in range(2):
            rows = [total[(2 * k + core) * MR : (2 * k + core + 1) * MR] for k in range(PC)]
            A[core, i] = jnp.concatenate(rows, axis=0).astype(BF16)

    def up_grad(i, carry):
        total = dot(R.hBT[0, tile(i, D // L), :], R.du[0])
        for k in range(1, PC):
            total = total + dot(R.hBT[k, tile(i, D // L), :], R.du[k])
        by_core(R.Au, i, total)
        return carry

    for k in range(PC):
        R.hBT[k] = R.hB[k].T
    lax.fori_loop(0, L, up_grad, 0)
    lu.pair()
    ld.line()
    sc = PlaneSum(w, at, R.bB, R.bBd, R.bBx)
    for k in (at.pd, at.px, at.py, at.p):
        for i in range(2):
            R.bB[i, k] = dot(R.active[k, i * TH : (i + 1) * TH, :], R.Wd[...]).astype(BF16)
    lu.line()
    dh = jnp.concatenate(sb.total(), axis=0)
    normed, rstd = norm_rows(R.middle[...])
    R.gm[:, part(3)] = total_rows(dh)
    R.gm[:, part(4)] = total_rows(dh * normed)
    dmid = R.g[...].astype(F32) + norm_back(dh * (1.0 + scale_b), normed, rstd)
    R.dmid[...] = dmid
    R.gm[:, part(2)] = total_rows(dmid * R.br_a[...])
    dba = (gate_a * dmid).astype(BF16)
    R.dba[...] = dba
    for h in range(2):
        R.dbah[h] = dba[:, h * DH : (h + 1) * DH]
    sib_dba = w.send(R.dbah.at[1 - at.c], R.dbas, at.at_sib())
    w.sent([ret])
    for j in range(PC):
        R.hsnd[j] = dot_t(R.Wo[j * GW : (j + 1) * GW, :], R.dba[...]).astype(BF16)
    dos = [w.send(R.hsnd.at[q], R.dOT.at[at.p], at.at_chip(q)) for q in at.others]
    own_do = w.local(R.hsnd.at[at.p], R.dOT.at[at.p])
    sc.far()
    sc.near(0)
    sc.near(1)
    own_do.wait()

    def unturn(first, second, q):
        cosine, sine = R.cos[q], R.sin[q]
        return jnp.concatenate([first * cosine + second * sine, second * cosine - first * sine], axis=0)

    for i, q in enumerate([at.p, at.px, at.py, at.pd]):
        seg = 2 * q + at.c
        if i:
            dos[i - 1].wait_recv()
        delta = [total_rows(R.dOT[q, head_rows(h), :].astype(F32) * R.OT[q, head_rows(h), :]) for h in range(HG)]

        def block(j, dqs, q=q, seg=seg, delta=delta):
            a = jnp.where(j > trunk, seg, j)
            out = []
            raw = [dot(R.kN[a, h], R.QT[q, head_rows(h), :]) for h in range(HG)]
            draw = [dot(R.vN[a, h], R.dOT[q, head_rows(h), :]) for h in range(HG)]
            pairs = []
            for h in range(HG):
                lse = R.lse[q, h : h + 1, :]
                prob = jnp.concatenate([jnp.exp(one - (lse - bias)) for one, bias in by_blocks(R, raw[h], q, a)], axis=0)
                pairs.append((prob.astype(BF16), (prob * (draw[h] - delta[h])).astype(BF16)))
            for h, (prob, ds) in enumerate(pairs):
                rows = head_rows(h)
                out.append(dqs[h] + dot(R.KVT[a, 0, rows, :], ds))
                R.acc[a, 0, rows, :] += dot_t(R.QT[q, rows, :], ds)
                R.acc[a, 1, rows, :] += dot_t(R.dOT[q, rows, :], prob)
            return tuple(out)

        dqs = lax.fori_loop(0, key_count(seg), block, (jnp.zeros((HD, T), F32),) * HG)
        for h in range(HG):
            dq = dqs[h] * HD**-0.5
            R.dpT[q, head_rows(h), :] = unturn(dq[: HD // 2], dq[HD // 2 :], q).astype(BF16)
        if i == 0:
            RB2 = D // (L * PC)
            sib_dba.wait_recv()
            sib_att.wait_recv()
            attT = [R.attT2[i].reshape(D, T) for i in range(2)]
            block = dot(attT[0], R.dbah[at.c]) + dot(attT[1], R.dbas[...])
            for i in range(L * PC):
                R.Ao[i // PC, i % PC] = block[i * RB2 : (i + 1) * RB2].astype(BF16)
            scat["o"].step0()
            scat["o"].step1((1, 3, 0, 2))
        if i == 2:
            sc.relay()
    sk = w.group(R.acs)
    for k in range(NK):
        sk.send(R.acc.at[2 * k + 1 - at.c], R.acs.at[k], at.at_sib())
    sk.wait_recv()
    for k in range(PC):
        for i in range(2):
            grad = R.acc[2 * k + at.c, i]
            if k < NK:
                grad = grad + R.acs[k, i]
            for h in range(HG):
                one = grad[head_rows(h)]
                if i == 0:
                    one = unturn(one[: HD // 2], one[HD // 2 :], k)
                R.dpT[k, (i + 1) * GW + h * HD : (i + 1) * GW + (h + 1) * HD, :] = one.astype(BF16)
    scat["o"].step1d()
    sa = PlaneSum(w, at, R.dA, R.dAd, R.dAx)
    for n, q in enumerate((at.pd, at.px, at.py, at.p)):
        for i in range(2):
            R.dA[i, q] = dot(R.Wh[i * DH : (i + 1) * DH, :], R.dpT[q]).astype(BF16)
        if n == 0:
            sa.far()
        elif n < 3:
            sa.near(n - 1)
    scat["o"].step2()
    def proj_grad(i, carry):
        total = dot_t(R.haT[0, tile(i, D // L), :], R.dpT[0])
        for k in range(1, PC):
            total = total + dot_t(R.haT[k, tile(i, D // L), :], R.dpT[k])
        by_core(R.Aq, i, total)
        return carry

    lax.fori_loop(0, L, proj_grad, 0)
    lq.pair()
    lq.line()
    sa.relay()
    branch = sc.total()
    for i in range(2):
        rows = slice(i * TH, (i + 1) * TH)
        R.vlo[rows, :] = (R.middle[rows, :] + gate_b * branch[i]).astype(BF16)
    R.gm[:, part(5)] = total_rows(R.g[...].astype(F32) * jnp.concatenate(branch, axis=0))
    results = [w.local(R.vlo, R.lo)]
    R.vd[...] = ld.total()
    results.append(w.local(R.vd, R.od))

    def to_chips(fin, buf):
        group = w.group(buf.at[0:3])
        mine = lambda q: fin.at[pl.ds(pl.multiple_of(q * MR, 8), MR)]
        for q in at.others:
            group.send(mine(q), buf.at[at.p], at.at_chip(q))
        return group, w.local(mine(at.p), buf.at[at.p])

    R.finu[...] = lu.total()
    ru = to_chips(R.finu, R.ru)
    scat["o"].step3()
    dh = jnp.concatenate([half.T for half in sa.total()], axis=1)
    normed, rstd = norm_rows(R.tok[...].astype(F32))
    R.gm[:, part(0)] = total_rows(dh)
    R.gm[:, part(1)] = total_rows(dh * normed)
    gp = w.group(R.gp)
    for i, peer in enumerate(at.tree):
        gp.send(R.gm, R.gp.at[i], peer)
    R.vgt[...] = R.dmid[...] + norm_back(dh * (1.0 + scale_a), normed, rstd)
    results.append(w.local(R.vgt, R.gt))
    R.finq[...] = lq.total()
    rq = to_chips(R.finq, R.rq)
    gp.wait_recv()
    total = R.gm[...]
    for i in range(S - 1):
        total = total + R.gp[i]
    R.gtree[at.l] = total
    gz = w.group(R.gtree.at[0:3])
    for k in range(1, L):
        gz.send(R.gtree.at[at.l], R.gtree.at[at.l], at.at_leaf(k))
    for copy in ru:
        (copy.wait_recv if copy is ru[0] else copy.wait)()
    R.vu[...] = jnp.concatenate([R.ru[q][:, k * HB : (k + 1) * HB] for k in range(L) for q in range(PC)], axis=1)
    results.append(w.local(R.vu, R.ou))
    scat["o"].step4()
    scat["o"].step5()
    results.append(w.local(R.vo, R.oo))
    rq[1].wait()
    rq[0].wait_recv()
    R.vq[...] = jnp.concatenate([R.rq[q][:, k * GW : (k + 1) * GW] for k in range(3) for q in range(PC)], axis=1)
    results.append(w.local(R.vq, R.oq))
    gz.wait_recv()
    total = R.cond[0] * R.gtree[0]
    for t in range(1, L):
        total = total + R.cond[t] * R.gtree[t]
    R.vm[...] = total
    results.append(w.local(R.vm, R.om))
    for copy in results:
        copy.wait()


class Refs:
    def __init__(self, **refs):
        self.__dict__.update(refs)


def call_layer(L, S, tok, g, time, parent, pos, live, wq, wo, wu, wd, modw):
    T, D = tok.shape
    FF = wu.shape[1]
    PC, HD = S // 2, D // HEADS
    HG = HEADS // PC
    GW = HG * HD
    CW = -(-3 * GW // 128) * 128
    NM, MR = L * S, wq.shape[0]
    sd = jax.ShapeDtypeStruct
    DM, V = pltpu.SemaphoreType.DMA, pltpu.VMEM
    entry = dict(wq=wq, modw=modw, tok=tok, pos=pos, wu=wu, g=g, live=live)
    ins = dict(time=time, parent=parent, wo=wo, wd=wd)
    ins.update({"in_" + k: v for k, v in entry.items()})
    HU = FF // PC
    outs = dict(Go=sd((L, PC, 2 * MR, D), BF16), Gh=sd((L, PC, 2 * MR, CW), BF16), Gu=sd((L, PC, 2 * MR, HU), BF16),
                Gd=sd((L, 2 * wd.shape[0], D), BF16))
    last = dict(lo=((T, D), BF16), gt=((T, D), F32), oq=((MR, 3 * D), F32), oo=((MR, D), F32),
                ou=((MR, FF), F32), od=((FF // NM, D), F32), om=((MR, 6 * D), F32))
    outs.update({k: sd(*v) for k, v in last.items()})
    M6 = 6 * D
    scr = dict(
        Wh=V((D, CW), BF16), Wo=V((D, D), BF16), Wu=V((D, HU), BF16), Wd=V((HU, D), BF16), wqs=V((PC, MR, CW), BF16), wus=V((PC, MR, HU), BF16),
        bias=pltpu.SMEM((PC, live.size), F32), cond=V((L, MR, 1), F32),
        pos2=V((PC, 1, T), F32), cos=V((PC, HD // 2, T), F32), sin=V((PC, HD // 2, T), F32),
        mpart=V((L, 1, M6), F32), mz=V((L - 1, 1, M6), F32), m1=V((1, M6), F32), mp=V((S - 1, 1, M6), F32),
        mod=V((1, M6), F32),
        tX=V((PC, T, D), BF16), gX=V((PC, T, D), BF16), hA=V((PC, T, D), BF16), haT=V((PC, D, T), BF16), QT=V((PC, GW, T), BF16),
        KVT=V((S, 2, GW, T), BF16), kN=V((S, HG, T, HD), BF16), OT=V((PC, GW, T), F32), lse=V((PC, 8, T), F32),
        hsnd=V((PC, GW, T), BF16), attT2=V((2, PC, GW, T), BF16), br_a=V((T, D), F32), middle=V((T, D), F32),
        hB=V((PC, T, D), BF16), hBT=V((PC, D, T), BF16), active=V((PC, T, HU), BF16), actT=V((PC, HU, T), BF16),
        dbb=V((PC, T, D), BF16), du=V((PC, T, HU), BF16), dh=V((T, D), F32), dmid=V((T, D), F32),
        dB=V((2, PC, T // 2, D), BF16), dBd=V((2, T // 2, D), BF16), dBx=V((2, 2, T // 2, D), BF16),
        bB=V((2, PC, T // 2, D), BF16), bBd=V((2, T // 2, D), BF16), bBx=V((2, 2, T // 2, D), BF16),
        Au=V((2, L, PC * MR, HU), BF16), Asu=V((L, PC * MR, HU), BF16), zru=V((L - 1, PC * MR, HU), BF16),
        finu=V((PC * MR, HU), F32), ru=V((PC, MR, HU), F32),
        Ad=V((2, L, HU // L // 2, D), BF16), Asd=V((L, HU // L // 2, D), BF16), zrd=V((L - 1, HU // L // 2, D), BF16),
        dba=V((T, D), BF16), dbah=V((2, T, D // 2), BF16), dbas=V((T, D // 2), BF16),
        dOT=V((PC, GW, T), BF16), vN=V((S, HG, T, HD), BF16),
        acc=V((S, 2, GW, T), F32), acs=V((PC // 2 + 1, 2, GW, T), F32), dpT=V((PC, CW, T), BF16),
        dA=V((2, PC, D // 2, T), BF16), dAd=V((2, D // 2, T), BF16), dAx=V((2, 2, D // 2, T), BF16),
        Aq=V((2, L, PC * MR, CW), BF16), Asq=V((L, PC * MR, CW), BF16), zrq=V((L - 1, PC * MR, CW), BF16),
        finq=V((PC * MR, CW), F32), rq=V((PC, MR, CW), F32),
        gm=V((1, M6), F32), gp=V((S - 1, 1, M6), F32), gtree=V((L, 1, M6), F32))
    for n, rows, cols in (("o", D, D),):
        rb, half = rows // (L * PC), cols // 2
        scr["A" + n] = V((L, PC, rb, half), BF16)
        scr["sw" + n] = V((2, rb, half), BF16)
        scr["dg" + n] = V((2, rb, half), BF16)
        scr["xy" + n] = V((2, L, rb, half), BF16)
        scr["zr" + n] = V((L - 1, rb, half), BF16)
        scr["fin" + n] = V((rb, half), F32)
        scr["sr" + n] = V((rb // 2, half), F32)
    scr.update({k: V(v.shape, v.dtype) for k, v in entry.items()})
    for k, v in last.items():
        scr["v" + k.removeprefix("o") if k != "lo" else "vlo"] = V(*v)
    scr.update(send_sems=DM((78,)), recv_sems=DM((93,)), local_sems=DM((26,)))
    space = dict.fromkeys((*ins, *outs), pltpu.HBM)
    space.update(dict.fromkeys(("time", "parent"), pltpu.SMEM))
    spec = lambda k: pl.BlockSpec(memory_space=space.get(k, pltpu.VMEM))

    def kernel(*refs):
        R = Refs(**dict(zip(list(ins) + list(outs) + list(scr), refs)))
        at = Place(L, S)
        w = Wires(at, R.send_sems, R.recv_sems, R.local_sems)
        layer(at, w, R)
        w.drain()

    res = pl.pallas_call(
        kernel, out_shape=list(outs.values()), in_specs=[spec(k) for k in ins], out_specs=[spec(k) for k in outs],
        scratch_shapes=list(scr.values()),
        compiler_params=pltpu.CompilerParams(collective_id=1, has_side_effects=True, vmem_limit_bytes=64 << 20),
    )(*ins.values())
    return dict(zip(outs, res))


def hand_out(*arrays):
    count = len(arrays)

    def kernel(*refs):
        sources, targets, held, sems = refs[:count], refs[count : 2 * count], refs[2 * count : 3 * count], refs[-1]
        arrive = [pltpu.make_async_copy(x, y, sems.at[0, i]) for i, (x, y) in enumerate(zip(sources, held))]
        leave = [pltpu.make_async_copy(x, y, sems.at[1, i]) for i, (x, y) in enumerate(zip(held, targets))]
        for copy in arrive:
            copy.start()
        for first, second in zip(arrive, leave):
            first.wait()
            second.start()
        for copy in leave:
            copy.wait()

    hbm = pl.BlockSpec(memory_space=pltpu.HBM)
    return pl.pallas_call(
        kernel, out_shape=[jax.ShapeDtypeStruct(a.shape, a.dtype) for a in arrays],
        in_specs=[hbm] * count, out_specs=[hbm] * count,
        scratch_shapes=[pltpu.VMEM(a.shape, a.dtype) for a in arrays] + [pltpu.SemaphoreType.DMA((2, count))],
    )(*arrays)


def layer_kernels(
    tokens, cotangent, timesteps, parent, positions, block_live, qkv_weight, out_weight, up_weight, down_weight, mod_weight
):
    f = call_layer(
        lax.axis_size("leaf"), lax.axis_size("seq"), tokens[0], cotangent[0], timesteps, parent, positions, jnp.swapaxes(block_live, 1, 2),
        qkv_weight, out_weight, up_weight, down_weight, mod_weight,
    )
    lo, gt, *rest = hand_out(*(f[k] for k in ("lo", "gt", "oq", "oo", "ou", "od", "om")))
    return (lo[None], gt[None], *rest)


def layer_norm(values):
    centred = values - jnp.mean(values, axis=-1, keepdims=True)
    variance = jnp.mean(centred * centred, axis=-1, keepdims=True)
    return centred * lax.rsqrt(variance + EPSILON)


def time_embed(step_values, model_width):
    half_width = model_width // 2
    freqs = jnp.exp(-math.log(10000.0) * jnp.arange(half_width, dtype=jnp.float32) / half_width)
    angles = step_values.astype(jnp.float32)[..., None] * freqs
    return jnp.concatenate([jnp.cos(angles), jnp.sin(angles)], axis=-1)


def rope_tables(places, head_dim):
    half_dim = head_dim // 2
    inverse = jnp.exp(-math.log(10000.0) * 2.0 * jnp.arange(half_dim, dtype=jnp.float32) / head_dim)
    angles = places.astype(jnp.float32)[:, None] * inverse[None, :]
    return (jnp.cos(angles), jnp.sin(angles))


def rotate(values, cosine, sine):
    half_dim = values.shape[-1] // 2
    first = values[..., :half_dim]
    second = values[..., half_dim:]
    cos_wide = cosine[:, None, :]
    sin_wide = sine[:, None, :]
    return jnp.concatenate(
        [first * cos_wide - second * sin_wide, second * cos_wide + first * sin_wide], axis=-1
    )


def rotate_back(grads, cosine, sine):
    half_dim = grads.shape[-1] // 2
    first = grads[..., :half_dim]
    second = grads[..., half_dim:]
    cos_wide = cosine[:, None, :]
    sin_wide = sine[:, None, :]
    return jnp.concatenate(
        [first * cos_wide + second * sin_wide, second * cos_wide - first * sin_wide], axis=-1
    )


def ancestor_row(parent_row, seg_index, seg_count):
    seg_range = jnp.arange(seg_count, dtype=jnp.int32)

    def climb(step_index, state_now):
        current, reached = state_now
        current = parent_row[current]
        return (current, reached | (seg_range == current))

    return lax.fori_loop(0, seg_count, climb, (seg_index, seg_range == seg_index))[1]


def attend_keys(state_now, query_rot, key_block, value_block, key_ok, score_scale):
    maximum_old, total_old, accum_old = state_now
    scores = (
        jnp.einsum("qhd,khd->hqk", query_rot, key_block, preferred_element_type=jnp.float32)
        * score_scale
    )
    visible = key_ok[None, None, :]
    scores = jnp.where(visible, scores, NEGATIVE)
    maximum_new = jnp.maximum(maximum_old, jnp.max(scores, axis=-1))
    weights_p = jnp.where(visible, jnp.exp(scores - maximum_new[..., None]), 0.0)
    rescale = jnp.exp(maximum_old - maximum_new)
    total_new = total_old * rescale + jnp.sum(weights_p, axis=-1)
    accum_new = accum_old * rescale[..., None] + jnp.einsum(
        "hqk,khd->hqd",
        weights_p.astype(jnp.bfloat16),
        value_block,
        preferred_element_type=jnp.float32,
    )
    return (maximum_new, total_new, accum_new)


def score_grads(
    query_rot, grad_attended, log_total, delta_rows, key_block, value_block, mask_wide, score_scale
):
    scores = (
        jnp.einsum("qhd,khd->hqk", query_rot, key_block, preferred_element_type=jnp.float32)
        * score_scale
    )
    probs = jnp.where(mask_wide, jnp.exp(scores - log_total[..., None]), 0.0)
    grad_probs = jnp.einsum(
        "qhd,khd->hqk", grad_attended, value_block, preferred_element_type=jnp.float32
    )
    grad_scores = (probs * (grad_probs - delta_rows[..., None])).astype(jnp.bfloat16)
    return (probs, grad_scores)


def query_only(
    grad_query,
    query_rot,
    grad_attended,
    log_total,
    delta_rows,
    key_block,
    value_block,
    key_ok,
    score_scale,
):
    probs, grad_scores = score_grads(
        query_rot,
        grad_attended,
        log_total,
        delta_rows,
        key_block,
        value_block,
        key_ok[None, None, :],
        score_scale,
    )
    return (
        grad_query
        + jnp.einsum("hqk,khd->qhd", grad_scores, key_block, preferred_element_type=jnp.float32)
        * score_scale
    )


def layer_native(
    tokens,
    cotangent,
    timesteps,
    parent,
    positions,
    block_live,
    qkv_weight,
    out_weight,
    up_weight,
    down_weight,
    mod_weight,
):
    seg_count = lax.axis_size("seq")
    seg_index = lax.axis_index("seq")
    tree_index = lax.axis_index("leaf")
    tok_rows = tokens.shape[1]
    model_width = tokens.shape[2]
    head_count = HEADS
    head_dim = model_width // head_count
    score_scale = head_dim ** (-0.5)
    tree_rows = tok_rows * seg_count
    qkv_all, out_all, up_all, down_all = (
        lax.all_gather(qkv_weight, ("leaf", "seq"), axis=0, tiled=True),
        lax.all_gather(out_weight, ("leaf", "seq"), axis=0, tiled=True),
        lax.all_gather(up_weight, ("leaf", "seq"), axis=0, tiled=True),
        lax.all_gather(down_weight, ("leaf", "seq"), axis=0, tiled=True),
    )
    condition = jax.nn.silu(time_embed(timesteps, model_width)).astype(jnp.bfloat16)
    mod_all = lax.all_gather(mod_weight, ("leaf", "seq"), axis=0, tiled=True)
    cond_own = lax.dynamic_index_in_dim(condition, tree_index, 0, keepdims=False)
    modulation = jnp.dot(cond_own[None, :], mod_all, preferred_element_type=jnp.float32)[0]
    shift_a, scale_a, gate_a, shift_b, scale_b, gate_b = jnp.split(modulation, 6)
    inputs_f = tokens[0].astype(jnp.float32)
    normed_a = layer_norm(inputs_f)
    hidden_a = (normed_a * (1.0 + scale_a) + shift_a).astype(jnp.bfloat16)
    projected = jnp.dot(hidden_a, qkv_all, preferred_element_type=jnp.float32).reshape(
        tok_rows, 3, head_count, head_dim
    )
    cosine, sine = rope_tables(positions[0], head_dim)
    query_rot = rotate(projected[:, 0], cosine, sine).astype(jnp.bfloat16)
    key_rot = rotate(projected[:, 1], cosine, sine).astype(jnp.bfloat16)
    value_rows = projected[:, 2].astype(jnp.bfloat16)
    key_flat = key_rot.reshape(tok_rows, model_width)
    value_flat = value_rows.reshape(tok_rows, model_width)
    reached = ancestor_row(parent[0], seg_index, seg_count)
    live_blocks = block_live.shape[2]
    live_tokens = jnp.repeat(block_live[0] > 0, tok_rows // live_blocks, axis=1)
    key_allowed = (reached[:, None] & live_tokens).reshape(tree_rows)
    start_state = (
        jnp.full((head_count, tok_rows), NEGATIVE, jnp.float32),
        jnp.zeros((head_count, tok_rows), jnp.float32),
        jnp.zeros((head_count, tok_rows, head_dim), jnp.float32),
    )
    key_part = lax.all_gather(key_flat, "seq", axis=0, tiled=True)
    value_part = lax.all_gather(value_flat, "seq", axis=0, tiled=True)
    count_keys = key_part.shape[0]
    block_size = tok_rows
    block_count = count_keys // block_size
    allow_part = key_allowed.reshape(block_count, block_size)
    key_blocks = key_part.reshape(block_count, block_size, head_count, head_dim)
    value_blocks = value_part.reshape(block_count, block_size, head_count, head_dim)

    def advance(state_now, block_in):
        return (
            attend_keys(state_now, query_rot, block_in[0], block_in[1], block_in[2], score_scale),
            None,
        )

    maximum_run, total_run, accum_run = lax.scan(
        advance, start_state, (key_blocks, value_blocks, allow_part)
    )[0]
    attended_heads = jnp.transpose(accum_run / total_run[..., None], (1, 0, 2))
    log_total = maximum_run + jnp.log(total_run)
    attended = attended_heads.reshape(tok_rows, model_width).astype(jnp.bfloat16)
    branch_a = jnp.dot(attended, out_all, preferred_element_type=jnp.float32)
    middle = inputs_f + gate_a * branch_a
    normed_b = layer_norm(middle)
    hidden_b = (normed_b * (1.0 + scale_b) + shift_b).astype(jnp.bfloat16)
    upper = jnp.dot(hidden_b, up_all, preferred_element_type=jnp.float32)
    active = jax.nn.gelu(upper).astype(jnp.bfloat16)
    branch_b = jnp.dot(active, down_all, preferred_element_type=jnp.float32)
    layer_out = (middle + gate_b * branch_b).astype(jnp.bfloat16)
    qkv_back, out_back, up_back, down_back = (
        lax.all_gather(qkv_weight, ("leaf", "seq"), axis=0, tiled=True),
        lax.all_gather(out_weight, ("leaf", "seq"), axis=0, tiled=True),
        lax.all_gather(up_weight, ("leaf", "seq"), axis=0, tiled=True),
        lax.all_gather(down_weight, ("leaf", "seq"), axis=0, tiled=True),
    )
    grad_out_rows = cotangent[0].astype(jnp.float32)
    grad_branch_b = (gate_b * grad_out_rows).astype(jnp.bfloat16)
    dgate_b = jnp.sum(grad_out_rows * branch_b, axis=0)
    grad_down = jnp.einsum("qf,qd->fd", active, grad_branch_b, preferred_element_type=jnp.float32)
    grad_active = jnp.einsum(
        "qd,fd->qf", grad_branch_b, down_back, preferred_element_type=jnp.float32
    )
    gelu_pull = jax.vjp(jax.nn.gelu, upper)[1]
    grad_upper = gelu_pull(grad_active)[0].astype(jnp.bfloat16)
    grad_up = jnp.einsum("qd,qf->df", hidden_b, grad_upper, preferred_element_type=jnp.float32)
    grad_hidden_b = jnp.einsum("qf,df->qd", grad_upper, up_back, preferred_element_type=jnp.float32)
    dshift_b = jnp.sum(grad_hidden_b, axis=0)
    dscale_b = jnp.sum(grad_hidden_b * normed_b, axis=0)
    norm_pull_b = jax.vjp(layer_norm, middle)[1]
    grad_middle = grad_out_rows + norm_pull_b(grad_hidden_b * (1.0 + scale_b))[0]
    grad_branch_a = (gate_a * grad_middle).astype(jnp.bfloat16)
    dgate_a = jnp.sum(grad_middle * branch_a, axis=0)
    grad_out = jnp.einsum("qi,qd->id", attended, grad_branch_a, preferred_element_type=jnp.float32)
    grad_attended = jnp.einsum(
        "qd,id->qi", grad_branch_a, out_back, preferred_element_type=jnp.float32
    ).astype(jnp.bfloat16)
    grad_att_heads = grad_attended.reshape(tok_rows, head_count, head_dim)
    delta_rows = jnp.einsum("qhd,qhd->hq", grad_att_heads.astype(jnp.float32), attended_heads)
    start_query = jnp.zeros((tok_rows, head_count, head_dim), jnp.float32)
    key_part = lax.all_gather(key_flat, "seq", axis=0, tiled=True)
    value_part = lax.all_gather(value_flat, "seq", axis=0, tiled=True)
    count_keys = key_part.shape[0]
    block_size = tok_rows
    block_count = count_keys // block_size
    allow_part = key_allowed.reshape(block_count, block_size)
    key_blocks = key_part.reshape(block_count, block_size, head_count, head_dim)
    value_blocks = value_part.reshape(block_count, block_size, head_count, head_dim)

    def advance(grad_now, block_in):
        return (
            query_only(
                grad_now,
                query_rot,
                grad_att_heads,
                log_total,
                delta_rows,
                block_in[0],
                block_in[1],
                block_in[2],
                score_scale,
            ),
            None,
        )

    grad_query = lax.scan(advance, start_query, (key_blocks, value_blocks, allow_part))[0]
    seg_range = jnp.arange(seg_count, dtype=jnp.int32)
    every_reach = jax.vmap(lambda one_seg: ancestor_row(parent[0], one_seg, seg_count))(seg_range)
    sees_mine = every_reach[:, seg_index]
    own_live = lax.dynamic_index_in_dim(live_tokens, seg_index, 0, keepdims=False)
    total_all, delta_all = (
        lax.all_gather(jnp.transpose(log_total), "seq", axis=0, tiled=True),
        lax.all_gather(jnp.transpose(delta_rows), "seq", axis=0, tiled=True),
    )
    query_flat = query_rot.reshape(tok_rows, model_width)
    grad_key_acc = jnp.zeros((tok_rows, head_count, head_dim), jnp.float32)
    grad_value_acc = jnp.zeros((tok_rows, head_count, head_dim), jnp.float32)
    query_part = lax.all_gather(query_flat, "seq", axis=0, tiled=True)
    grad_part = lax.all_gather(grad_attended, "seq", axis=0, tiled=True)
    count_rows = query_part.shape[0]
    block_size = tok_rows
    block_count = count_rows // block_size
    row_seg = jnp.arange(count_rows, dtype=jnp.int32) // tok_rows
    row_ok = sees_mine[row_seg].reshape(block_count, block_size)
    total_part = total_all.reshape(block_count, block_size, head_count)
    delta_part = delta_all.reshape(block_count, block_size, head_count)
    query_blocks = query_part.reshape(block_count, block_size, head_count, head_dim)
    grad_blocks = grad_part.reshape(block_count, block_size, head_count, head_dim)

    def advance(acc_now, block_in):
        key_acc, value_acc = acc_now
        query_block, grad_block, total_block, delta_block, ok_block = block_in
        mask_wide = ok_block[None, :, None] & own_live[None, None, :]
        probs, grad_scores = score_grads(
            query_block,
            grad_block,
            jnp.transpose(total_block),
            jnp.transpose(delta_block),
            key_rot,
            value_rows,
            mask_wide,
            score_scale,
        )
        key_acc = (
            key_acc
            + jnp.einsum(
                "hqk,qhd->khd", grad_scores, query_block, preferred_element_type=jnp.float32
            )
            * score_scale
        )
        value_acc = value_acc + jnp.einsum(
            "hqk,qhd->khd",
            probs.astype(jnp.bfloat16),
            grad_block,
            preferred_element_type=jnp.float32,
        )
        return ((key_acc, value_acc), None)

    grad_key_rows, grad_value_heads = lax.scan(
        advance,
        (grad_key_acc, grad_value_acc),
        (query_blocks, grad_blocks, total_part, delta_part, row_ok),
    )[0]
    grad_value_rows = grad_value_heads.reshape(tok_rows, model_width)
    grad_query_pre = rotate_back(grad_query, cosine, sine).reshape(tok_rows, model_width)
    grad_key_pre = rotate_back(grad_key_rows, cosine, sine).reshape(tok_rows, model_width)
    grad_projected = jnp.concatenate(
        [grad_query_pre, grad_key_pre, grad_value_rows], axis=-1
    ).astype(jnp.bfloat16)
    grad_qkv = jnp.einsum("qi,qj->ij", hidden_a, grad_projected, preferred_element_type=jnp.float32)
    grad_hidden_a = jnp.einsum(
        "qj,ij->qi", grad_projected, qkv_back, preferred_element_type=jnp.float32
    )
    dshift_a = jnp.sum(grad_hidden_a, axis=0)
    dscale_a = jnp.sum(grad_hidden_a * normed_a, axis=0)
    norm_pull_a = jax.vjp(layer_norm, inputs_f)[1]
    grad_tokens = grad_middle + norm_pull_a(grad_hidden_a * (1.0 + scale_a))[0]
    grad_modulation = jnp.concatenate([dshift_a, dscale_a, dgate_a, dshift_b, dscale_b, dgate_b])
    sum_qkv, sum_out, sum_up, sum_down = (
        lax.psum_scatter(grad_qkv, ("leaf", "seq"), scatter_dimension=0, tiled=True),
        lax.psum_scatter(grad_out, ("leaf", "seq"), scatter_dimension=0, tiled=True),
        lax.psum_scatter(grad_up, ("leaf", "seq"), scatter_dimension=0, tiled=True),
        lax.psum_scatter(grad_down, ("leaf", "seq"), scatter_dimension=0, tiled=True),
    )
    mod_term = cond_own.astype(jnp.float32)[:, None] * grad_modulation[None, :]
    sum_mod = lax.psum_scatter(mod_term, ("leaf", "seq"), scatter_dimension=0, tiled=True)
    return (layer_out[None], grad_tokens[None], sum_qkv, sum_out, sum_up, sum_down, sum_mod)


def solution(mesh):
    rows = P("leaf", "seq", None)
    held = P(("leaf", "seq"), None)
    placed = (rows, rows, P(), P("leaf", None), P("leaf", "seq"), P("leaf", None, None), held, held, held, held, held)
    kernels = mesh.shape["seq"] == 8 and mesh.shape["leaf"] == 4
    return jax.shard_map(
        layer_kernels if kernels else layer_native,
        mesh=mesh,
        in_specs=placed,
        out_specs=(rows, rows, held, held, held, held, held),
        check_vma=False,
    )
```
